32 devices in a mesh: dp: 8 (over z, y), mp: 4 (over x, core).
Axes of the slice: x: 2, y: 2, z: 4, core: 2. Of those that a mesh axis runs over, the one named last changes fastest.
Arguments:
- tokens: bfloat16 [16384, 1024], P(('dp', 'mp')), may hold values from -60 to 60
- cotangent: bfloat16 [16384, 1024], P(('dp', 'mp')), may hold values from -6 to 6
- item_lengths: int32 [128], P('dp'), may hold values from 49 to 196, as said below
- item_group: int32 [128], P('dp'), may hold values from 0 to 7
- group_count: int32 [8], replicated, may hold values from 1 to 4
- grid_scale: float32 [8], replicated, may hold values from 0.5 to 2
- norm_gain: float32 [1024], replicated, may hold values from 0.5 to 1.5
- norm_shift: float32 [1024], replicated, may hold values from -2 to 2
- query_weight: bfloat16 [1024, 1024], P(None, 'mp'), may hold values from -0.1875 to 0.1875
- query_bias: float32 [1024], P('mp'), may hold values from -2 to 2
- key_weight: bfloat16 [1024, 1024], P(None, 'mp'), may hold values from -0.1875 to 0.1875
- value_weight: bfloat16 [1024, 1024], P(None, 'mp'), may hold values from -0.1875 to 0.1875
- value_bias: float32 [1024], P('mp'), may hold values from -2 to 2
- output_weight: bfloat16 [1024, 1024], P('mp'), may hold values from -1.5 to 1.5
- output_bias: float32 [1024], replicated, may hold values from -2 to 2
- hidden_gain: float32 [1024], replicated, may hold values from 0.5 to 1.5
- hidden_shift: float32 [1024], replicated, may hold values from -2 to 2
- up_weight: bfloat16 [1024, 4096], P(None, 'mp'), may hold values from -0.1875 to 0.1875
- up_bias: float32 [4096], P('mp'), may hold values from -2 to 2
- down_weight: bfloat16 [4096, 1024], P('mp'), may hold values from -0.09375 to 0.09375
- down_bias: float32 [1024], replicated, may hold values from -2 to 2
Outputs:
- layer_output: bfloat16 [16384, 1024], P(('dp', 'mp'))
- tokens_grad: float32 [16384, 1024], P(('dp', 'mp'))
- norm_gain_grad: float32 [1024], replicated
- norm_shift_grad: float32 [1024], replicated
- query_weight_grad: float32 [1024, 1024], P(None, 'mp')
- query_bias_grad: float32 [1024], P('mp')
- key_weight_grad: float32 [1024, 1024], P(None, 'mp')
- value_weight_grad: float32 [1024, 1024], P(None, 'mp')
- value_bias_grad: float32 [1024], P('mp')
- output_weight_grad: float32 [1024, 1024], P('mp')
- output_bias_grad: float32 [1024], replicated
- hidden_gain_grad: float32 [1024], replicated
- hidden_shift_grad: float32 [1024], replicated
- up_weight_grad: float32 [1024, 4096], P(None, 'mp')
- up_bias_grad: float32 [4096], P('mp')
- down_weight_grad: float32 [4096, 1024], P('mp')
- down_bias_grad: float32 [1024], replicated
The draws below stay inside these ranges and needn't reach their ends.
Inputs may be any that keep to these rules, and one draw needn't show every extreme that they name: `item_lengths`: the items of a slice take its first 1960 rows: items 2i and 2i + 1 of a slice have lengths that add up to 245, and every slice has one pair of lengths 196 and 49.
All inputs are finite; a program needn't handle non-finite values.
Results may differ from the reference program's by a relative error of at most 0.018.
Values may be sent and summed in bfloat16 or wider, within the bound.
A program may use at most 192 MiB of HBM per device.

```python
import math
import jax
import jax.numpy as jnp
from jax import lax

D = 1024
HEAD_DIM = 64
FF = 4096
SIDE = 14
GROUPS = 8
PAIRS = 8
LONGEST = 196
SHORTEST = 49
PAIR_LEN = 245
TOK_DEV = 2048
ITEMS_DEV = 16
TOKENS = 16384
VALID = 15680
N_DP = 8
N_MP = 4


def draw_tokens(key, part):
    noise_key, offset_key = jax.random.split(key, 2)
    fraction = jnp.arange(TOKENS, dtype=jnp.float32)[:, None] / TOKENS
    offset = jnp.clip(0.5 * jax.random.normal(offset_key, (1, D), jnp.float32), -1.5, 1.5)
    noise = jnp.clip(jax.random.normal(noise_key, (TOKENS, D), jnp.float32), -4.0, 4.0)
    factor = 1.0 + 2.0 * fraction
    return ((noise + offset) * factor).astype(jnp.bfloat16)


def draw_item_lengths(key, part):
    pair_key, where_key, which_key = jax.random.split(key, 3)
    slices = TOKENS // TOK_DEV
    first_len = jax.random.randint(pair_key, (slices, PAIRS), SHORTEST, LONGEST + 1)
    chosen = jax.random.randint(where_key, (slices, 1), 0, PAIRS)
    extreme = SHORTEST + (LONGEST - SHORTEST) * jax.random.randint(which_key, (slices, 1), 0, 2)
    first_len = jnp.where(jnp.arange(PAIRS)[None, :] == chosen, extreme, first_len)
    return jnp.stack([first_len, PAIR_LEN - first_len], axis=-1).reshape(slices * ITEMS_DEV).astype(jnp.int32)


def with_ends(entries, key, smallest, top_value):
    extent = entries.shape
    spot = [jax.random.randint(jax.random.fold_in(key, axis), (), 0, extent[axis]) for axis in range(len(extent))]
    entries = entries.at[tuple(spot)].set(smallest)
    longest = extent.index(max(extent))
    spot[longest] = (spot[longest] + 1) % extent[longest]
    return entries.at[tuple(spot)].set(top_value)


def shard_levels(stream_key, extent, cuts, smallest, top_value):
    loudness = 1.0
    for dim, blocks in cuts:
        heights = jax.random.uniform(jax.random.fold_in(jax.random.fold_in(stream_key, 6), dim), (blocks,), jnp.float32, smallest / len(cuts), top_value / len(cuts))
        loudness = loudness * jnp.repeat(jnp.exp(heights), extent[dim] // blocks).reshape((-1,) + (1,) * (len(extent) - 1 - dim))
    return loudness


def scatter_about(rng, dims, scale, most, shards=(), kind=jnp.bfloat16):
    values = scale * jax.random.normal(rng, dims, jnp.float32)
    if shards:
        values = values * shard_levels(rng, dims, shards, -0.22, 0.18)
    return jnp.clip(values, -most, most).astype(kind)


def setup_inputs(seed: int = 0) -> dict:
    keys = jax.random.split(jax.random.key(seed), 22)
    return {
        "tokens": draw_tokens(jax.random.fold_in(keys[21], 71), 0),
        "cotangent": scatter_about(keys[1], (TOKENS, D), 1.0, 6.0, ((0, 32),)),
        "item_lengths": draw_item_lengths(jax.random.fold_in(keys[21], 71), 0),
        "item_group": with_ends(jax.random.randint(keys[3], (N_DP * ITEMS_DEV,), 0, GROUPS), jax.random.fold_in(keys[3], 1), 0, GROUPS - 1).astype(jnp.int32),
        "group_count": with_ends(jax.random.randint(keys[4], (GROUPS,), 1, 5), jax.random.fold_in(keys[4], 1), 1, 4).astype(jnp.int32),
        "grid_scale": jnp.clip(jnp.exp(jax.random.uniform(keys[5], (GROUPS,), jnp.float32, math.log(0.5), math.log(2.0))), 0.5, 2.0),
        "norm_gain": jnp.clip(1.0 + 0.1 * jax.random.normal(keys[6], (D,), jnp.float32), 0.5, 1.5),
        "norm_shift": scatter_about(keys[7], (D,), 0.3, 2.0, (), jnp.float32),
        "query_weight": scatter_about(keys[8], (D, D), D ** -0.5, 0.1875, ((1, 4),)),
        "query_bias": scatter_about(keys[9], (D,), 0.3, 2.0, ((0, 4),), jnp.float32),
        "key_weight": scatter_about(keys[10], (D, D), D ** -0.5, 0.1875, ((1, 4),)),
        "value_weight": scatter_about(keys[11], (D, D), D ** -0.5, 0.1875, ((1, 4),)),
        "value_bias": scatter_about(keys[12], (D,), 0.3, 2.0, ((0, 4),), jnp.float32),
        "output_weight": scatter_about(keys[13], (D, D), (D // 64) ** -0.5, 1.5, ((0, 4),)),
        "output_bias": scatter_about(keys[14], (D,), 0.3, 2.0, (), jnp.float32),
        "hidden_gain": jnp.clip(1.0 + 0.1 * jax.random.normal(keys[15], (D,), jnp.float32), 0.5, 1.5),
        "hidden_shift": scatter_about(keys[16], (D,), 0.3, 2.0, (), jnp.float32),
        "up_weight": scatter_about(keys[17], (D, FF), D ** -0.5, 0.1875, ((1, 4),)),
        "up_bias": scatter_about(keys[18], (FF,), 0.3, 2.0, ((0, 4),), jnp.float32),
        "down_weight": scatter_about(keys[19], (FF, D), FF ** -0.5, 0.09375, ((0, 4),)),
        "down_bias": scatter_about(keys[20], (D,), 0.3, 2.0, (), jnp.float32),
    }


@jax.custom_vjp
def low(v):
    return lax.optimization_barrier(v.astype(jnp.bfloat16)).astype(jnp.float32)

@jax.custom_vjp
def low_back(v):
    return v

def low_keep(v):
    return (low(v), None)

def low_pass(kept, grad):
    return (grad,)

def back_keep(v):
    return (v, None)

def back_low(kept, grad):
    return (low(grad),)
low.defvjp(low_keep, low_pass)
low_back.defvjp(back_keep, back_low)
precise = lax.Precision.HIGHEST

def matmul(first_matrix, second_matrix):
    return jnp.dot(first_matrix, second_matrix, precision=precise, preferred_element_type=jnp.float32)

def normalize(values, gain, shift):
    center = values - lax.optimization_barrier(jnp.mean(values, axis=-1, keepdims=True))
    spread = lax.optimization_barrier(jnp.mean(center * center, axis=-1, keepdims=True))
    return center * lax.rsqrt(spread + 1e-06) * gain + shift

def position_table(position, row_scale):
    quarter = D // 4
    frequency = jnp.exp(-math.log(10000.0) * jnp.arange(quarter, dtype=jnp.float32) / quarter)
    across = (position // SIDE).astype(jnp.float32) * row_scale
    sideways = (position % SIDE).astype(jnp.float32) * row_scale
    first_angle = across[..., None] * frequency
    second_angle = sideways[..., None] * frequency
    return jnp.concatenate([jnp.sin(first_angle), jnp.cos(first_angle), jnp.sin(second_angle), jnp.cos(second_angle)], axis=-1)

def layout(item_lengths, item_group, group_count, grid_scale):
    lengths = item_lengths.reshape(N_DP, ITEMS_DEV)
    item_ends = jnp.cumsum(lengths, axis=1)
    starts = item_ends - lengths
    rowids = jnp.arange(TOK_DEV, dtype=jnp.int32)
    owner_ids = lax.optimization_barrier(jnp.sum((rowids[None, :, None] >= item_ends[:, None, :]).astype(jnp.int32), axis=2))
    member = owner_ids[:, :, None] == jnp.arange(ITEMS_DEV, dtype=jnp.int32)[None, None, :]
    first_row = lax.optimization_barrier(jnp.sum(jnp.where(member, starts[:, None, :], 0), axis=2))
    position = rowids[None, :] - first_row
    groups = item_group.reshape(N_DP, ITEMS_DEV)
    chosen = groups[:, :, None] == jnp.arange(GROUPS, dtype=jnp.int32)[None, None, :]
    item_scale = lax.optimization_barrier(jnp.sum(jnp.where(chosen, grid_scale[None, None, :], 0.0), axis=2))
    item_weight = lax.optimization_barrier(jnp.sum(jnp.where(chosen, group_count[None, None, :], 0), axis=2)).astype(jnp.float32)
    member_f = member.astype(jnp.float32)
    row_scale = lax.optimization_barrier(jnp.sum(member_f * item_scale[:, None, :], axis=2))
    row_weight = lax.optimization_barrier(jnp.sum(member_f * item_weight[:, None, :], axis=2)) / jnp.mean(item_weight)
    valid_rows = (owner_ids < ITEMS_DEV).astype(jnp.float32)
    grid_table = position_table(position, row_scale) * valid_rows[..., None]
    return (owner_ids, valid_rows.reshape(TOKENS), row_weight.reshape(TOKENS), grid_table.reshape(TOKENS, D))

def attend(queries, keys_here, values_here, owner_ids):
    head_width = queries.shape[1]
    head_count = head_width // HEAD_DIM

    def one_slice(pieces):
        query_rows, key_rows, value_rows, owner_rows = pieces
        query_heads = query_rows.reshape(TOK_DEV, head_count, HEAD_DIM)
        key_heads = key_rows.reshape(TOK_DEV, head_count, HEAD_DIM)
        value_heads = value_rows.reshape(TOK_DEV, head_count, HEAD_DIM)
        scores = jnp.einsum('qhd,khd->hqk', query_heads, key_heads, precision=precise) / math.sqrt(HEAD_DIM)
        scores = low_back(scores)
        same_item = owner_rows[:, None] == owner_rows[None, :]
        scores = jnp.where(same_item[None], scores, -1e+30)
        weights_soft = jax.nn.softmax(scores, axis=-1)
        context = jnp.einsum('hqk,khd->qhd', low(weights_soft), value_heads, precision=precise)
        return context.reshape(TOK_DEV, head_width)
    result = lax.map(jax.checkpoint(one_slice), (queries.reshape(N_DP, TOK_DEV, head_width), keys_here.reshape(N_DP, TOK_DEV, head_width), values_here.reshape(N_DP, TOK_DEV, head_width), owner_ids))
    return result.reshape(TOKENS, head_width)

def forward(params, tokens_f, owner_ids, valid_rows, grid_table):
    norm_gain, norm_shift, query_weight, query_bias, key_weight, value_weight, value_bias, output_weight, output_bias, hidden_gain, hidden_shift, up_weight, up_bias, down_weight, down_bias = params
    weighted = tokens_f * valid_rows[:, None]
    column_mean = lax.optimization_barrier(jnp.sum(weighted, axis=0)) / VALID
    spread = lax.optimization_barrier(jnp.sum(weighted * tokens_f, axis=0)) / VALID - column_mean * column_mean
    stream = (tokens_f - column_mean) * lax.rsqrt(spread + 1e-05) + grid_table
    normed = low(normalize(stream, norm_gain, norm_shift))
    head_width = D // N_MP
    hidden_width = FF // N_MP
    attended = output_bias
    for shard_index in range(N_MP):
        columns = slice(shard_index * head_width, (shard_index + 1) * head_width)
        copied = low_back(normed)
        queries = low(low_back(matmul(copied, query_weight[:, columns]) + query_bias[columns]))
        keys_here = low(low_back(matmul(copied, key_weight[:, columns])))
        values_here = low(low_back(matmul(copied, value_weight[:, columns]) + value_bias[columns]))
        context = low(low_back(attend(queries, keys_here, values_here, owner_ids)))
        attended = attended + low(matmul(context, output_weight[columns, :]))
    attended = low_back(attended)
    middle = stream + attended
    hidden_in = low(normalize(middle, hidden_gain, hidden_shift))
    mixed = down_bias
    for shard_index in range(N_MP):
        columns = slice(shard_index * hidden_width, (shard_index + 1) * hidden_width)
        copied = low_back(hidden_in)
        preact = low_back(matmul(copied, up_weight[:, columns]) + up_bias[columns])
        active = low(jax.nn.gelu(preact, approximate=False))
        mixed = mixed + low(matmul(active, down_weight[columns, :]))
    mixed = low_back(mixed)
    return middle + mixed

def reference(tokens, cotangent, item_lengths, item_group, group_count, grid_scale, norm_gain, norm_shift, query_weight, query_bias, key_weight, value_weight, value_bias, output_weight, output_bias, hidden_gain, hidden_shift, up_weight, up_bias, down_weight, down_bias):
    owner_ids, valid_rows, row_weight, grid_table = layout(item_lengths, item_group, group_count, grid_scale)
    params = tuple((weight.astype(jnp.float32) for weight in (norm_gain, norm_shift, query_weight, query_bias, key_weight, value_weight, value_bias, output_weight, output_bias, hidden_gain, hidden_shift, up_weight, up_bias, down_weight, down_bias)))
    tokens_f = tokens.astype(jnp.float32)

    def apply(params_in, tokens_in):
        return forward(params_in, tokens_in, owner_ids, valid_rows, grid_table)
    result, pullback = jax.vjp(apply, params, tokens_f)
    grad_out = cotangent.astype(jnp.float32) * row_weight[:, None]
    param_grads, tokens_grad = pullback(grad_out)
    return (result.astype(jnp.bfloat16), tokens_grad, param_grads[0], param_grads[1], param_grads[2], param_grads[3], param_grads[4], param_grads[5], param_grads[6], param_grads[7], param_grads[8], param_grads[9], param_grads[10], param_grads[11], param_grads[12], param_grads[13], param_grads[14])
```

```python
import functools
import math

import jax
import jax.numpy as jnp
from jax import lax
from jax.experimental import pallas as pl
from jax.experimental.pallas import tpu as pltpu
from jax.sharding import PartitionSpec as P

D = 1024
HEAD_DIM = 64
SIDE = 14
PAIRS = 8
PAIR_LEN = 245
WINDOW = 256
BF = jnp.bfloat16
F32 = jnp.float32
PADDING = 88


def dot(a, b):
    return lax.dot_general(a, b, (((1,), (0,)), ((), ())), preferred_element_type=F32)


def dot_rows(a, b):
    return lax.dot_general(a, b, (((0,), (0,)), ((), ())), preferred_element_type=F32)


def dot_cols(a, b):
    return lax.dot_general(a, b, (((1,), (1,)), ((), ())), preferred_element_type=F32)


def swap_mp(v, mask):
    count = lax.axis_size("mp")
    return lax.ppermute(v, "mp", [(i, i ^ mask) for i in range(count)])


def swap_dp(v, mask):
    count = lax.axis_size("dp")
    return lax.ppermute(v, "dp", [(i, i ^ mask) for i in range(count)])


def dp_bits():
    return lax.axis_size("dp").bit_length() - 1


def all_sum(v):
    v = v + swap_mp(v, 1) + swap_mp(v, 2) + swap_mp(v, 3)
    bit = 0
    bits = dp_bits()
    while bit < bits:
        if bit + 1 < bits:
            v = v + swap_dp(v, 1 << bit) + swap_dp(v, 2 << bit) + swap_dp(v, 3 << bit)
            bit += 2
        else:
            v = v + swap_dp(v, 1 << bit)
            bit += 1
    return v


def dp_bit(bit):
    return (lax.axis_index("dp") >> bit) & 1


def join(mine, other, bit):
    return jnp.where(
        dp_bit(bit) == 0,
        jnp.concatenate([mine, other], axis=0),
        jnp.concatenate([other, mine], axis=0),
    )


def chunk_index():
    index = jnp.int32(0)
    for bit in range(dp_bits()):
        index = index * 2 + dp_bit(bit)
    return index


def fetch_across(w):
    rows = w.shape[0] // lax.axis_size("dp")
    mine = lax.dynamic_slice_in_dim(w, chunk_index() * rows, rows, axis=0)
    got = swap_mp(mine, 2)
    for bit in reversed(range(dp_bits())):
        got = join(got, swap_dp(got, 1 << bit), bit)
    return got


def reduce_pieces(pieces):
    half = pieces[1].shape[0]
    got = swap_mp(jnp.concatenate([pieces[1], pieces[3]], axis=0), 1)
    across = pieces[2].astype(F32) + got[half:].astype(F32)
    own = pieces[0].astype(F32) + got[:half].astype(F32)
    total = own + swap_mp(across.astype(BF), 2).astype(F32)
    for bit in range(dp_bits()):
        size = total.shape[0] // 2
        side = dp_bit(bit)
        send = lax.dynamic_slice_in_dim(total, (1 - side) * size, size, axis=0).astype(BF)
        keep = lax.dynamic_slice_in_dim(total, side * size, size, axis=0)
        total = keep + swap_dp(send, 1 << bit).astype(F32)
    total = total.astype(BF)
    for bit in reversed(range(dp_bits())):
        total = join(total, swap_dp(total, 1 << bit), bit)
    return total.astype(F32)


def stats(v):
    mean = jnp.mean(v, axis=-1, keepdims=True)
    center = v - mean
    spread = jnp.mean(center * center, axis=-1, keepdims=True)
    inverse = lax.rsqrt(spread + 1e-06)
    return center * inverse, inverse


def norm_back(grad, unit, inverse, gain):
    f = grad * gain
    return inverse * (
        f
        - jnp.mean(f, axis=-1, keepdims=True)
        - unit * jnp.mean(f * unit, axis=-1, keepdims=True)
    )


def blocks_of(rows):
    return [(first, min(WINDOW, rows - first)) for first in range(0, rows, WINDOW)]


def head_scores(qkv_ref, same, first, size, h, width):
    q = qkv_ref[first : first + size, h * HEAD_DIM : (h + 1) * HEAD_DIM]
    k = qkv_ref[first : first + size, width + h * HEAD_DIM : width + (h + 1) * HEAD_DIM]
    v = qkv_ref[first : first + size, 2 * width + h * HEAD_DIM : 2 * width + (h + 1) * HEAD_DIM]
    scores = jnp.where(same, dot_cols(q, k) * (1.0 / math.sqrt(HEAD_DIM)), -1e30)
    weights = jnp.exp(scores - jnp.max(scores, axis=-1, keepdims=True))
    weights = weights * (1.0 / jnp.sum(weights, axis=-1, keepdims=True))
    return q, k, v, weights


def attend_kernel(qkv_ref, col_ref, row_ref, out_ref):
    rows, width = out_ref.shape
    for first, size in blocks_of(rows):
        same = col_ref[first : first + size, :] == row_ref[:, first : first + size]
        for h in range(width // HEAD_DIM):
            q, k, v, weights = head_scores(qkv_ref, same, first, size, h, width)
            out_ref[first : first + size, h * HEAD_DIM : (h + 1) * HEAD_DIM] = dot(
                weights.astype(BF), v
            ).astype(BF)


def attend_back_kernel(qkv_ref, grad_ref, col_ref, row_ref, out_ref):
    rows, width = grad_ref.shape
    factor = 1.0 / math.sqrt(HEAD_DIM)
    for first, size in blocks_of(rows):
        same = col_ref[first : first + size, :] == row_ref[:, first : first + size]
        for h in range(width // HEAD_DIM):
            q, k, v, weights = head_scores(qkv_ref, same, first, size, h, width)
            grad = grad_ref[first : first + size, h * HEAD_DIM : (h + 1) * HEAD_DIM]
            soft = dot_cols(grad, v)
            center = jnp.sum(weights * soft, axis=-1, keepdims=True)
            grad_scores = (weights * (soft - center)).astype(BF)
            for part, value in enumerate(
                (
                    dot(grad_scores, k) * factor,
                    dot_rows(grad_scores, q) * factor,
                    dot_rows(weights.astype(BF), grad),
                )
            ):
                lane = part * width + h * HEAD_DIM
                out_ref[first : first + size, lane : lane + HEAD_DIM] = value.astype(BF)


def attend(qkv, owner_col, owner_row, groups):
    rows, width = qkv.shape[0], qkv.shape[1] // (3 * groups)
    return pl.pallas_call(
        attend_kernel,
        grid=(groups,),
        in_specs=[
            pl.BlockSpec((rows, 3 * width), lambda r: (0, r)),
            pl.BlockSpec((rows, 1), lambda r: (0, 0)),
            pl.BlockSpec((1, rows), lambda r: (0, 0)),
        ],
        out_specs=pl.BlockSpec((rows, width), lambda r: (0, r)),
        out_shape=jax.ShapeDtypeStruct((rows, groups * width), BF),
        name="attend",
    )(qkv, owner_col, owner_row)


def attend_back(qkv, grad, owner_col, owner_row, groups):
    rows, width = grad.shape[0], grad.shape[1] // groups
    return pl.pallas_call(
        attend_back_kernel,
        grid=(groups,),
        in_specs=[
            pl.BlockSpec((rows, 3 * width), lambda r: (0, r)),
            pl.BlockSpec((rows, width), lambda r: (0, r)),
            pl.BlockSpec((rows, 1), lambda r: (0, 0)),
            pl.BlockSpec((1, rows), lambda r: (0, 0)),
        ],
        out_specs=pl.BlockSpec((rows, 3 * width), lambda r: (0, r)),
        out_shape=jax.ShapeDtypeStruct((rows, 3 * groups * width), BF),
        name="attend_back",
    )(qkv, grad, owner_col, owner_row)


def gelu_parts(preact):
    phi = 0.5 * (1.0 + lax.erf(preact * (1.0 / math.sqrt(2.0))))
    slope = phi + preact * jnp.exp(-0.5 * preact * preact) * (1.0 / math.sqrt(2.0 * math.pi))
    return (preact * phi).astype(BF), slope


HALO = 80
MESH = pl.DeviceIdType.MESH


def places():
    mp = lax.axis_index("mp")
    dp = lax.axis_index("dp")
    y = dp % 2
    z = dp // 2
    sibling = mp + 1 - 2 * (mp % 2)
    opposite = mp + 2 - 4 * (mp // 2)
    across = opposite + 1 - 2 * (mp % 2)
    mp_peers = [{"mp": sibling}, {"mp": opposite}, {"mp": across}]
    y_peer = {"dp": dp + 1 - 2 * y}
    z_places = [(z + m) % 4 for m in (1, 2, 3)]
    z_peers = [{"dp": place * 2 + y} for place in z_places]
    return mp, y, z, mp_peers, y_peer, z_places, z_peers


def greet(peers):
    barrier = pltpu.get_barrier_semaphore()
    for peer in peers:
        pl.semaphore_signal(barrier, inc=1, device_id=peer, device_id_type=MESH)
    pl.semaphore_wait(barrier, len(peers))


def remote(source, target, send, recv, peer):
    return pltpu.make_async_remote_copy(
        src_ref=source,
        dst_ref=target,
        send_sem=send,
        recv_sem=recv,
        device_id=peer,
        device_id_type=MESH,
    )


def loop(count, body):
    def step(i, carry):
        body(i)
        return carry

    lax.fori_loop(0, count, step, 0)


def block_rows(i, size):
    return pl.ds(pl.multiple_of(i * size, size), size)


def start_all(copies):
    for copy in copies:
        copy.start()


def wait_recv_all(copies):
    for copy in copies:
        copy.wait_recv()


def item_of_rows(row, lengths, mp):
    window = row >> 8
    offset = row & (WINDOW - 1)
    length = jnp.where(window == 0, lengths[4 * mp], lengths[4 * mp + 2])
    second = jnp.where(offset >= length, 1, 0)
    in_pair = (window < 2) & (offset < PAIR_LEN)
    is_padding = (window == 2) & (offset < PADDING) & (mp == 3)
    return 2 * window + second, offset - second * length, in_pair, is_padding


def owner_of_rows(row, lengths, mp):
    item, _, in_pair, is_padding = item_of_rows(row, lengths, mp)
    return jnp.where(in_pair, item, jnp.where(is_padding, 16, -1))


def choose_item(item, values):
    result = jnp.where(item == 0, values[0], 0.0)
    for j in (1, 2, 3):
        result = jnp.where(item == j, values[j], result)
    return result


def joined(tiles, first):
    return jnp.concatenate([tiles[first + j : first + j + 1, :] for j in range(8)], axis=1)


def forward_kernel(
    lengths,
    groups,
    counts,
    scales,
    gain,
    shift,
    output_bias,
    hidden_gain,
    hidden_shift,
    query_bias,
    value_bias,
    up_bias,
    tokens_ref,
    cotangent_ref,
    query_ref,
    key_ref,
    value_ref,
    output_ref,
    up_ref,
    down_ref,
    tokens_out,
    cotangent_out,
    sums_out,
    stream_out,
    middle_out,
    normed_out,
    qkv_out,
    context_out,
    hidden_out,
    grad_mixed_out,
    active_out,
    grad_pre_out,
    wqkv_out,
    wo_out,
    wup_out,
    wdown_out,
    tokens_ext,
    cotangent_ext,
    tokens,
    cotangent,
    stream,
    middle,
    normed,
    qkv,
    context,
    hidden,
    grad_mixed,
    active,
    grad_pre,
    wqkv,
    wo,
    wup,
    wdown,
    sums,
    bias,
    part,
    from_mp,
    from_y,
    from_z,
    own_sem,
    halo_sem,
    store_sem,
    stat_send,
    stat_recv,
    bias_send,
    bias_recv,
    pair_send,
    pair_recv,
    x_send,
    x_recv,
    z_send,
    z_recv,
    y_send,
    y_recv,
    fwd_send,
    fwd_recv,
):
    mp, y, z, mp_peers, y_peer, z_places, z_peers = places()
    sibling, opposite, _ = mp_peers
    rows_here = tokens_ref.shape[0]
    rows = tokens.shape[0]
    width = query_ref.shape[1]
    blocks = rows // 32

    items = [
        (key_ref, 0, D, wqkv, width, width, False),
        (value_ref, 0, D, wqkv, 2 * width, width, False),
        (query_ref, 0, D, wqkv, 0, width, True),
        (output_ref, 0, width, wo, 0, D, False),
        (up_ref, 0, D // 2, wup, 0, D, False),
        (up_ref, D // 2, D // 2, wup, 0, D, False),
        (down_ref, 3 * D // 4, D // 4, wdown, 0, D, False),
        (down_ref, 0, 3 * D // 4, wdown, 0, D, True),
    ]
    KEY, VALUE, QUERY, OUTPUT, UP_A, UP_B, DOWN_A, DOWN_B = range(8)

    def source(i, start, size):
        return items[i][0].at[pl.ds(items[i][1] + start, size)]

    def place(i, r, start, size):
        _, first, _, ref, column, columns, _ = items[i]
        return ref.at[r, pl.ds(first + start, size), pl.ds(column, columns)]

    def part_of(i, first, eighths):
        size = items[i][2] // 8
        return pl.multiple_of(first * size, size), eighths * size

    own_copies = [
        pltpu.make_async_copy(
            source(i, 0, items[i][2]), place(i, 0, 0, items[i][2]), own_sem.at[i]
        )
        for i in range(8)
    ]
    pair_copies = [
        remote(
            source(i, 0, items[i][2]),
            place(i, 1, 0, items[i][2]),
            pair_send.at[i],
            pair_recv.at[i],
            sibling,
        )
        for i in range(8)
    ]

    def x_copy(i):
        start, size = (0, items[i][2]) if items[i][6] else part_of(i, y * 4 + z, 1)
        return remote(
            source(i, start, size), place(i, 2, start, size), x_send.at[i], x_recv.at[i], opposite
        )

    def z_copies(i):
        start, size = part_of(i, y * 4 + z, 1)
        view = place(i, 2, start, size)
        return [
            remote(view, view, z_send.at[i, m], z_recv.at[i, m], peer)
            for m, peer in enumerate(z_peers)
        ]

    def y_copy(i):
        start, size = part_of(i, y * 4, 4)
        view = place(i, 2, start, size)
        return remote(view, view, y_send.at[i], y_recv.at[i], y_peer)

    def fwd_copy(i):
        size = items[i][2]
        return remote(
            place(i, 2, 0, size), place(i, 3, 0, size), fwd_send.at[i], fwd_recv.at[i], sibling
        )

    def x_to_z(i):
        x_copy(i).wait_recv()
        start_all(z_copies(i))

    def z_to_y(i):
        wait_recv_all(z_copies(i))
        y_copy(i).start()

    def y_to_pair(i):
        (x_copy(i) if items[i][6] else y_copy(i)).wait_recv()
        fwd_copy(i).start()

    keep = [
        pltpu.make_async_copy(ref, ext.at[pl.ds(HALO, rows_here)], halo_sem.at[which, 2])
        for which, (ref, ext) in enumerate(
            ((tokens_ref, tokens_ext), (cotangent_ref, cotangent_ext))
        )
    ]
    start_all(keep)
    start_all(own_copies)
    bias[0, 0:1, :] = query_bias[...]
    bias[0, 1:2, :] = value_bias[...]
    for j in range(4):
        bias[0, 2 + j : 3 + j, :] = up_bias[:, j * width : (j + 1) * width]
    bias[0, 6:8, :] = jnp.zeros((2, width), F32)

    weights = [counts[groups[4 * mp + j]].astype(F32) for j in range(4)]
    weight_part = weights[0] + weights[1] + weights[2] + weights[3]
    keep[0].wait()

    def add_rows(i, carry):
        block = tokens_ext[pl.ds(pl.multiple_of(HALO + i * 16, 16), 16), :].astype(F32)
        row = mp * rows_here + i * 16 + lax.broadcasted_iota(jnp.int32, (16, 1), 0)
        kept = jnp.where(row < PAIRS * PAIR_LEN, block, 0.0)
        return carry[0] + kept, carry[1] + kept * block

    zero = jnp.zeros((16, D), F32)
    first, second = lax.fori_loop(0, rows_here // 16, add_rows, (zero, zero))
    first = jnp.sum(first, axis=0, keepdims=True)
    second = jnp.sum(second, axis=0, keepdims=True)
    for j in range(8):
        part[0, j : j + 1, :] = first[:, j * 128 : (j + 1) * 128]
        part[0, 8 + j : 9 + j, :] = second[:, j * 128 : (j + 1) * 128]
    part[0, 16:24, :] = jnp.zeros((8, 128), F32) + weight_part
    greet(mp_peers + [y_peer] + z_peers)

    def exchange(stage, peers, slots):
        copies = [
            remote(
                part.at[stage],
                slots.at[m],
                stat_send.at[stage, m],
                stat_recv.at[stage, m],
                peer,
            )
            for m, peer in enumerate(peers)
        ]
        start_all(copies)
        return copies

    def total(stage, copies, slots):
        value = part[stage]
        for m, copy in enumerate(copies):
            copy.wait_recv()
            value = value + slots[m]
        return value

    sums_a = exchange(0, mp_peers, from_mp)
    after = {"mp": (mp + 1) % 4}
    halo_copies = [
        remote(
            ref.at[pl.ds(rows_here - HALO, HALO)],
            ext.at[pl.ds(0, HALO)],
            halo_sem.at[which, 0],
            halo_sem.at[which, 1],
            after,
        )
        for which, (ref, ext) in enumerate(
            ((tokens_ref, tokens_ext), (cotangent_ref, cotangent_ext))
        )
    ]
    bias_copies = [
        remote(bias.at[0], bias.at[r + 1], bias_send.at[r], bias_recv.at[r], peer)
        for r, peer in enumerate(mp_peers)
    ]
    start_all(halo_copies + bias_copies)
    start_all([x_copy(i) for i in range(8)])
    start_all([pair_copies[i] for i in (QUERY, KEY, VALUE, OUTPUT, UP_A, UP_B, DOWN_A, DOWN_B)])
    part[1] = total(0, sums_a, from_mp)
    sums_b = exchange(1, [y_peer], from_y)

    place_id = lax.broadcasted_iota(jnp.int32, (64, 1), 0)
    table_scale = choose_item(
        place_id >> 4, [scales[groups[4 * mp + j]] for j in range(4)]
    )
    quarter = D // 4
    lane = lax.broadcasted_iota(jnp.int32, (1, quarter), 1).astype(F32)
    frequency = jnp.exp(-math.log(10000.0) * lane / quarter)
    angle = ((place_id & 15).astype(F32) * table_scale) * frequency
    table = jnp.concatenate([jnp.sin(angle), jnp.cos(angle)], axis=1)
    row = lax.broadcasted_iota(jnp.int32, (rows, 64), 0)
    column = lax.broadcasted_iota(jnp.int32, (rows, 64), 1)
    item, position, in_pair, _ = item_of_rows(row, lengths, mp)
    across = (position * 9363) >> 17
    for half, code in enumerate((across, position - SIDE * across)):
        chosen = jnp.where(in_pair & (column == item * 16 + code), 1.0, 0.0)
        stream[:, half * 2 * quarter : (half + 1) * 2 * quarter] = lax.dot_general(
            chosen,
            table,
            (((1,), (0,)), ((), ())),
            precision=lax.Precision.HIGHEST,
            preferred_element_type=F32,
        )
    part[2] = total(1, sums_b, from_y)
    sums_c = exchange(2, z_peers, from_z)
    x_to_z(KEY)
    x_to_z(VALUE)

    wait_recv_all(halo_copies)
    keep[1].wait()
    own_len = 2 * PAIR_LEN
    row = lax.broadcasted_iota(jnp.int32, (rows, HALO + rows_here), 0)
    column = lax.broadcasted_iota(jnp.int32, (rows, HALO + rows_here), 1)
    window = row >> 8
    offset = row & (WINDOW - 1)
    wanted = HALO - (rows_here - own_len) * mp + window * PAIR_LEN + offset
    tail = jnp.where(mp == 3, HALO + rows_here - PADDING, 4096) + offset
    wanted = jnp.where(window < 2, jnp.where(offset < PAIR_LEN, wanted, -1), tail)
    chosen = jnp.where(column == wanted, 1.0, 0.0).astype(BF)
    tokens[...] = dot(chosen, tokens_ext[...]).astype(BF)
    cotangent[...] = dot(chosen, cotangent_ext[...]).astype(BF)
    sums[...] = total(2, sums_c, from_z)

    slices = lax.axis_size("dp")
    count_valid = slices * PAIRS * PAIR_LEN
    column_mean = joined(sums, 0) / count_valid
    spread = joined(sums, 8) / count_valid - column_mean * column_mean
    inverse = lax.rsqrt(spread + 1e-05)
    mean_weight = sums[16:17, 0:1] / (slices * 16)

    def first_norm(i):
        here = block_rows(i, 32)
        value = (tokens[here, :].astype(F32) - column_mean) * inverse + stream[here, :]
        stream[here, :] = value
        unit, _ = stats(value)
        normed[here, :] = (unit * gain[...] + shift[...]).astype(BF)
        row = i * 32 + lax.broadcasted_iota(jnp.int32, (32, 1), 0)
        item, _, in_pair, _ = item_of_rows(row, lengths, mp)
        row_weight = jnp.where(in_pair, choose_item(item, weights), 0.0) / mean_weight
        grad_mixed[here, :] = (cotangent[here, :].astype(F32) * row_weight).astype(BF)

    loop(blocks, first_norm)

    def store(i, value, ref):
        return pltpu.make_async_copy(value, ref, store_sem.at[i])

    stores = [
        store(0, tokens, tokens_out),
        store(1, cotangent, cotangent_out),
        store(2, sums, sums_out),
        store(3, stream, stream_out),
        store(4, normed, normed_out),
        store(5, grad_mixed, grad_mixed_out),
        store(6, qkv, qkv_out),
        store(7, context, context_out),
        store(8, wqkv, wqkv_out),
        store(9, middle, middle_out),
        store(10, hidden, hidden_out),
        store(11, wo, wo_out),
        store(12, active, active_out),
        store(13, grad_pre, grad_pre_out),
        store(14, wup, wup_out),
        store(15, wdown, wdown_out),
    ]
    start_all(stores[:6])

    for copy in bias_copies:
        copy.wait_recv()

    def head_group(r):
        @pl.when(r == 0)
        def _():
            for i in (QUERY, KEY, VALUE):
                own_copies[i].wait()

        @pl.when(r == 1)
        def _():
            for i in (OUTPUT, UP_A, UP_B, DOWN_A):
                x_to_z(i)
            for i in (QUERY, KEY, VALUE):
                pair_copies[i].wait_recv()

        @pl.when(r == 2)
        def _():
            for i in (QUERY, KEY, VALUE):
                y_to_pair(i)
            z_to_y(OUTPUT)

        @pl.when(r == 3)
        def _():
            for i in (QUERY, KEY, VALUE):
                fwd_copy(i).wait_recv()
            y_to_pair(OUTPUT)

        base = r * 3 * width
        for n in range(3):
            value = dot(normed[...], wqkv[r, :, n * width : (n + 1) * width])
            if n != 1:
                value = value + bias[r, n // 2 : n // 2 + 1, :]
            qkv[:, pl.ds(pl.multiple_of(base + n * width, width), width)] = value.astype(BF)

        @pl.when(r == 0)
        def _():
            z_to_y(KEY)
            z_to_y(VALUE)

        def head_pair(p):
            lanes = [
                pl.ds(pl.multiple_of(base + n * width + p * 128, 128), 128) for n in range(3)
            ]
            target = pl.ds(pl.multiple_of(r * width + p * 128, 128), 128)
            for first, size in blocks_of(rows):
                here = pl.ds(first, size)
                same = owner_of_rows(
                    first + lax.broadcasted_iota(jnp.int32, (size, 1), 0), lengths, mp
                ) == owner_of_rows(
                    first + lax.broadcasted_iota(jnp.int32, (1, size), 1), lengths, mp
                )
                q, k, v = [qkv[here, lane] for lane in lanes]
                results = []
                for h in range(2):
                    cut = slice(h * HEAD_DIM, (h + 1) * HEAD_DIM)
                    low = softmax_rows(q[:, cut], k[:, cut], same).astype(BF)
                    results.append(dot(low, v[:, cut]).astype(BF))
                context[here, target] = jnp.concatenate(results, axis=1)

        loop(width // 128, head_pair)

    loop(4, head_group)
    start_all(stores[6:9])
    z_to_y(UP_A)

    own_copies[OUTPUT].wait()
    pair_copies[OUTPUT].wait_recv()
    fwd_copy(OUTPUT).wait_recv()

    def attention_output(n):
        columns = block_rows(n, 256)
        value = stream[:, columns] + output_bias[:, columns]
        for r in range(4):
            value = value + dot(context[:, r * width : (r + 1) * width], wo[r, :, columns])
        middle[:, columns] = value

    loop(4, attention_output)

    def second_norm(i):
        here = block_rows(i, 32)
        unit, _ = stats(middle[here, :])
        hidden[here, :] = (unit * hidden_gain[...] + hidden_shift[...]).astype(BF)

    loop(blocks, second_norm)
    start_all(stores[9:12])

    def hidden_group(r):
        @pl.when(r == 0)
        def _():
            for i in (UP_A, UP_B, DOWN_A, DOWN_B):
                own_copies[i].wait()
            z_to_y(UP_B)

        @pl.when(r == 1)
        def _():
            y_to_pair(UP_A)
            z_to_y(DOWN_A)
            for i in (UP_A, UP_B, DOWN_A, DOWN_B):
                pair_copies[i].wait_recv()

        @pl.when(r == 2)
        def _():
            for i in (DOWN_B, UP_B, DOWN_A):
                y_to_pair(i)

        @pl.when(r == 3)
        def _():
            for i in (UP_A, UP_B, DOWN_A, DOWN_B):
                fwd_copy(i).wait_recv()

        def hidden_tile(n):
            columns = block_rows(n, 256)
            target = pl.ds(pl.multiple_of(r * D + n * 256, 256), 256)
            preact = dot(hidden[...], wup[r, :, columns]) + bias[r, pl.ds(2 + n, 1), :]
            value, slope = gelu_parts(preact)
            active[:, target] = value
            grad = dot_cols(grad_mixed[...], wdown[r, columns, :])
            grad_pre[:, target] = (grad * slope).astype(BF)

        loop(4, hidden_tile)

    loop(4, hidden_group)
    start_all(stores[12:])

    for i in range(8):
        pair_copies[i].wait_send()
        x_copy(i).wait_send()
        fwd_copy(i).wait_send()
        if not items[i][6]:
            for copy in z_copies(i):
                copy.wait_send()
            y_copy(i).wait_send()
    for copy in bias_copies + halo_copies + sums_a + sums_b + sums_c:
        copy.wait_send()
    for copy in stores:
        copy.wait()


def softmax_rows(q, k, same):
    scores = jnp.where(same, dot_cols(q, k) * (1.0 / math.sqrt(HEAD_DIM)), -1e30)
    weights = jnp.exp(scores - jnp.max(scores, axis=-1, keepdims=True))
    return weights * (1.0 / jnp.sum(weights, axis=-1, keepdims=True))


def forward(smalls, vectors, tokens, cotangent, weights, rows):
    width = weights[0].shape[1]
    shape = jax.ShapeDtypeStruct
    full = shape((rows, D), F32)
    low = shape((rows, D), BF)
    wide = shape((rows, 4 * D), BF)
    outs = (
        low,
        low,
        shape((24, 128), F32),
        full,
        full,
        low,
        shape((rows, 12 * width), BF),
        low,
        low,
        low,
        wide,
        wide,
        shape((4, D, 3 * width), BF),
        shape((4, width, D), BF),
        shape((4, D, D), BF),
        shape((4, D, D), BF),
    )
    scratch = [shape((HALO + tokens.shape[0], D), BF)] * 2 + [
        low,
        low,
        full,
        full,
        low,
        outs[6],
        low,
        low,
        low,
        wide,
        wide,
    ]
    scratch += list(outs[12:]) + [
        shape((24, 128), F32),
        shape((4, 8, width), F32),
        shape((3, 24, 128), F32),
        shape((3, 24, 128), F32),
        shape((1, 24, 128), F32),
        shape((3, 24, 128), F32),
    ]
    dma = pltpu.SemaphoreType.DMA
    any_space = pl.BlockSpec(memory_space=pl.ANY)
    return pl.pallas_call(
        forward_kernel,
        out_shape=outs,
        in_specs=[pl.BlockSpec(memory_space=pltpu.SMEM)] * 4
        + [pl.BlockSpec(memory_space=pltpu.VMEM)] * 8
        + [any_space] * 8,
        out_specs=(any_space,) * len(outs),
        scratch_shapes=[pltpu.VMEM(v.shape, v.dtype) for v in scratch]
        + [
            dma((8,)),
            dma((2, 3)),
            dma((16,)),
            dma((3, 3)),
            dma((3, 3)),
            dma((3,)),
            dma((3,)),
            dma((8,)),
            dma((8,)),
            dma((8,)),
            dma((8,)),
            dma((8, 3)),
            dma((8, 3)),
            dma((8,)),
            dma((8,)),
            dma((8,)),
            dma((8,)),
        ],
        compiler_params=pltpu.CompilerParams(
            collective_id=1, has_side_effects=True, vmem_limit_bytes=67043328
        ),
        name="forward",
    )(*smalls, *vectors, tokens, cotangent, *weights)


CHUNK = 256
STAGE_DELAY = (0, 1, 3, 5, 7, 9, 11)


def gradient_kernel(
    active_ref,
    grad_mixed_ref,
    hidden_ref,
    grad_pre_ref,
    context_ref,
    grad_attended_ref,
    grad_qkv_ref,
    normed_ref,
    out_ref,
    active,
    grad_mixed,
    hidden,
    grad_pre,
    context,
    grad_attended,
    grad_qkv,
    normed,
    made,
    pair,
    across,
    over_y,
    over_z,
    final,
    load_sem,
    pair_send,
    pair_recv,
    across_send,
    across_recv,
    y_send,
    y_recv,
    z_send,
    z_recv,
    back_z_send,
    back_z_recv,
    back_y_send,
    back_y_recv,
    out_sem,
):
    mp = lax.axis_index("mp")
    dp = lax.axis_index("dp")
    y = dp % 2
    z = dp // 2
    sibling = {"mp": mp + 1 - 2 * (mp % 2)}
    opposite = {"mp": mp + 2 - 4 * (mp // 2)}
    y_peer = {"dp": dp + 1 - 2 * y}
    z_places = [(z + m) % 4 for m in (1, 2, 3)]
    z_peers = [{"dp": place * 2 + y} for place in z_places]
    half = CHUNK // 2
    eighth = CHUNK // 8
    chunks = final.shape[0]
    width = final.shape[2]

    loads = [
        pltpu.make_async_copy(source, target, load_sem.at[i])
        for i, (source, target) in enumerate(
            (
                (active_ref, active),
                (grad_mixed_ref, grad_mixed),
                (hidden_ref, hidden),
                (grad_pre_ref, grad_pre),
                (context_ref, context),
                (grad_attended_ref, grad_attended),
                (grad_qkv_ref, grad_qkv),
                (normed_ref, normed),
            )
        )
    ]
    for load in loads:
        load.start()
    barrier = pltpu.get_barrier_semaphore()
    for peer in [sibling, opposite, y_peer] + z_peers:
        pl.semaphore_signal(barrier, inc=1, device_id=peer, device_id_type=MESH)
    pl.semaphore_wait(barrier, 6)

    def pair_copy(c):
        return pltpu.make_async_remote_copy(
            src_ref=made.at[c % 2, pl.ds(0, 2)],
            dst_ref=pair.at[c],
            send_sem=pair_send.at[c],
            recv_sem=pair_recv.at[c],
            device_id=sibling,
            device_id_type=MESH,
        )

    def across_copy(c):
        return pltpu.make_async_remote_copy(
            src_ref=pair.at[c, 1],
            dst_ref=across.at[c],
            send_sem=across_send.at[c],
            recv_sem=across_recv.at[c],
            device_id=opposite,
            device_id_type=MESH,
        )

    def y_copy(c):
        return pltpu.make_async_remote_copy(
            src_ref=across.at[c, pl.ds(pl.multiple_of((1 - y) * half, half), half)],
            dst_ref=over_y.at[c],
            send_sem=y_send.at[c],
            recv_sem=y_recv.at[c],
            device_id=y_peer,
            device_id_type=MESH,
        )

    def z_copies(c):
        return [
            pltpu.make_async_remote_copy(
                src_ref=over_y.at[c, pl.ds(pl.multiple_of(place * eighth, eighth), eighth)],
                dst_ref=over_z.at[c, m],
                send_sem=z_send.at[c, m],
                recv_sem=z_recv.at[c, m],
                device_id=peer,
                device_id_type=MESH,
            )
            for m, (place, peer) in enumerate(zip(z_places, z_peers))
        ]

    def back_z_copies(c):
        rows = pl.ds(pl.multiple_of(y * half + z * eighth, eighth), eighth)
        return [
            pltpu.make_async_remote_copy(
                src_ref=final.at[c, rows],
                dst_ref=final.at[c, rows],
                send_sem=back_z_send.at[c, m],
                recv_sem=back_z_recv.at[c, m],
                device_id=peer,
                device_id_type=MESH,
            )
            for m, peer in enumerate(z_peers)
        ]

    def back_y_copy(c):
        rows = pl.ds(pl.multiple_of(y * half, half), half)
        return pltpu.make_async_remote_copy(
            src_ref=final.at[c, rows],
            dst_ref=final.at[c, rows],
            send_sem=back_y_send.at[c],
            recv_sem=back_y_recv.at[c],
            device_id=y_peer,
            device_id_type=MESH,
        )

    def out_copy(c):
        return pltpu.make_async_copy(final.at[c], out_ref.at[c], out_sem.at[c])

    def block_loop(count, body):
        def step(i, carry):
            body(pl.ds(pl.multiple_of(i * eighth, eighth), eighth))
            return carry

        lax.fori_loop(0, count, step, 0)

    def make(c):
        def part(j, carry):
            r = 2 * j + 1 - 5 * (j // 2)

            def store(left, right):
                made[c % 2, j] = dot_rows(left, right).astype(BF)

            @pl.when(c < 4)
            def _():
                left = active[:, pl.ds(pl.multiple_of((r * 4 + c) * CHUNK, CHUNK), CHUNK)]
                store(left, grad_mixed[...])

            @pl.when((c >= 4) & (c < 8))
            def _():
                left = hidden[:, pl.ds(pl.multiple_of((c - 4) * CHUNK, CHUNK), CHUNK)]
                store(left, grad_pre[:, pl.ds(pl.multiple_of(r * width, width), width)])

            @pl.when(c == 8)
            def _():
                left = context[:, pl.ds(pl.multiple_of(r * CHUNK, CHUNK), CHUNK)]
                store(left, grad_attended[...])

            @pl.when(c > 8)
            def _():
                left = grad_qkv[:, pl.ds(pl.multiple_of((r * 3 + c - 9) * CHUNK, CHUNK), CHUNK)]
                store(left, normed[...])

            return carry

        lax.fori_loop(0, 4, part, 0)

    def add_pair(c):
        pair_copy(c).wait_recv()
        pair_copy(c).wait_send()

        def body(rows):
            for which in (1, 0):
                pair[c, which, rows, :] = (
                    pair[c, which, rows, :].astype(F32)
                    + made[c % 2, 2 + which, rows, :].astype(F32)
                ).astype(BF)

        block_loop(8, body)

    def add_across(c):
        across_copy(c).wait_recv()

        def body(rows):
            across[c, rows, :] = (
                across[c, rows, :].astype(F32) + pair[c, 0, rows, :].astype(F32)
            ).astype(BF)

        block_loop(8, body)

    def add_y(c):
        y_copy(c).wait_recv()

        def step(i, carry):
            rows = pl.ds(pl.multiple_of(i * eighth, eighth), eighth)
            own = pl.ds(pl.multiple_of(y * half + i * eighth, eighth), eighth)
            over_y[c, rows, :] = (
                over_y[c, rows, :].astype(F32) + across[c, own, :].astype(F32)
            ).astype(BF)
            return carry

        lax.fori_loop(0, 4, step, 0)

    def add_z(c):
        for copy in z_copies(c):
            copy.wait_recv()
        total = over_y[c, pl.ds(pl.multiple_of(z * eighth, eighth), eighth), :].astype(F32)
        for m in range(3):
            total = total + over_z[c, m].astype(F32)
        final[c, pl.ds(pl.multiple_of(y * half + z * eighth, eighth), eighth), :] = total.astype(BF)

    def wait_back_z(c):
        for copy in back_z_copies(c):
            copy.wait_recv()

    def wait_back_y(c):
        back_y_copy(c).wait_recv()

    def start_all(copies):
        for copy in copies:
            copy.start()

    handle = (make, add_pair, add_across, add_y, add_z, wait_back_z, wait_back_y)
    send = (
        lambda c: [pair_copy(c)],
        lambda c: [across_copy(c)],
        lambda c: [y_copy(c)],
        z_copies,
        back_z_copies,
        lambda c: [back_y_copy(c)],
        lambda c: [out_copy(c)],
    )

    def tick(k, carry):
        for when, count in ((0, 2), (4, 2), (8, 2), (9, 2)):
            first = {0: 0, 4: 2, 8: 4, 9: 6}[when]

            @pl.when(k == when)
            def _(first=first, count=count):
                for load in loads[first : first + count]:
                    load.wait()

        for stage in (6, 5, 4, 3, 2, 0, 1):
            c = k - STAGE_DELAY[stage]

            @pl.when((c >= 0) & (c < chunks))
            def _(stage=stage, c=c):
                handle[stage](c)

        for stage in (1, 2, 3, 4, 5, 0, 6):
            c = k - STAGE_DELAY[stage]

            @pl.when((c >= 0) & (c < chunks))
            def _(stage=stage, c=c):
                start_all(send[stage](c))

        return carry

    lax.fori_loop(0, chunks + STAGE_DELAY[-1], tick, 0)

    def finish(c, carry):
        across_copy(c).wait_send()
        y_copy(c).wait_send()
        for copy in z_copies(c) + back_z_copies(c):
            copy.wait_send()
        back_y_copy(c).wait_send()
        out_copy(c).wait()
        return carry

    lax.fori_loop(0, chunks, finish, 0)


def reduce_gradients(*inputs):
    chunks = 12
    return pl.pallas_call(
        gradient_kernel,
        out_shape=jax.ShapeDtypeStruct((chunks, CHUNK, D), BF),
        in_specs=[pl.BlockSpec(memory_space=pl.ANY)] * 8,
        out_specs=pl.BlockSpec(memory_space=pl.ANY),
        scratch_shapes=[pltpu.VMEM(v.shape, v.dtype) for v in inputs]
        + [
            pltpu.VMEM((2, 4, CHUNK, D), BF),
            pltpu.VMEM((chunks, 2, CHUNK, D), BF),
            pltpu.VMEM((chunks, CHUNK, D), BF),
            pltpu.VMEM((chunks, CHUNK // 2, D), BF),
            pltpu.VMEM((chunks, 3, CHUNK // 8, D), BF),
            pltpu.VMEM((chunks, CHUNK, D), BF),
            pltpu.SemaphoreType.DMA((8,)),
            pltpu.SemaphoreType.DMA((chunks,)),
            pltpu.SemaphoreType.DMA((chunks,)),
            pltpu.SemaphoreType.DMA((chunks,)),
            pltpu.SemaphoreType.DMA((chunks,)),
            pltpu.SemaphoreType.DMA((chunks,)),
            pltpu.SemaphoreType.DMA((chunks,)),
            pltpu.SemaphoreType.DMA((chunks, 3)),
            pltpu.SemaphoreType.DMA((chunks, 3)),
            pltpu.SemaphoreType.DMA((chunks, 3)),
            pltpu.SemaphoreType.DMA((chunks, 3)),
            pltpu.SemaphoreType.DMA((chunks,)),
            pltpu.SemaphoreType.DMA((chunks,)),
            pltpu.SemaphoreType.DMA((chunks,)),
        ],
        compiler_params=pltpu.CompilerParams(
            collective_id=0, has_side_effects=True, vmem_limit_bytes=67043328
        ),
        name="reduce_gradients",
    )(*inputs)


def general_shards(
    tokens,
    cotangent,
    item_lengths,
    item_group,
    group_count,
    grid_scale,
    norm_gain,
    norm_shift,
    query_weight,
    query_bias,
    key_weight,
    value_weight,
    value_bias,
    output_weight,
    output_bias,
    hidden_gain,
    hidden_shift,
    up_weight,
    up_bias,
    down_weight,
    down_bias,
):
    shard_count = lax.axis_size("mp")
    slice_count = lax.axis_size("dp")
    mp = lax.axis_index("mp")
    rows_here = tokens.shape[0]
    item_count = item_lengths.shape[0]
    pairs_here = PAIRS // shard_count
    own_rows = pairs_here * PAIR_LEN
    shift = rows_here - own_rows
    halo = shift * (shard_count - 1)
    padding = rows_here * shard_count - PAIRS * PAIR_LEN
    tail_block = -(-padding // 32) * 32
    rows = pairs_here * WINDOW + tail_block
    is_last = mp == shard_count - 1

    width = query_weight.shape[1]
    qkv_own = jnp.concatenate([query_weight, key_weight, value_weight], axis=1)
    bias_own = jnp.concatenate([query_bias, value_bias, up_bias])[None, :]
    bias_across = swap_mp(bias_own, 2)
    bias_pair = swap_mp(jnp.concatenate([bias_own, bias_across], axis=0), 1)
    biases = [bias_own[0], bias_pair[0], bias_across[0], bias_pair[1]]

    def gather(own, direct):
        across = swap_mp(own, 2) if direct else fetch_across(own)
        return [own, swap_mp(own, 1), across, swap_mp(across, 1)]

    tokens_f = tokens.astype(F32)
    slice_row = mp * rows_here + jnp.arange(rows_here, dtype=jnp.int32)
    weighted = tokens_f * (slice_row < PAIRS * PAIR_LEN).astype(F32)[:, None]
    chosen = item_group[:, None] == jnp.arange(group_count.shape[0], dtype=jnp.int32)[None, :]
    item_scale = jnp.sum(jnp.where(chosen, grid_scale[None, :], 0.0), axis=1)
    item_weight = jnp.sum(jnp.where(chosen, group_count[None, :], 0), axis=1).astype(F32)
    sums = all_sum(
        jnp.stack(
            [
                jnp.sum(weighted, axis=0),
                jnp.sum(weighted * tokens_f, axis=0),
                jnp.broadcast_to(jnp.sum(item_weight) / shard_count, (D,)),
            ]
        )
    )

    def windows(v):
        before = lax.ppermute(
            v[rows_here - halo :], "mp", [(i, i + 1) for i in range(shard_count - 1)]
        )
        joined = jnp.concatenate([before, v], axis=0)
        start = halo - shift * mp
        parts = []
        for pair in range(pairs_here):
            parts.append(
                lax.dynamic_slice_in_dim(joined, start + pair * PAIR_LEN, PAIR_LEN, axis=0)
            )
            parts.append(jnp.zeros((WINDOW - PAIR_LEN, D), v.dtype))
        parts.append(jnp.where(is_last, v[rows_here - padding :], jnp.zeros((), v.dtype)))
        parts.append(jnp.zeros((tail_block - padding, D), v.dtype))
        return jnp.concatenate(parts, axis=0)

    def unwindows(v):
        own = jnp.concatenate(
            [v[pair * WINDOW : pair * WINDOW + PAIR_LEN] for pair in range(pairs_here)], axis=0
        )
        after = lax.ppermute(own[:halo], "mp", [(i + 1, i) for i in range(shard_count - 1)])
        after = jnp.concatenate([after, jnp.zeros((padding - halo, D), v.dtype)], axis=0)
        tail = v[pairs_here * WINDOW : pairs_here * WINDOW + padding]
        joined = jnp.concatenate([own, jnp.where(is_last, tail, after)], axis=0)
        return lax.dynamic_slice_in_dim(joined, shift * mp, rows_here, axis=0)

    tokens_w = windows(tokens).astype(F32)
    cotangent_w = windows(cotangent).astype(F32)

    row = jnp.arange(rows, dtype=jnp.int32)
    window = row // WINDOW
    offset = row % WINDOW
    in_pair = (window < pairs_here) & (offset < PAIR_LEN)
    is_padding = (window == pairs_here) & (offset < padding) & is_last
    pair = pairs_here * mp + window
    item_ids = jnp.arange(item_count, dtype=jnp.int32)
    first_len = jnp.sum(
        jnp.where(item_ids[None, :] == (2 * pair)[:, None], item_lengths[None, :], 0), axis=1
    )
    second = (offset >= first_len).astype(jnp.int32)
    owner = jnp.where(in_pair, 2 * pair + second, jnp.where(is_padding, item_count, -1))
    position = offset - second * first_len
    member = owner[:, None] == item_ids[None, :]
    row_scale = jnp.sum(jnp.where(member, item_scale[None, :], 0.0), axis=1)
    row_count = jnp.sum(jnp.where(member, item_weight[None, :], 0.0), axis=1)
    valid = in_pair.astype(F32)[:, None]
    quarter = D // 4
    frequency = jnp.exp(-math.log(10000.0) * jnp.arange(quarter, dtype=F32) / quarter)
    across_angle = ((position // SIDE).astype(F32) * row_scale)[:, None] * frequency
    side_angle = ((position % SIDE).astype(F32) * row_scale)[:, None] * frequency
    grid_table = (
        jnp.concatenate(
            [
                jnp.sin(across_angle),
                jnp.cos(across_angle),
                jnp.sin(side_angle),
                jnp.cos(side_angle),
            ],
            axis=-1,
        )
        * valid
    )
    owner_col = owner[:, None]
    owner_row = owner[None, :]

    qkv_weights = jnp.concatenate(gather(qkv_own, True), axis=1)
    output_weights = jnp.concatenate(gather(output_weight, False), axis=0)
    up_weights = jnp.concatenate(gather(up_weight, False), axis=1)
    down_weights = jnp.concatenate(gather(down_weight, False), axis=0)
    hidden_width = up_weight.shape[1]
    no_bias = jnp.zeros((width,), F32)
    qkv_bias = jnp.concatenate(
        [v for b in biases for v in (b[:width], no_bias, b[width : 2 * width])]
    )
    up_biases = jnp.concatenate([b[2 * width :] for b in biases])

    count_valid = slice_count * PAIRS * PAIR_LEN
    column_mean = sums[0] / count_valid
    spread = sums[1] / count_valid - column_mean * column_mean
    inverse = lax.rsqrt(spread + 1e-05)
    row_weight = row_count / (sums[2, 0] / (slice_count * item_count))
    standard = (tokens_w - column_mean) * inverse
    stream = standard + grid_table
    unit, unit_inverse = stats(stream)
    normed = (unit * norm_gain + norm_shift).astype(BF)

    qkv = (dot(normed, qkv_weights) + qkv_bias).astype(BF)
    context = attend(qkv, owner_col, owner_row, shard_count)
    middle = stream + (dot(context, output_weights) + output_bias)
    middle_unit, middle_inverse = stats(middle)
    hidden_in = (middle_unit * hidden_gain + hidden_shift).astype(BF)

    grad_out = cotangent_w * row_weight[:, None]
    grad_mixed = grad_out.astype(BF)
    active, slope = gelu_parts(dot(hidden_in, up_weights) + up_biases)
    mixed = dot(active, down_weights) + down_bias
    grad_pre = (dot_cols(grad_mixed, down_weights) * slope).astype(BF)
    grad_hidden = dot_cols(grad_pre, up_weights)
    layer_output = unwindows((middle + mixed).astype(BF))
    grad_middle = grad_out + norm_back(grad_hidden, middle_unit, middle_inverse, hidden_gain)
    grad_attended = grad_middle.astype(BF)

    grad_context = dot_cols(grad_attended, output_weights).astype(BF)
    grad_qkv = attend_back(qkv, grad_context, owner_col, owner_row, shard_count)
    grad_normed = dot_cols(grad_qkv, qkv_weights)

    pieces = range(shard_count)
    def columns(v, r, size):
        return v[:, r * size : (r + 1) * size]

    def reduced(left, right):
        return reduce_pieces([dot_rows(left(r), right(r)).astype(BF) for r in pieces])

    down_weight_grad = reduced(
        lambda r: columns(active, r, hidden_width), lambda r: grad_mixed
    )
    up_weight_grad = reduced(
        lambda r: hidden_in, lambda r: columns(grad_pre, r, hidden_width)
    )
    output_weight_grad = reduced(
        lambda r: columns(context, r, width), lambda r: grad_attended
    )
    qkv_weight_grad = reduced(lambda r: normed, lambda r: columns(grad_qkv, r, 3 * width))
    qkv_weight_grads = [columns(qkv_weight_grad, i, width) for i in range(3)]
    grad_stream = grad_middle + norm_back(grad_normed, unit, unit_inverse, norm_gain)

    def column_sums(v):
        return jnp.sum(v.astype(F32), axis=0)

    qkv_sums = column_sums(grad_qkv)
    up_sums = column_sums(grad_pre)
    bias_grads = [
        jnp.concatenate(
            [
                qkv_sums[3 * r * width : (3 * r + 1) * width],
                qkv_sums[(3 * r + 2) * width : 3 * (r + 1) * width],
                up_sums[r * hidden_width : (r + 1) * hidden_width],
            ]
        )[None, :]
        for r in pieces
    ]
    got = swap_mp(jnp.concatenate([bias_grads[1], bias_grads[3]], axis=0), 1)
    bias_grad = bias_grads[0] + got[:1] + swap_mp(bias_grads[2] + got[1:], 2)
    for bit in range(dp_bits()):
        bias_grad = bias_grad + swap_dp(bias_grad, 1 << bit)
    bias_grad = bias_grad[0]
    finals = all_sum(
        jnp.stack(
            [
                column_sums(grad_stream),
                column_sums(grad_stream * standard),
                column_sums(grad_normed * unit),
                column_sums(grad_normed),
                column_sums(grad_hidden * middle_unit),
                column_sums(grad_hidden),
                column_sums(grad_attended),
                column_sums(grad_mixed),
            ]
        )
    )
    tokens_grad = unwindows(
        inverse * (grad_stream - valid / count_valid * (finals[0] + finals[1] * standard))
    )
    return (
        layer_output,
        tokens_grad,
        finals[2],
        finals[3],
        qkv_weight_grads[0],
        bias_grad[:width],
        qkv_weight_grads[1],
        qkv_weight_grads[2],
        bias_grad[width : 2 * width],
        output_weight_grad,
        finals[6],
        finals[4],
        finals[5],
        up_weight_grad,
        bias_grad[2 * width :],
        down_weight_grad,
        finals[7],
    )


def fast_shards(
    tokens,
    cotangent,
    item_lengths,
    item_group,
    group_count,
    grid_scale,
    norm_gain,
    norm_shift,
    query_weight,
    query_bias,
    key_weight,
    value_weight,
    value_bias,
    output_weight,
    output_bias,
    hidden_gain,
    hidden_shift,
    up_weight,
    up_bias,
    down_weight,
    down_bias,
):
    shard_count = lax.axis_size("mp")
    slice_count = lax.axis_size("dp")
    mp = lax.axis_index("mp")
    rows_here = tokens.shape[0]
    item_count = item_lengths.shape[0]
    pairs_here = PAIRS // shard_count
    shift = rows_here - pairs_here * PAIR_LEN
    halo = shift * (shard_count - 1)
    padding = rows_here * shard_count - PAIRS * PAIR_LEN
    tail_block = -(-padding // 32) * 32
    rows = pairs_here * WINDOW + tail_block
    is_last = mp == shard_count - 1
    width = query_weight.shape[1]
    hidden_width = up_weight.shape[1]
    chosen = item_group[:, None] == jnp.arange(group_count.shape[0], dtype=jnp.int32)[None, :]
    item_scale = jnp.sum(jnp.where(chosen, grid_scale[None, :], 0.0), axis=1)
    item_weight = jnp.sum(jnp.where(chosen, group_count[None, :], 0), axis=1).astype(F32)

    def unwindows(v):
        own = jnp.concatenate(
            [v[pair * WINDOW : pair * WINDOW + PAIR_LEN] for pair in range(pairs_here)], axis=0
        )
        after = lax.ppermute(own[:halo], "mp", [(i + 1, i) for i in range(shard_count - 1)])
        after = jnp.concatenate([after, jnp.zeros((padding - halo, D), v.dtype)], axis=0)
        tail = v[pairs_here * WINDOW : pairs_here * WINDOW + padding]
        joined = jnp.concatenate([own, jnp.where(is_last, tail, after)], axis=0)
        return lax.dynamic_slice_in_dim(joined, shift * mp, rows_here, axis=0)

    (
        tokens_w,
        cotangent_w,
        sums,
        stream,
        middle,
        normed,
        qkv,
        context,
        hidden_in,
        grad_mixed,
        active,
        grad_pre,
        qkv_weights,
        output_weights,
        up_weights,
        down_weights,
    ) = forward(
        (item_lengths, item_group, group_count, grid_scale),
        [
            v[None, :]
            for v in (
                norm_gain,
                norm_shift,
                output_bias,
                hidden_gain,
                hidden_shift,
                query_bias,
                value_bias,
                up_bias,
            )
        ],
        tokens,
        cotangent,
        (query_weight, key_weight, value_weight, output_weight, up_weight, down_weight),
        rows,
    )
    tokens_w = tokens_w.astype(F32)
    sums = sums.reshape(3, D)
    row = jnp.arange(rows, dtype=jnp.int32)
    window = row // WINDOW
    offset = row % WINDOW
    in_pair = (window < pairs_here) & (offset < PAIR_LEN)
    is_padding = (window == pairs_here) & (offset < padding) & is_last
    pair = pairs_here * mp + window
    item_ids = jnp.arange(item_count, dtype=jnp.int32)
    first_len = jnp.sum(
        jnp.where(item_ids[None, :] == (2 * pair)[:, None], item_lengths[None, :], 0), axis=1
    )
    second = (offset >= first_len).astype(jnp.int32)
    owner = jnp.where(in_pair, 2 * pair + second, jnp.where(is_padding, item_count, -1))
    position = offset - second * first_len
    member = owner[:, None] == item_ids[None, :]
    row_scale = jnp.sum(jnp.where(member, item_scale[None, :], 0.0), axis=1)
    row_count = jnp.sum(jnp.where(member, item_weight[None, :], 0.0), axis=1)
    valid = in_pair.astype(F32)[:, None]
    count_valid = slice_count * PAIRS * PAIR_LEN
    column_mean = sums[0] / count_valid
    spread = sums[1] / count_valid - column_mean * column_mean
    inverse = lax.rsqrt(spread + 1e-05)
    row_weight = row_count / (sums[2, 0] / (slice_count * item_count))
    standard = (tokens_w - column_mean) * inverse
    unit, unit_inverse = stats(stream)
    middle_unit, middle_inverse = stats(middle)
    grad_out = cotangent_w.astype(F32) * row_weight[:, None]
    mixed = dot(active, down_weights.reshape(-1, D)) + down_bias
    layer_output = unwindows((middle + mixed).astype(BF))
    pieces = range(shard_count)

    def columns(v, r, size):
        return v[:, r * size : (r + 1) * size]

    grad_hidden = sum(dot_cols(columns(grad_pre, r, hidden_width), up_weights[r]) for r in pieces)
    grad_middle = grad_out + norm_back(grad_hidden, middle_unit, middle_inverse, hidden_gain)
    grad_attended = grad_middle.astype(BF)

    owner_col = owner[:, None]
    owner_row = owner[None, :]
    grad_context = dot_cols(grad_attended, output_weights.reshape(-1, D)).astype(BF)
    grad_qkv = attend_back(qkv, grad_context, owner_col, owner_row, shard_count)
    grad_normed = sum(dot_cols(columns(grad_qkv, r, 3 * width), qkv_weights[r]) for r in pieces)

    reduced = reduce_gradients(
        active,
        grad_mixed,
        hidden_in,
        grad_pre,
        context,
        grad_attended,
        grad_qkv,
        normed,
    )
    down_weight_grad = reduced[:4].reshape(hidden_width, D).astype(F32)
    up_weight_grad = reduced[4:8].reshape(D, hidden_width).astype(F32)
    output_weight_grad = reduced[8].astype(F32)
    qkv_weight_grads = [reduced[9 + i].T.astype(F32) for i in range(3)]
    grad_stream = grad_middle + norm_back(grad_normed, unit, unit_inverse, norm_gain)

    def column_sums(v):
        return jnp.sum(v.astype(F32), axis=0)

    qkv_sums = column_sums(grad_qkv)
    up_sums = column_sums(grad_pre)
    bias_grads = [
        jnp.concatenate(
            [
                qkv_sums[3 * r * width : (3 * r + 1) * width],
                qkv_sums[(3 * r + 2) * width : 3 * (r + 1) * width],
                up_sums[r * hidden_width : (r + 1) * hidden_width],
            ]
        )[None, :]
        for r in pieces
    ]
    got = swap_mp(jnp.concatenate([bias_grads[1], bias_grads[3]], axis=0), 1)
    bias_grad = bias_grads[0] + got[:1] + swap_mp(bias_grads[2] + got[1:], 2)
    for bit in range(dp_bits()):
        bias_grad = bias_grad + swap_dp(bias_grad, 1 << bit)
    bias_grad = bias_grad[0]
    finals = all_sum(
        jnp.stack(
            [
                column_sums(grad_stream),
                column_sums(grad_stream * standard),
                column_sums(grad_normed * unit),
                column_sums(grad_normed),
                column_sums(grad_hidden * middle_unit),
                column_sums(grad_hidden),
                column_sums(grad_attended),
                column_sums(grad_mixed),
            ]
        )
    )
    tokens_grad = unwindows(
        inverse * (grad_stream - valid / count_valid * (finals[0] + finals[1] * standard))
    )
    return (
        layer_output,
        tokens_grad,
        finals[2],
        finals[3],
        qkv_weight_grads[0],
        bias_grad[:width],
        qkv_weight_grads[1],
        qkv_weight_grads[2],
        bias_grad[width : 2 * width],
        output_weight_grad,
        finals[6],
        finals[4],
        finals[5],
        up_weight_grad,
        bias_grad[2 * width :],
        down_weight_grad,
        finals[7],
    )


def shards(*args):
    if lax.axis_size("dp") == 8 and lax.axis_size("mp") == 4 and args[0].shape == (512, D):
        return fast_shards(*args)
    return general_shards(*args)


def solution(mesh):
    rows = P(("dp", "mp"), None)
    columns = P(None, "mp")
    return jax.shard_map(
        shards,
        mesh=mesh,
        in_specs=(
            rows,
            rows,
            P("dp"),
            P("dp"),
            P(),
            P(),
            P(),
            P(),
            columns,
            P("mp"),
            columns,
            columns,
            P("mp"),
            P("mp", None),
            P(),
            P(),
            P(),
            columns,
            P("mp"),
            P("mp", None),
            P(),
        ),
        out_specs=(
            rows,
            rows,
            P(),
            P(),
            columns,
            P("mp"),
            columns,
            columns,
            P("mp"),
            P("mp", None),
            P(),
            P(),
            P(),
            columns,
            P("mp"),
            P("mp", None),
            P(),
        ),
        check_vma=False,
    )
```

```python
import functools
import math

import jax
import jax.numpy as jnp
from jax import lax
from jax.experimental import pallas as pl
from jax.experimental.pallas import tpu as pltpu
from jax.sharding import PartitionSpec as P

D = 1024
HEAD_DIM = 64
SIDE = 14
PAIRS = 8
PAIR_LEN = 245
WINDOW = 256
BF = jnp.bfloat16
F32 = jnp.float32
PADDING = 88


def dot(a, b):
    return lax.dot_general(a, b, (((1,), (0,)), ((), ())), preferred_element_type=F32)


def dot_rows(a, b):
    return lax.dot_general(a, b, (((0,), (0,)), ((), ())), preferred_element_type=F32)


def dot_cols(a, b):
    return lax.dot_general(a, b, (((1,), (1,)), ((), ())), preferred_element_type=F32)


def swap_mp(v, mask):
    count = lax.axis_size("mp")
    return lax.ppermute(v, "mp", [(i, i ^ mask) for i in range(count)])


def swap_dp(v, mask):
    count = lax.axis_size("dp")
    return lax.ppermute(v, "dp", [(i, i ^ mask) for i in range(count)])


def dp_bits():
    return lax.axis_size("dp").bit_length() - 1


def all_sum(v):
    v = v + swap_mp(v, 1) + swap_mp(v, 2) + swap_mp(v, 3)
    bit = 0
    bits = dp_bits()
    while bit < bits:
        if bit + 1 < bits:
            v = v + swap_dp(v, 1 << bit) + swap_dp(v, 2 << bit) + swap_dp(v, 3 << bit)
            bit += 2
        else:
            v = v + swap_dp(v, 1 << bit)
            bit += 1
    return v


def dp_bit(bit):
    return (lax.axis_index("dp") >> bit) & 1


def join(mine, other, bit):
    return jnp.where(
        dp_bit(bit) == 0,
        jnp.concatenate([mine, other], axis=0),
        jnp.concatenate([other, mine], axis=0),
    )


def chunk_index():
    index = jnp.int32(0)
    for bit in range(dp_bits()):
        index = index * 2 + dp_bit(bit)
    return index


def fetch_across(w):
    rows = w.shape[0] // lax.axis_size("dp")
    mine = lax.dynamic_slice_in_dim(w, chunk_index() * rows, rows, axis=0)
    got = swap_mp(mine, 2)
    for bit in reversed(range(dp_bits())):
        got = join(got, swap_dp(got, 1 << bit), bit)
    return got


def reduce_pieces(pieces):
    half = pieces[1].shape[0]
    got = swap_mp(jnp.concatenate([pieces[1], pieces[3]], axis=0), 1)
    across = pieces[2].astype(F32) + got[half:].astype(F32)
    own = pieces[0].astype(F32) + got[:half].astype(F32)
    total = own + swap_mp(across.astype(BF), 2).astype(F32)
    for bit in range(dp_bits()):
        size = total.shape[0] // 2
        side = dp_bit(bit)
        send = lax.dynamic_slice_in_dim(total, (1 - side) * size, size, axis=0).astype(BF)
        keep = lax.dynamic_slice_in_dim(total, side * size, size, axis=0)
        total = keep + swap_dp(send, 1 << bit).astype(F32)
    total = total.astype(BF)
    for bit in reversed(range(dp_bits())):
        total = join(total, swap_dp(total, 1 << bit), bit)
    return total.astype(F32)


def stats(v):
    mean = jnp.mean(v, axis=-1, keepdims=True)
    center = v - mean
    spread = jnp.mean(center * center, axis=-1, keepdims=True)
    inverse = lax.rsqrt(spread + 1e-06)
    return center * inverse, inverse


def norm_back(grad, unit, inverse, gain):
    f = grad * gain
    return inverse * (
        f
        - jnp.mean(f, axis=-1, keepdims=True)
        - unit * jnp.mean(f * unit, axis=-1, keepdims=True)
    )


def blocks_of(rows):
    return [(first, min(WINDOW, rows - first)) for first in range(0, rows, WINDOW)]


def head_scores(qkv_ref, same, first, size, h, width):
    q = qkv_ref[first : first + size, h * HEAD_DIM : (h + 1) * HEAD_DIM]
    k = qkv_ref[first : first + size, width + h * HEAD_DIM : width + (h + 1) * HEAD_DIM]
    v = qkv_ref[first : first + size, 2 * width + h * HEAD_DIM : 2 * width + (h + 1) * HEAD_DIM]
    scores = jnp.where(same, dot_cols(q, k) * (1.0 / math.sqrt(HEAD_DIM)), -1e30)
    weights = jnp.exp(scores - jnp.max(scores, axis=-1, keepdims=True))
    weights = weights * (1.0 / jnp.sum(weights, axis=-1, keepdims=True))
    return q, k, v, weights


def attend_kernel(qkv_ref, col_ref, row_ref, out_ref):
    rows, width = out_ref.shape
    for first, size in blocks_of(rows):
        same = col_ref[first : first + size, :] == row_ref[:, first : first + size]
        for h in range(width // HEAD_DIM):
            q, k, v, weights = head_scores(qkv_ref, same, first, size, h, width)
            out_ref[first : first + size, h * HEAD_DIM : (h + 1) * HEAD_DIM] = dot(
                weights.astype(BF), v
            ).astype(BF)


def attend_back_kernel(qkv_ref, grad_ref, col_ref, row_ref, out_ref):
    rows, width = grad_ref.shape
    factor = 1.0 / math.sqrt(HEAD_DIM)
    for first, size in blocks_of(rows):
        same = col_ref[first : first + size, :] == row_ref[:, first : first + size]
        for h in range(width // HEAD_DIM):
            q, k, v, weights = head_scores(qkv_ref, same, first, size, h, width)
            grad = grad_ref[first : first + size, h * HEAD_DIM : (h + 1) * HEAD_DIM]
            soft = dot_cols(grad, v)
            center = jnp.sum(weights * soft, axis=-1, keepdims=True)
            grad_scores = (weights * (soft - center)).astype(BF)
            for part, value in enumerate(
                (
                    dot(grad_scores, k) * factor,
                    dot_rows(grad_scores, q) * factor,
                    dot_rows(weights.astype(BF), grad),
                )
            ):
                lane = part * width + h * HEAD_DIM
                out_ref[first : first + size, lane : lane + HEAD_DIM] = value.astype(BF)


def attend(qkv, owner_col, owner_row, groups):
    rows, width = qkv.shape[0], qkv.shape[1] // (3 * groups)
    return pl.pallas_call(
        attend_kernel,
        grid=(groups,),
        in_specs=[
            pl.BlockSpec((rows, 3 * width), lambda r: (0, r)),
            pl.BlockSpec((rows, 1), lambda r: (0, 0)),
            pl.BlockSpec((1, rows), lambda r: (0, 0)),
        ],
        out_specs=pl.BlockSpec((rows, width), lambda r: (0, r)),
        out_shape=jax.ShapeDtypeStruct((rows, groups * width), BF),
        name="attend",
    )(qkv, owner_col, owner_row)


def attend_back(qkv, grad, owner_col, owner_row, groups):
    rows, width = grad.shape[0], grad.shape[1] // groups
    return pl.pallas_call(
        attend_back_kernel,
        grid=(groups,),
        in_specs=[
            pl.BlockSpec((rows, 3 * width), lambda r: (0, r)),
            pl.BlockSpec((rows, width), lambda r: (0, r)),
            pl.BlockSpec((rows, 1), lambda r: (0, 0)),
            pl.BlockSpec((1, rows), lambda r: (0, 0)),
        ],
        out_specs=pl.BlockSpec((rows, 3 * width), lambda r: (0, r)),
        out_shape=jax.ShapeDtypeStruct((rows, 3 * groups * width), BF),
        name="attend_back",
    )(qkv, grad, owner_col, owner_row)


def gelu_parts(preact):
    phi = 0.5 * (1.0 + lax.erf(preact * (1.0 / math.sqrt(2.0))))
    slope = phi + preact * jnp.exp(-0.5 * preact * preact) * (1.0 / math.sqrt(2.0 * math.pi))
    return (preact * phi).astype(BF), slope


HALO = 80
MESH = pl.DeviceIdType.MESH


def places():
    mp = lax.axis_index("mp")
    dp = lax.axis_index("dp")
    y = dp % 2
    z = dp // 2
    sibling = mp + 1 - 2 * (mp % 2)
    opposite = mp + 2 - 4 * (mp // 2)
    across = opposite + 1 - 2 * (mp % 2)
    mp_peers = [{"mp": sibling}, {"mp": opposite}, {"mp": across}]
    y_peer = {"dp": dp + 1 - 2 * y}
    z_places = [(z + m) % 4 for m in (1, 2, 3)]
    z_peers = [{"dp": place * 2 + y} for place in z_places]
    return mp, y, z, mp_peers, y_peer, z_places, z_peers


def greet(peers):
    barrier = pltpu.get_barrier_semaphore()
    for peer in peers:
        pl.semaphore_signal(barrier, inc=1, device_id=peer, device_id_type=MESH)
    pl.semaphore_wait(barrier, len(peers))


def remote(source, target, send, recv, peer):
    return pltpu.make_async_remote_copy(
        src_ref=source,
        dst_ref=target,
        send_sem=send,
        recv_sem=recv,
        device_id=peer,
        device_id_type=MESH,
    )


def loop(count, body):
    def step(i, carry):
        body(i)
        return carry

    lax.fori_loop(0, count, step, 0)


def block_rows(i, size):
    return pl.ds(pl.multiple_of(i * size, size), size)


def start_all(copies):
    for copy in copies:
        copy.start()


def wait_recv_all(copies):
    for copy in copies:
        copy.wait_recv()


def item_of_rows(row, lengths, mp):
    window = row >> 8
    offset = row & (WINDOW - 1)
    length = jnp.where(window == 0, lengths[4 * mp], lengths[4 * mp + 2])
    second = jnp.where(offset >= length, 1, 0)
    in_pair = (window < 2) & (offset < PAIR_LEN)
    is_padding = (window == 2) & (offset < PADDING) & (mp == 3)
    return 2 * window + second, offset - second * length, in_pair, is_padding


def owner_of_rows(row, lengths, mp):
    item, _, in_pair, is_padding = item_of_rows(row, lengths, mp)
    return jnp.where(in_pair, item, jnp.where(is_padding, 16, -1))


def choose_item(item, values):
    result = jnp.where(item == 0, values[0], 0.0)
    for j in (1, 2, 3):
        result = jnp.where(item == j, values[j], result)
    return result


def joined(tiles, first):
    return jnp.concatenate([tiles[first + j : first + j + 1, :] for j in range(8)], axis=1)


def forward_kernel(
    lengths,
    groups,
    counts,
    scales,
    gain,
    shift,
    output_bias,
    hidden_gain,
    hidden_shift,
    query_bias,
    value_bias,
    up_bias,
    tokens_ref,
    cotangent_ref,
    query_ref,
    key_ref,
    value_ref,
    output_ref,
    up_ref,
    down_ref,
    tokens_out,
    cotangent_out,
    sums_out,
    stream_out,
    middle_out,
    normed_out,
    qkv_out,
    context_out,
    hidden_out,
    grad_mixed_out,
    active_out,
    grad_pre_out,
    wqkv_out,
    wo_out,
    wup_out,
    wdown_out,
    tokens_ext,
    cotangent_ext,
    tokens,
    cotangent,
    stream,
    middle,
    normed,
    qkv,
    context,
    hidden,
    grad_mixed,
    active,
    grad_pre,
    wqkv,
    wo,
    wup,
    wdown,
    sums,
    bias,
    part,
    from_mp,
    from_y,
    from_z,
    own_sem,
    halo_sem,
    store_sem,
    stat_send,
    stat_recv,
    bias_send,
    bias_recv,
    pair_send,
    pair_recv,
    x_send,
    x_recv,
    z_send,
    z_recv,
    y_send,
    y_recv,
    fwd_send,
    fwd_recv,
):
    mp, y, z, mp_peers, y_peer, z_places, z_peers = places()
    sibling, opposite, _ = mp_peers
    rows_here = tokens_ref.shape[0]
    rows = tokens.shape[0]
    width = query_ref.shape[1]
    blocks = rows // 32

    items = [
        (key_ref, 0, D, wqkv, width, width, False),
        (value_ref, 0, D, wqkv, 2 * width, width, False),
        (query_ref, 0, D, wqkv, 0, width, True),
        (output_ref, 0, width, wo, 0, D, False),
        (up_ref, 0, D // 2, wup, 0, D, False),
        (up_ref, D // 2, D // 2, wup, 0, D, False),
        (down_ref, 3 * D // 4, D // 4, wdown, 0, D, False),
        (down_ref, 0, 3 * D // 4, wdown, 0, D, True),
    ]
    KEY, VALUE, QUERY, OUTPUT, UP_A, UP_B, DOWN_A, DOWN_B = range(8)

    def source(i, start, size):
        return items[i][0].at[pl.ds(items[i][1] + start, size)]

    def place(i, r, start, size):
        _, first, _, ref, column, columns, _ = items[i]
        return ref.at[r, pl.ds(first + start, size), pl.ds(column, columns)]

    def part_of(i, first, eighths):
        size = items[i][2] // 8
        return pl.multiple_of(first * size, size), eighths * size

    own_copies = [
        pltpu.make_async_copy(
            source(i, 0, items[i][2]), place(i, 0, 0, items[i][2]), own_sem.at[i]
        )
        for i in range(8)
    ]
    pair_copies = [
        remote(
            source(i, 0, items[i][2]),
            place(i, 1, 0, items[i][2]),
            pair_send.at[i],
            pair_recv.at[i],
            sibling,
        )
        for i in range(8)
    ]

    def x_copy(i):
        start, size = (0, items[i][2]) if items[i][6] else part_of(i, y * 4 + z, 1)
        return remote(
            source(i, start, size), place(i, 2, start, size), x_send.at[i], x_recv.at[i], opposite
        )

    def z_copies(i):
        start, size = part_of(i, y * 4 + z, 1)
        view = place(i, 2, start, size)
        return [
            remote(view, view, z_send.at[i, m], z_recv.at[i, m], peer)
            for m, peer in enumerate(z_peers)
        ]

    def y_copy(i):
        start, size = part_of(i, y * 4, 4)
        view = place(i, 2, start, size)
        return remote(view, view, y_send.at[i], y_recv.at[i], y_peer)

    def fwd_copy(i):
        size = items[i][2]
        return remote(
            place(i, 2, 0, size), place(i, 3, 0, size), fwd_send.at[i], fwd_recv.at[i], sibling
        )

    def x_to_z(i):
        x_copy(i).wait_recv()
        start_all(z_copies(i))

    def z_to_y(i):
        wait_recv_all(z_copies(i))
        y_copy(i).start()

    def y_to_pair(i):
        (x_copy(i) if items[i][6] else y_copy(i)).wait_recv()
        fwd_copy(i).start()

    keep = [
        pltpu.make_async_copy(ref, ext.at[pl.ds(HALO, rows_here)], halo_sem.at[which, 2])
        for which, (ref, ext) in enumerate(
            ((tokens_ref, tokens_ext), (cotangent_ref, cotangent_ext))
        )
    ]
    start_all(keep)
    start_all(own_copies)
    bias[0, 0:1, :] = query_bias[...]
    bias[0, 1:2, :] = value_bias[...]
    for j in range(4):
        bias[0, 2 + j : 3 + j, :] = up_bias[:, j * width : (j + 1) * width]
    bias[0, 6:8, :] = jnp.zeros((2, width), F32)

    weights = [counts[groups[4 * mp + j]].astype(F32) for j in range(4)]
    weight_part = weights[0] + weights[1] + weights[2] + weights[3]
    keep[0].wait()

    def add_rows(i, carry):
        block = tokens_ext[pl.ds(pl.multiple_of(HALO + i * 16, 16), 16), :].astype(F32)
        row = mp * rows_here + i * 16 + lax.broadcasted_iota(jnp.int32, (16, 1), 0)
        kept = jnp.where(row < PAIRS * PAIR_LEN, block, 0.0)
        return carry[0] + kept, carry[1] + kept * block

    zero = jnp.zeros((16, D), F32)
    first, second = lax.fori_loop(0, rows_here // 16, add_rows, (zero, zero))
    first = jnp.sum(first, axis=0, keepdims=True)
    second = jnp.sum(second, axis=0, keepdims=True)
    for j in range(8):
        part[0, j : j + 1, :] = first[:, j * 128 : (j + 1) * 128]
        part[0, 8 + j : 9 + j, :] = second[:, j * 128 : (j + 1) * 128]
    part[0, 16:24, :] = jnp.zeros((8, 128), F32) + weight_part
    greet(mp_peers + [y_peer] + z_peers)

    def exchange(stage, peers, slots):
        copies = [
            remote(
                part.at[stage],
                slots.at[m],
                stat_send.at[stage, m],
                stat_recv.at[stage, m],
                peer,
            )
            for m, peer in enumerate(peers)
        ]
        start_all(copies)
        return copies

    def total(stage, copies, slots):
        value = part[stage]
        for m, copy in enumerate(copies):
            copy.wait_recv()
            value = value + slots[m]
        return value

    sums_a = exchange(0, mp_peers, from_mp)
    after = {"mp": (mp + 1) % 4}
    halo_copies = [
        remote(
            ref.at[pl.ds(rows_here - HALO, HALO)],
            ext.at[pl.ds(0, HALO)],
            halo_sem.at[which, 0],
            halo_sem.at[which, 1],
            after,
        )
        for which, (ref, ext) in enumerate(
            ((tokens_ref, tokens_ext), (cotangent_ref, cotangent_ext))
        )
    ]
    bias_copies = [
        remote(bias.at[0], bias.at[r + 1], bias_send.at[r], bias_recv.at[r], peer)
        for r, peer in enumerate(mp_peers)
    ]
    start_all(halo_copies + bias_copies)
    start_all([x_copy(i) for i in range(8)])
    start_all([pair_copies[i] for i in (QUERY, KEY, VALUE, OUTPUT, UP_A, UP_B, DOWN_A, DOWN_B)])
    part[1] = total(0, sums_a, from_mp)
    sums_b = exchange(1, [y_peer], from_y)

    place_id = lax.broadcasted_iota(jnp.int32, (64, 1), 0)
    table_scale = choose_item(
        place_id >> 4, [scales[groups[4 * mp + j]] for j in range(4)]
    )
    quarter = D // 4
    lane = lax.broadcasted_iota(jnp.int32, (1, quarter), 1).astype(F32)
    frequency = jnp.exp(-math.log(10000.0) * lane / quarter)
    angle = ((place_id & 15).astype(F32) * table_scale) * frequency
    table = jnp.concatenate([jnp.sin(angle), jnp.cos(angle)], axis=1)
    row = lax.broadcasted_iota(jnp.int32, (rows, 64), 0)
    column = lax.broadcasted_iota(jnp.int32, (rows, 64), 1)
    item, position, in_pair, _ = item_of_rows(row, lengths, mp)
    across = (position * 9363) >> 17
    for half, code in enumerate((across, position - SIDE * across)):
        chosen = jnp.where(in_pair & (column == item * 16 + code), 1.0, 0.0)
        stream[:, half * 2 * quarter : (half + 1) * 2 * quarter] = lax.dot_general(
            chosen,
            table,
            (((1,), (0,)), ((), ())),
            precision=lax.Precision.HIGHEST,
            preferred_element_type=F32,
        )
    part[2] = total(1, sums_b, from_y)
    sums_c = exchange(2, z_peers, from_z)
    x_to_z(KEY)
    x_to_z(VALUE)

    wait_recv_all(halo_copies)
    keep[1].wait()
    own_len = 2 * PAIR_LEN
    row = lax.broadcasted_iota(jnp.int32, (rows, HALO + rows_here), 0)
    column = lax.broadcasted_iota(jnp.int32, (rows, HALO + rows_here), 1)
    window = row >> 8
    offset = row & (WINDOW - 1)
    wanted = HALO - (rows_here - own_len) * mp + window * PAIR_LEN + offset
    tail = jnp.where(mp == 3, HALO + rows_here - PADDING, 4096) + offset
    wanted = jnp.where(window < 2, jnp.where(offset < PAIR_LEN, wanted, -1), tail)
    chosen = jnp.where(column == wanted, 1.0, 0.0).astype(BF)
    tokens[...] = dot(chosen, tokens_ext[...]).astype(BF)
    cotangent[...] = dot(chosen, cotangent_ext[...]).astype(BF)
    sums[...] = total(2, sums_c, from_z)

    slices = lax.axis_size("dp")
    count_valid = slices * PAIRS * PAIR_LEN
    column_mean = joined(sums, 0) / count_valid
    spread = joined(sums, 8) / count_valid - column_mean * column_mean
    inverse = lax.rsqrt(spread + 1e-05)
    mean_weight = sums[16:17, 0:1] / (slices * 16)

    def first_norm(i):
        here = block_rows(i, 32)
        value = (tokens[here, :].astype(F32) - column_mean) * inverse + stream[here, :]
        stream[here, :] = value
        unit, _ = stats(value)
        normed[here, :] = (unit * gain[...] + shift[...]).astype(BF)
        row = i * 32 + lax.broadcasted_iota(jnp.int32, (32, 1), 0)
        item, _, in_pair, _ = item_of_rows(row, lengths, mp)
        row_weight = jnp.where(in_pair, choose_item(item, weights), 0.0) / mean_weight
        grad_mixed[here, :] = (cotangent[here, :].astype(F32) * row_weight).astype(BF)

    loop(blocks, first_norm)

    def store(i, value, ref):
        return pltpu.make_async_copy(value, ref, store_sem.at[i])

    stores = [
        store(0, tokens, tokens_out),
        store(1, cotangent, cotangent_out),
        store(2, sums, sums_out),
        store(3, stream, stream_out),
        store(4, normed, normed_out),
        store(5, grad_mixed, grad_mixed_out),
        store(6, qkv, qkv_out),
        store(7, context, context_out),
        store(8, wqkv, wqkv_out),
        store(9, middle, middle_out),
        store(10, hidden, hidden_out),
        store(11, wo, wo_out),
        store(12, active, active_out),
        store(13, grad_pre, grad_pre_out),
        store(14, wup, wup_out),
        store(15, wdown, wdown_out),
    ]
    start_all(stores[:6])

    for copy in bias_copies:
        copy.wait_recv()

    def head_group(r):
        @pl.when(r == 0)
        def _():
            for i in (QUERY, KEY, VALUE):
                own_copies[i].wait()

        @pl.when(r == 1)
        def _():
            for i in (OUTPUT, UP_A, UP_B, DOWN_A):
                x_to_z(i)
            for i in (QUERY, KEY, VALUE):
                pair_copies[i].wait_recv()

        @pl.when(r == 2)
        def _():
            for i in (QUERY, KEY, VALUE):
                y_to_pair(i)
            z_to_y(OUTPUT)

        @pl.when(r == 3)
        def _():
            for i in (QUERY, KEY, VALUE):
                fwd_copy(i).wait_recv()
            y_to_pair(OUTPUT)

        base = r * 3 * width
        for n in range(3):
            value = dot(normed[...], wqkv[r, :, n * width : (n + 1) * width])
            if n != 1:
                value = value + bias[r, n // 2 : n // 2 + 1, :]
            qkv[:, pl.ds(pl.multiple_of(base + n * width, width), width)] = value.astype(BF)

        @pl.when(r == 0)
        def _():
            z_to_y(KEY)
            z_to_y(VALUE)

        def head_pair(p):
            lanes = [
                pl.ds(pl.multiple_of(base + n * width + p * 128, 128), 128) for n in range(3)
            ]
            target = pl.ds(pl.multiple_of(r * width + p * 128, 128), 128)
            for first, size in blocks_of(rows):
                here = pl.ds(first, size)
                same = owner_of_rows(
                    first + lax.broadcasted_iota(jnp.int32, (size, 1), 0), lengths, mp
                ) == owner_of_rows(
                    first + lax.broadcasted_iota(jnp.int32, (1, size), 1), lengths, mp
                )
                q, k, v = [qkv[here, lane] for lane in lanes]
                results = []
                for h in range(2):
                    cut = slice(h * HEAD_DIM, (h + 1) * HEAD_DIM)
                    low = softmax_rows(q[:, cut], k[:, cut], same).astype(BF)
                    results.append(dot(low, v[:, cut]).astype(BF))
                context[here, target] = jnp.concatenate(results, axis=1)

        loop(width // 128, head_pair)

    loop(4, head_group)
    start_all(stores[6:9])
    z_to_y(UP_A)

    own_copies[OUTPUT].wait()
    pair_copies[OUTPUT].wait_recv()
    fwd_copy(OUTPUT).wait_recv()

    def attention_output(n):
        columns = block_rows(n, 256)
        value = stream[:, columns] + output_bias[:, columns]
        for r in range(4):
            value = value + dot(context[:, r * width : (r + 1) * width], wo[r, :, columns])
        middle[:, columns] = value

    loop(4, attention_output)

    def second_norm(i):
        here = block_rows(i, 32)
        unit, _ = stats(middle[here, :])
        hidden[here, :] = (unit * hidden_gain[...] + hidden_shift[...]).astype(BF)

    loop(blocks, second_norm)
    start_all(stores[9:12])

    def hidden_group(r):
        @pl.when(r == 0)
        def _():
            for i in (UP_A, UP_B, DOWN_A, DOWN_B):
                own_copies[i].wait()
            z_to_y(UP_B)

        @pl.when(r == 1)
        def _():
            y_to_pair(UP_A)
            z_to_y(DOWN_A)
            for i in (UP_A, UP_B, DOWN_A, DOWN_B):
                pair_copies[i].wait_recv()

        @pl.when(r == 2)
        def _():
            for i in (DOWN_B, UP_B, DOWN_A):
                y_to_pair(i)

        @pl.when(r == 3)
        def _():
            for i in (UP_A, UP_B, DOWN_A, DOWN_B):
                fwd_copy(i).wait_recv()

        def hidden_tile(n):
            columns = block_rows(n, 256)
            target = pl.ds(pl.multiple_of(r * D + n * 256, 256), 256)
            preact = dot(hidden[...], wup[r, :, columns]) + bias[r, pl.ds(2 + n, 1), :]
            value, slope = gelu_parts(preact)
            active[:, target] = value
            grad = dot_cols(grad_mixed[...], wdown[r, columns, :])
            grad_pre[:, target] = (grad * slope).astype(BF)

        loop(4, hidden_tile)

    loop(4, hidden_group)
    start_all(stores[12:])

    for i in range(8):
        pair_copies[i].wait_send()
        x_copy(i).wait_send()
        fwd_copy(i).wait_send()
        if not items[i][6]:
            for copy in z_copies(i):
                copy.wait_send()
            y_copy(i).wait_send()
    for copy in bias_copies + halo_copies + sums_a + sums_b + sums_c:
        copy.wait_send()
    for copy in stores:
        copy.wait()


def softmax_rows(q, k, same):
    scores = jnp.where(same, dot_cols(q, k) * (1.0 / math.sqrt(HEAD_DIM)), -1e30)
    weights = jnp.exp(scores - jnp.max(scores, axis=-1, keepdims=True))
    return weights * (1.0 / jnp.sum(weights, axis=-1, keepdims=True))


def forward(smalls, vectors, tokens, cotangent, weights, rows):
    width = weights[0].shape[1]
    shape = jax.ShapeDtypeStruct
    full = shape((rows, D), F32)
    low = shape((rows, D), BF)
    wide = shape((rows, 4 * D), BF)
    outs = (
        low,
        low,
        shape((24, 128), F32),
        full,
        full,
        low,
        shape((rows, 12 * width), BF),
        low,
        low,
        low,
        wide,
        wide,
        shape((4, D, 3 * width), BF),
        shape((4, width, D), BF),
        shape((4, D, D), BF),
        shape((4, D, D), BF),
    )
    scratch = [shape((HALO + tokens.shape[0], D), BF)] * 2 + [
        low,
        low,
        full,
        full,
        low,
        outs[6],
        low,
        low,
        low,
        wide,
        wide,
    ]
    scratch += list(outs[12:]) + [
        shape((24, 128), F32),
        shape((4, 8, width), F32),
        shape((3, 24, 128), F32),
        shape((3, 24, 128), F32),
        shape((1, 24, 128), F32),
        shape((3, 24, 128), F32),
    ]
    dma = pltpu.SemaphoreType.DMA
    any_space = pl.BlockSpec(memory_space=pl.ANY)
    return pl.pallas_call(
        forward_kernel,
        out_shape=outs,
        in_specs=[pl.BlockSpec(memory_space=pltpu.SMEM)] * 4
        + [pl.BlockSpec(memory_space=pltpu.VMEM)] * 8
        + [any_space] * 8,
        out_specs=(any_space,) * len(outs),
        scratch_shapes=[pltpu.VMEM(v.shape, v.dtype) for v in scratch]
        + [
            dma((8,)),
            dma((2, 3)),
            dma((16,)),
            dma((3, 3)),
            dma((3, 3)),
            dma((3,)),
            dma((3,)),
            dma((8,)),
            dma((8,)),
            dma((8,)),
            dma((8,)),
            dma((8, 3)),
            dma((8, 3)),
            dma((8,)),
            dma((8,)),
            dma((8,)),
            dma((8,)),
        ],
        compiler_params=pltpu.CompilerParams(
            collective_id=1, has_side_effects=True, vmem_limit_bytes=67043328
        ),
        name="forward",
    )(*smalls, *vectors, tokens, cotangent, *weights)


CHUNK = 128
CHUNKS = 24
STAGE_DELAY = (0, 1, 3, 5, 7, 9, 11)
TICK_HIDDEN, TICK_SECOND, TICK_CONTEXT, TICK_HEADS = 0, 4, 5, 6
TICK_NORMED, TICK_FIRST, TICK_MIXED = 14, 18, 19
TICK_SUMS = (18, 20, 22, 24)


def backward_kernel(
    lengths,
    groups,
    counts,
    gain,
    hidden_gain,
    down_bias,
    sums,
    tokens_ref,
    cotangent_ref,
    stream_ref,
    middle_ref,
    normed_ref,
    qkv_ref,
    context_ref,
    hidden_ref,
    grad_mixed_ref,
    active_ref,
    grad_pre_ref,
    wqkv_ref,
    wo_ref,
    wup_ref,
    wdown_ref,
    reduced_out,
    finals_out,
    layer_out,
    tokens_grad_out,
    made,
    pair,
    across,
    over_y,
    over_z,
    final,
    act,
    grad_pre,
    hidden,
    grad_mixed,
    context,
    normed,
    grad_attended,
    qkv,
    grad_context,
    rowbuf,
    gradient,
    trunk,
    stream,
    weight,
    packet,
    from_mp,
    from_y,
    from_z,
    load_sem,
    act_sem,
    weight_sem,
    pair_send,
    pair_recv,
    across_send,
    across_recv,
    y_send,
    y_recv,
    z_send,
    z_recv,
    back_z_send,
    back_z_recv,
    back_y_send,
    back_y_recv,
    out_sem,
    stat_send,
    stat_recv,
):
    mp, y, z, mp_peers, y_peer, z_places, z_peers = places()
    sibling, opposite, _ = mp_peers
    half = CHUNK // 2
    eighth = CHUNK // 8
    rows = normed.shape[0]
    width = context.shape[1] // 4
    blocks = rows // 32

    loads = {
        name: pltpu.make_async_copy(source, target, load_sem.at[i])
        for i, (name, source, target) in enumerate(
            (
                ("grad_mixed", grad_mixed_ref, grad_mixed),
                ("grad_pre", grad_pre_ref, grad_pre),
                ("middle", middle_ref, trunk),
                ("cotangent", cotangent_ref, rowbuf),
                ("qkv", qkv_ref, qkv),
                ("hidden", hidden_ref, hidden),
                ("context", context_ref, context),
                ("normed", normed_ref, normed),
                ("stream", stream_ref, stream),
                ("tokens", tokens_ref, rowbuf),
                ("active", active_ref, grad_pre),
                ("middle again", middle_ref, stream),
                ("layer", hidden, layer_out),
                ("tokens_grad", gradient, tokens_grad_out),
            )
        )
    }

    def act_loads(c):
        return [
            pltpu.make_async_copy(
                active_ref.at[:, pl.ds(pl.multiple_of(r * D + c * CHUNK, CHUNK), CHUNK)],
                act.at[c % 2, r],
                act_sem.at[c % 2, r],
            )
            for r in range(4)
        ]

    def weight_load(s):
        if s < 4:
            source = wup_ref.at[s]
        elif s == 4:
            source = wo_ref
        elif s < 9:
            source = wqkv_ref.at[s - 5]
        else:
            source = wdown_ref.at[s - 9]
        target = weight.at[s % 2, :, pl.ds(0, 3 * width)] if 5 <= s < 9 else weight.at[s % 2]
        return pltpu.make_async_copy(source, target, weight_sem.at[s % 2])

    for c in range(2):
        start_all(act_loads(c))
    loads["grad_mixed"].start()
    weight_load(0).start()
    loads["grad_pre"].start()
    weight_load(1).start()
    for name in ("middle", "cotangent", "qkv", "hidden", "context", "normed", "stream"):
        loads[name].start()
    greet(mp_peers + [y_peer] + z_peers)

    weights = [counts[groups[4 * mp + j]].astype(F32) for j in range(4)]
    slices = lax.axis_size("dp")
    count_valid = slices * PAIRS * PAIR_LEN
    column_mean = joined(sums, 0) / count_valid
    spread = joined(sums, 8) / count_valid - column_mean * column_mean
    inverse = lax.rsqrt(spread + 1e-05)
    mean_weight = sums[16:17, 0:1] / (slices * 16)

    def pair_copy(c):
        return remote(
            made.at[c % 2, pl.ds(0, 2)], pair.at[c], pair_send.at[c], pair_recv.at[c], sibling
        )

    def across_copy(c):
        return remote(
            pair.at[c, 1], across.at[c], across_send.at[c], across_recv.at[c], opposite
        )

    def y_copy(c):
        return remote(
            across.at[c, pl.ds(pl.multiple_of((1 - y) * half, half), half)],
            over_y.at[c],
            y_send.at[c],
            y_recv.at[c],
            y_peer,
        )

    def z_copies(c):
        return [
            remote(
                over_y.at[c, pl.ds(pl.multiple_of(place * eighth, eighth), eighth)],
                over_z.at[c, m],
                z_send.at[c, m],
                z_recv.at[c, m],
                peer,
            )
            for m, (place, peer) in enumerate(zip(z_places, z_peers))
        ]

    def back_z_copies(c):
        view = final.at[c, pl.ds(pl.multiple_of(y * half + z * eighth, eighth), eighth)]
        return [
            remote(view, view, back_z_send.at[c, m], back_z_recv.at[c, m], peer)
            for m, peer in enumerate(z_peers)
        ]

    def back_y_copy(c):
        view = final.at[c, pl.ds(pl.multiple_of(y * half, half), half)]
        return remote(view, view, back_y_send.at[c], back_y_recv.at[c], y_peer)

    def out_copy(c):
        return pltpu.make_async_copy(final.at[c], reduced_out.at[c], out_sem.at[c])

    def make(c):
        @pl.when(c < 8)
        def _():
            for copy in act_loads(c):
                copy.wait()

        def one(j):
            r = 2 * j + 1 - 5 * (j // 2)

            def store(left, right):
                made[c % 2, j] = dot_rows(left, right).astype(BF)

            @pl.when(c < 8)
            def _():
                store(act[c % 2, r], grad_mixed[...])

            @pl.when((c >= 8) & (c < 16))
            def _():
                store(
                    hidden[:, block_rows(c - 8, CHUNK)], grad_pre[:, block_rows(r, D)]
                )

            @pl.when((c >= 16) & (c < 18))
            def _():
                store(context[:, block_rows(2 * r + c - 16, CHUNK)], grad_attended[...])

            @pl.when(c >= 18)
            def _():
                store(qkv[:, block_rows(6 * r + c - 18, CHUNK)], normed[...])

        loop(4, one)

        @pl.when(c < 6)
        def _():
            start_all(act_loads(c + 2))

    def add_pair(c):
        pair_copy(c).wait()

        def body(i):
            here = block_rows(i, 32)
            for which in (1, 0):
                pair[c, which, here, :] = (
                    pair[c, which, here, :].astype(F32)
                    + made[c % 2, 2 + which, here, :].astype(F32)
                ).astype(BF)

        loop(CHUNK // 32, body)

    def add_across(c):
        across_copy(c).wait_recv()

        def body(i):
            here = block_rows(i, 32)
            across[c, here, :] = (
                across[c, here, :].astype(F32) + pair[c, 0, here, :].astype(F32)
            ).astype(BF)

        loop(CHUNK // 32, body)

    def add_y(c):
        y_copy(c).wait_recv()

        def body(i):
            here = block_rows(i, 32)
            own = pl.ds(pl.multiple_of(y * half + i * 32, 32), 32)
            over_y[c, here, :] = (
                over_y[c, here, :].astype(F32) + across[c, own, :].astype(F32)
            ).astype(BF)

        loop(half // 32, body)

    def add_z(c):
        wait_recv_all(z_copies(c))
        value = over_y[c, block_rows(z, eighth), :].astype(F32)
        for m in range(3):
            value = value + over_z[c, m].astype(F32)
        final[c, pl.ds(pl.multiple_of(y * half + z * eighth, eighth), eighth), :] = value.astype(BF)

    handle = (
        make,
        add_pair,
        add_across,
        add_y,
        add_z,
        lambda c: wait_recv_all(back_z_copies(c)),
        lambda c: back_y_copy(c).wait_recv(),
    )
    send = (
        lambda c: [pair_copy(c)],
        lambda c: [across_copy(c)],
        lambda c: [y_copy(c)],
        z_copies,
        back_z_copies,
        lambda c: [back_y_copy(c)],
        lambda c: [out_copy(c)],
    )

    def hidden_step(r):
        left = block_rows(r, D)

        def tile(n):
            columns = block_rows(n, 256)
            value = dot_cols(grad_pre[:, left], weight[r % 2, columns, :])

            @pl.when(r == 0)
            def _():
                gradient[:, columns] = value

            @pl.when(r > 0)
            def _():
                gradient[:, columns] = gradient[:, columns] + value

        loop(4, tile)

    def fold(value):
        return jnp.sum(value.reshape(4, 8, D), axis=0)

    def put(index, value):
        for j in range(8):
            packet[0, 8 * index + j : 8 * index + j + 1, :] = value[:, j * 128 : (j + 1) * 128]

    def put_all(first, values):
        for i, value in enumerate(values):
            put(first + i, jnp.sum(value, axis=0, keepdims=True))

    def ones_dot(value):
        return dot(jnp.ones((16, rows), BF), value)[0:1, :]

    def row_weight_of(i):
        row = i * 32 + lax.broadcasted_iota(jnp.int32, (32, 1), 0)
        item, _, in_pair, _ = item_of_rows(row, lengths, mp)
        return jnp.where(in_pair, choose_item(item, weights), 0.0) / mean_weight, in_pair

    zero = jnp.zeros((8, D), F32)

    def second_norm_back():
        def body(i, carry):
            here = block_rows(i, 32)
            unit, scale = stats(trunk[here, :])
            grad = gradient[here, :]
            row_weight, _ = row_weight_of(i)
            value = rowbuf[here, :].astype(F32) * row_weight + norm_back(
                grad, unit, scale, hidden_gain[...]
            )
            trunk[here, :] = value
            low = value.astype(BF)
            grad_attended[here, :] = low
            return (
                carry[0] + fold(grad * unit),
                carry[1] + fold(grad),
                carry[2] + fold(low.astype(F32)),
            )

        put_all(4, lax.fori_loop(0, blocks, body, (zero, zero, zero)))
        put(7, ones_dot(grad_mixed[...]))

    def context_step():
        def tile(n):
            columns = block_rows(n, 256)
            grad_context[:, columns] = dot_cols(grad_attended[...], weight[0, columns, :]).astype(BF)

        loop(4, tile)

    def head_pair_back(index):
        r = index // 2
        p = index % 2
        lanes = [block_rows(6 * r + 2 * n + p, 128) for n in range(3)]
        source = block_rows(2 * r + p, 128)
        factor = 1.0 / math.sqrt(HEAD_DIM)
        for first, size in blocks_of(rows):
            here = pl.ds(first, size)
            same = owner_of_rows(
                first + lax.broadcasted_iota(jnp.int32, (size, 1), 0), lengths, mp
            ) == owner_of_rows(first + lax.broadcasted_iota(jnp.int32, (1, size), 1), lengths, mp)
            q, k, v = [qkv[here, lane] for lane in lanes]
            g = grad_context[here, source]
            results = []
            for h in range(2):
                cut = slice(h * HEAD_DIM, (h + 1) * HEAD_DIM)
                soft = softmax_rows(q[:, cut], k[:, cut], same)
                grad_soft = dot_cols(g[:, cut], v[:, cut])
                center = jnp.sum(soft * grad_soft, axis=-1, keepdims=True)
                grad_scores = (soft * (grad_soft - center)).astype(BF)
                results.append(
                    (
                        (dot(grad_scores, k[:, cut]) * factor).astype(BF),
                        (dot_rows(grad_scores, q[:, cut]) * factor).astype(BF),
                        dot_rows(soft.astype(BF), g[:, cut]).astype(BF),
                    )
                )
            for n in range(3):
                qkv[here, lanes[n]] = jnp.concatenate([results[0][n], results[1][n]], axis=1)

    def normed_step(r):
        left = qkv[:, block_rows(r, 3 * width)]

        def tile(n):
            columns = block_rows(n, 256)
            value = dot_cols(left, weight[(r + 1) % 2, columns, 0 : 3 * width])

            @pl.when(r == 0)
            def _():
                gradient[:, columns] = value

            @pl.when(r > 0)
            def _():
                gradient[:, columns] = gradient[:, columns] + value

        loop(4, tile)

    def first_norm_back():
        def body(i, carry):
            here = block_rows(i, 32)
            unit, scale = stats(stream[here, :])
            grad = gradient[here, :]
            value = trunk[here, :] + norm_back(grad, unit, scale, gain[...])
            standard = (rowbuf[here, :].astype(F32) - column_mean) * inverse
            gradient[here, :] = value
            return (
                carry[0] + fold(value),
                carry[1] + fold(value * standard),
                carry[2] + fold(grad * unit),
                carry[3] + fold(grad),
            )

        put_all(0, lax.fori_loop(0, blocks, body, (zero, zero, zero, zero)))
        for r in range(4):
            if r:
                packet[r, 0:64, :] = packet[0, 0:64, :]
            parts = [
                ones_dot(qkv[:, (3 * r + n) * width : (3 * r + n + 1) * width]) for n in (0, 2)
            ] + [
                ones_dot(grad_pre[:, r * D + n * width : r * D + (n + 1) * width]) for n in range(4)
            ]
            for i, value in enumerate(parts):
                for j in range(2):
                    packet[r, 64 + 2 * i + j : 65 + 2 * i + j, :] = value[
                        :, j * 128 : (j + 1) * 128
                    ]
            packet[r, 76:80, :] = jnp.zeros((4, 128), F32)

    def mixed_step(r):
        left = grad_pre[:, block_rows(r, D)]

        def tile(n):
            columns = block_rows(n, 256)
            stream[:, columns] = stream[:, columns] + dot(left, weight[(r + 1) % 2, :, columns])

        loop(4, tile)

    def layer_step():
        def body(i):
            here = block_rows(i, 32)
            hidden[here, :] = (stream[here, :] + down_bias[...]).astype(BF)

        loop(blocks, body)

    def exchange(stage, sources, peers, slots):
        return [
            remote(
                source, slots.at[m], stat_send.at[stage, m], stat_recv.at[stage, m], peer
            )
            for m, (source, peer) in enumerate(zip(sources, peers))
        ]

    sums_a = exchange(0, [packet.at[r] for r in (1, 2, 3)], mp_peers, from_mp)
    sums_b = exchange(1, [packet.at[4]], [y_peer], from_y)
    sums_c = exchange(2, [packet.at[5]] * 3, z_peers, from_z)

    def gather_sums(first, copies, slots, target):
        value = packet[first]
        for m, copy in enumerate(copies):
            copy.wait_recv()
            value = value + slots[m]
        packet[target] = value

    def tokens_step():
        total = joined(packet[6], 0), joined(packet[6], 8)

        def body(i):
            here = block_rows(i, 32)
            standard = (rowbuf[here, :].astype(F32) - column_mean) * inverse
            _, in_pair = row_weight_of(i)
            share = jnp.where(in_pair, 1.0 / count_valid, 0.0)
            gradient[here, :] = inverse * (
                gradient[here, :] - share * (total[0] + total[1] * standard)
            )

        loop(blocks, body)

    def work(k):
        for s in range(4):

            @pl.when(k == TICK_HIDDEN + s)
            def _(s=s):
                if s == 0:
                    loads["grad_pre"].wait()
                weight_load(s).wait()

        @pl.when((k >= TICK_HIDDEN) & (k < TICK_HIDDEN + 4))
        def _():
            hidden_step(k - TICK_HIDDEN)

        for s in range(4):

            @pl.when(k == TICK_HIDDEN + s)
            def _(s=s):
                weight_load(s + 2).start()

        @pl.when(k == TICK_SECOND)
        def _():
            loads["middle"].wait()
            loads["cotangent"].wait()
            second_norm_back()
            loads["tokens"].start()

        @pl.when(k == TICK_CONTEXT)
        def _():
            weight_load(4).wait()
            context_step()
            weight_load(6).start()
            loads["qkv"].wait()

        @pl.when((k >= TICK_HEADS) & (k < TICK_HEADS + 8))
        def _():
            head_pair_back(k - TICK_HEADS)

        for s in range(4):

            @pl.when(k == TICK_NORMED + s)
            def _(s=s):
                weight_load(5 + s).wait()

        @pl.when((k >= TICK_NORMED) & (k < TICK_NORMED + 4))
        def _():
            normed_step(k - TICK_NORMED)

        for s in range(4):

            @pl.when(k == TICK_NORMED + s)
            def _(s=s):
                weight_load(7 + s).start()

        @pl.when(k == TICK_FIRST)
        def _():
            loads["stream"].wait()
            loads["tokens"].wait()
            first_norm_back()
            loads["active"].start()
            loads["middle again"].start()
            start_all(sums_a)

        for s in range(4):

            @pl.when(k == TICK_MIXED + s)
            def _(s=s):
                if s == 0:
                    loads["active"].wait()
                    loads["middle again"].wait()
                weight_load(9 + s).wait()

        @pl.when((k >= TICK_MIXED) & (k < TICK_MIXED + 4))
        def _():
            mixed_step(k - TICK_MIXED)

        for s in range(2):

            @pl.when(k == TICK_MIXED + s)
            def _(s=s):
                weight_load(11 + s).start()

        @pl.when(k == TICK_MIXED + 3)
        def _():
            layer_step()
            loads["layer"].start()

        @pl.when(k == TICK_SUMS[1])
        def _():
            gather_sums(0, sums_a, from_mp, 4)
            start_all(sums_b)

        @pl.when(k == TICK_SUMS[2])
        def _():
            gather_sums(4, sums_b, from_y, 5)
            start_all(sums_c)

        @pl.when(k == TICK_SUMS[3])
        def _():
            gather_sums(5, sums_c, from_z, 6)
            finals_out[...] = packet[6]
            tokens_step()
            loads["tokens_grad"].start()

    waits = {0: ("grad_mixed",), 8: ("hidden",), 16: ("context",), 18: ("normed",)}

    def tick(k, carry):
        for when, names in waits.items():

            @pl.when(k == when)
            def _(names=names):
                for name in names:
                    loads[name].wait()

        def staged(stage, actions):
            c = k - STAGE_DELAY[stage]

            @pl.when((c >= 0) & (c < CHUNKS))
            def _():
                actions[stage](c)

        sends = tuple(lambda c, f=f: start_all(f(c)) for f in send)
        for stage in (6, 5, 4, 3, 2):
            staged(stage, handle)
        for stage in (2, 3, 4, 5, 6):
            staged(stage, sends)
        staged(0, handle)
        staged(1, handle)
        staged(0, sends)
        staged(1, sends)
        work(k)
        return carry

    lax.fori_loop(0, CHUNKS + STAGE_DELAY[-1], tick, 0)

    def finish(c):
        across_copy(c).wait_send()
        y_copy(c).wait_send()
        for copy in z_copies(c) + back_z_copies(c):
            copy.wait_send()
        back_y_copy(c).wait_send()
        out_copy(c).wait()

    loop(CHUNKS, finish)
    for copy in sums_a + sums_b + sums_c:
        copy.wait_send()
    loads["layer"].wait()
    loads["tokens_grad"].wait()


def backward(smalls, vectors, sums, saved):
    (
        tokens,
        cotangent,
        stream,
        middle,
        normed,
        qkv,
        context,
        hidden,
        grad_mixed,
        active,
        grad_pre,
        wqkv,
        wo,
        wup,
        wdown,
    ) = saved
    rows = normed.shape[0]
    shape = jax.ShapeDtypeStruct
    low = shape((rows, D), BF)
    full = shape((rows, D), F32)
    packed = shape((80, 128), F32)
    scratch = [
        shape((2, 4, CHUNK, D), BF),
        shape((CHUNKS, 2, CHUNK, D), BF),
        shape((CHUNKS, CHUNK, D), BF),
        shape((CHUNKS, CHUNK // 2, D), BF),
        shape((CHUNKS, 3, CHUNK // 8, D), BF),
        shape((CHUNKS, CHUNK, D), BF),
        shape((2, 4, rows, CHUNK), BF),
        shape(grad_pre.shape, BF),
        low,
        low,
        low,
        low,
        low,
        shape(qkv.shape, BF),
        low,
        low,
        full,
        full,
        full,
        shape((2, D, D), BF),
        shape((7, 80, 128), F32),
        shape((3, 80, 128), F32),
        shape((1, 80, 128), F32),
        shape((3, 80, 128), F32),
    ]
    dma = pltpu.SemaphoreType.DMA
    any_space = pl.BlockSpec(memory_space=pl.ANY)
    vmem = pl.BlockSpec(memory_space=pltpu.VMEM)
    return pl.pallas_call(
        backward_kernel,
        out_shape=(shape((CHUNKS, CHUNK, D), BF), packed, low, full),
        in_specs=[pl.BlockSpec(memory_space=pltpu.SMEM)] * 3 + [vmem] * 4 + [any_space] * 15,
        out_specs=(any_space, vmem, any_space, any_space),
        scratch_shapes=[pltpu.VMEM(v.shape, v.dtype) for v in scratch]
        + [
            dma((14,)),
            dma((2, 4)),
            dma((2,)),
            dma((CHUNKS,)),
            dma((CHUNKS,)),
            dma((CHUNKS,)),
            dma((CHUNKS,)),
            dma((CHUNKS,)),
            dma((CHUNKS,)),
            dma((CHUNKS, 3)),
            dma((CHUNKS, 3)),
            dma((CHUNKS, 3)),
            dma((CHUNKS, 3)),
            dma((CHUNKS,)),
            dma((CHUNKS,)),
            dma((CHUNKS,)),
            dma((3, 3)),
            dma((3, 3)),
        ],
        compiler_params=pltpu.CompilerParams(
            collective_id=2, has_side_effects=True, vmem_limit_bytes=67043328
        ),
        name="backward",
    )(
        *smalls,
        *vectors,
        sums,
        tokens,
        cotangent,
        stream,
        middle,
        normed,
        qkv,
        context,
        hidden,
        grad_mixed,
        active,
        grad_pre,
        wqkv,
        wo.reshape(D, D),
        wup,
        wdown,
    )


def general_shards(
    tokens,
    cotangent,
    item_lengths,
    item_group,
    group_count,
    grid_scale,
    norm_gain,
    norm_shift,
    query_weight,
    query_bias,
    key_weight,
    value_weight,
    value_bias,
    output_weight,
    output_bias,
    hidden_gain,
    hidden_shift,
    up_weight,
    up_bias,
    down_weight,
    down_bias,
):
    shard_count = lax.axis_size("mp")
    slice_count = lax.axis_size("dp")
    mp = lax.axis_index("mp")
    rows_here = tokens.shape[0]
    item_count = item_lengths.shape[0]
    pairs_here = PAIRS // shard_count
    own_rows = pairs_here * PAIR_LEN
    shift = rows_here - own_rows
    halo = shift * (shard_count - 1)
    padding = rows_here * shard_count - PAIRS * PAIR_LEN
    tail_block = -(-padding // 32) * 32
    rows = pairs_here * WINDOW + tail_block
    is_last = mp == shard_count - 1

    width = query_weight.shape[1]
    qkv_own = jnp.concatenate([query_weight, key_weight, value_weight], axis=1)
    bias_own = jnp.concatenate([query_bias, value_bias, up_bias])[None, :]
    bias_across = swap_mp(bias_own, 2)
    bias_pair = swap_mp(jnp.concatenate([bias_own, bias_across], axis=0), 1)
    biases = [bias_own[0], bias_pair[0], bias_across[0], bias_pair[1]]

    def gather(own, direct):
        across = swap_mp(own, 2) if direct else fetch_across(own)
        return [own, swap_mp(own, 1), across, swap_mp(across, 1)]

    tokens_f = tokens.astype(F32)
    slice_row = mp * rows_here + jnp.arange(rows_here, dtype=jnp.int32)
    weighted = tokens_f * (slice_row < PAIRS * PAIR_LEN).astype(F32)[:, None]
    chosen = item_group[:, None] == jnp.arange(group_count.shape[0], dtype=jnp.int32)[None, :]
    item_scale = jnp.sum(jnp.where(chosen, grid_scale[None, :], 0.0), axis=1)
    item_weight = jnp.sum(jnp.where(chosen, group_count[None, :], 0), axis=1).astype(F32)
    sums = all_sum(
        jnp.stack(
            [
                jnp.sum(weighted, axis=0),
                jnp.sum(weighted * tokens_f, axis=0),
                jnp.broadcast_to(jnp.sum(item_weight) / shard_count, (D,)),
            ]
        )
    )

    def windows(v):
        before = lax.ppermute(
            v[rows_here - halo :], "mp", [(i, i + 1) for i in range(shard_count - 1)]
        )
        joined = jnp.concatenate([before, v], axis=0)
        start = halo - shift * mp
        parts = []
        for pair in range(pairs_here):
            parts.append(
                lax.dynamic_slice_in_dim(joined, start + pair * PAIR_LEN, PAIR_LEN, axis=0)
            )
            parts.append(jnp.zeros((WINDOW - PAIR_LEN, D), v.dtype))
        parts.append(jnp.where(is_last, v[rows_here - padding :], jnp.zeros((), v.dtype)))
        parts.append(jnp.zeros((tail_block - padding, D), v.dtype))
        return jnp.concatenate(parts, axis=0)

    def unwindows(v):
        own = jnp.concatenate(
            [v[pair * WINDOW : pair * WINDOW + PAIR_LEN] for pair in range(pairs_here)], axis=0
        )
        after = lax.ppermute(own[:halo], "mp", [(i + 1, i) for i in range(shard_count - 1)])
        after = jnp.concatenate([after, jnp.zeros((padding - halo, D), v.dtype)], axis=0)
        tail = v[pairs_here * WINDOW : pairs_here * WINDOW + padding]
        joined = jnp.concatenate([own, jnp.where(is_last, tail, after)], axis=0)
        return lax.dynamic_slice_in_dim(joined, shift * mp, rows_here, axis=0)

    tokens_w = windows(tokens).astype(F32)
    cotangent_w = windows(cotangent).astype(F32)

    row = jnp.arange(rows, dtype=jnp.int32)
    window = row // WINDOW
    offset = row % WINDOW
    in_pair = (window < pairs_here) & (offset < PAIR_LEN)
    is_padding = (window == pairs_here) & (offset < padding) & is_last
    pair = pairs_here * mp + window
    item_ids = jnp.arange(item_count, dtype=jnp.int32)
    first_len = jnp.sum(
        jnp.where(item_ids[None, :] == (2 * pair)[:, None], item_lengths[None, :], 0), axis=1
    )
    second = (offset >= first_len).astype(jnp.int32)
    owner = jnp.where(in_pair, 2 * pair + second, jnp.where(is_padding, item_count, -1))
    position = offset - second * first_len
    member = owner[:, None] == item_ids[None, :]
    row_scale = jnp.sum(jnp.where(member, item_scale[None, :], 0.0), axis=1)
    row_count = jnp.sum(jnp.where(member, item_weight[None, :], 0.0), axis=1)
    valid = in_pair.astype(F32)[:, None]
    quarter = D // 4
    frequency = jnp.exp(-math.log(10000.0) * jnp.arange(quarter, dtype=F32) / quarter)
    across_angle = ((position // SIDE).astype(F32) * row_scale)[:, None] * frequency
    side_angle = ((position % SIDE).astype(F32) * row_scale)[:, None] * frequency
    grid_table = (
        jnp.concatenate(
            [
                jnp.sin(across_angle),
                jnp.cos(across_angle),
                jnp.sin(side_angle),
                jnp.cos(side_angle),
            ],
            axis=-1,
        )
        * valid
    )
    owner_col = owner[:, None]
    owner_row = owner[None, :]

    qkv_weights = jnp.concatenate(gather(qkv_own, True), axis=1)
    output_weights = jnp.concatenate(gather(output_weight, False), axis=0)
    up_weights = jnp.concatenate(gather(up_weight, False), axis=1)
    down_weights = jnp.concatenate(gather(down_weight, False), axis=0)
    hidden_width = up_weight.shape[1]
    no_bias = jnp.zeros((width,), F32)
    qkv_bias = jnp.concatenate(
        [v for b in biases for v in (b[:width], no_bias, b[width : 2 * width])]
    )
    up_biases = jnp.concatenate([b[2 * width :] for b in biases])

    count_valid = slice_count * PAIRS * PAIR_LEN
    column_mean = sums[0] / count_valid
    spread = sums[1] / count_valid - column_mean * column_mean
    inverse = lax.rsqrt(spread + 1e-05)
    row_weight = row_count / (sums[2, 0] / (slice_count * item_count))
    standard = (tokens_w - column_mean) * inverse
    stream = standard + grid_table
    unit, unit_inverse = stats(stream)
    normed = (unit * norm_gain + norm_shift).astype(BF)

    qkv = (dot(normed, qkv_weights) + qkv_bias).astype(BF)
    context = attend(qkv, owner_col, owner_row, shard_count)
    middle = stream + (dot(context, output_weights) + output_bias)
    middle_unit, middle_inverse = stats(middle)
    hidden_in = (middle_unit * hidden_gain + hidden_shift).astype(BF)

    grad_out = cotangent_w * row_weight[:, None]
    grad_mixed = grad_out.astype(BF)
    active, slope = gelu_parts(dot(hidden_in, up_weights) + up_biases)
    mixed = dot(active, down_weights) + down_bias
    grad_pre = (dot_cols(grad_mixed, down_weights) * slope).astype(BF)
    grad_hidden = dot_cols(grad_pre, up_weights)
    layer_output = unwindows((middle + mixed).astype(BF))
    grad_middle = grad_out + norm_back(grad_hidden, middle_unit, middle_inverse, hidden_gain)
    grad_attended = grad_middle.astype(BF)

    grad_context = dot_cols(grad_attended, output_weights).astype(BF)
    grad_qkv = attend_back(qkv, grad_context, owner_col, owner_row, shard_count)
    grad_normed = dot_cols(grad_qkv, qkv_weights)

    pieces = range(shard_count)
    def columns(v, r, size):
        return v[:, r * size : (r + 1) * size]

    def reduced(left, right):
        return reduce_pieces([dot_rows(left(r), right(r)).astype(BF) for r in pieces])

    down_weight_grad = reduced(
        lambda r: columns(active, r, hidden_width), lambda r: grad_mixed
    )
    up_weight_grad = reduced(
        lambda r: hidden_in, lambda r: columns(grad_pre, r, hidden_width)
    )
    output_weight_grad = reduced(
        lambda r: columns(context, r, width), lambda r: grad_attended
    )
    qkv_weight_grad = reduced(lambda r: normed, lambda r: columns(grad_qkv, r, 3 * width))
    qkv_weight_grads = [columns(qkv_weight_grad, i, width) for i in range(3)]
    grad_stream = grad_middle + norm_back(grad_normed, unit, unit_inverse, norm_gain)

    def column_sums(v):
        return jnp.sum(v.astype(F32), axis=0)

    qkv_sums = column_sums(grad_qkv)
    up_sums = column_sums(grad_pre)
    bias_grads = [
        jnp.concatenate(
            [
                qkv_sums[3 * r * width : (3 * r + 1) * width],
                qkv_sums[(3 * r + 2) * width : 3 * (r + 1) * width],
                up_sums[r * hidden_width : (r + 1) * hidden_width],
            ]
        )[None, :]
        for r in pieces
    ]
    got = swap_mp(jnp.concatenate([bias_grads[1], bias_grads[3]], axis=0), 1)
    bias_grad = bias_grads[0] + got[:1] + swap_mp(bias_grads[2] + got[1:], 2)
    for bit in range(dp_bits()):
        bias_grad = bias_grad + swap_dp(bias_grad, 1 << bit)
    bias_grad = bias_grad[0]
    finals = all_sum(
        jnp.stack(
            [
                column_sums(grad_stream),
                column_sums(grad_stream * standard),
                column_sums(grad_normed * unit),
                column_sums(grad_normed),
                column_sums(grad_hidden * middle_unit),
                column_sums(grad_hidden),
                column_sums(grad_attended),
                column_sums(grad_mixed),
            ]
        )
    )
    tokens_grad = unwindows(
        inverse * (grad_stream - valid / count_valid * (finals[0] + finals[1] * standard))
    )
    return (
        layer_output,
        tokens_grad,
        finals[2],
        finals[3],
        qkv_weight_grads[0],
        bias_grad[:width],
        qkv_weight_grads[1],
        qkv_weight_grads[2],
        bias_grad[width : 2 * width],
        output_weight_grad,
        finals[6],
        finals[4],
        finals[5],
        up_weight_grad,
        bias_grad[2 * width :],
        down_weight_grad,
        finals[7],
    )


def fast_shards(
    tokens,
    cotangent,
    item_lengths,
    item_group,
    group_count,
    grid_scale,
    norm_gain,
    norm_shift,
    query_weight,
    query_bias,
    key_weight,
    value_weight,
    value_bias,
    output_weight,
    output_bias,
    hidden_gain,
    hidden_shift,
    up_weight,
    up_bias,
    down_weight,
    down_bias,
):
    shard_count = lax.axis_size("mp")
    mp = lax.axis_index("mp")
    rows_here = tokens.shape[0]
    pairs_here = PAIRS // shard_count
    shift = rows_here - pairs_here * PAIR_LEN
    halo = shift * (shard_count - 1)
    padding = rows_here * shard_count - PAIRS * PAIR_LEN
    rows = pairs_here * WINDOW + -(-padding // 32) * 32
    is_last = mp == shard_count - 1
    width = query_weight.shape[1]
    hidden_width = up_weight.shape[1]

    def unwindows(v):
        own = jnp.concatenate(
            [v[pair * WINDOW : pair * WINDOW + PAIR_LEN] for pair in range(pairs_here)], axis=0
        )
        after = lax.ppermute(own[:halo], "mp", [(i + 1, i) for i in range(shard_count - 1)])
        after = jnp.concatenate([after, jnp.zeros((padding - halo, D), v.dtype)], axis=0)
        tail = v[pairs_here * WINDOW : pairs_here * WINDOW + padding]
        joined = jnp.concatenate([own, jnp.where(is_last, tail, after)], axis=0)
        return lax.dynamic_slice_in_dim(joined, shift * mp, rows_here, axis=0)

    saved = forward(
        (item_lengths, item_group, group_count, grid_scale),
        [
            v[None, :]
            for v in (
                norm_gain,
                norm_shift,
                output_bias,
                hidden_gain,
                hidden_shift,
                query_bias,
                value_bias,
                up_bias,
            )
        ],
        tokens,
        cotangent,
        (query_weight, key_weight, value_weight, output_weight, up_weight, down_weight),
        rows,
    )
    reduced, finals, layer_output, tokens_grad = backward(
        (item_lengths, item_group, group_count),
        [v[None, :] for v in (norm_gain, hidden_gain, down_bias)],
        saved[2],
        saved[:2] + saved[3:],
    )
    down_weight_grad = reduced[:8].reshape(hidden_width, D).astype(F32)
    up_weight_grad = reduced[8:16].reshape(D, hidden_width).astype(F32)
    output_weight_grad = reduced[16:18].reshape(width, D).astype(F32)
    qkv_weight_grads = [
        reduced[18 + 2 * i : 20 + 2 * i].reshape(width, D).T.astype(F32) for i in range(3)
    ]
    bias_grad = finals[64:76].reshape(-1)
    finals = finals[:64].reshape(8, D)
    layer_output = unwindows(layer_output)
    tokens_grad = unwindows(tokens_grad)
    return (
        layer_output,
        tokens_grad,
        finals[2],
        finals[3],
        qkv_weight_grads[0],
        bias_grad[:width],
        qkv_weight_grads[1],
        qkv_weight_grads[2],
        bias_grad[width : 2 * width],
        output_weight_grad,
        finals[6],
        finals[4],
        finals[5],
        up_weight_grad,
        bias_grad[2 * width :],
        down_weight_grad,
        finals[7],
    )


def shards(*args):
    if lax.axis_size("dp") == 8 and lax.axis_size("mp") == 4 and args[0].shape == (512, D):
        return fast_shards(*args)
    return general_shards(*args)


def solution(mesh):
    rows = P(("dp", "mp"), None)
    columns = P(None, "mp")
    return jax.shard_map(
        shards,
        mesh=mesh,
        in_specs=(
            rows,
            rows,
            P("dp"),
            P("dp"),
            P(),
            P(),
            P(),
            P(),
            columns,
            P("mp"),
            columns,
            columns,
            P("mp"),
            P("mp", None),
            P(),
            P(),
            P(),
            columns,
            P("mp"),
            P("mp", None),
            P(),
        ),
        out_specs=(
            rows,
            rows,
            P(),
            P(),
            columns,
            P("mp"),
            columns,
            columns,
            P("mp"),
            P("mp", None),
            P(),
            P(),
            P(),
            columns,
            P("mp"),
            P("mp", None),
            P(),
        ),
        check_vma=False,
    )
```

```python
import functools
import math

import jax
import jax.numpy as jnp
from jax import lax
from jax.experimental import pallas as pl
from jax.experimental.pallas import tpu as pltpu
from jax.sharding import PartitionSpec as P

D = 1024
HEAD_DIM = 64
SIDE = 14
PAIRS = 8
PAIR_LEN = 245
WINDOW = 256
BF = jnp.bfloat16
F32 = jnp.float32
PADDING = 88


def dot(a, b):
    return lax.dot_general(a, b, (((1,), (0,)), ((), ())), preferred_element_type=F32)


def dot_rows(a, b):
    return lax.dot_general(a, b, (((0,), (0,)), ((), ())), preferred_element_type=F32)


def dot_cols(a, b):
    return lax.dot_general(a, b, (((1,), (1,)), ((), ())), preferred_element_type=F32)


def swap_mp(v, mask):
    count = lax.axis_size("mp")
    return lax.ppermute(v, "mp", [(i, i ^ mask) for i in range(count)])


def swap_dp(v, mask):
    count = lax.axis_size("dp")
    return lax.ppermute(v, "dp", [(i, i ^ mask) for i in range(count)])


def dp_bits():
    return lax.axis_size("dp").bit_length() - 1


def all_sum(v):
    v = v + swap_mp(v, 1) + swap_mp(v, 2) + swap_mp(v, 3)
    bit = 0
    bits = dp_bits()
    while bit < bits:
        if bit + 1 < bits:
            v = v + swap_dp(v, 1 << bit) + swap_dp(v, 2 << bit) + swap_dp(v, 3 << bit)
            bit += 2
        else:
            v = v + swap_dp(v, 1 << bit)
            bit += 1
    return v


def dp_bit(bit):
    return (lax.axis_index("dp") >> bit) & 1


def join(mine, other, bit):
    return jnp.where(
        dp_bit(bit) == 0,
        jnp.concatenate([mine, other], axis=0),
        jnp.concatenate([other, mine], axis=0),
    )


def chunk_index():
    index = jnp.int32(0)
    for bit in range(dp_bits()):
        index = index * 2 + dp_bit(bit)
    return index


def fetch_across(w):
    rows = w.shape[0] // lax.axis_size("dp")
    mine = lax.dynamic_slice_in_dim(w, chunk_index() * rows, rows, axis=0)
    got = swap_mp(mine, 2)
    for bit in reversed(range(dp_bits())):
        got = join(got, swap_dp(got, 1 << bit), bit)
    return got


def reduce_pieces(pieces):
    half = pieces[1].shape[0]
    got = swap_mp(jnp.concatenate([pieces[1], pieces[3]], axis=0), 1)
    across = pieces[2].astype(F32) + got[half:].astype(F32)
    own = pieces[0].astype(F32) + got[:half].astype(F32)
    total = own + swap_mp(across.astype(BF), 2).astype(F32)
    for bit in range(dp_bits()):
        size = total.shape[0] // 2
        side = dp_bit(bit)
        send = lax.dynamic_slice_in_dim(total, (1 - side) * size, size, axis=0).astype(BF)
        keep = lax.dynamic_slice_in_dim(total, side * size, size, axis=0)
        total = keep + swap_dp(send, 1 << bit).astype(F32)
    total = total.astype(BF)
    for bit in reversed(range(dp_bits())):
        total = join(total, swap_dp(total, 1 << bit), bit)
    return total.astype(F32)


def stats(v):
    mean = jnp.mean(v, axis=-1, keepdims=True)
    center = v - mean
    spread = jnp.mean(center * center, axis=-1, keepdims=True)
    inverse = lax.rsqrt(spread + 1e-06)
    return center * inverse, inverse


def norm_back(grad, unit, inverse, gain):
    f = grad * gain
    return inverse * (
        f
        - jnp.mean(f, axis=-1, keepdims=True)
        - unit * jnp.mean(f * unit, axis=-1, keepdims=True)
    )


def blocks_of(rows):
    return [(first, min(WINDOW, rows - first)) for first in range(0, rows, WINDOW)]


def head_scores(qkv_ref, same, first, size, h, width):
    q = qkv_ref[first : first + size, h * HEAD_DIM : (h + 1) * HEAD_DIM]
    k = qkv_ref[first : first + size, width + h * HEAD_DIM : width + (h + 1) * HEAD_DIM]
    v = qkv_ref[first : first + size, 2 * width + h * HEAD_DIM : 2 * width + (h + 1) * HEAD_DIM]
    scores = jnp.where(same, dot_cols(q, k) * (1.0 / math.sqrt(HEAD_DIM)), -1e30)
    weights = jnp.exp(scores - jnp.max(scores, axis=-1, keepdims=True))
    weights = weights * (1.0 / jnp.sum(weights, axis=-1, keepdims=True))
    return q, k, v, weights


def attend_kernel(qkv_ref, col_ref, row_ref, out_ref):
    rows, width = out_ref.shape
    for first, size in blocks_of(rows):
        same = col_ref[first : first + size, :] == row_ref[:, first : first + size]
        for h in range(width // HEAD_DIM):
            q, k, v, weights = head_scores(qkv_ref, same, first, size, h, width)
            out_ref[first : first + size, h * HEAD_DIM : (h + 1) * HEAD_DIM] = dot(
                weights.astype(BF), v
            ).astype(BF)


def attend_back_kernel(qkv_ref, grad_ref, col_ref, row_ref, out_ref):
    rows, width = grad_ref.shape
    factor = 1.0 / math.sqrt(HEAD_DIM)
    for first, size in blocks_of(rows):
        same = col_ref[first : first + size, :] == row_ref[:, first : first + size]
        for h in range(width // HEAD_DIM):
            q, k, v, weights = head_scores(qkv_ref, same, first, size, h, width)
            grad = grad_ref[first : first + size, h * HEAD_DIM : (h + 1) * HEAD_DIM]
            soft = dot_cols(grad, v)
            center = jnp.sum(weights * soft, axis=-1, keepdims=True)
            grad_scores = (weights * (soft - center)).astype(BF)
            for part, value in enumerate(
                (
                    dot(grad_scores, k) * factor,
                    dot_rows(grad_scores, q) * factor,
                    dot_rows(weights.astype(BF), grad),
                )
            ):
                lane = part * width + h * HEAD_DIM
                out_ref[first : first + size, lane : lane + HEAD_DIM] = value.astype(BF)


def attend(qkv, owner_col, owner_row, groups):
    rows, width = qkv.shape[0], qkv.shape[1] // (3 * groups)
    return pl.pallas_call(
        attend_kernel,
        grid=(groups,),
        in_specs=[
            pl.BlockSpec((rows, 3 * width), lambda r: (0, r)),
            pl.BlockSpec((rows, 1), lambda r: (0, 0)),
            pl.BlockSpec((1, rows), lambda r: (0, 0)),
        ],
        out_specs=pl.BlockSpec((rows, width), lambda r: (0, r)),
        out_shape=jax.ShapeDtypeStruct((rows, groups * width), BF),
        name="attend",
    )(qkv, owner_col, owner_row)


def attend_back(qkv, grad, owner_col, owner_row, groups):
    rows, width = grad.shape[0], grad.shape[1] // groups
    return pl.pallas_call(
        attend_back_kernel,
        grid=(groups,),
        in_specs=[
            pl.BlockSpec((rows, 3 * width), lambda r: (0, r)),
            pl.BlockSpec((rows, width), lambda r: (0, r)),
            pl.BlockSpec((rows, 1), lambda r: (0, 0)),
            pl.BlockSpec((1, rows), lambda r: (0, 0)),
        ],
        out_specs=pl.BlockSpec((rows, 3 * width), lambda r: (0, r)),
        out_shape=jax.ShapeDtypeStruct((rows, 3 * groups * width), BF),
        name="attend_back",
    )(qkv, grad, owner_col, owner_row)


def gelu_parts(preact):
    phi = 0.5 * (1.0 + lax.erf(preact * (1.0 / math.sqrt(2.0))))
    slope = phi + preact * jnp.exp(-0.5 * preact * preact) * (1.0 / math.sqrt(2.0 * math.pi))
    return (preact * phi).astype(BF), slope


HALO = 80
MESH = pl.DeviceIdType.MESH


def places():
    mp = lax.axis_index("mp")
    dp = lax.axis_index("dp")
    y = dp % 2
    z = dp // 2
    sibling = mp + 1 - 2 * (mp % 2)
    opposite = mp + 2 - 4 * (mp // 2)
    across = opposite + 1 - 2 * (mp % 2)
    mp_peers = [{"mp": sibling}, {"mp": opposite}, {"mp": across}]
    y_peer = {"dp": dp + 1 - 2 * y}
    z_places = [(z + m) % 4 for m in (1, 2, 3)]
    z_peers = [{"dp": place * 2 + y} for place in z_places]
    return mp, y, z, mp_peers, y_peer, z_places, z_peers


def greet(peers):
    barrier = pltpu.get_barrier_semaphore()
    for peer in peers:
        pl.semaphore_signal(barrier, inc=1, device_id=peer, device_id_type=MESH)
    pl.semaphore_wait(barrier, len(peers))


def remote(source, target, send, recv, peer):
    return pltpu.make_async_remote_copy(
        src_ref=source,
        dst_ref=target,
        send_sem=send,
        recv_sem=recv,
        device_id=peer,
        device_id_type=MESH,
    )


def loop(count, body):
    def step(i, carry):
        body(i)
        return carry

    lax.fori_loop(0, count, step, 0)


def block_rows(i, size):
    return pl.ds(pl.multiple_of(i * size, size), size)


def start_all(copies):
    for copy in copies:
        copy.start()


def wait_recv_all(copies):
    for copy in copies:
        copy.wait_recv()


def item_of_rows(row, lengths, mp):
    window = row >> 8
    offset = row & (WINDOW - 1)
    length = jnp.where(window == 0, lengths[4 * mp], lengths[4 * mp + 2])
    second = jnp.where(offset >= length, 1, 0)
    in_pair = (window < 2) & (offset < PAIR_LEN)
    is_padding = (window == 2) & (offset < PADDING) & (mp == 3)
    return 2 * window + second, offset - second * length, in_pair, is_padding


def owner_of_rows(row, lengths, mp):
    item, _, in_pair, is_padding = item_of_rows(row, lengths, mp)
    return jnp.where(in_pair, item, jnp.where(is_padding, 16, -1))


def choose_item(item, values):
    result = jnp.where(item == 0, values[0], 0.0)
    for j in (1, 2, 3):
        result = jnp.where(item == j, values[j], result)
    return result


def joined(tiles, first):
    return jnp.concatenate([tiles[first + j : first + j + 1, :] for j in range(8)], axis=1)


def forward_kernel(
    lengths,
    groups,
    counts,
    scales,
    gain,
    shift,
    output_bias,
    hidden_gain,
    hidden_shift,
    query_bias,
    value_bias,
    up_bias,
    tokens_ref,
    cotangent_ref,
    query_ref,
    key_ref,
    value_ref,
    output_ref,
    up_ref,
    down_ref,
    tokens_out,
    cotangent_out,
    sums_out,
    stream_out,
    middle_out,
    normed_out,
    qkv_out,
    context_out,
    hidden_out,
    grad_mixed_out,
    active_out,
    grad_pre_out,
    wqkv_out,
    wo_out,
    wup_out,
    wdown_out,
    tokens_ext,
    cotangent_ext,
    tokens,
    cotangent,
    stream,
    middle,
    normed,
    qkv,
    context,
    hidden,
    grad_mixed,
    active,
    grad_pre,
    wqkv,
    wo,
    wup,
    wdown,
    sums,
    bias,
    part,
    from_mp,
    from_y,
    from_z,
    own_sem,
    halo_sem,
    store_sem,
    stat_send,
    stat_recv,
    bias_send,
    bias_recv,
    pair_send,
    pair_recv,
    x_send,
    x_recv,
    z_send,
    z_recv,
    y_send,
    y_recv,
    fwd_send,
    fwd_recv,
):
    mp, y, z, mp_peers, y_peer, z_places, z_peers = places()
    sibling, opposite, _ = mp_peers
    rows_here = tokens_ref.shape[0]
    rows = tokens.shape[0]
    width = query_ref.shape[1]
    blocks = rows // 32

    items = [
        (key_ref, 0, D, wqkv, width, width, False),
        (value_ref, 0, D, wqkv, 2 * width, width, False),
        (query_ref, 0, D, wqkv, 0, width, True),
        (output_ref, 0, width, wo, 0, D, False),
        (up_ref, 0, D // 2, wup, 0, D, False),
        (up_ref, D // 2, D // 2, wup, 0, D, False),
        (down_ref, 3 * D // 4, D // 4, wdown, 0, D, False),
        (down_ref, 0, 3 * D // 4, wdown, 0, D, True),
    ]
    KEY, VALUE, QUERY, OUTPUT, UP_A, UP_B, DOWN_A, DOWN_B = range(8)

    def source(i, start, size):
        return items[i][0].at[pl.ds(items[i][1] + start, size)]

    def place(i, r, start, size):
        _, first, _, ref, column, columns, _ = items[i]
        return ref.at[r, pl.ds(first + start, size), pl.ds(column, columns)]

    def part_of(i, first, eighths):
        size = items[i][2] // 8
        return pl.multiple_of(first * size, size), eighths * size

    own_copies = [
        pltpu.make_async_copy(
            source(i, 0, items[i][2]), place(i, 0, 0, items[i][2]), own_sem.at[i]
        )
        for i in range(8)
    ]
    pair_copies = [
        remote(
            source(i, 0, items[i][2]),
            place(i, 1, 0, items[i][2]),
            pair_send.at[i],
            pair_recv.at[i],
            sibling,
        )
        for i in range(8)
    ]

    def x_copy(i):
        start, size = (0, items[i][2]) if items[i][6] else part_of(i, y * 4 + z, 1)
        return remote(
            source(i, start, size), place(i, 2, start, size), x_send.at[i], x_recv.at[i], opposite
        )

    def z_copies(i):
        start, size = part_of(i, y * 4 + z, 1)
        view = place(i, 2, start, size)
        return [
            remote(view, view, z_send.at[i, m], z_recv.at[i, m], peer)
            for m, peer in enumerate(z_peers)
        ]

    def y_copy(i):
        start, size = part_of(i, y * 4, 4)
        view = place(i, 2, start, size)
        return remote(view, view, y_send.at[i], y_recv.at[i], y_peer)

    def fwd_copy(i):
        size = items[i][2]
        return remote(
            place(i, 2, 0, size), place(i, 3, 0, size), fwd_send.at[i], fwd_recv.at[i], sibling
        )

    def x_to_z(i):
        x_copy(i).wait_recv()
        start_all(z_copies(i))

    def z_to_y(i):
        wait_recv_all(z_copies(i))
        y_copy(i).start()

    def y_to_pair(i):
        (x_copy(i) if items[i][6] else y_copy(i)).wait_recv()
        fwd_copy(i).start()

    keep = [
        pltpu.make_async_copy(ref, ext.at[pl.ds(HALO, rows_here)], halo_sem.at[which, 2])
        for which, (ref, ext) in enumerate(
            ((tokens_ref, tokens_ext), (cotangent_ref, cotangent_ext))
        )
    ]
    start_all(keep)
    start_all(own_copies)
    bias[0, 0:1, :] = query_bias[...]
    bias[0, 1:2, :] = value_bias[...]
    for j in range(4):
        bias[0, 2 + j : 3 + j, :] = up_bias[:, j * width : (j + 1) * width]
    bias[0, 6:8, :] = jnp.zeros((2, width), F32)

    weights = [counts[groups[4 * mp + j]].astype(F32) for j in range(4)]
    weight_part = weights[0] + weights[1] + weights[2] + weights[3]
    keep[0].wait()

    def add_rows(i, carry):
        block = tokens_ext[pl.ds(pl.multiple_of(HALO + i * 16, 16), 16), :].astype(F32)
        row = mp * rows_here + i * 16 + lax.broadcasted_iota(jnp.int32, (16, 1), 0)
        kept = jnp.where(row < PAIRS * PAIR_LEN, block, 0.0)
        return carry[0] + kept, carry[1] + kept * block

    zero = jnp.zeros((16, D), F32)
    first, second = lax.fori_loop(0, rows_here // 16, add_rows, (zero, zero))
    first = jnp.sum(first, axis=0, keepdims=True)
    second = jnp.sum(second, axis=0, keepdims=True)
    for j in range(8):
        part[0, j : j + 1, :] = first[:, j * 128 : (j + 1) * 128]
        part[0, 8 + j : 9 + j, :] = second[:, j * 128 : (j + 1) * 128]
    part[0, 16:24, :] = jnp.zeros((8, 128), F32) + weight_part
    greet(mp_peers + [y_peer] + z_peers)

    def exchange(stage, peers, slots):
        copies = [
            remote(
                part.at[stage],
                slots.at[m],
                stat_send.at[stage, m],
                stat_recv.at[stage, m],
                peer,
            )
            for m, peer in enumerate(peers)
        ]
        start_all(copies)
        return copies

    def total(stage, copies, slots):
        value = part[stage]
        for m, copy in enumerate(copies):
            copy.wait_recv()
            value = value + slots[m]
        return value

    sums_a = exchange(0, mp_peers, from_mp)
    after = {"mp": (mp + 1) % 4}
    halo_copies = [
        remote(
            ref.at[pl.ds(rows_here - HALO, HALO)],
            ext.at[pl.ds(0, HALO)],
            halo_sem.at[which, 0],
            halo_sem.at[which, 1],
            after,
        )
        for which, (ref, ext) in enumerate(
            ((tokens_ref, tokens_ext), (cotangent_ref, cotangent_ext))
        )
    ]
    bias_copies = [
        remote(bias.at[0], bias.at[r + 1], bias_send.at[r], bias_recv.at[r], peer)
        for r, peer in enumerate(mp_peers)
    ]
    start_all(halo_copies + bias_copies)
    start_all([x_copy(i) for i in range(8)])
    start_all([pair_copies[i] for i in (QUERY, KEY, VALUE, OUTPUT, UP_A, UP_B, DOWN_A, DOWN_B)])
    part[1] = total(0, sums_a, from_mp)
    sums_b = exchange(1, [y_peer], from_y)

    place_id = lax.broadcasted_iota(jnp.int32, (64, 1), 0)
    table_scale = choose_item(
        place_id >> 4, [scales[groups[4 * mp + j]] for j in range(4)]
    )
    quarter = D // 4
    lane = lax.broadcasted_iota(jnp.int32, (1, quarter), 1).astype(F32)
    frequency = jnp.exp(-math.log(10000.0) * lane / quarter)
    angle = ((place_id & 15).astype(F32) * table_scale) * frequency
    table = jnp.concatenate([jnp.sin(angle), jnp.cos(angle)], axis=1)
    row = lax.broadcasted_iota(jnp.int32, (rows, 64), 0)
    column = lax.broadcasted_iota(jnp.int32, (rows, 64), 1)
    item, position, in_pair, _ = item_of_rows(row, lengths, mp)
    across = (position * 9363) >> 17
    for half, code in enumerate((across, position - SIDE * across)):
        chosen = jnp.where(in_pair & (column == item * 16 + code), 1.0, 0.0)
        stream[:, half * 2 * quarter : (half + 1) * 2 * quarter] = lax.dot_general(
            chosen,
            table,
            (((1,), (0,)), ((), ())),
            precision=lax.Precision.HIGHEST,
            preferred_element_type=F32,
        )
    part[2] = total(1, sums_b, from_y)
    sums_c = exchange(2, z_peers, from_z)
    x_to_z(KEY)
    x_to_z(VALUE)

    wait_recv_all(halo_copies)
    keep[1].wait()
    own_len = 2 * PAIR_LEN
    row = lax.broadcasted_iota(jnp.int32, (rows, HALO + rows_here), 0)
    column = lax.broadcasted_iota(jnp.int32, (rows, HALO + rows_here), 1)
    window = row >> 8
    offset = row & (WINDOW - 1)
    wanted = HALO - (rows_here - own_len) * mp + window * PAIR_LEN + offset
    tail = jnp.where(mp == 3, HALO + rows_here - PADDING, 4096) + offset
    wanted = jnp.where(window < 2, jnp.where(offset < PAIR_LEN, wanted, -1), tail)
    chosen = jnp.where(column == wanted, 1.0, 0.0).astype(BF)
    tokens[...] = dot(chosen, tokens_ext[...]).astype(BF)
    cotangent[...] = dot(chosen, cotangent_ext[...]).astype(BF)
    sums[...] = total(2, sums_c, from_z)

    slices = lax.axis_size("dp")
    count_valid = slices * PAIRS * PAIR_LEN
    column_mean = joined(sums, 0) / count_valid
    spread = joined(sums, 8) / count_valid - column_mean * column_mean
    inverse = lax.rsqrt(spread + 1e-05)
    mean_weight = sums[16:17, 0:1] / (slices * 16)

    def first_norm(i):
        here = block_rows(i, 32)
        value = (tokens[here, :].astype(F32) - column_mean) * inverse + stream[here, :]
        stream[here, :] = value
        unit, _ = stats(value)
        normed[here, :] = (unit * gain[...] + shift[...]).astype(BF)
        row = i * 32 + lax.broadcasted_iota(jnp.int32, (32, 1), 0)
        item, _, in_pair, _ = item_of_rows(row, lengths, mp)
        row_weight = jnp.where(in_pair, choose_item(item, weights), 0.0) / mean_weight
        grad_mixed[here, :] = (cotangent[here, :].astype(F32) * row_weight).astype(BF)

    loop(blocks, first_norm)

    def store(i, value, ref):
        return pltpu.make_async_copy(value, ref, store_sem.at[i])

    stores = [
        store(0, tokens, tokens_out),
        store(1, cotangent, cotangent_out),
        store(2, sums, sums_out),
        store(3, stream, stream_out),
        store(4, normed, normed_out),
        store(5, grad_mixed, grad_mixed_out),
        store(6, qkv, qkv_out),
        store(7, context, context_out),
        store(8, wqkv, wqkv_out),
        store(9, middle, middle_out),
        store(10, hidden, hidden_out),
        store(11, wo, wo_out),
        store(12, active, active_out),
        store(13, grad_pre, grad_pre_out),
        store(14, wup, wup_out),
        store(15, wdown, wdown_out),
    ]
    start_all(stores[:6])

    for copy in bias_copies:
        copy.wait_recv()

    def head_group(r):
        @pl.when(r == 0)
        def _():
            for i in (QUERY, KEY, VALUE):
                own_copies[i].wait()

        @pl.when(r == 1)
        def _():
            for i in (OUTPUT, UP_A, UP_B, DOWN_A):
                x_to_z(i)
            for i in (QUERY, KEY, VALUE):
                pair_copies[i].wait_recv()

        @pl.when(r == 2)
        def _():
            for i in (QUERY, KEY, VALUE):
                y_to_pair(i)
            z_to_y(OUTPUT)

        @pl.when(r == 3)
        def _():
            for i in (QUERY, KEY, VALUE):
                fwd_copy(i).wait_recv()
            y_to_pair(OUTPUT)

        base = r * 3 * width
        for n in range(3):
            value = dot(normed[...], wqkv[r, :, n * width : (n + 1) * width])
            if n != 1:
                value = value + bias[r, n // 2 : n // 2 + 1, :]
            qkv[:, pl.ds(pl.multiple_of(base + n * width, width), width)] = value.astype(BF)

        @pl.when(r == 0)
        def _():
            z_to_y(KEY)
            z_to_y(VALUE)

        def head_pair(p):
            lanes = [
                pl.ds(pl.multiple_of(base + n * width + p * 128, 128), 128) for n in range(3)
            ]
            target = pl.ds(pl.multiple_of(r * width + p * 128, 128), 128)
            for first, size in blocks_of(rows):
                here = pl.ds(first, size)
                same = owner_of_rows(
                    first + lax.broadcasted_iota(jnp.int32, (size, 1), 0), lengths, mp
                ) == owner_of_rows(
                    first + lax.broadcasted_iota(jnp.int32, (1, size), 1), lengths, mp
                )
                q, k, v = [qkv[here, lane] for lane in lanes]
                results = []
                for h in range(2):
                    cut = slice(h * HEAD_DIM, (h + 1) * HEAD_DIM)
                    low = softmax_rows(q[:, cut], k[:, cut], same).astype(BF)
                    results.append(dot(low, v[:, cut]).astype(BF))
                context[here, target] = jnp.concatenate(results, axis=1)

        loop(width // 128, head_pair)

    loop(4, head_group)
    start_all(stores[6:9])
    z_to_y(UP_A)

    own_copies[OUTPUT].wait()
    pair_copies[OUTPUT].wait_recv()
    fwd_copy(OUTPUT).wait_recv()

    def attention_output(n):
        columns = block_rows(n, 256)
        value = stream[:, columns] + output_bias[:, columns]
        for r in range(4):
            value = value + dot(context[:, r * width : (r + 1) * width], wo[r, :, columns])
        middle[:, columns] = value

    loop(4, attention_output)

    def second_norm(i):
        here = block_rows(i, 32)
        unit, _ = stats(middle[here, :])
        hidden[here, :] = (unit * hidden_gain[...] + hidden_shift[...]).astype(BF)

    loop(blocks, second_norm)
    start_all(stores[9:12])

    def hidden_group(r):
        @pl.when(r == 0)
        def _():
            for i in (UP_A, UP_B, DOWN_A, DOWN_B):
                own_copies[i].wait()
            z_to_y(UP_B)

        @pl.when(r == 1)
        def _():
            y_to_pair(UP_A)
            z_to_y(DOWN_A)
            for i in (UP_A, UP_B, DOWN_A, DOWN_B):
                pair_copies[i].wait_recv()

        @pl.when(r == 2)
        def _():
            for i in (DOWN_B, UP_B, DOWN_A):
                y_to_pair(i)

        @pl.when(r == 3)
        def _():
            for i in (UP_A, UP_B, DOWN_A, DOWN_B):
                fwd_copy(i).wait_recv()

        def hidden_tile(n):
            columns = block_rows(n, 256)
            target = pl.ds(pl.multiple_of(r * D + n * 256, 256), 256)
            preact = dot(hidden[...], wup[r, :, columns]) + bias[r, pl.ds(2 + n, 1), :]
            value, slope = gelu_parts(preact)
            active[:, target] = value
            grad = dot_cols(grad_mixed[...], wdown[r, columns, :])
            grad_pre[:, target] = (grad * slope).astype(BF)

        loop(4, hidden_tile)

    loop(4, hidden_group)
    start_all(stores[12:])

    for i in range(8):
        pair_copies[i].wait_send()
        x_copy(i).wait_send()
        fwd_copy(i).wait_send()
        if not items[i][6]:
            for copy in z_copies(i):
                copy.wait_send()
            y_copy(i).wait_send()
    for copy in bias_copies + halo_copies + sums_a + sums_b + sums_c:
        copy.wait_send()
    for copy in stores:
        copy.wait()


def softmax_rows(q, k, same):
    scores = jnp.where(same, dot_cols(q, k) * (1.0 / math.sqrt(HEAD_DIM)), -1e30)
    weights = jnp.exp(scores - jnp.max(scores, axis=-1, keepdims=True))
    return weights * (1.0 / jnp.sum(weights, axis=-1, keepdims=True))


def forward(smalls, vectors, tokens, cotangent, weights, rows):
    width = weights[0].shape[1]
    shape = jax.ShapeDtypeStruct
    full = shape((rows, D), F32)
    low = shape((rows, D), BF)
    wide = shape((rows, 4 * D), BF)
    outs = (
        low,
        low,
        shape((24, 128), F32),
        full,
        full,
        low,
        shape((rows, 12 * width), BF),
        low,
        low,
        low,
        wide,
        wide,
        shape((4, D, 3 * width), BF),
        shape((4, width, D), BF),
        shape((4, D, D), BF),
        shape((4, D, D), BF),
    )
    scratch = [shape((HALO + tokens.shape[0], D), BF)] * 2 + [
        low,
        low,
        full,
        full,
        low,
        outs[6],
        low,
        low,
        low,
        wide,
        wide,
    ]
    scratch += list(outs[12:]) + [
        shape((24, 128), F32),
        shape((4, 8, width), F32),
        shape((3, 24, 128), F32),
        shape((3, 24, 128), F32),
        shape((1, 24, 128), F32),
        shape((3, 24, 128), F32),
    ]
    dma = pltpu.SemaphoreType.DMA
    any_space = pl.BlockSpec(memory_space=pl.ANY)
    return pl.pallas_call(
        forward_kernel,
        out_shape=outs,
        in_specs=[pl.BlockSpec(memory_space=pltpu.SMEM)] * 4
        + [pl.BlockSpec(memory_space=pltpu.VMEM)] * 8
        + [any_space] * 8,
        out_specs=(any_space,) * len(outs),
        scratch_shapes=[pltpu.VMEM(v.shape, v.dtype) for v in scratch]
        + [
            dma((8,)),
            dma((2, 3)),
            dma((16,)),
            dma((3, 3)),
            dma((3, 3)),
            dma((3,)),
            dma((3,)),
            dma((8,)),
            dma((8,)),
            dma((8,)),
            dma((8,)),
            dma((8, 3)),
            dma((8, 3)),
            dma((8,)),
            dma((8,)),
            dma((8,)),
            dma((8,)),
        ],
        compiler_params=pltpu.CompilerParams(
            collective_id=1, has_side_effects=True, vmem_limit_bytes=67043328
        ),
        name="forward",
    )(*smalls, *vectors, tokens, cotangent, *weights)


CHUNK = 128
CHUNKS = 24
STAGE_DELAY = (0, 1, 3, 5, 7, 9, 11)
TICK_HIDDEN, TICK_SECOND, TICK_CONTEXT, TICK_HEADS = 0, 4, 5, 6
TICK_NORMED, TICK_FIRST, TICK_MIXED = 14, 18, 19
TICK_SUMS = (18, 20, 22, 24)
TICK_NEXT, TICK_LAYER, TICK_TOKENS = 25, 27, 28


def backward_kernel(
    lengths,
    groups,
    counts,
    gain,
    hidden_gain,
    down_bias,
    sums,
    tokens_ref,
    cotangent_ref,
    stream_ref,
    middle_ref,
    normed_ref,
    qkv_ref,
    context_ref,
    hidden_ref,
    grad_mixed_ref,
    active_ref,
    grad_pre_ref,
    wqkv_ref,
    wo_ref,
    wup_ref,
    wdown_ref,
    reduced_out,
    finals_out,
    layer_out,
    tokens_grad_out,
    made,
    pair,
    across,
    over_y,
    over_z,
    final,
    act,
    grad_pre,
    hidden,
    grad_mixed,
    context,
    normed,
    grad_attended,
    qkv,
    grad_context,
    rowbuf,
    gradient,
    trunk,
    stream,
    weight,
    packet,
    from_mp,
    from_y,
    from_z,
    layer_next,
    tokens_next,
    load_sem,
    act_sem,
    weight_sem,
    pair_send,
    pair_recv,
    across_send,
    across_recv,
    y_send,
    y_recv,
    z_send,
    z_recv,
    back_z_send,
    back_z_recv,
    back_y_send,
    back_y_recv,
    out_sem,
    stat_send,
    stat_recv,
    next_send,
    next_recv,
):
    mp, y, z, mp_peers, y_peer, z_places, z_peers = places()
    sibling, opposite, _ = mp_peers
    half = CHUNK // 2
    eighth = CHUNK // 8
    rows = normed.shape[0]
    rows_here = layer_out.shape[0]
    width = context.shape[1] // 4
    blocks = rows // 32

    loads = {
        name: pltpu.make_async_copy(source, target, load_sem.at[i])
        for i, (name, source, target) in enumerate(
            (
                ("grad_mixed", grad_mixed_ref, grad_mixed),
                ("grad_pre", grad_pre_ref, grad_pre),
                ("middle", middle_ref, trunk),
                ("cotangent", cotangent_ref, rowbuf),
                ("qkv", qkv_ref, qkv),
                ("hidden", hidden_ref, hidden),
                ("context", context_ref, context),
                ("normed", normed_ref, normed),
                ("stream", stream_ref, stream),
                ("tokens", tokens_ref, rowbuf),
                ("active", active_ref, grad_pre),
                ("middle again", middle_ref, stream),
                ("layer", normed.at[pl.ds(0, rows_here)], layer_out),
                ("tokens_grad", trunk.at[pl.ds(0, rows_here)], tokens_grad_out),
            )
        )
    }

    def act_loads(c):
        return [
            pltpu.make_async_copy(
                active_ref.at[:, pl.ds(pl.multiple_of(r * D + c * CHUNK, CHUNK), CHUNK)],
                act.at[c % 2, r],
                act_sem.at[c % 2, r],
            )
            for r in range(4)
        ]

    def weight_load(s):
        if s < 4:
            source = wup_ref.at[s]
        elif s == 4:
            source = wo_ref
        elif s < 9:
            source = wqkv_ref.at[s - 5]
        else:
            source = wdown_ref.at[s - 9]
        target = weight.at[s % 2, :, pl.ds(0, 3 * width)] if 5 <= s < 9 else weight.at[s % 2]
        return pltpu.make_async_copy(source, target, weight_sem.at[s % 2])

    for c in range(2):
        start_all(act_loads(c))
    loads["grad_mixed"].start()
    weight_load(0).start()
    loads["grad_pre"].start()
    weight_load(1).start()
    for name in ("middle", "cotangent", "qkv", "hidden", "context", "normed", "stream"):
        loads[name].start()
    greet(mp_peers + [y_peer] + z_peers)

    weights = [counts[groups[4 * mp + j]].astype(F32) for j in range(4)]
    slices = lax.axis_size("dp")
    count_valid = slices * PAIRS * PAIR_LEN
    column_mean = joined(sums, 0) / count_valid
    spread = joined(sums, 8) / count_valid - column_mean * column_mean
    inverse = lax.rsqrt(spread + 1e-05)
    mean_weight = sums[16:17, 0:1] / (slices * 16)

    def pair_copy(c):
        return remote(
            made.at[c % 2, pl.ds(0, 2)], pair.at[c], pair_send.at[c], pair_recv.at[c], sibling
        )

    def across_copy(c):
        return remote(
            pair.at[c, 1], across.at[c], across_send.at[c], across_recv.at[c], opposite
        )

    def y_copy(c):
        return remote(
            across.at[c, pl.ds(pl.multiple_of((1 - y) * half, half), half)],
            over_y.at[c],
            y_send.at[c],
            y_recv.at[c],
            y_peer,
        )

    def z_copies(c):
        return [
            remote(
                over_y.at[c, pl.ds(pl.multiple_of(place * eighth, eighth), eighth)],
                over_z.at[c, m],
                z_send.at[c, m],
                z_recv.at[c, m],
                peer,
            )
            for m, (place, peer) in enumerate(zip(z_places, z_peers))
        ]

    def back_z_copies(c):
        view = final.at[c, pl.ds(pl.multiple_of(y * half + z * eighth, eighth), eighth)]
        return [
            remote(view, view, back_z_send.at[c, m], back_z_recv.at[c, m], peer)
            for m, peer in enumerate(z_peers)
        ]

    def back_y_copy(c):
        view = final.at[c, pl.ds(pl.multiple_of(y * half, half), half)]
        return remote(view, view, back_y_send.at[c], back_y_recv.at[c], y_peer)

    def out_copy(c):
        return pltpu.make_async_copy(final.at[c], reduced_out.at[c], out_sem.at[c])

    def make(c):
        @pl.when(c < 8)
        def _():
            for copy in act_loads(c):
                copy.wait()

        def one(j):
            r = 2 * j + 1 - 5 * (j // 2)

            def store(left, right):
                made[c % 2, j] = dot_rows(left, right).astype(BF)

            @pl.when(c < 8)
            def _():
                store(act[c % 2, r], grad_mixed[...])

            @pl.when((c >= 8) & (c < 16))
            def _():
                store(
                    hidden[:, block_rows(c - 8, CHUNK)], grad_pre[:, block_rows(r, D)]
                )

            @pl.when((c >= 16) & (c < 18))
            def _():
                store(context[:, block_rows(2 * r + c - 16, CHUNK)], grad_attended[...])

            @pl.when(c >= 18)
            def _():
                store(qkv[:, block_rows(6 * r + c - 18, CHUNK)], normed[...])

        loop(4, one)

        @pl.when(c < 6)
        def _():
            start_all(act_loads(c + 2))

    def add_pair(c):
        pair_copy(c).wait()

        def body(i):
            here = block_rows(i, 32)
            for which in (1, 0):
                pair[c, which, here, :] = (
                    pair[c, which, here, :].astype(F32)
                    + made[c % 2, 2 + which, here, :].astype(F32)
                ).astype(BF)

        loop(CHUNK // 32, body)

    def add_across(c):
        across_copy(c).wait_recv()

        def body(i):
            here = block_rows(i, 32)
            across[c, here, :] = (
                across[c, here, :].astype(F32) + pair[c, 0, here, :].astype(F32)
            ).astype(BF)

        loop(CHUNK // 32, body)

    def add_y(c):
        y_copy(c).wait_recv()

        def body(i):
            here = block_rows(i, 32)
            own = pl.ds(pl.multiple_of(y * half + i * 32, 32), 32)
            over_y[c, here, :] = (
                over_y[c, here, :].astype(F32) + across[c, own, :].astype(F32)
            ).astype(BF)

        loop(half // 32, body)

    def add_z(c):
        wait_recv_all(z_copies(c))
        value = over_y[c, block_rows(z, eighth), :].astype(F32)
        for m in range(3):
            value = value + over_z[c, m].astype(F32)
        final[c, pl.ds(pl.multiple_of(y * half + z * eighth, eighth), eighth), :] = value.astype(BF)

    handle = (
        make,
        add_pair,
        add_across,
        add_y,
        add_z,
        lambda c: wait_recv_all(back_z_copies(c)),
        lambda c: back_y_copy(c).wait_recv(),
    )
    send = (
        lambda c: [pair_copy(c)],
        lambda c: [across_copy(c)],
        lambda c: [y_copy(c)],
        z_copies,
        back_z_copies,
        lambda c: [back_y_copy(c)],
        lambda c: [out_copy(c)],
    )

    def hidden_step(r):
        left = block_rows(r, D)

        def tile(n):
            columns = block_rows(n, 256)
            value = dot_cols(grad_pre[:, left], weight[r % 2, columns, :])

            @pl.when(r == 0)
            def _():
                gradient[:, columns] = value

            @pl.when(r > 0)
            def _():
                gradient[:, columns] = gradient[:, columns] + value

        loop(4, tile)

    def fold(value):
        return jnp.sum(value.reshape(4, 8, D), axis=0)

    def put(index, value):
        for j in range(8):
            packet[0, 8 * index + j : 8 * index + j + 1, :] = value[:, j * 128 : (j + 1) * 128]

    def put_all(first, values):
        for i, value in enumerate(values):
            put(first + i, jnp.sum(value, axis=0, keepdims=True))

    def ones_dot(value):
        return dot(jnp.ones((16, rows), BF), value)[0:1, :]

    def row_weight_of(i):
        row = i * 32 + lax.broadcasted_iota(jnp.int32, (32, 1), 0)
        item, _, in_pair, _ = item_of_rows(row, lengths, mp)
        return jnp.where(in_pair, choose_item(item, weights), 0.0) / mean_weight, in_pair

    zero = jnp.zeros((8, D), F32)

    def second_norm_back():
        def body(i, carry):
            here = block_rows(i, 32)
            unit, scale = stats(trunk[here, :])
            grad = gradient[here, :]
            row_weight, _ = row_weight_of(i)
            value = rowbuf[here, :].astype(F32) * row_weight + norm_back(
                grad, unit, scale, hidden_gain[...]
            )
            trunk[here, :] = value
            low = value.astype(BF)
            grad_attended[here, :] = low
            return (
                carry[0] + fold(grad * unit),
                carry[1] + fold(grad),
                carry[2] + fold(low.astype(F32)),
            )

        put_all(4, lax.fori_loop(0, blocks, body, (zero, zero, zero)))
        put(7, ones_dot(grad_mixed[...]))

    def context_step():
        def tile(n):
            columns = block_rows(n, 256)
            grad_context[:, columns] = dot_cols(grad_attended[...], weight[0, columns, :]).astype(BF)

        loop(4, tile)

    def head_pair_back(index):
        r = index // 2
        p = index % 2
        lanes = [block_rows(6 * r + 2 * n + p, 128) for n in range(3)]
        source = block_rows(2 * r + p, 128)
        factor = 1.0 / math.sqrt(HEAD_DIM)
        for first, size in blocks_of(rows):
            here = pl.ds(first, size)
            same = owner_of_rows(
                first + lax.broadcasted_iota(jnp.int32, (size, 1), 0), lengths, mp
            ) == owner_of_rows(first + lax.broadcasted_iota(jnp.int32, (1, size), 1), lengths, mp)
            q, k, v = [qkv[here, lane] for lane in lanes]
            g = grad_context[here, source]
            results = []
            for h in range(2):
                cut = slice(h * HEAD_DIM, (h + 1) * HEAD_DIM)
                soft = softmax_rows(q[:, cut], k[:, cut], same)
                grad_soft = dot_cols(g[:, cut], v[:, cut])
                center = jnp.sum(soft * grad_soft, axis=-1, keepdims=True)
                grad_scores = (soft * (grad_soft - center)).astype(BF)
                results.append(
                    (
                        (dot(grad_scores, k[:, cut]) * factor).astype(BF),
                        (dot_rows(grad_scores, q[:, cut]) * factor).astype(BF),
                        dot_rows(soft.astype(BF), g[:, cut]).astype(BF),
                    )
                )
            for n in range(3):
                qkv[here, lanes[n]] = jnp.concatenate([results[0][n], results[1][n]], axis=1)

    def normed_step(r):
        left = qkv[:, block_rows(r, 3 * width)]

        def tile(n):
            columns = block_rows(n, 256)
            value = dot_cols(left, weight[(r + 1) % 2, columns, 0 : 3 * width])

            @pl.when(r == 0)
            def _():
                gradient[:, columns] = value

            @pl.when(r > 0)
            def _():
                gradient[:, columns] = gradient[:, columns] + value

        loop(4, tile)

    def first_norm_back():
        def body(i, carry):
            here = block_rows(i, 32)
            unit, scale = stats(stream[here, :])
            grad = gradient[here, :]
            value = trunk[here, :] + norm_back(grad, unit, scale, gain[...])
            standard = (rowbuf[here, :].astype(F32) - column_mean) * inverse
            gradient[here, :] = value
            return (
                carry[0] + fold(value),
                carry[1] + fold(value * standard),
                carry[2] + fold(grad * unit),
                carry[3] + fold(grad),
            )

        put_all(0, lax.fori_loop(0, blocks, body, (zero, zero, zero, zero)))
        for r in range(4):
            if r:
                packet[r, 0:64, :] = packet[0, 0:64, :]
            parts = [
                ones_dot(qkv[:, (3 * r + n) * width : (3 * r + n + 1) * width]) for n in (0, 2)
            ] + [
                ones_dot(grad_pre[:, r * D + n * width : r * D + (n + 1) * width]) for n in range(4)
            ]
            for i, value in enumerate(parts):
                for j in range(2):
                    packet[r, 64 + 2 * i + j : 65 + 2 * i + j, :] = value[
                        :, j * 128 : (j + 1) * 128
                    ]
            packet[r, 76:80, :] = jnp.zeros((4, 128), F32)

    def mixed_step(r):
        left = grad_pre[:, block_rows(r, D)]

        def tile(n):
            columns = block_rows(n, 256)
            stream[:, columns] = stream[:, columns] + dot(left, weight[(r + 1) % 2, :, columns])

        loop(4, tile)

    def layer_step():
        def body(i):
            here = block_rows(i, 32)
            hidden[here, :] = (stream[here, :] + down_bias[...]).astype(BF)

        loop(blocks, body)

    def exchange(stage, sources, peers, slots):
        return [
            remote(
                source, slots.at[m], stat_send.at[stage, m], stat_recv.at[stage, m], peer
            )
            for m, (source, peer) in enumerate(zip(sources, peers))
        ]

    sums_a = exchange(0, [packet.at[r] for r in (1, 2, 3)], mp_peers, from_mp)
    sums_b = exchange(1, [packet.at[4]], [y_peer], from_y)
    sums_c = exchange(2, [packet.at[5]] * 3, z_peers, from_z)

    def gather_sums(first, copies, slots, target):
        value = packet[first]
        for m, copy in enumerate(copies):
            copy.wait_recv()
            value = value + slots[m]
        packet[target] = value

    def tokens_step():
        total = joined(packet[6], 0), joined(packet[6], 8)

        def body(i):
            here = block_rows(i, 32)
            standard = (rowbuf[here, :].astype(F32) - column_mean) * inverse
            _, in_pair = row_weight_of(i)
            share = jnp.where(in_pair, 1.0 / count_valid, 0.0)
            gradient[here, :] = inverse * (
                gradient[here, :] - share * (total[0] + total[1] * standard)
            )

        loop(blocks, body)

    before = {"mp": (mp + 3) % 4}
    layer_next_copy = remote(
        hidden.at[pl.ds(0, HALO)], layer_next, next_send.at[0], next_recv.at[0], before
    )
    tokens_next_copy = remote(
        gradient.at[pl.ds(0, HALO)], tokens_next, next_send.at[1], next_recv.at[1], before
    )

    def choose_rows(count, first):
        row = lax.broadcasted_iota(jnp.int32, (rows_here, count), 0)
        column = lax.broadcasted_iota(jnp.int32, (rows_here, count), 1) + first
        place = row + (rows_here - 2 * PAIR_LEN) * mp
        after = jnp.where(mp == 3, 2 * WINDOW, rows) - 2 * PAIR_LEN
        wanted = jnp.where(
            place < PAIR_LEN,
            place,
            jnp.where(place < 2 * PAIR_LEN, place + (WINDOW - PAIR_LEN), place + after),
        )
        return jnp.where(column == wanted, 1.0, 0.0).astype(BF)

    def own_rows(value, following, target):
        chosen, chosen_next = choose_rows(rows, 0), choose_rows(HALO, rows)
        pairs = ((chosen, value), (chosen_next, following))

        def tile(n):
            columns = block_rows(n, 256)
            total = jnp.zeros((rows_here, 256), F32)
            for matrix, ref in pairs:
                block = ref[:, columns]
                high = block.astype(BF)
                total = total + dot(matrix, high)
                if ref.dtype == F32:
                    middle_part = block - high.astype(F32)
                    low = middle_part.astype(BF)
                    total = total + dot(matrix, low)
                    total = total + dot(matrix, (middle_part - low.astype(F32)).astype(BF))
            target[0:rows_here, columns] = total.astype(target.dtype)

        loop(4, tile)

    def work(k):
        for s in range(4):

            @pl.when(k == TICK_HIDDEN + s)
            def _(s=s):
                if s == 0:
                    loads["grad_pre"].wait()
                weight_load(s).wait()

        @pl.when((k >= TICK_HIDDEN) & (k < TICK_HIDDEN + 4))
        def _():
            hidden_step(k - TICK_HIDDEN)

        for s in range(4):

            @pl.when(k == TICK_HIDDEN + s)
            def _(s=s):
                weight_load(s + 2).start()

        @pl.when(k == TICK_SECOND)
        def _():
            loads["middle"].wait()
            loads["cotangent"].wait()
            second_norm_back()
            loads["tokens"].start()

        @pl.when(k == TICK_CONTEXT)
        def _():
            weight_load(4).wait()
            context_step()
            weight_load(6).start()
            loads["qkv"].wait()

        @pl.when((k >= TICK_HEADS) & (k < TICK_HEADS + 8))
        def _():
            head_pair_back(k - TICK_HEADS)

        for s in range(4):

            @pl.when(k == TICK_NORMED + s)
            def _(s=s):
                weight_load(5 + s).wait()

        @pl.when((k >= TICK_NORMED) & (k < TICK_NORMED + 4))
        def _():
            normed_step(k - TICK_NORMED)

        for s in range(4):

            @pl.when(k == TICK_NORMED + s)
            def _(s=s):
                weight_load(7 + s).start()

        @pl.when(k == TICK_FIRST)
        def _():
            loads["stream"].wait()
            loads["tokens"].wait()
            first_norm_back()
            loads["active"].start()
            loads["middle again"].start()
            start_all(sums_a)

        for s in range(4):

            @pl.when(k == TICK_MIXED + s)
            def _(s=s):
                if s == 0:
                    loads["active"].wait()
                    loads["middle again"].wait()
                weight_load(9 + s).wait()

        @pl.when((k >= TICK_MIXED) & (k < TICK_MIXED + 4))
        def _():
            mixed_step(k - TICK_MIXED)

        for s in range(2):

            @pl.when(k == TICK_MIXED + s)
            def _(s=s):
                weight_load(11 + s).start()

        @pl.when(k == TICK_MIXED + 3)
        def _():
            layer_step()

        @pl.when(k == TICK_NEXT)
        def _():
            layer_next_copy.start()
            tokens_next_copy.start()

        @pl.when(k == TICK_LAYER)
        def _():
            layer_next_copy.wait_recv()
            own_rows(hidden, layer_next, normed)
            loads["layer"].start()

        @pl.when(k == TICK_TOKENS)
        def _():
            tokens_next_copy.wait_recv()
            own_rows(gradient, tokens_next, trunk)
            loads["tokens_grad"].start()

        @pl.when(k == TICK_SUMS[1])
        def _():
            gather_sums(0, sums_a, from_mp, 4)
            start_all(sums_b)

        @pl.when(k == TICK_SUMS[2])
        def _():
            gather_sums(4, sums_b, from_y, 5)
            start_all(sums_c)

        @pl.when(k == TICK_SUMS[3])
        def _():
            gather_sums(5, sums_c, from_z, 6)
            finals_out[...] = packet[6]
            tokens_step()

    waits = {0: ("grad_mixed",), 8: ("hidden",), 16: ("context",), 18: ("normed",)}

    def tick(k, carry):
        for when, names in waits.items():

            @pl.when(k == when)
            def _(names=names):
                for name in names:
                    loads[name].wait()

        def staged(stage, actions):
            c = k - STAGE_DELAY[stage]

            @pl.when((c >= 0) & (c < CHUNKS))
            def _():
                actions[stage](c)

        sends = tuple(lambda c, f=f: start_all(f(c)) for f in send)
        for stage in (6, 5, 4, 3, 2):
            staged(stage, handle)
        for stage in (2, 3, 4, 5, 6):
            staged(stage, sends)
        staged(0, handle)
        staged(1, handle)
        staged(0, sends)
        staged(1, sends)
        work(k)
        return carry

    lax.fori_loop(0, CHUNKS + STAGE_DELAY[-1], tick, 0)

    def finish(c):
        across_copy(c).wait_send()
        y_copy(c).wait_send()
        for copy in z_copies(c) + back_z_copies(c):
            copy.wait_send()
        back_y_copy(c).wait_send()
        out_copy(c).wait()

    loop(CHUNKS, finish)
    for copy in sums_a + sums_b + sums_c:
        copy.wait_send()
    layer_next_copy.wait_send()
    tokens_next_copy.wait_send()
    loads["layer"].wait()
    loads["tokens_grad"].wait()


def backward(smalls, vectors, sums, saved, rows_here):
    (
        tokens,
        cotangent,
        stream,
        middle,
        normed,
        qkv,
        context,
        hidden,
        grad_mixed,
        active,
        grad_pre,
        wqkv,
        wo,
        wup,
        wdown,
    ) = saved
    rows = normed.shape[0]
    shape = jax.ShapeDtypeStruct
    low = shape((rows, D), BF)
    full = shape((rows, D), F32)
    packed = shape((80, 128), F32)
    scratch = [
        shape((2, 4, CHUNK, D), BF),
        shape((CHUNKS, 2, CHUNK, D), BF),
        shape((CHUNKS, CHUNK, D), BF),
        shape((CHUNKS, CHUNK // 2, D), BF),
        shape((CHUNKS, 3, CHUNK // 8, D), BF),
        shape((CHUNKS, CHUNK, D), BF),
        shape((2, 4, rows, CHUNK), BF),
        shape(grad_pre.shape, BF),
        low,
        low,
        low,
        low,
        low,
        shape(qkv.shape, BF),
        low,
        low,
        full,
        full,
        full,
        shape((2, D, D), BF),
        shape((7, 80, 128), F32),
        shape((3, 80, 128), F32),
        shape((1, 80, 128), F32),
        shape((3, 80, 128), F32),
        shape((HALO, D), BF),
        shape((HALO, D), F32),
    ]
    dma = pltpu.SemaphoreType.DMA
    any_space = pl.BlockSpec(memory_space=pl.ANY)
    vmem = pl.BlockSpec(memory_space=pltpu.VMEM)
    return pl.pallas_call(
        backward_kernel,
        out_shape=(
            shape((CHUNKS, CHUNK, D), BF),
            packed,
            shape((rows_here, D), BF),
            shape((rows_here, D), F32),
        ),
        in_specs=[pl.BlockSpec(memory_space=pltpu.SMEM)] * 3 + [vmem] * 4 + [any_space] * 15,
        out_specs=(any_space, vmem, any_space, any_space),
        scratch_shapes=[pltpu.VMEM(v.shape, v.dtype) for v in scratch]
        + [
            dma((14,)),
            dma((2, 4)),
            dma((2,)),
            dma((CHUNKS,)),
            dma((CHUNKS,)),
            dma((CHUNKS,)),
            dma((CHUNKS,)),
            dma((CHUNKS,)),
            dma((CHUNKS,)),
            dma((CHUNKS, 3)),
            dma((CHUNKS, 3)),
            dma((CHUNKS, 3)),
            dma((CHUNKS, 3)),
            dma((CHUNKS,)),
            dma((CHUNKS,)),
            dma((CHUNKS,)),
            dma((3, 3)),
            dma((3, 3)),
            dma((2,)),
            dma((2,)),
        ],
        compiler_params=pltpu.CompilerParams(
            collective_id=2, has_side_effects=True, vmem_limit_bytes=67043328
        ),
        name="backward",
    )(
        *smalls,
        *vectors,
        sums,
        tokens,
        cotangent,
        stream,
        middle,
        normed,
        qkv,
        context,
        hidden,
        grad_mixed,
        active,
        grad_pre,
        wqkv,
        wo.reshape(D, D),
        wup,
        wdown,
    )


def finish_kernel(
    down_ref,
    up_ref,
    output_ref,
    query_ref,
    key_ref,
    value_ref,
    finals_ref,
    layer_ref,
    tokens_ref,
    down,
    up,
    output,
    query,
    key,
    value,
    layer,
    tokens,
    *vectors,
):
    down[...] = down_ref[0].astype(F32)
    up[...] = up_ref[0].astype(F32)
    output[...] = output_ref[0].astype(F32)
    for source, target in ((query_ref, query), (key_ref, key), (value_ref, value)):
        for half in range(2):
            target[:, half * CHUNK : (half + 1) * CHUNK] = source[half].astype(F32).T
    layer[...] = layer_ref[...]
    tokens[...] = tokens_ref[...]

    @pl.when(pl.program_id(0) == 0)
    def _():
        first = 0
        for target in vectors:
            size = target.shape[0]
            target[...] = finals_ref[first : first + size, :]
            first += size


def finish(reduced, finals, layer, tokens, width):
    shape = jax.ShapeDtypeStruct
    rows_here = layer.shape[0]
    share = rows_here // 8
    sizes = (8,) * 8 + (2, 2, 8)
    own = [pl.BlockSpec((share, D), lambda c: (c, 0))] * 2
    specs = (
        [
            pl.BlockSpec((CHUNK, D), lambda c: (c, 0)),
            pl.BlockSpec((CHUNK, D), lambda c: (c, 0)),
            pl.BlockSpec((width // 8, D), lambda c: (c, 0)),
        ]
        + [pl.BlockSpec((CHUNK, width), lambda c: (c, 0))] * 3
        + own
    )
    shapes = [
        shape((D, D), F32),
        shape((D, D), F32),
        shape((width, D), F32),
        shape((D, width), F32),
        shape((D, width), F32),
        shape((D, width), F32),
        shape((rows_here, D), BF),
        shape((rows_here, D), F32),
    ]
    return pl.pallas_call(
        finish_kernel,
        grid=(8,),
        in_specs=[
            pl.BlockSpec((1, CHUNK, D), lambda c: (c, 0, 0)),
            pl.BlockSpec((1, CHUNK, D), lambda c: (8 + c, 0, 0)),
            pl.BlockSpec((1, width // 8, D), lambda c: (16 + c // 4, c % 4, 0)),
        ]
        + [
            pl.BlockSpec((2, CHUNK, CHUNK), lambda c, first=first: (first, 0, c))
            for first in (9, 10, 11)
        ]
        + [pl.BlockSpec(finals.shape, lambda c: (0, 0))]
        + own,
        out_specs=specs + [pl.BlockSpec((size, 128), lambda c: (0, 0)) for size in sizes],
        out_shape=shapes + [shape((size, 128), F32) for size in sizes],
        name="finish",
    )(*[reduced] * 6, finals, layer, tokens)


def general_shards(
    tokens,
    cotangent,
    item_lengths,
    item_group,
    group_count,
    grid_scale,
    norm_gain,
    norm_shift,
    query_weight,
    query_bias,
    key_weight,
    value_weight,
    value_bias,
    output_weight,
    output_bias,
    hidden_gain,
    hidden_shift,
    up_weight,
    up_bias,
    down_weight,
    down_bias,
):
    shard_count = lax.axis_size("mp")
    slice_count = lax.axis_size("dp")
    mp = lax.axis_index("mp")
    rows_here = tokens.shape[0]
    item_count = item_lengths.shape[0]
    pairs_here = PAIRS // shard_count
    own_rows = pairs_here * PAIR_LEN
    shift = rows_here - own_rows
    halo = shift * (shard_count - 1)
    padding = rows_here * shard_count - PAIRS * PAIR_LEN
    tail_block = -(-padding // 32) * 32
    rows = pairs_here * WINDOW + tail_block
    is_last = mp == shard_count - 1

    width = query_weight.shape[1]
    qkv_own = jnp.concatenate([query_weight, key_weight, value_weight], axis=1)
    bias_own = jnp.concatenate([query_bias, value_bias, up_bias])[None, :]
    bias_across = swap_mp(bias_own, 2)
    bias_pair = swap_mp(jnp.concatenate([bias_own, bias_across], axis=0), 1)
    biases = [bias_own[0], bias_pair[0], bias_across[0], bias_pair[1]]

    def gather(own, direct):
        across = swap_mp(own, 2) if direct else fetch_across(own)
        return [own, swap_mp(own, 1), across, swap_mp(across, 1)]

    tokens_f = tokens.astype(F32)
    slice_row = mp * rows_here + jnp.arange(rows_here, dtype=jnp.int32)
    weighted = tokens_f * (slice_row < PAIRS * PAIR_LEN).astype(F32)[:, None]
    chosen = item_group[:, None] == jnp.arange(group_count.shape[0], dtype=jnp.int32)[None, :]
    item_scale = jnp.sum(jnp.where(chosen, grid_scale[None, :], 0.0), axis=1)
    item_weight = jnp.sum(jnp.where(chosen, group_count[None, :], 0), axis=1).astype(F32)
    sums = all_sum(
        jnp.stack(
            [
                jnp.sum(weighted, axis=0),
                jnp.sum(weighted * tokens_f, axis=0),
                jnp.broadcast_to(jnp.sum(item_weight) / shard_count, (D,)),
            ]
        )
    )

    def windows(v):
        before = lax.ppermute(
            v[rows_here - halo :], "mp", [(i, i + 1) for i in range(shard_count - 1)]
        )
        joined = jnp.concatenate([before, v], axis=0)
        start = halo - shift * mp
        parts = []
        for pair in range(pairs_here):
            parts.append(
                lax.dynamic_slice_in_dim(joined, start + pair * PAIR_LEN, PAIR_LEN, axis=0)
            )
            parts.append(jnp.zeros((WINDOW - PAIR_LEN, D), v.dtype))
        parts.append(jnp.where(is_last, v[rows_here - padding :], jnp.zeros((), v.dtype)))
        parts.append(jnp.zeros((tail_block - padding, D), v.dtype))
        return jnp.concatenate(parts, axis=0)

    def unwindows(v):
        own = jnp.concatenate(
            [v[pair * WINDOW : pair * WINDOW + PAIR_LEN] for pair in range(pairs_here)], axis=0
        )
        after = lax.ppermute(own[:halo], "mp", [(i + 1, i) for i in range(shard_count - 1)])
        after = jnp.concatenate([after, jnp.zeros((padding - halo, D), v.dtype)], axis=0)
        tail = v[pairs_here * WINDOW : pairs_here * WINDOW + padding]
        joined = jnp.concatenate([own, jnp.where(is_last, tail, after)], axis=0)
        return lax.dynamic_slice_in_dim(joined, shift * mp, rows_here, axis=0)

    tokens_w = windows(tokens).astype(F32)
    cotangent_w = windows(cotangent).astype(F32)

    row = jnp.arange(rows, dtype=jnp.int32)
    window = row // WINDOW
    offset = row % WINDOW
    in_pair = (window < pairs_here) & (offset < PAIR_LEN)
    is_padding = (window == pairs_here) & (offset < padding) & is_last
    pair = pairs_here * mp + window
    item_ids = jnp.arange(item_count, dtype=jnp.int32)
    first_len = jnp.sum(
        jnp.where(item_ids[None, :] == (2 * pair)[:, None], item_lengths[None, :], 0), axis=1
    )
    second = (offset >= first_len).astype(jnp.int32)
    owner = jnp.where(in_pair, 2 * pair + second, jnp.where(is_padding, item_count, -1))
    position = offset - second * first_len
    member = owner[:, None] == item_ids[None, :]
    row_scale = jnp.sum(jnp.where(member, item_scale[None, :], 0.0), axis=1)
    row_count = jnp.sum(jnp.where(member, item_weight[None, :], 0.0), axis=1)
    valid = in_pair.astype(F32)[:, None]
    quarter = D // 4
    frequency = jnp.exp(-math.log(10000.0) * jnp.arange(quarter, dtype=F32) / quarter)
    across_angle = ((position // SIDE).astype(F32) * row_scale)[:, None] * frequency
    side_angle = ((position % SIDE).astype(F32) * row_scale)[:, None] * frequency
    grid_table = (
        jnp.concatenate(
            [
                jnp.sin(across_angle),
                jnp.cos(across_angle),
                jnp.sin(side_angle),
                jnp.cos(side_angle),
            ],
            axis=-1,
        )
        * valid
    )
    owner_col = owner[:, None]
    owner_row = owner[None, :]

    qkv_weights = jnp.concatenate(gather(qkv_own, True), axis=1)
    output_weights = jnp.concatenate(gather(output_weight, False), axis=0)
    up_weights = jnp.concatenate(gather(up_weight, False), axis=1)
    down_weights = jnp.concatenate(gather(down_weight, False), axis=0)
    hidden_width = up_weight.shape[1]
    no_bias = jnp.zeros((width,), F32)
    qkv_bias = jnp.concatenate(
        [v for b in biases for v in (b[:width], no_bias, b[width : 2 * width])]
    )
    up_biases = jnp.concatenate([b[2 * width :] for b in biases])

    count_valid = slice_count * PAIRS * PAIR_LEN
    column_mean = sums[0] / count_valid
    spread = sums[1] / count_valid - column_mean * column_mean
    inverse = lax.rsqrt(spread + 1e-05)
    row_weight = row_count / (sums[2, 0] / (slice_count * item_count))
    standard = (tokens_w - column_mean) * inverse
    stream = standard + grid_table
    unit, unit_inverse = stats(stream)
    normed = (unit * norm_gain + norm_shift).astype(BF)

    qkv = (dot(normed, qkv_weights) + qkv_bias).astype(BF)
    context = attend(qkv, owner_col, owner_row, shard_count)
    middle = stream + (dot(context, output_weights) + output_bias)
    middle_unit, middle_inverse = stats(middle)
    hidden_in = (middle_unit * hidden_gain + hidden_shift).astype(BF)

    grad_out = cotangent_w * row_weight[:, None]
    grad_mixed = grad_out.astype(BF)
    active, slope = gelu_parts(dot(hidden_in, up_weights) + up_biases)
    mixed = dot(active, down_weights) + down_bias
    grad_pre = (dot_cols(grad_mixed, down_weights) * slope).astype(BF)
    grad_hidden = dot_cols(grad_pre, up_weights)
    layer_output = unwindows((middle + mixed).astype(BF))
    grad_middle = grad_out + norm_back(grad_hidden, middle_unit, middle_inverse, hidden_gain)
    grad_attended = grad_middle.astype(BF)

    grad_context = dot_cols(grad_attended, output_weights).astype(BF)
    grad_qkv = attend_back(qkv, grad_context, owner_col, owner_row, shard_count)
    grad_normed = dot_cols(grad_qkv, qkv_weights)

    pieces = range(shard_count)
    def columns(v, r, size):
        return v[:, r * size : (r + 1) * size]

    def reduced(left, right):
        return reduce_pieces([dot_rows(left(r), right(r)).astype(BF) for r in pieces])

    down_weight_grad = reduced(
        lambda r: columns(active, r, hidden_width), lambda r: grad_mixed
    )
    up_weight_grad = reduced(
        lambda r: hidden_in, lambda r: columns(grad_pre, r, hidden_width)
    )
    output_weight_grad = reduced(
        lambda r: columns(context, r, width), lambda r: grad_attended
    )
    qkv_weight_grad = reduced(lambda r: normed, lambda r: columns(grad_qkv, r, 3 * width))
    qkv_weight_grads = [columns(qkv_weight_grad, i, width) for i in range(3)]
    grad_stream = grad_middle + norm_back(grad_normed, unit, unit_inverse, norm_gain)

    def column_sums(v):
        return jnp.sum(v.astype(F32), axis=0)

    qkv_sums = column_sums(grad_qkv)
    up_sums = column_sums(grad_pre)
    bias_grads = [
        jnp.concatenate(
            [
                qkv_sums[3 * r * width : (3 * r + 1) * width],
                qkv_sums[(3 * r + 2) * width : 3 * (r + 1) * width],
                up_sums[r * hidden_width : (r + 1) * hidden_width],
            ]
        )[None, :]
        for r in pieces
    ]
    got = swap_mp(jnp.concatenate([bias_grads[1], bias_grads[3]], axis=0), 1)
    bias_grad = bias_grads[0] + got[:1] + swap_mp(bias_grads[2] + got[1:], 2)
    for bit in range(dp_bits()):
        bias_grad = bias_grad + swap_dp(bias_grad, 1 << bit)
    bias_grad = bias_grad[0]
    finals = all_sum(
        jnp.stack(
            [
                column_sums(grad_stream),
                column_sums(grad_stream * standard),
                column_sums(grad_normed * unit),
                column_sums(grad_normed),
                column_sums(grad_hidden * middle_unit),
                column_sums(grad_hidden),
                column_sums(grad_attended),
                column_sums(grad_mixed),
            ]
        )
    )
    tokens_grad = unwindows(
        inverse * (grad_stream - valid / count_valid * (finals[0] + finals[1] * standard))
    )
    return (
        layer_output,
        tokens_grad,
        finals[2],
        finals[3],
        qkv_weight_grads[0],
        bias_grad[:width],
        qkv_weight_grads[1],
        qkv_weight_grads[2],
        bias_grad[width : 2 * width],
        output_weight_grad,
        finals[6],
        finals[4],
        finals[5],
        up_weight_grad,
        bias_grad[2 * width :],
        down_weight_grad,
        finals[7],
    )


def fast_shards(
    tokens,
    cotangent,
    item_lengths,
    item_group,
    group_count,
    grid_scale,
    norm_gain,
    norm_shift,
    query_weight,
    query_bias,
    key_weight,
    value_weight,
    value_bias,
    output_weight,
    output_bias,
    hidden_gain,
    hidden_shift,
    up_weight,
    up_bias,
    down_weight,
    down_bias,
):
    rows = 2 * WINDOW + 96
    saved = forward(
        (item_lengths, item_group, group_count, grid_scale),
        [
            v[None, :]
            for v in (
                norm_gain,
                norm_shift,
                output_bias,
                hidden_gain,
                hidden_shift,
                query_bias,
                value_bias,
                up_bias,
            )
        ],
        tokens,
        cotangent,
        (query_weight, key_weight, value_weight, output_weight, up_weight, down_weight),
        rows,
    )
    reduced, finals, layer_output, tokens_grad = backward(
        (item_lengths, item_group, group_count),
        [v[None, :] for v in (norm_gain, hidden_gain, down_bias)],
        saved[2],
        saved[:2] + saved[3:],
        tokens.shape[0],
    )
    (
        down_weight_grad,
        up_weight_grad,
        output_weight_grad,
        query_weight_grad,
        key_weight_grad,
        value_weight_grad,
        layer_output,
        tokens_grad,
        *vectors,
    ) = finish(reduced, finals, layer_output, tokens_grad, query_weight.shape[1])
    vectors = [v.reshape(-1) for v in vectors]
    return (
        layer_output,
        tokens_grad,
        vectors[2],
        vectors[3],
        query_weight_grad,
        vectors[8],
        key_weight_grad,
        value_weight_grad,
        vectors[9],
        output_weight_grad,
        vectors[6],
        vectors[4],
        vectors[5],
        up_weight_grad,
        vectors[10],
        down_weight_grad,
        vectors[7],
    )


def shards(*args):
    if lax.axis_size("dp") == 8 and lax.axis_size("mp") == 4 and args[0].shape == (512, D):
        return fast_shards(*args)
    return general_shards(*args)


def solution(mesh):
    rows = P(("dp", "mp"), None)
    columns = P(None, "mp")
    return jax.shard_map(
        shards,
        mesh=mesh,
        in_specs=(
            rows,
            rows,
            P("dp"),
            P("dp"),
            P(),
            P(),
            P(),
            P(),
            columns,
            P("mp"),
            columns,
            columns,
            P("mp"),
            P("mp", None),
            P(),
            P(),
            P(),
            columns,
            P("mp"),
            P("mp", None),
            P(),
        ),
        out_specs=(
            rows,
            rows,
            P(),
            P(),
            columns,
            P("mp"),
            columns,
            columns,
            P("mp"),
            P("mp", None),
            P(),
            P(),
            P(),
            columns,
            P("mp"),
            P("mp", None),
            P(),
        ),
        check_vma=False,
    )
```

```python
import functools
import math

import jax
import jax.numpy as jnp
from jax import lax
from jax.experimental import pallas as pl
from jax.experimental.pallas import tpu as pltpu
from jax.sharding import PartitionSpec as P

D = 1024
HEAD_DIM = 64
SIDE = 14
PAIRS = 8
PAIR_LEN = 245
WINDOW = 256
BF = jnp.bfloat16
F32 = jnp.float32
PADDING = 88


def dot(a, b):
    return lax.dot_general(a, b, (((1,), (0,)), ((), ())), preferred_element_type=F32)


def dot_rows(a, b):
    return lax.dot_general(a, b, (((0,), (0,)), ((), ())), preferred_element_type=F32)


def dot_cols(a, b):
    return lax.dot_general(a, b, (((1,), (1,)), ((), ())), preferred_element_type=F32)


def swap_mp(v, mask):
    count = lax.axis_size("mp")
    return lax.ppermute(v, "mp", [(i, i ^ mask) for i in range(count)])


def swap_dp(v, mask):
    count = lax.axis_size("dp")
    return lax.ppermute(v, "dp", [(i, i ^ mask) for i in range(count)])


def dp_bits():
    return lax.axis_size("dp").bit_length() - 1


def all_sum(v):
    v = v + swap_mp(v, 1) + swap_mp(v, 2) + swap_mp(v, 3)
    bit = 0
    bits = dp_bits()
    while bit < bits:
        if bit + 1 < bits:
            v = v + swap_dp(v, 1 << bit) + swap_dp(v, 2 << bit) + swap_dp(v, 3 << bit)
            bit += 2
        else:
            v = v + swap_dp(v, 1 << bit)
            bit += 1
    return v


def dp_bit(bit):
    return (lax.axis_index("dp") >> bit) & 1


def join(mine, other, bit):
    return jnp.where(
        dp_bit(bit) == 0,
        jnp.concatenate([mine, other], axis=0),
        jnp.concatenate([other, mine], axis=0),
    )


def chunk_index():
    index = jnp.int32(0)
    for bit in range(dp_bits()):
        index = index * 2 + dp_bit(bit)
    return index


def fetch_across(w):
    rows = w.shape[0] // lax.axis_size("dp")
    mine = lax.dynamic_slice_in_dim(w, chunk_index() * rows, rows, axis=0)
    got = swap_mp(mine, 2)
    for bit in reversed(range(dp_bits())):
        got = join(got, swap_dp(got, 1 << bit), bit)
    return got


def reduce_pieces(pieces):
    half = pieces[1].shape[0]
    got = swap_mp(jnp.concatenate([pieces[1], pieces[3]], axis=0), 1)
    across = pieces[2].astype(F32) + got[half:].astype(F32)
    own = pieces[0].astype(F32) + got[:half].astype(F32)
    total = own + swap_mp(across.astype(BF), 2).astype(F32)
    for bit in range(dp_bits()):
        size = total.shape[0] // 2
        side = dp_bit(bit)
        send = lax.dynamic_slice_in_dim(total, (1 - side) * size, size, axis=0).astype(BF)
        keep = lax.dynamic_slice_in_dim(total, side * size, size, axis=0)
        total = keep + swap_dp(send, 1 << bit).astype(F32)
    total = total.astype(BF)
    for bit in reversed(range(dp_bits())):
        total = join(total, swap_dp(total, 1 << bit), bit)
    return total.astype(F32)


def stats(v):
    mean = jnp.mean(v, axis=-1, keepdims=True)
    center = v - mean
    spread = jnp.mean(center * center, axis=-1, keepdims=True)
    inverse = lax.rsqrt(spread + 1e-06)
    return center * inverse, inverse


def norm_back(grad, unit, inverse, gain):
    f = grad * gain
    return inverse * (
        f
        - jnp.mean(f, axis=-1, keepdims=True)
        - unit * jnp.mean(f * unit, axis=-1, keepdims=True)
    )


def blocks_of(rows):
    return [(first, min(WINDOW, rows - first)) for first in range(0, rows, WINDOW)]


def head_scores(qkv_ref, same, first, size, h, width):
    q = qkv_ref[first : first + size, h * HEAD_DIM : (h + 1) * HEAD_DIM]
    k = qkv_ref[first : first + size, width + h * HEAD_DIM : width + (h + 1) * HEAD_DIM]
    v = qkv_ref[first : first + size, 2 * width + h * HEAD_DIM : 2 * width + (h + 1) * HEAD_DIM]
    scores = jnp.where(same, dot_cols(q, k) * (1.0 / math.sqrt(HEAD_DIM)), -1e30)
    weights = jnp.exp(scores - jnp.max(scores, axis=-1, keepdims=True))
    weights = weights * (1.0 / jnp.sum(weights, axis=-1, keepdims=True))
    return q, k, v, weights


def attend_kernel(qkv_ref, col_ref, row_ref, out_ref):
    rows, width = out_ref.shape
    for first, size in blocks_of(rows):
        same = col_ref[first : first + size, :] == row_ref[:, first : first + size]
        for h in range(width // HEAD_DIM):
            q, k, v, weights = head_scores(qkv_ref, same, first, size, h, width)
            out_ref[first : first + size, h * HEAD_DIM : (h + 1) * HEAD_DIM] = dot(
                weights.astype(BF), v
            ).astype(BF)


def attend_back_kernel(qkv_ref, grad_ref, col_ref, row_ref, out_ref):
    rows, width = grad_ref.shape
    factor = 1.0 / math.sqrt(HEAD_DIM)
    for first, size in blocks_of(rows):
        same = col_ref[first : first + size, :] == row_ref[:, first : first + size]
        for h in range(width // HEAD_DIM):
            q, k, v, weights = head_scores(qkv_ref, same, first, size, h, width)
            grad = grad_ref[first : first + size, h * HEAD_DIM : (h + 1) * HEAD_DIM]
            soft = dot_cols(grad, v)
            center = jnp.sum(weights * soft, axis=-1, keepdims=True)
            grad_scores = (weights * (soft - center)).astype(BF)
            for part, value in enumerate(
                (
                    dot(grad_scores, k) * factor,
                    dot_rows(grad_scores, q) * factor,
                    dot_rows(weights.astype(BF), grad),
                )
            ):
                lane = part * width + h * HEAD_DIM
                out_ref[first : first + size, lane : lane + HEAD_DIM] = value.astype(BF)


def attend(qkv, owner_col, owner_row, groups):
    rows, width = qkv.shape[0], qkv.shape[1] // (3 * groups)
    return pl.pallas_call(
        attend_kernel,
        grid=(groups,),
        in_specs=[
            pl.BlockSpec((rows, 3 * width), lambda r: (0, r)),
            pl.BlockSpec((rows, 1), lambda r: (0, 0)),
            pl.BlockSpec((1, rows), lambda r: (0, 0)),
        ],
        out_specs=pl.BlockSpec((rows, width), lambda r: (0, r)),
        out_shape=jax.ShapeDtypeStruct((rows, groups * width), BF),
        name="attend",
    )(qkv, owner_col, owner_row)


def attend_back(qkv, grad, owner_col, owner_row, groups):
    rows, width = grad.shape[0], grad.shape[1] // groups
    return pl.pallas_call(
        attend_back_kernel,
        grid=(groups,),
        in_specs=[
            pl.BlockSpec((rows, 3 * width), lambda r: (0, r)),
            pl.BlockSpec((rows, width), lambda r: (0, r)),
            pl.BlockSpec((rows, 1), lambda r: (0, 0)),
            pl.BlockSpec((1, rows), lambda r: (0, 0)),
        ],
        out_specs=pl.BlockSpec((rows, 3 * width), lambda r: (0, r)),
        out_shape=jax.ShapeDtypeStruct((rows, 3 * groups * width), BF),
        name="attend_back",
    )(qkv, grad, owner_col, owner_row)


def gelu_parts(preact):
    phi = 0.5 * (1.0 + lax.erf(preact * (1.0 / math.sqrt(2.0))))
    slope = phi + preact * jnp.exp(-0.5 * preact * preact) * (1.0 / math.sqrt(2.0 * math.pi))
    return (preact * phi).astype(BF), slope


HALO = 80
ROUTE_TICKS = (
    (0, 0, 0, 0, 1, 1, 2, 2, 3, 4),
    (1, 1, 1, 1, 2, 3, 4, 5, 6, 7),
    (2, 2, 3, 3, 4, 5, 6, 7, 8, 9),
    (5, 5, 6, 6, 9, 11, 13, 15, 17, 19),
)
AT_HEADS, AT_PAIRED, AT_QUERY, AT_OUTPUT, AT_HIDDEN, AT_DOWN = 4, 8, 10, 16, 19, 22
MESH = pl.DeviceIdType.MESH


def places():
    mp = lax.axis_index("mp")
    dp = lax.axis_index("dp")
    y = dp % 2
    z = dp // 2
    sibling = mp + 1 - 2 * (mp % 2)
    opposite = mp + 2 - 4 * (mp // 2)
    across = opposite + 1 - 2 * (mp % 2)
    mp_peers = [{"mp": sibling}, {"mp": opposite}, {"mp": across}]
    y_peer = {"dp": dp + 1 - 2 * y}
    z_places = [(z + m) % 4 for m in (1, 2, 3)]
    z_peers = [{"dp": place * 2 + y} for place in z_places]
    return mp, y, z, mp_peers, y_peer, z_places, z_peers


def greet(peers):
    barrier = pltpu.get_barrier_semaphore()
    for peer in peers:
        pl.semaphore_signal(barrier, inc=1, device_id=peer, device_id_type=MESH)
    pl.semaphore_wait(barrier, len(peers))


def remote(source, target, send, recv, peer):
    return pltpu.make_async_remote_copy(
        src_ref=source,
        dst_ref=target,
        send_sem=send,
        recv_sem=recv,
        device_id=peer,
        device_id_type=MESH,
    )


def loop(count, body):
    def step(i, carry):
        body(i)
        return carry

    lax.fori_loop(0, count, step, 0)


def block_rows(i, size):
    return pl.ds(pl.multiple_of(i * size, size), size)


def start_all(copies):
    for copy in copies:
        copy.start()


def wait_recv_all(copies):
    for copy in copies:
        copy.wait_recv()


def item_of_rows(row, lengths, mp):
    window = row >> 8
    offset = row & (WINDOW - 1)
    length = jnp.where(window == 0, lengths[4 * mp], lengths[4 * mp + 2])
    second = jnp.where(offset >= length, 1, 0)
    in_pair = (window < 2) & (offset < PAIR_LEN)
    is_padding = (window == 2) & (offset < PADDING) & (mp == 3)
    return 2 * window + second, offset - second * length, in_pair, is_padding


def owner_of_rows(row, lengths, mp):
    item, _, in_pair, is_padding = item_of_rows(row, lengths, mp)
    return jnp.where(in_pair, item, jnp.where(is_padding, 16, -1))


def choose_item(item, values):
    result = jnp.where(item == 0, values[0], 0.0)
    for j in (1, 2, 3):
        result = jnp.where(item == j, values[j], result)
    return result


def joined(tiles, first):
    return jnp.concatenate([tiles[first + j : first + j + 1, :] for j in range(8)], axis=1)


def forward_kernel(
    lengths,
    groups,
    counts,
    scales,
    gain,
    shift,
    output_bias,
    hidden_gain,
    hidden_shift,
    query_bias,
    value_bias,
    up_bias,
    tokens_ref,
    cotangent_ref,
    query_ref,
    key_ref,
    value_ref,
    output_ref,
    up_ref,
    down_ref,
    tokens_out,
    cotangent_out,
    sums_out,
    stream_out,
    middle_out,
    normed_out,
    qkv_out,
    context_out,
    hidden_out,
    grad_mixed_out,
    active_out,
    grad_pre_out,
    wqkv_out,
    wo_out,
    wup_out,
    wdown_out,
    tokens_ext,
    cotangent_ext,
    tokens,
    cotangent,
    stream,
    middle,
    normed,
    qkv,
    context,
    hidden,
    grad_mixed,
    active,
    grad_pre,
    wqkv,
    wo,
    wup,
    wdown,
    sums,
    bias,
    part,
    from_mp,
    from_y,
    from_z,
    own_sem,
    halo_sem,
    store_sem,
    stat_send,
    stat_recv,
    bias_send,
    bias_recv,
    pair_send,
    pair_recv,
    x_send,
    x_recv,
    far_send,
    far_recv,
    near_send,
    near_recv,
    y_send,
    y_recv,
    fwd_send,
    fwd_recv,
):
    mp, y, z, mp_peers, y_peer, z_places, z_peers = places()
    sibling, opposite, _ = mp_peers
    rows_here = tokens_ref.shape[0]
    rows = tokens.shape[0]
    width = query_ref.shape[1]
    blocks = rows // 32

    items = (
        [(key_ref, first, D // 2, wqkv, width, width, False) for first in (0, D // 2)]
        + [(value_ref, first, D // 2, wqkv, 2 * width, width, False) for first in (0, D // 2)]
        + [(output_ref, 0, width, wo, 0, D, False)]
        + [(up_ref, first, D // 4, wup, 0, D, False) for first in range(0, D, D // 4)]
        + [(down_ref, first, D // 4, wdown, 0, D, False) for first in (3 * D // 4,)]
        + [(query_ref, 0, D, wqkv, 0, width, True), (down_ref, 0, 3 * D // 4, wdown, 0, D, True)]
    )
    relayed = range(10)
    QUERY, DOWN = 10, 11
    HEADS, OUTPUT, HIDDEN = (0, 1, 2, 3, QUERY), 4, (5, 6, 7, 8, 9, DOWN)
    everything = range(len(items))
    near = z % 2
    far = z // 2
    near_peer = {"dp": (z + 1 - 2 * near) * 2 + y}
    far_peer = {"dp": ((z + 2) % 4) * 2 + y}

    def source(i, start, size):
        return items[i][0].at[pl.ds(items[i][1] + start, size)]

    def place(i, r, start, size):
        _, first, _, ref, column, columns, _ = items[i]
        return ref.at[r, pl.ds(first + start, size), pl.ds(column, columns)]

    def part_of(i, first, eighths):
        size = items[i][2] // 8
        return pl.multiple_of(first * size, size), eighths * size

    own_copies = [
        pltpu.make_async_copy(
            source(i, 0, items[i][2]), place(i, 0, 0, items[i][2]), own_sem.at[i]
        )
        for i in everything
    ]
    pair_copies = [
        remote(
            source(i, 0, items[i][2]),
            place(i, 1, 0, items[i][2]),
            pair_send.at[i],
            pair_recv.at[i],
            sibling,
        )
        for i in everything
    ]

    def x_copy(i):
        start, size = (
            (0, items[i][2]) if items[i][6] else part_of(i, y * 4 + near * 2 + far, 1)
        )
        return remote(
            source(i, start, size), place(i, 2, start, size), x_send.at[i], x_recv.at[i], opposite
        )

    def hop(i, first, eighths, send, recv, peer):
        start, size = part_of(i, first, eighths)
        view = place(i, 2, start, size)
        return remote(view, view, send.at[i], recv.at[i], peer)

    def far_copy(i):
        return hop(i, y * 4 + near * 2 + far, 1, far_send, far_recv, far_peer)

    def near_copy(i):
        return hop(i, y * 4 + near * 2, 2, near_send, near_recv, near_peer)

    def y_copy(i):
        return hop(i, y * 4, 4, y_send, y_recv, y_peer)

    def fwd_copy(i):
        size = items[i][2]
        return remote(
            place(i, 2, 0, size), place(i, 3, 0, size), fwd_send.at[i], fwd_recv.at[i], sibling
        )

    route = (x_copy, far_copy, near_copy, y_copy, fwd_copy)

    keep = [
        pltpu.make_async_copy(ref, ext.at[pl.ds(HALO, rows_here)], halo_sem.at[which, 2])
        for which, (ref, ext) in enumerate(
            ((tokens_ref, tokens_ext), (cotangent_ref, cotangent_ext))
        )
    ]
    start_all(keep)
    start_all(own_copies)
    bias[0, 0:1, :] = query_bias[...]
    bias[0, 1:2, :] = value_bias[...]
    for j in range(4):
        bias[0, 2 + j : 3 + j, :] = up_bias[:, j * width : (j + 1) * width]
    bias[0, 6:8, :] = jnp.zeros((2, width), F32)

    weights = [counts[groups[4 * mp + j]].astype(F32) for j in range(4)]
    weight_part = weights[0] + weights[1] + weights[2] + weights[3]
    keep[0].wait()

    def add_rows(i, carry):
        block = tokens_ext[pl.ds(pl.multiple_of(HALO + i * 16, 16), 16), :].astype(F32)
        row = mp * rows_here + i * 16 + lax.broadcasted_iota(jnp.int32, (16, 1), 0)
        kept = jnp.where(row < PAIRS * PAIR_LEN, block, 0.0)
        return carry[0] + kept, carry[1] + kept * block

    zero = jnp.zeros((16, D), F32)
    first, second = lax.fori_loop(0, rows_here // 16, add_rows, (zero, zero))
    first = jnp.sum(first, axis=0, keepdims=True)
    second = jnp.sum(second, axis=0, keepdims=True)
    for j in range(8):
        part[0, j : j + 1, :] = first[:, j * 128 : (j + 1) * 128]
        part[0, 8 + j : 9 + j, :] = second[:, j * 128 : (j + 1) * 128]
    part[0, 16:24, :] = jnp.zeros((8, 128), F32) + weight_part
    greet(mp_peers + [y_peer] + z_peers)

    sums_a = [
        remote(part.at[0], from_mp.at[m], stat_send.at[0, m], stat_recv.at[0, m], peer)
        for m, peer in enumerate(mp_peers)
    ]
    start_all(sums_a)
    after = {"mp": (mp + 1) % 4}
    halo_copies = [
        remote(
            ref.at[pl.ds(rows_here - HALO, HALO)],
            ext.at[pl.ds(0, HALO)],
            halo_sem.at[which, 0],
            halo_sem.at[which, 1],
            after,
        )
        for which, (ref, ext) in enumerate(
            ((tokens_ref, tokens_ext), (cotangent_ref, cotangent_ext))
        )
    ]
    bias_copies = [
        remote(bias.at[0], bias.at[r + 1], bias_send.at[r], bias_recv.at[r], peer)
        for r, peer in enumerate(mp_peers)
    ]
    start_all(halo_copies + bias_copies)
    start_all([x_copy(i) for i in everything])
    start_all([pair_copies[i] for i in HEADS + (OUTPUT,) + HIDDEN])
    sums_b = [
        remote(part.at[1], from_y.at[0], stat_send.at[1, 0], stat_recv.at[1, 0], y_peer)
    ]
    sums_c = [
        remote(part.at[2], from_z.at[m], stat_send.at[2, m], stat_recv.at[2, m], peer)
        for m, peer in enumerate(z_peers)
    ]

    def position_table():
        place_id = lax.broadcasted_iota(jnp.int32, (64, 1), 0)
        table_scale = choose_item(
            place_id >> 4, [scales[groups[4 * mp + j]] for j in range(4)]
        )
        quarter = D // 4
        lane = lax.broadcasted_iota(jnp.int32, (1, quarter), 1).astype(F32)
        frequency = jnp.exp(-math.log(10000.0) * lane / quarter)
        angle = ((place_id & 15).astype(F32) * table_scale) * frequency
        table = jnp.concatenate([jnp.sin(angle), jnp.cos(angle)], axis=1)
        row = lax.broadcasted_iota(jnp.int32, (rows, 64), 0)
        column = lax.broadcasted_iota(jnp.int32, (rows, 64), 1)
        item, position, in_pair, _ = item_of_rows(row, lengths, mp)
        across = (position * 9363) >> 17
        for half, code in enumerate((across, position - SIDE * across)):
            chosen = jnp.where(in_pair & (column == item * 16 + code), 1.0, 0.0)
            stream[:, half * 2 * quarter : (half + 1) * 2 * quarter] = lax.dot_general(
                chosen,
                table,
                (((1,), (0,)), ((), ())),
                precision=lax.Precision.HIGHEST,
                preferred_element_type=F32,
            )

    def place_rows():
        wait_recv_all(halo_copies)
        keep[1].wait()
        own_len = 2 * PAIR_LEN
        row = lax.broadcasted_iota(jnp.int32, (rows, HALO + rows_here), 0)
        column = lax.broadcasted_iota(jnp.int32, (rows, HALO + rows_here), 1)
        window = row >> 8
        offset = row & (WINDOW - 1)
        wanted = HALO - (rows_here - own_len) * mp + window * PAIR_LEN + offset
        tail = jnp.where(mp == 3, HALO + rows_here - PADDING, 4096) + offset
        wanted = jnp.where(window < 2, jnp.where(offset < PAIR_LEN, wanted, -1), tail)
        chosen = jnp.where(column == wanted, 1.0, 0.0).astype(BF)
        tokens[...] = dot(chosen, tokens_ext[...]).astype(BF)
        cotangent[...] = dot(chosen, cotangent_ext[...]).astype(BF)

    def norm_rows(first, count):
        slices = lax.axis_size("dp")
        count_valid = slices * PAIRS * PAIR_LEN
        column_mean = joined(sums, 0) / count_valid
        spread = joined(sums, 8) / count_valid - column_mean * column_mean
        inverse = lax.rsqrt(spread + 1e-05)
        mean_weight = sums[16:17, 0:1] / (slices * 16)

        def first_norm(i):
            here = block_rows(i, 32)
            value = (tokens[here, :].astype(F32) - column_mean) * inverse + stream[here, :]
            stream[here, :] = value
            unit, _ = stats(value)
            normed[here, :] = (unit * gain[...] + shift[...]).astype(BF)
            row = i * 32 + lax.broadcasted_iota(jnp.int32, (32, 1), 0)
            item, _, in_pair, _ = item_of_rows(row, lengths, mp)
            row_weight = jnp.where(in_pair, choose_item(item, weights), 0.0) / mean_weight
            grad_mixed[here, :] = (cotangent[here, :].astype(F32) * row_weight).astype(BF)

        def body(i):
            first_norm(first + i)

        loop(count, body)

    def group_stores(value, target, r):
        return value.at[r], target.at[r]

    def column_stores(value, target, r):
        columns = pl.ds(r * D, D)
        return value.at[:, columns], target.at[:, columns]

    plan = (
        [
            (AT_HEADS, ref, target)
            for ref, target in (
                (tokens, tokens_out),
                (cotangent, cotangent_out),
                (sums, sums_out),
                (stream, stream_out),
                (normed, normed_out),
                (grad_mixed, grad_mixed_out),
            )
        ]
        + [
            (AT_OUTPUT, ref, target)
            for ref, target in ((qkv, qkv_out), (context, context_out), (wqkv, wqkv_out))
        ]
        + [
            (AT_HIDDEN, ref, target)
            for ref, target in ((middle, middle_out), (hidden, hidden_out), (wo, wo_out))
        ]
        + [
            (when,) + group_stores(ref, target, r)
            for r, when in enumerate((AT_PAIRED, AT_PAIRED, AT_HIDDEN + 6, AT_HIDDEN + 6))
            for ref, target in ((wup, wup_out), (wdown, wdown_out))
        ]
        + [
            (AT_HIDDEN + 2 * r + 2,) + column_stores(ref, target, r)
            for r in range(4)
            for ref, target in ((active, active_out), (grad_pre, grad_pre_out))
        ]
    )
    stores = [
        pltpu.make_async_copy(ref, target, store_sem.at[i])
        for i, (_, ref, target) in enumerate(plan)
    ]
    last_tick = AT_HIDDEN + 8

    def head_product(r):
        base = r * 3 * width
        for n in range(3):
            value = dot(normed[...], wqkv[r, :, n * width : (n + 1) * width])
            if n != 1:
                value = value + bias[r, n // 2 : n // 2 + 1, :]
            qkv[:, pl.ds(pl.multiple_of(base + n * width, width), width)] = value.astype(BF)

    def head_pair(r, p):
        base = r * 3 * width
        lanes = [pl.ds(pl.multiple_of(base + n * width + p * 128, 128), 128) for n in range(3)]
        target = pl.ds(pl.multiple_of(r * width + p * 128, 128), 128)
        for first, size in blocks_of(rows):
            here = pl.ds(first, size)
            same = owner_of_rows(
                first + lax.broadcasted_iota(jnp.int32, (size, 1), 0), lengths, mp
            ) == owner_of_rows(first + lax.broadcasted_iota(jnp.int32, (1, size), 1), lengths, mp)
            q, k, v = [qkv[here, lane] for lane in lanes]
            results = []
            for h in range(2):
                cut = slice(h * HEAD_DIM, (h + 1) * HEAD_DIM)
                low = softmax_rows(q[:, cut], k[:, cut], same).astype(BF)
                results.append(dot(low, v[:, cut]).astype(BF))
            context[here, target] = jnp.concatenate(results, axis=1)

    def attention_output(n):
        columns = block_rows(n, 256)
        value = stream[:, columns] + output_bias[:, columns]
        for r in range(4):
            value = value + dot(context[:, r * width : (r + 1) * width], wo[r, :, columns])
        middle[:, columns] = value

    def second_norm(i):
        here = block_rows(i, 32)
        unit, _ = stats(middle[here, :])
        hidden[here, :] = (unit * hidden_gain[...] + hidden_shift[...]).astype(BF)

    def hidden_tile(r, n):
        columns = block_rows(n, 256)
        target = pl.ds(pl.multiple_of(r * D + n * 256, 256), 256)
        preact = dot(hidden[...], wup[r, :, columns]) + bias[r, pl.ds(2 + n, 1), :]
        value, slope = gelu_parts(preact)
        active[:, target] = value
        grad = dot_cols(grad_mixed[...], wdown[r, columns, :])
        grad_pre[:, target] = (grad * slope).astype(BF)

    actions = {}

    def at(k, action):
        actions.setdefault(k, []).append(action)

    for stage in reversed(range(4)):
        for i in relayed:

            def advance(i=i, stage=stage):
                route[stage](i).wait_recv()
                route[stage + 1](i).start()

            at(ROUTE_TICKS[stage][i], advance)

    def pass_on(i):
        x_copy(i).wait_recv()
        fwd_copy(i).start()

    def sums_stage(target, copies, slots, following):
        def action():
            value = part[target - 1]
            for m, copy in enumerate(copies):
                copy.wait_recv()
                value = value + slots[m]
            if following:
                part[target] = value
                start_all(following)
            else:
                sums[...] = value

        return action

    def received(indices, copies):
        def action():
            for i in indices:
                copies(i)

        return action

    def own(i):
        own_copies[i].wait()

    def paired(i):
        pair_copies[i].wait_recv()

    def forwarded(i):
        fwd_copy(i).wait_recv()

    at(0, sums_stage(1, sums_a, from_mp, sums_b))
    at(1, sums_stage(2, sums_b, from_y, sums_c))
    at(2, sums_stage(3, sums_c, from_z, None))
    at(AT_HEADS, lambda: wait_recv_all(bias_copies))
    at(AT_HEADS, received(HEADS, own))
    at(AT_HEADS + 3, received(HEADS, paired))
    at(AT_QUERY, lambda: pass_on(QUERY))
    at(AT_HEADS + 9, received(HEADS, forwarded))
    at(AT_OUTPUT, received((OUTPUT,), own))
    at(AT_OUTPUT, received((OUTPUT,), paired))
    at(AT_OUTPUT, received((OUTPUT,), forwarded))
    at(AT_PAIRED, received(HIDDEN, own))
    at(AT_PAIRED, received(HIDDEN, paired))
    at(AT_DOWN, lambda: pass_on(DOWN))
    at(AT_HIDDEN + 6, received(HIDDEN, forwarded))
    for copy, (when, _, _) in zip(stores, plan):
        if when < last_tick:
            at(when, copy.start)

    def tick(k, carry):
        for when, todo in sorted(actions.items()):

            @pl.when(k == when)
            def _(todo=todo):
                for action in todo:
                    action()

        @pl.when(k == 0)
        def _():
            position_table()

        @pl.when(k == 1)
        def _():
            place_rows()

        @pl.when((k >= 2) & (k < 4))
        def _():
            norm_rows((k - 2) * 10, 10 - (k - 2))

        step = k - AT_HEADS

        @pl.when((step >= 0) & (step < 12) & (step % 3 == 0))
        def _():
            head_product(step // 3)

        @pl.when((step >= 0) & (step < 12) & (step % 3 > 0))
        def _():
            head_pair(step // 3, step % 3 - 1)

        @pl.when((k >= AT_OUTPUT) & (k < AT_OUTPUT + 2))
        def _():
            def body(n):
                attention_output(2 * (k - AT_OUTPUT) + n)

            loop(2, body)

        @pl.when(k == AT_OUTPUT + 2)
        def _():
            loop(blocks, second_norm)

        @pl.when((k >= AT_HIDDEN) & (k < AT_HIDDEN + 8))
        def _():
            def body(n):
                j = 2 * (k - AT_HIDDEN) + n
                hidden_tile(j // 4, j % 4)

            loop(2, body)

        return carry

    lax.fori_loop(0, last_tick, tick, 0)
    start_all([copy for copy, (when, _, _) in zip(stores, plan) if when >= last_tick])
    for i in everything:
        pair_copies[i].wait_send()
        x_copy(i).wait_send()
        fwd_copy(i).wait_send()
        if not items[i][6]:
            for copy in (far_copy, near_copy, y_copy):
                copy(i).wait_send()
    for copy in bias_copies + halo_copies + sums_a + sums_b + sums_c:
        copy.wait_send()
    for copy in stores:
        copy.wait()


def softmax_rows(q, k, same):
    scores = jnp.where(same, dot_cols(q, k) * (1.0 / math.sqrt(HEAD_DIM)), -1e30)
    weights = jnp.exp(scores - jnp.max(scores, axis=-1, keepdims=True))
    return weights * (1.0 / jnp.sum(weights, axis=-1, keepdims=True))


def forward(smalls, vectors, tokens, cotangent, weights, rows):
    width = weights[0].shape[1]
    shape = jax.ShapeDtypeStruct
    full = shape((rows, D), F32)
    low = shape((rows, D), BF)
    wide = shape((rows, 4 * D), BF)
    outs = (
        low,
        low,
        shape((24, 128), F32),
        full,
        full,
        low,
        shape((rows, 12 * width), BF),
        low,
        low,
        low,
        wide,
        wide,
        shape((4, D, 3 * width), BF),
        shape((4, width, D), BF),
        shape((4, D, D), BF),
        shape((4, D, D), BF),
    )
    scratch = [shape((HALO + tokens.shape[0], D), BF)] * 2 + [
        low,
        low,
        full,
        full,
        low,
        outs[6],
        low,
        low,
        low,
        wide,
        wide,
    ]
    scratch += list(outs[12:]) + [
        shape((24, 128), F32),
        shape((4, 8, width), F32),
        shape((3, 24, 128), F32),
        shape((3, 24, 128), F32),
        shape((1, 24, 128), F32),
        shape((3, 24, 128), F32),
    ]
    dma = pltpu.SemaphoreType.DMA
    any_space = pl.BlockSpec(memory_space=pl.ANY)
    return pl.pallas_call(
        forward_kernel,
        out_shape=outs,
        in_specs=[pl.BlockSpec(memory_space=pltpu.SMEM)] * 4
        + [pl.BlockSpec(memory_space=pltpu.VMEM)] * 8
        + [any_space] * 8,
        out_specs=(any_space,) * len(outs),
        scratch_shapes=[pltpu.VMEM(v.shape, v.dtype) for v in scratch]
        + [
            dma((13,)),
            dma((2, 3)),
            dma((28,)),
            dma((3, 3)),
            dma((3, 3)),
            dma((3,)),
            dma((3,)),
        ]
        + [dma((13,))] * 12,
        compiler_params=pltpu.CompilerParams(
            collective_id=1, has_side_effects=True, vmem_limit_bytes=67043328
        ),
        name="forward",
    )(*smalls, *vectors, tokens, cotangent, *weights)


CHUNK = 128
CHUNKS = 24
STAGE_DELAY = (0, 1, 3, 5, 7, 9, 11)
TICK_HIDDEN, TICK_SECOND, TICK_CONTEXT, TICK_HEADS = 0, 4, 5, 6
TICK_NORMED, TICK_FIRST, TICK_MIXED = 14, 18, 19
TICK_SUMS = (18, 20, 22, 24)
TICK_NEXT, TICK_LAYER, TICK_TOKENS = 25, 27, 28


def backward_kernel(
    lengths,
    groups,
    counts,
    gain,
    hidden_gain,
    down_bias,
    sums,
    tokens_ref,
    cotangent_ref,
    stream_ref,
    middle_ref,
    normed_ref,
    qkv_ref,
    context_ref,
    hidden_ref,
    grad_mixed_ref,
    active_ref,
    grad_pre_ref,
    wqkv_ref,
    wo_ref,
    wup_ref,
    wdown_ref,
    reduced_out,
    finals_out,
    layer_out,
    tokens_grad_out,
    made,
    pair,
    across,
    over_y,
    over_z,
    final,
    act,
    grad_pre,
    hidden,
    grad_mixed,
    context,
    normed,
    grad_attended,
    qkv,
    grad_context,
    rowbuf,
    gradient,
    trunk,
    stream,
    weight,
    packet,
    from_mp,
    from_y,
    from_z,
    layer_next,
    tokens_next,
    load_sem,
    act_sem,
    weight_sem,
    pair_send,
    pair_recv,
    across_send,
    across_recv,
    y_send,
    y_recv,
    z_send,
    z_recv,
    back_z_send,
    back_z_recv,
    back_y_send,
    back_y_recv,
    out_sem,
    stat_send,
    stat_recv,
    next_send,
    next_recv,
):
    mp, y, z, mp_peers, y_peer, z_places, z_peers = places()
    sibling, opposite, _ = mp_peers
    half = CHUNK // 2
    eighth = CHUNK // 8
    rows = normed.shape[0]
    rows_here = layer_out.shape[0]
    width = context.shape[1] // 4
    blocks = rows // 32

    loads = {
        name: pltpu.make_async_copy(source, target, load_sem.at[i])
        for i, (name, source, target) in enumerate(
            (
                ("grad_mixed", grad_mixed_ref, grad_mixed),
                ("grad_pre", grad_pre_ref, grad_pre),
                ("middle", middle_ref, trunk),
                ("cotangent", cotangent_ref, rowbuf),
                ("qkv", qkv_ref, qkv),
                ("hidden", hidden_ref, hidden),
                ("context", context_ref, context),
                ("normed", normed_ref, normed),
                ("stream", stream_ref, stream),
                ("tokens", tokens_ref, rowbuf),
                ("active", active_ref, grad_pre),
                ("middle again", middle_ref, stream),
                ("layer", normed.at[pl.ds(0, rows_here)], layer_out),
                ("tokens_grad", trunk.at[pl.ds(0, rows_here)], tokens_grad_out),
            )
        )
    }

    def act_loads(c):
        return [
            pltpu.make_async_copy(
                active_ref.at[:, pl.ds(pl.multiple_of(r * D + c * CHUNK, CHUNK), CHUNK)],
                act.at[c % 2, r],
                act_sem.at[c % 2, r],
            )
            for r in range(4)
        ]

    def weight_load(s):
        if s < 4:
            source = wup_ref.at[s]
        elif s == 4:
            source = wo_ref
        elif s < 9:
            source = wqkv_ref.at[s - 5]
        else:
            source = wdown_ref.at[s - 9]
        target = weight.at[s % 2, :, pl.ds(0, 3 * width)] if 5 <= s < 9 else weight.at[s % 2]
        return pltpu.make_async_copy(source, target, weight_sem.at[s % 2])

    for c in range(2):
        start_all(act_loads(c))
    loads["grad_mixed"].start()
    weight_load(0).start()
    loads["grad_pre"].start()
    weight_load(1).start()
    for name in ("middle", "cotangent", "qkv", "hidden", "context", "normed", "stream"):
        loads[name].start()
    greet(mp_peers + [y_peer] + z_peers)

    weights = [counts[groups[4 * mp + j]].astype(F32) for j in range(4)]
    slices = lax.axis_size("dp")
    count_valid = slices * PAIRS * PAIR_LEN
    column_mean = joined(sums, 0) / count_valid
    spread = joined(sums, 8) / count_valid - column_mean * column_mean
    inverse = lax.rsqrt(spread + 1e-05)
    mean_weight = sums[16:17, 0:1] / (slices * 16)

    def pair_copy(c):
        return remote(
            made.at[c % 2, pl.ds(0, 2)], pair.at[c], pair_send.at[c], pair_recv.at[c], sibling
        )

    def across_copy(c):
        return remote(
            pair.at[c, 1], across.at[c], across_send.at[c], across_recv.at[c], opposite
        )

    def y_copy(c):
        return remote(
            across.at[c, pl.ds(pl.multiple_of((1 - y) * half, half), half)],
            over_y.at[c],
            y_send.at[c],
            y_recv.at[c],
            y_peer,
        )

    def z_copies(c):
        return [
            remote(
                over_y.at[c, pl.ds(pl.multiple_of(place * eighth, eighth), eighth)],
                over_z.at[c, m],
                z_send.at[c, m],
                z_recv.at[c, m],
                peer,
            )
            for m, (place, peer) in enumerate(zip(z_places, z_peers))
        ]

    def back_z_copies(c):
        view = final.at[c, pl.ds(pl.multiple_of(y * half + z * eighth, eighth), eighth)]
        return [
            remote(view, view, back_z_send.at[c, m], back_z_recv.at[c, m], peer)
            for m, peer in enumerate(z_peers)
        ]

    def back_y_copy(c):
        view = final.at[c, pl.ds(pl.multiple_of(y * half, half), half)]
        return remote(view, view, back_y_send.at[c], back_y_recv.at[c], y_peer)

    def out_copy(c):
        return pltpu.make_async_copy(final.at[c], reduced_out.at[c], out_sem.at[c])

    def make(c):
        @pl.when(c < 8)
        def _():
            for copy in act_loads(c):
                copy.wait()

        def one(j):
            r = 2 * j + 1 - 5 * (j // 2)

            def store(left, right):
                made[c % 2, j] = dot_rows(left, right).astype(BF)

            @pl.when(c < 8)
            def _():
                store(act[c % 2, r], grad_mixed[...])

            @pl.when((c >= 8) & (c < 16))
            def _():
                store(
                    hidden[:, block_rows(c - 8, CHUNK)], grad_pre[:, block_rows(r, D)]
                )

            @pl.when((c >= 16) & (c < 18))
            def _():
                store(context[:, block_rows(2 * r + c - 16, CHUNK)], grad_attended[...])

            @pl.when(c >= 18)
            def _():
                store(qkv[:, block_rows(6 * r + c - 18, CHUNK)], normed[...])

        loop(4, one)

        @pl.when(c < 6)
        def _():
            start_all(act_loads(c + 2))

    def add_pair(c):
        pair_copy(c).wait()

        def body(i):
            here = block_rows(i, 32)
            for which in (1, 0):
                pair[c, which, here, :] = (
                    pair[c, which, here, :].astype(F32)
                    + made[c % 2, 2 + which, here, :].astype(F32)
                ).astype(BF)

        loop(CHUNK // 32, body)

    def add_across(c):
        across_copy(c).wait_recv()

        def body(i):
            here = block_rows(i, 32)
            across[c, here, :] = (
                across[c, here, :].astype(F32) + pair[c, 0, here, :].astype(F32)
            ).astype(BF)

        loop(CHUNK // 32, body)

    def add_y(c):
        y_copy(c).wait_recv()

        def body(i):
            here = block_rows(i, 32)
            own = pl.ds(pl.multiple_of(y * half + i * 32, 32), 32)
            over_y[c, here, :] = (
                over_y[c, here, :].astype(F32) + across[c, own, :].astype(F32)
            ).astype(BF)

        loop(half // 32, body)

    def add_z(c):
        wait_recv_all(z_copies(c))
        value = over_y[c, block_rows(z, eighth), :].astype(F32)
        for m in range(3):
            value = value + over_z[c, m].astype(F32)
        final[c, pl.ds(pl.multiple_of(y * half + z * eighth, eighth), eighth), :] = value.astype(BF)

    handle = (
        make,
        add_pair,
        add_across,
        add_y,
        add_z,
        lambda c: wait_recv_all(back_z_copies(c)),
        lambda c: back_y_copy(c).wait_recv(),
    )
    send = (
        lambda c: [pair_copy(c)],
        lambda c: [across_copy(c)],
        lambda c: [y_copy(c)],
        z_copies,
        back_z_copies,
        lambda c: [back_y_copy(c)],
        lambda c: [out_copy(c)],
    )

    def hidden_step(r):
        left = block_rows(r, D)

        def tile(n):
            columns = block_rows(n, 256)
            value = dot_cols(grad_pre[:, left], weight[r % 2, columns, :])

            @pl.when(r == 0)
            def _():
                gradient[:, columns] = value

            @pl.when(r > 0)
            def _():
                gradient[:, columns] = gradient[:, columns] + value

        loop(4, tile)

    def fold(value):
        return jnp.sum(value.reshape(4, 8, D), axis=0)

    def put(index, value):
        for j in range(8):
            packet[0, 8 * index + j : 8 * index + j + 1, :] = value[:, j * 128 : (j + 1) * 128]

    def put_all(first, values):
        for i, value in enumerate(values):
            put(first + i, jnp.sum(value, axis=0, keepdims=True))

    def ones_dot(value):
        return dot(jnp.ones((16, rows), BF), value)[0:1, :]

    def row_weight_of(i):
        row = i * 32 + lax.broadcasted_iota(jnp.int32, (32, 1), 0)
        item, _, in_pair, _ = item_of_rows(row, lengths, mp)
        return jnp.where(in_pair, choose_item(item, weights), 0.0) / mean_weight, in_pair

    zero = jnp.zeros((8, D), F32)

    def second_norm_back():
        def body(i, carry):
            here = block_rows(i, 32)
            unit, scale = stats(trunk[here, :])
            grad = gradient[here, :]
            row_weight, _ = row_weight_of(i)
            value = rowbuf[here, :].astype(F32) * row_weight + norm_back(
                grad, unit, scale, hidden_gain[...]
            )
            trunk[here, :] = value
            low = value.astype(BF)
            grad_attended[here, :] = low
            return (
                carry[0] + fold(grad * unit),
                carry[1] + fold(grad),
                carry[2] + fold(low.astype(F32)),
            )

        put_all(4, lax.fori_loop(0, blocks, body, (zero, zero, zero)))
        put(7, ones_dot(grad_mixed[...]))

    def context_step():
        def tile(n):
            columns = block_rows(n, 256)
            grad_context[:, columns] = dot_cols(grad_attended[...], weight[0, columns, :]).astype(BF)

        loop(4, tile)

    def head_pair_back(index):
        r = index // 2
        p = index % 2
        lanes = [block_rows(6 * r + 2 * n + p, 128) for n in range(3)]
        source = block_rows(2 * r + p, 128)
        factor = 1.0 / math.sqrt(HEAD_DIM)
        for first, size in blocks_of(rows):
            here = pl.ds(first, size)
            same = owner_of_rows(
                first + lax.broadcasted_iota(jnp.int32, (size, 1), 0), lengths, mp
            ) == owner_of_rows(first + lax.broadcasted_iota(jnp.int32, (1, size), 1), lengths, mp)
            q, k, v = [qkv[here, lane] for lane in lanes]
            g = grad_context[here, source]
            results = []
            for h in range(2):
                cut = slice(h * HEAD_DIM, (h + 1) * HEAD_DIM)
                soft = softmax_rows(q[:, cut], k[:, cut], same)
                grad_soft = dot_cols(g[:, cut], v[:, cut])
                center = jnp.sum(soft * grad_soft, axis=-1, keepdims=True)
                grad_scores = (soft * (grad_soft - center)).astype(BF)
                results.append(
                    (
                        (dot(grad_scores, k[:, cut]) * factor).astype(BF),
                        (dot_rows(grad_scores, q[:, cut]) * factor).astype(BF),
                        dot_rows(soft.astype(BF), g[:, cut]).astype(BF),
                    )
                )
            for n in range(3):
                qkv[here, lanes[n]] = jnp.concatenate([results[0][n], results[1][n]], axis=1)

    def normed_step(r):
        left = qkv[:, block_rows(r, 3 * width)]

        def tile(n):
            columns = block_rows(n, 256)
            value = dot_cols(left, weight[(r + 1) % 2, columns, 0 : 3 * width])

            @pl.when(r == 0)
            def _():
                gradient[:, columns] = value

            @pl.when(r > 0)
            def _():
                gradient[:, columns] = gradient[:, columns] + value

        loop(4, tile)

    def first_norm_back():
        def body(i, carry):
            here = block_rows(i, 32)
            unit, scale = stats(stream[here, :])
            grad = gradient[here, :]
            value = trunk[here, :] + norm_back(grad, unit, scale, gain[...])
            standard = (rowbuf[here, :].astype(F32) - column_mean) * inverse
            gradient[here, :] = value
            return (
                carry[0] + fold(value),
                carry[1] + fold(value * standard),
                carry[2] + fold(grad * unit),
                carry[3] + fold(grad),
            )

        put_all(0, lax.fori_loop(0, blocks, body, (zero, zero, zero, zero)))
        for r in range(4):
            if r:
                packet[r, 0:64, :] = packet[0, 0:64, :]
            parts = [
                ones_dot(qkv[:, (3 * r + n) * width : (3 * r + n + 1) * width]) for n in (0, 2)
            ] + [
                ones_dot(grad_pre[:, r * D + n * width : r * D + (n + 1) * width]) for n in range(4)
            ]
            for i, value in enumerate(parts):
                for j in range(2):
                    packet[r, 64 + 2 * i + j : 65 + 2 * i + j, :] = value[
                        :, j * 128 : (j + 1) * 128
                    ]
            packet[r, 76:80, :] = jnp.zeros((4, 128), F32)

    def mixed_step(r):
        left = grad_pre[:, block_rows(r, D)]

        def tile(n):
            columns = block_rows(n, 256)
            stream[:, columns] = stream[:, columns] + dot(left, weight[(r + 1) % 2, :, columns])

        loop(4, tile)

    def layer_step():
        def body(i):
            here = block_rows(i, 32)
            hidden[here, :] = (stream[here, :] + down_bias[...]).astype(BF)

        loop(blocks, body)

    def exchange(stage, sources, peers, slots):
        return [
            remote(
                source, slots.at[m], stat_send.at[stage, m], stat_recv.at[stage, m], peer
            )
            for m, (source, peer) in enumerate(zip(sources, peers))
        ]

    sums_a = exchange(0, [packet.at[r] for r in (1, 2, 3)], mp_peers, from_mp)
    sums_b = exchange(1, [packet.at[4]], [y_peer], from_y)
    sums_c = exchange(2, [packet.at[5]] * 3, z_peers, from_z)

    def gather_sums(first, copies, slots, target):
        value = packet[first]
        for m, copy in enumerate(copies):
            copy.wait_recv()
            value = value + slots[m]
        packet[target] = value

    def tokens_step():
        total = joined(packet[6], 0), joined(packet[6], 8)

        def body(i):
            here = block_rows(i, 32)
            standard = (rowbuf[here, :].astype(F32) - column_mean) * inverse
            _, in_pair = row_weight_of(i)
            share = jnp.where(in_pair, 1.0 / count_valid, 0.0)
            gradient[here, :] = inverse * (
                gradient[here, :] - share * (total[0] + total[1] * standard)
            )

        loop(blocks, body)

    before = {"mp": (mp + 3) % 4}
    layer_next_copy = remote(
        hidden.at[pl.ds(0, HALO)], layer_next, next_send.at[0], next_recv.at[0], before
    )
    tokens_next_copy = remote(
        gradient.at[pl.ds(0, HALO)], tokens_next, next_send.at[1], next_recv.at[1], before
    )

    def choose_rows(count, first):
        row = lax.broadcasted_iota(jnp.int32, (rows_here, count), 0)
        column = lax.broadcasted_iota(jnp.int32, (rows_here, count), 1) + first
        place = row + (rows_here - 2 * PAIR_LEN) * mp
        after = jnp.where(mp == 3, 2 * WINDOW, rows) - 2 * PAIR_LEN
        wanted = jnp.where(
            place < PAIR_LEN,
            place,
            jnp.where(place < 2 * PAIR_LEN, place + (WINDOW - PAIR_LEN), place + after),
        )
        return jnp.where(column == wanted, 1.0, 0.0).astype(BF)

    def own_rows(value, following, target):
        chosen, chosen_next = choose_rows(rows, 0), choose_rows(HALO, rows)
        pairs = ((chosen, value), (chosen_next, following))

        def tile(n):
            columns = block_rows(n, 256)
            total = jnp.zeros((rows_here, 256), F32)
            for matrix, ref in pairs:
                block = ref[:, columns]
                high = block.astype(BF)
                total = total + dot(matrix, high)
                if ref.dtype == F32:
                    middle_part = block - high.astype(F32)
                    low = middle_part.astype(BF)
                    total = total + dot(matrix, low)
                    total = total + dot(matrix, (middle_part - low.astype(F32)).astype(BF))
            target[0:rows_here, columns] = total.astype(target.dtype)

        loop(4, tile)

    def work(k):
        for s in range(4):

            @pl.when(k == TICK_HIDDEN + s)
            def _(s=s):
                if s == 0:
                    loads["grad_pre"].wait()
                weight_load(s).wait()

        @pl.when((k >= TICK_HIDDEN) & (k < TICK_HIDDEN + 4))
        def _():
            hidden_step(k - TICK_HIDDEN)

        for s in range(4):

            @pl.when(k == TICK_HIDDEN + s)
            def _(s=s):
                weight_load(s + 2).start()

        @pl.when(k == TICK_SECOND)
        def _():
            loads["middle"].wait()
            loads["cotangent"].wait()
            second_norm_back()
            loads["tokens"].start()

        @pl.when(k == TICK_CONTEXT)
        def _():
            weight_load(4).wait()
            context_step()
            weight_load(6).start()
            loads["qkv"].wait()

        @pl.when((k >= TICK_HEADS) & (k < TICK_HEADS + 8))
        def _():
            head_pair_back(k - TICK_HEADS)

        for s in range(4):

            @pl.when(k == TICK_NORMED + s)
            def _(s=s):
                weight_load(5 + s).wait()

        @pl.when((k >= TICK_NORMED) & (k < TICK_NORMED + 4))
        def _():
            normed_step(k - TICK_NORMED)

        for s in range(4):

            @pl.when(k == TICK_NORMED + s)
            def _(s=s):
                weight_load(7 + s).start()

        @pl.when(k == TICK_FIRST)
        def _():
            loads["stream"].wait()
            loads["tokens"].wait()
            first_norm_back()
            loads["active"].start()
            loads["middle again"].start()
            start_all(sums_a)

        for s in range(4):

            @pl.when(k == TICK_MIXED + s)
            def _(s=s):
                if s == 0:
                    loads["active"].wait()
                    loads["middle again"].wait()
                weight_load(9 + s).wait()

        @pl.when((k >= TICK_MIXED) & (k < TICK_MIXED + 4))
        def _():
            mixed_step(k - TICK_MIXED)

        for s in range(2):

            @pl.when(k == TICK_MIXED + s)
            def _(s=s):
                weight_load(11 + s).start()

        @pl.when(k == TICK_MIXED + 3)
        def _():
            layer_step()

        @pl.when(k == TICK_NEXT)
        def _():
            layer_next_copy.start()
            tokens_next_copy.start()

        @pl.when(k == TICK_LAYER)
        def _():
            layer_next_copy.wait_recv()
            own_rows(hidden, layer_next, normed)
            loads["layer"].start()

        @pl.when(k == TICK_TOKENS)
        def _():
            tokens_next_copy.wait_recv()
            own_rows(gradient, tokens_next, trunk)
            loads["tokens_grad"].start()

        @pl.when(k == TICK_SUMS[1])
        def _():
            gather_sums(0, sums_a, from_mp, 4)
            start_all(sums_b)

        @pl.when(k == TICK_SUMS[2])
        def _():
            gather_sums(4, sums_b, from_y, 5)
            start_all(sums_c)

        @pl.when(k == TICK_SUMS[3])
        def _():
            gather_sums(5, sums_c, from_z, 6)
            finals_out[...] = packet[6]
            tokens_step()

    waits = {0: ("grad_mixed",), 8: ("hidden",), 16: ("context",), 18: ("normed",)}

    def tick(k, carry):
        for when, names in waits.items():

            @pl.when(k == when)
            def _(names=names):
                for name in names:
                    loads[name].wait()

        def staged(stage, actions):
            c = k - STAGE_DELAY[stage]

            @pl.when((c >= 0) & (c < CHUNKS))
            def _():
                actions[stage](c)

        sends = tuple(lambda c, f=f: start_all(f(c)) for f in send)
        for stage in (6, 5, 4, 3, 2):
            staged(stage, handle)
        for stage in (2, 3, 4, 5, 6):
            staged(stage, sends)
        staged(0, handle)
        staged(1, handle)
        staged(0, sends)
        staged(1, sends)
        work(k)
        return carry

    lax.fori_loop(0, CHUNKS + STAGE_DELAY[-1], tick, 0)

    def finish(c):
        across_copy(c).wait_send()
        y_copy(c).wait_send()
        for copy in z_copies(c) + back_z_copies(c):
            copy.wait_send()
        back_y_copy(c).wait_send()
        out_copy(c).wait()

    loop(CHUNKS, finish)
    for copy in sums_a + sums_b + sums_c:
        copy.wait_send()
    layer_next_copy.wait_send()
    tokens_next_copy.wait_send()
    loads["layer"].wait()
    loads["tokens_grad"].wait()


def backward(smalls, vectors, sums, saved, rows_here):
    (
        tokens,
        cotangent,
        stream,
        middle,
        normed,
        qkv,
        context,
        hidden,
        grad_mixed,
        active,
        grad_pre,
        wqkv,
        wo,
        wup,
        wdown,
    ) = saved
    rows = normed.shape[0]
    shape = jax.ShapeDtypeStruct
    low = shape((rows, D), BF)
    full = shape((rows, D), F32)
    packed = shape((80, 128), F32)
    scratch = [
        shape((2, 4, CHUNK, D), BF),
        shape((CHUNKS, 2, CHUNK, D), BF),
        shape((CHUNKS, CHUNK, D), BF),
        shape((CHUNKS, CHUNK // 2, D), BF),
        shape((CHUNKS, 3, CHUNK // 8, D), BF),
        shape((CHUNKS, CHUNK, D), BF),
        shape((2, 4, rows, CHUNK), BF),
        shape(grad_pre.shape, BF),
        low,
        low,
        low,
        low,
        low,
        shape(qkv.shape, BF),
        low,
        low,
        full,
        full,
        full,
        shape((2, D, D), BF),
        shape((7, 80, 128), F32),
        shape((3, 80, 128), F32),
        shape((1, 80, 128), F32),
        shape((3, 80, 128), F32),
        shape((HALO, D), BF),
        shape((HALO, D), F32),
    ]
    dma = pltpu.SemaphoreType.DMA
    any_space = pl.BlockSpec(memory_space=pl.ANY)
    vmem = pl.BlockSpec(memory_space=pltpu.VMEM)
    return pl.pallas_call(
        backward_kernel,
        out_shape=(
            shape((CHUNKS, CHUNK, D), BF),
            packed,
            shape((rows_here, D), BF),
            shape((rows_here, D), F32),
        ),
        in_specs=[pl.BlockSpec(memory_space=pltpu.SMEM)] * 3 + [vmem] * 4 + [any_space] * 15,
        out_specs=(any_space, vmem, any_space, any_space),
        scratch_shapes=[pltpu.VMEM(v.shape, v.dtype) for v in scratch]
        + [
            dma((14,)),
            dma((2, 4)),
            dma((2,)),
            dma((CHUNKS,)),
            dma((CHUNKS,)),
            dma((CHUNKS,)),
            dma((CHUNKS,)),
            dma((CHUNKS,)),
            dma((CHUNKS,)),
            dma((CHUNKS, 3)),
            dma((CHUNKS, 3)),
            dma((CHUNKS, 3)),
            dma((CHUNKS, 3)),
            dma((CHUNKS,)),
            dma((CHUNKS,)),
            dma((CHUNKS,)),
            dma((3, 3)),
            dma((3, 3)),
            dma((2,)),
            dma((2,)),
        ],
        compiler_params=pltpu.CompilerParams(
            collective_id=2, has_side_effects=True, vmem_limit_bytes=67043328
        ),
        name="backward",
    )(
        *smalls,
        *vectors,
        sums,
        tokens,
        cotangent,
        stream,
        middle,
        normed,
        qkv,
        context,
        hidden,
        grad_mixed,
        active,
        grad_pre,
        wqkv,
        wo.reshape(D, D),
        wup,
        wdown,
    )


def finish_kernel(
    down_ref,
    up_ref,
    output_ref,
    query_ref,
    key_ref,
    value_ref,
    finals_ref,
    layer_ref,
    tokens_ref,
    down,
    up,
    output,
    query,
    key,
    value,
    layer,
    tokens,
    *vectors,
):
    down[...] = down_ref[0].astype(F32)
    up[...] = up_ref[0].astype(F32)
    output[...] = output_ref[0].astype(F32)
    for source, target in ((query_ref, query), (key_ref, key), (value_ref, value)):
        for half in range(2):
            target[:, half * CHUNK : (half + 1) * CHUNK] = source[half].astype(F32).T
    layer[...] = layer_ref[...]
    tokens[...] = tokens_ref[...]

    @pl.when(pl.program_id(0) == 0)
    def _():
        first = 0
        for target in vectors:
            size = target.shape[0]
            target[...] = finals_ref[first : first + size, :]
            first += size


def finish(reduced, finals, layer, tokens, width):
    shape = jax.ShapeDtypeStruct
    rows_here = layer.shape[0]
    share = rows_here // 8
    sizes = (8,) * 8 + (2, 2, 8)
    own = [pl.BlockSpec((share, D), lambda c: (c, 0))] * 2
    specs = (
        [
            pl.BlockSpec((CHUNK, D), lambda c: (c, 0)),
            pl.BlockSpec((CHUNK, D), lambda c: (c, 0)),
            pl.BlockSpec((width // 8, D), lambda c: (c, 0)),
        ]
        + [pl.BlockSpec((CHUNK, width), lambda c: (c, 0))] * 3
        + own
    )
    shapes = [
        shape((D, D), F32),
        shape((D, D), F32),
        shape((width, D), F32),
        shape((D, width), F32),
        shape((D, width), F32),
        shape((D, width), F32),
        shape((rows_here, D), BF),
        shape((rows_here, D), F32),
    ]
    return pl.pallas_call(
        finish_kernel,
        grid=(8,),
        in_specs=[
            pl.BlockSpec((1, CHUNK, D), lambda c: (c, 0, 0)),
            pl.BlockSpec((1, CHUNK, D), lambda c: (8 + c, 0, 0)),
            pl.BlockSpec((1, width // 8, D), lambda c: (16 + c // 4, c % 4, 0)),
        ]
        + [
            pl.BlockSpec((2, CHUNK, CHUNK), lambda c, first=first: (first, 0, c))
            for first in (9, 10, 11)
        ]
        + [pl.BlockSpec(finals.shape, lambda c: (0, 0))]
        + own,
        out_specs=specs + [pl.BlockSpec((size, 128), lambda c: (0, 0)) for size in sizes],
        out_shape=shapes + [shape((size, 128), F32) for size in sizes],
        name="finish",
    )(*[reduced] * 6, finals, layer, tokens)


def general_shards(
    tokens,
    cotangent,
    item_lengths,
    item_group,
    group_count,
    grid_scale,
    norm_gain,
    norm_shift,
    query_weight,
    query_bias,
    key_weight,
    value_weight,
    value_bias,
    output_weight,
    output_bias,
    hidden_gain,
    hidden_shift,
    up_weight,
    up_bias,
    down_weight,
    down_bias,
):
    shard_count = lax.axis_size("mp")
    slice_count = lax.axis_size("dp")
    mp = lax.axis_index("mp")
    rows_here = tokens.shape[0]
    item_count = item_lengths.shape[0]
    pairs_here = PAIRS // shard_count
    own_rows = pairs_here * PAIR_LEN
    shift = rows_here - own_rows
    halo = shift * (shard_count - 1)
    padding = rows_here * shard_count - PAIRS * PAIR_LEN
    tail_block = -(-padding // 32) * 32
    rows = pairs_here * WINDOW + tail_block
    is_last = mp == shard_count - 1

    width = query_weight.shape[1]
    qkv_own = jnp.concatenate([query_weight, key_weight, value_weight], axis=1)
    bias_own = jnp.concatenate([query_bias, value_bias, up_bias])[None, :]
    bias_across = swap_mp(bias_own, 2)
    bias_pair = swap_mp(jnp.concatenate([bias_own, bias_across], axis=0), 1)
    biases = [bias_own[0], bias_pair[0], bias_across[0], bias_pair[1]]

    def gather(own, direct):
        across = swap_mp(own, 2) if direct else fetch_across(own)
        return [own, swap_mp(own, 1), across, swap_mp(across, 1)]

    tokens_f = tokens.astype(F32)
    slice_row = mp * rows_here + jnp.arange(rows_here, dtype=jnp.int32)
    weighted = tokens_f * (slice_row < PAIRS * PAIR_LEN).astype(F32)[:, None]
    chosen = item_group[:, None] == jnp.arange(group_count.shape[0], dtype=jnp.int32)[None, :]
    item_scale = jnp.sum(jnp.where(chosen, grid_scale[None, :], 0.0), axis=1)
    item_weight = jnp.sum(jnp.where(chosen, group_count[None, :], 0), axis=1).astype(F32)
    sums = all_sum(
        jnp.stack(
            [
                jnp.sum(weighted, axis=0),
                jnp.sum(weighted * tokens_f, axis=0),
                jnp.broadcast_to(jnp.sum(item_weight) / shard_count, (D,)),
            ]
        )
    )

    def windows(v):
        before = lax.ppermute(
            v[rows_here - halo :], "mp", [(i, i + 1) for i in range(shard_count - 1)]
        )
        joined = jnp.concatenate([before, v], axis=0)
        start = halo - shift * mp
        parts = []
        for pair in range(pairs_here):
            parts.append(
                lax.dynamic_slice_in_dim(joined, start + pair * PAIR_LEN, PAIR_LEN, axis=0)
            )
            parts.append(jnp.zeros((WINDOW - PAIR_LEN, D), v.dtype))
        parts.append(jnp.where(is_last, v[rows_here - padding :], jnp.zeros((), v.dtype)))
        parts.append(jnp.zeros((tail_block - padding, D), v.dtype))
        return jnp.concatenate(parts, axis=0)

    def unwindows(v):
        own = jnp.concatenate(
            [v[pair * WINDOW : pair * WINDOW + PAIR_LEN] for pair in range(pairs_here)], axis=0
        )
        after = lax.ppermute(own[:halo], "mp", [(i + 1, i) for i in range(shard_count - 1)])
        after = jnp.concatenate([after, jnp.zeros((padding - halo, D), v.dtype)], axis=0)
        tail = v[pairs_here * WINDOW : pairs_here * WINDOW + padding]
        joined = jnp.concatenate([own, jnp.where(is_last, tail, after)], axis=0)
        return lax.dynamic_slice_in_dim(joined, shift * mp, rows_here, axis=0)

    tokens_w = windows(tokens).astype(F32)
    cotangent_w = windows(cotangent).astype(F32)

    row = jnp.arange(rows, dtype=jnp.int32)
    window = row // WINDOW
    offset = row % WINDOW
    in_pair = (window < pairs_here) & (offset < PAIR_LEN)
    is_padding = (window == pairs_here) & (offset < padding) & is_last
    pair = pairs_here * mp + window
    item_ids = jnp.arange(item_count, dtype=jnp.int32)
    first_len = jnp.sum(
        jnp.where(item_ids[None, :] == (2 * pair)[:, None], item_lengths[None, :], 0), axis=1
    )
    second = (offset >= first_len).astype(jnp.int32)
    owner = jnp.where(in_pair, 2 * pair + second, jnp.where(is_padding, item_count, -1))
    position = offset - second * first_len
    member = owner[:, None] == item_ids[None, :]
    row_scale = jnp.sum(jnp.where(member, item_scale[None, :], 0.0), axis=1)
    row_count = jnp.sum(jnp.where(member, item_weight[None, :], 0.0), axis=1)
    valid = in_pair.astype(F32)[:, None]
    quarter = D // 4
    frequency = jnp.exp(-math.log(10000.0) * jnp.arange(quarter, dtype=F32) / quarter)
    across_angle = ((position // SIDE).astype(F32) * row_scale)[:, None] * frequency
    side_angle = ((position % SIDE).astype(F32) * row_scale)[:, None] * frequency
    grid_table = (
        jnp.concatenate(
            [
                jnp.sin(across_angle),
                jnp.cos(across_angle),
                jnp.sin(side_angle),
                jnp.cos(side_angle),
            ],
            axis=-1,
        )
        * valid
    )
    owner_col = owner[:, None]
    owner_row = owner[None, :]

    qkv_weights = jnp.concatenate(gather(qkv_own, True), axis=1)
    output_weights = jnp.concatenate(gather(output_weight, False), axis=0)
    up_weights = jnp.concatenate(gather(up_weight, False), axis=1)
    down_weights = jnp.concatenate(gather(down_weight, False), axis=0)
    hidden_width = up_weight.shape[1]
    no_bias = jnp.zeros((width,), F32)
    qkv_bias = jnp.concatenate(
        [v for b in biases for v in (b[:width], no_bias, b[width : 2 * width])]
    )
    up_biases = jnp.concatenate([b[2 * width :] for b in biases])

    count_valid = slice_count * PAIRS * PAIR_LEN
    column_mean = sums[0] / count_valid
    spread = sums[1] / count_valid - column_mean * column_mean
    inverse = lax.rsqrt(spread + 1e-05)
    row_weight = row_count / (sums[2, 0] / (slice_count * item_count))
    standard = (tokens_w - column_mean) * inverse
    stream = standard + grid_table
    unit, unit_inverse = stats(stream)
    normed = (unit * norm_gain + norm_shift).astype(BF)

    qkv = (dot(normed, qkv_weights) + qkv_bias).astype(BF)
    context = attend(qkv, owner_col, owner_row, shard_count)
    middle = stream + (dot(context, output_weights) + output_bias)
    middle_unit, middle_inverse = stats(middle)
    hidden_in = (middle_unit * hidden_gain + hidden_shift).astype(BF)

    grad_out = cotangent_w * row_weight[:, None]
    grad_mixed = grad_out.astype(BF)
    active, slope = gelu_parts(dot(hidden_in, up_weights) + up_biases)
    mixed = dot(active, down_weights) + down_bias
    grad_pre = (dot_cols(grad_mixed, down_weights) * slope).astype(BF)
    grad_hidden = dot_cols(grad_pre, up_weights)
    layer_output = unwindows((middle + mixed).astype(BF))
    grad_middle = grad_out + norm_back(grad_hidden, middle_unit, middle_inverse, hidden_gain)
    grad_attended = grad_middle.astype(BF)

    grad_context = dot_cols(grad_attended, output_weights).astype(BF)
    grad_qkv = attend_back(qkv, grad_context, owner_col, owner_row, shard_count)
    grad_normed = dot_cols(grad_qkv, qkv_weights)

    pieces = range(shard_count)
    def columns(v, r, size):
        return v[:, r * size : (r + 1) * size]

    def reduced(left, right):
        return reduce_pieces([dot_rows(left(r), right(r)).astype(BF) for r in pieces])

    down_weight_grad = reduced(
        lambda r: columns(active, r, hidden_width), lambda r: grad_mixed
    )
    up_weight_grad = reduced(
        lambda r: hidden_in, lambda r: columns(grad_pre, r, hidden_width)
    )
    output_weight_grad = reduced(
        lambda r: columns(context, r, width), lambda r: grad_attended
    )
    qkv_weight_grad = reduced(lambda r: normed, lambda r: columns(grad_qkv, r, 3 * width))
    qkv_weight_grads = [columns(qkv_weight_grad, i, width) for i in range(3)]
    grad_stream = grad_middle + norm_back(grad_normed, unit, unit_inverse, norm_gain)

    def column_sums(v):
        return jnp.sum(v.astype(F32), axis=0)

    qkv_sums = column_sums(grad_qkv)
    up_sums = column_sums(grad_pre)
    bias_grads = [
        jnp.concatenate(
            [
                qkv_sums[3 * r * width : (3 * r + 1) * width],
                qkv_sums[(3 * r + 2) * width : 3 * (r + 1) * width],
                up_sums[r * hidden_width : (r + 1) * hidden_width],
            ]
        )[None, :]
        for r in pieces
    ]
    got = swap_mp(jnp.concatenate([bias_grads[1], bias_grads[3]], axis=0), 1)
    bias_grad = bias_grads[0] + got[:1] + swap_mp(bias_grads[2] + got[1:], 2)
    for bit in range(dp_bits()):
        bias_grad = bias_grad + swap_dp(bias_grad, 1 << bit)
    bias_grad = bias_grad[0]
    finals = all_sum(
        jnp.stack(
            [
                column_sums(grad_stream),
                column_sums(grad_stream * standard),
                column_sums(grad_normed * unit),
                column_sums(grad_normed),
                column_sums(grad_hidden * middle_unit),
                column_sums(grad_hidden),
                column_sums(grad_attended),
                column_sums(grad_mixed),
            ]
        )
    )
    tokens_grad = unwindows(
        inverse * (grad_stream - valid / count_valid * (finals[0] + finals[1] * standard))
    )
    return (
        layer_output,
        tokens_grad,
        finals[2],
        finals[3],
        qkv_weight_grads[0],
        bias_grad[:width],
        qkv_weight_grads[1],
        qkv_weight_grads[2],
        bias_grad[width : 2 * width],
        output_weight_grad,
        finals[6],
        finals[4],
        finals[5],
        up_weight_grad,
        bias_grad[2 * width :],
        down_weight_grad,
        finals[7],
    )


def fast_shards(
    tokens,
    cotangent,
    item_lengths,
    item_group,
    group_count,
    grid_scale,
    norm_gain,
    norm_shift,
    query_weight,
    query_bias,
    key_weight,
    value_weight,
    value_bias,
    output_weight,
    output_bias,
    hidden_gain,
    hidden_shift,
    up_weight,
    up_bias,
    down_weight,
    down_bias,
):
    rows = 2 * WINDOW + 96
    saved = forward(
        (item_lengths, item_group, group_count, grid_scale),
        [
            v[None, :]
            for v in (
                norm_gain,
                norm_shift,
                output_bias,
                hidden_gain,
                hidden_shift,
                query_bias,
                value_bias,
                up_bias,
            )
        ],
        tokens,
        cotangent,
        (query_weight, key_weight, value_weight, output_weight, up_weight, down_weight),
        rows,
    )
    reduced, finals, layer_output, tokens_grad = backward(
        (item_lengths, item_group, group_count),
        [v[None, :] for v in (norm_gain, hidden_gain, down_bias)],
        saved[2],
        saved[:2] + saved[3:],
        tokens.shape[0],
    )
    (
        down_weight_grad,
        up_weight_grad,
        output_weight_grad,
        query_weight_grad,
        key_weight_grad,
        value_weight_grad,
        layer_output,
        tokens_grad,
        *vectors,
    ) = finish(reduced, finals, layer_output, tokens_grad, query_weight.shape[1])
    vectors = [v.reshape(-1) for v in vectors]
    return (
        layer_output,
        tokens_grad,
        vectors[2],
        vectors[3],
        query_weight_grad,
        vectors[8],
        key_weight_grad,
        value_weight_grad,
        vectors[9],
        output_weight_grad,
        vectors[6],
        vectors[4],
        vectors[5],
        up_weight_grad,
        vectors[10],
        down_weight_grad,
        vectors[7],
    )


def shards(*args):
    if lax.axis_size("dp") == 8 and lax.axis_size("mp") == 4 and args[0].shape == (512, D):
        return fast_shards(*args)
    return general_shards(*args)


def solution(mesh):
    rows = P(("dp", "mp"), None)
    columns = P(None, "mp")
    return jax.shard_map(
        shards,
        mesh=mesh,
        in_specs=(
            rows,
            rows,
            P("dp"),
            P("dp"),
            P(),
            P(),
            P(),
            P(),
            columns,
            P("mp"),
            columns,
            columns,
            P("mp"),
            P("mp", None),
            P(),
            P(),
            P(),
            columns,
            P("mp"),
            P("mp", None),
            P(),
        ),
        out_specs=(
            rows,
            rows,
            P(),
            P(),
            columns,
            P("mp"),
            columns,
            columns,
            P("mp"),
            P("mp", None),
            P(),
            P(),
            P(),
            columns,
            P("mp"),
            P("mp", None),
            P(),
        ),
        check_vma=False,
    )
```

```python
import functools
import math

import jax
import jax.numpy as jnp
from jax import lax
from jax.experimental import pallas as pl
from jax.experimental.pallas import tpu as pltpu
from jax.sharding import PartitionSpec as P

D = 1024
HEAD_DIM = 64
SIDE = 14
PAIRS = 8
PAIR_LEN = 245
WINDOW = 256
BF = jnp.bfloat16
F32 = jnp.float32
PADDING = 88


def dot(a, b):
    return lax.dot_general(a, b, (((1,), (0,)), ((), ())), preferred_element_type=F32)


def dot_rows(a, b):
    return lax.dot_general(a, b, (((0,), (0,)), ((), ())), preferred_element_type=F32)


def dot_cols(a, b):
    return lax.dot_general(a, b, (((1,), (1,)), ((), ())), preferred_element_type=F32)


def swap_mp(v, mask):
    count = lax.axis_size("mp")
    return lax.ppermute(v, "mp", [(i, i ^ mask) for i in range(count)])


def swap_dp(v, mask):
    count = lax.axis_size("dp")
    return lax.ppermute(v, "dp", [(i, i ^ mask) for i in range(count)])


def dp_bits():
    return lax.axis_size("dp").bit_length() - 1


def all_sum(v):
    v = v + swap_mp(v, 1) + swap_mp(v, 2) + swap_mp(v, 3)
    bit = 0
    bits = dp_bits()
    while bit < bits:
        if bit + 1 < bits:
            v = v + swap_dp(v, 1 << bit) + swap_dp(v, 2 << bit) + swap_dp(v, 3 << bit)
            bit += 2
        else:
            v = v + swap_dp(v, 1 << bit)
            bit += 1
    return v


def dp_bit(bit):
    return (lax.axis_index("dp") >> bit) & 1


def join(mine, other, bit):
    return jnp.where(
        dp_bit(bit) == 0,
        jnp.concatenate([mine, other], axis=0),
        jnp.concatenate([other, mine], axis=0),
    )


def chunk_index():
    index = jnp.int32(0)
    for bit in range(dp_bits()):
        index = index * 2 + dp_bit(bit)
    return index


def fetch_across(w):
    rows = w.shape[0] // lax.axis_size("dp")
    mine = lax.dynamic_slice_in_dim(w, chunk_index() * rows, rows, axis=0)
    got = swap_mp(mine, 2)
    for bit in reversed(range(dp_bits())):
        got = join(got, swap_dp(got, 1 << bit), bit)
    return got


def reduce_pieces(pieces):
    half = pieces[1].shape[0]
    got = swap_mp(jnp.concatenate([pieces[1], pieces[3]], axis=0), 1)
    across = pieces[2].astype(F32) + got[half:].astype(F32)
    own = pieces[0].astype(F32) + got[:half].astype(F32)
    total = own + swap_mp(across.astype(BF), 2).astype(F32)
    for bit in range(dp_bits()):
        size = total.shape[0] // 2
        side = dp_bit(bit)
        send = lax.dynamic_slice_in_dim(total, (1 - side) * size, size, axis=0).astype(BF)
        keep = lax.dynamic_slice_in_dim(total, side * size, size, axis=0)
        total = keep + swap_dp(send, 1 << bit).astype(F32)
    total = total.astype(BF)
    for bit in reversed(range(dp_bits())):
        total = join(total, swap_dp(total, 1 << bit), bit)
    return total.astype(F32)


def stats(v):
    mean = jnp.mean(v, axis=-1, keepdims=True)
    center = v - mean
    spread = jnp.mean(center * center, axis=-1, keepdims=True)
    inverse = lax.rsqrt(spread + 1e-06)
    return center * inverse, inverse


def norm_back(grad, unit, inverse, gain):
    f = grad * gain
    return inverse * (
        f
        - jnp.mean(f, axis=-1, keepdims=True)
        - unit * jnp.mean(f * unit, axis=-1, keepdims=True)
    )


def blocks_of(rows):
    return [(first, min(WINDOW, rows - first)) for first in range(0, rows, WINDOW)]


def head_scores(qkv_ref, same, first, size, h, width):
    q = qkv_ref[first : first + size, h * HEAD_DIM : (h + 1) * HEAD_DIM]
    k = qkv_ref[first : first + size, width + h * HEAD_DIM : width + (h + 1) * HEAD_DIM]
    v = qkv_ref[first : first + size, 2 * width + h * HEAD_DIM : 2 * width + (h + 1) * HEAD_DIM]
    scores = jnp.where(same, dot_cols(q, k) * (1.0 / math.sqrt(HEAD_DIM)), -1e30)
    weights = jnp.exp(scores - jnp.max(scores, axis=-1, keepdims=True))
    weights = weights * (1.0 / jnp.sum(weights, axis=-1, keepdims=True))
    return q, k, v, weights


def attend_kernel(qkv_ref, col_ref, row_ref, out_ref):
    rows, width = out_ref.shape
    for first, size in blocks_of(rows):
        same = col_ref[first : first + size, :] == row_ref[:, first : first + size]
        for h in range(width // HEAD_DIM):
            q, k, v, weights = head_scores(qkv_ref, same, first, size, h, width)
            out_ref[first : first + size, h * HEAD_DIM : (h + 1) * HEAD_DIM] = dot(
                weights.astype(BF), v
            ).astype(BF)


def attend_back_kernel(qkv_ref, grad_ref, col_ref, row_ref, out_ref):
    rows, width = grad_ref.shape
    factor = 1.0 / math.sqrt(HEAD_DIM)
    for first, size in blocks_of(rows):
        same = col_ref[first : first + size, :] == row_ref[:, first : first + size]
        for h in range(width // HEAD_DIM):
            q, k, v, weights = head_scores(qkv_ref, same, first, size, h, width)
            grad = grad_ref[first : first + size, h * HEAD_DIM : (h + 1) * HEAD_DIM]
            soft = dot_cols(grad, v)
            center = jnp.sum(weights * soft, axis=-1, keepdims=True)
            grad_scores = (weights * (soft - center)).astype(BF)
            for part, value in enumerate(
                (
                    dot(grad_scores, k) * factor,
                    dot_rows(grad_scores, q) * factor,
                    dot_rows(weights.astype(BF), grad),
                )
            ):
                lane = part * width + h * HEAD_DIM
                out_ref[first : first + size, lane : lane + HEAD_DIM] = value.astype(BF)


def attend(qkv, owner_col, owner_row, groups):
    rows, width = qkv.shape[0], qkv.shape[1] // (3 * groups)
    return pl.pallas_call(
        attend_kernel,
        grid=(groups,),
        in_specs=[
            pl.BlockSpec((rows, 3 * width), lambda r: (0, r)),
            pl.BlockSpec((rows, 1), lambda r: (0, 0)),
            pl.BlockSpec((1, rows), lambda r: (0, 0)),
        ],
        out_specs=pl.BlockSpec((rows, width), lambda r: (0, r)),
        out_shape=jax.ShapeDtypeStruct((rows, groups * width), BF),
        name="attend",
    )(qkv, owner_col, owner_row)


def attend_back(qkv, grad, owner_col, owner_row, groups):
    rows, width = grad.shape[0], grad.shape[1] // groups
    return pl.pallas_call(
        attend_back_kernel,
        grid=(groups,),
        in_specs=[
            pl.BlockSpec((rows, 3 * width), lambda r: (0, r)),
            pl.BlockSpec((rows, width), lambda r: (0, r)),
            pl.BlockSpec((rows, 1), lambda r: (0, 0)),
            pl.BlockSpec((1, rows), lambda r: (0, 0)),
        ],
        out_specs=pl.BlockSpec((rows, 3 * width), lambda r: (0, r)),
        out_shape=jax.ShapeDtypeStruct((rows, 3 * groups * width), BF),
        name="attend_back",
    )(qkv, grad, owner_col, owner_row)


def gelu_parts(preact):
    phi = 0.5 * (1.0 + lax.erf(preact * (1.0 / math.sqrt(2.0))))
    slope = phi + preact * jnp.exp(-0.5 * preact * preact) * (1.0 / math.sqrt(2.0 * math.pi))
    return (preact * phi).astype(BF), slope


HALO = 80
ROUTE_TICKS = (
    (0, 0, 0, 0, 1, 1, 2, 2, 3, 4),
    (1, 1, 1, 1, 2, 3, 4, 5, 6, 7),
    (2, 2, 3, 3, 4, 5, 6, 7, 8, 9),
    (5, 5, 6, 6, 9, 11, 13, 15, 17, 19),
)
AT_HEADS, AT_PAIRED, AT_QUERY, AT_OUTPUT, AT_HIDDEN, AT_DOWN = 4, 8, 10, 16, 19, 22
MESH = pl.DeviceIdType.MESH


def places():
    mp = lax.axis_index("mp")
    dp = lax.axis_index("dp")
    y = dp % 2
    z = dp // 2
    sibling = mp + 1 - 2 * (mp % 2)
    opposite = mp + 2 - 4 * (mp // 2)
    across = opposite + 1 - 2 * (mp % 2)
    mp_peers = [{"mp": sibling}, {"mp": opposite}, {"mp": across}]
    y_peer = {"dp": dp + 1 - 2 * y}
    z_places = [(z + m) % 4 for m in (1, 2, 3)]
    z_peers = [{"dp": place * 2 + y} for place in z_places]
    return mp, y, z, mp_peers, y_peer, z_places, z_peers


def greet(peers):
    barrier = pltpu.get_barrier_semaphore()
    for peer in peers:
        pl.semaphore_signal(barrier, inc=1, device_id=peer, device_id_type=MESH)
    pl.semaphore_wait(barrier, len(peers))


def remote(source, target, send, recv, peer):
    return pltpu.make_async_remote_copy(
        src_ref=source,
        dst_ref=target,
        send_sem=send,
        recv_sem=recv,
        device_id=peer,
        device_id_type=MESH,
    )


def loop(count, body):
    def step(i, carry):
        body(i)
        return carry

    lax.fori_loop(0, count, step, 0)


def block_rows(i, size):
    return pl.ds(pl.multiple_of(i * size, size), size)


def start_all(copies):
    for copy in copies:
        copy.start()


def wait_recv_all(copies):
    for copy in copies:
        copy.wait_recv()


def item_of_rows(row, lengths, mp):
    window = row >> 8
    offset = row & (WINDOW - 1)
    length = jnp.where(window == 0, lengths[4 * mp], lengths[4 * mp + 2])
    second = jnp.where(offset >= length, 1, 0)
    in_pair = (window < 2) & (offset < PAIR_LEN)
    is_padding = (window == 2) & (offset < PADDING) & (mp == 3)
    return 2 * window + second, offset - second * length, in_pair, is_padding


def owner_of_rows(row, lengths, mp):
    item, _, in_pair, is_padding = item_of_rows(row, lengths, mp)
    return jnp.where(in_pair, item, jnp.where(is_padding, 16, -1))


def choose_item(item, values):
    result = jnp.where(item == 0, values[0], 0.0)
    for j in (1, 2, 3):
        result = jnp.where(item == j, values[j], result)
    return result


def joined(tiles, first):
    return jnp.concatenate([tiles[first + j : first + j + 1, :] for j in range(8)], axis=1)


def forward_kernel(
    lengths,
    groups,
    counts,
    scales,
    gain,
    shift,
    output_bias,
    hidden_gain,
    hidden_shift,
    query_bias,
    value_bias,
    up_bias,
    tokens_ref,
    cotangent_ref,
    query_ref,
    key_ref,
    value_ref,
    output_ref,
    up_ref,
    down_ref,
    tokens_out,
    cotangent_out,
    sums_out,
    stream_out,
    middle_out,
    normed_out,
    qkv_out,
    context_out,
    hidden_out,
    grad_mixed_out,
    active_out,
    grad_pre_out,
    wqkv_out,
    wo_out,
    wup_out,
    wdown_out,
    tokens_ext,
    cotangent_ext,
    tokens,
    cotangent,
    stream,
    middle,
    normed,
    qkv,
    context,
    hidden,
    grad_mixed,
    active,
    grad_pre,
    wqkv,
    wo,
    wup,
    wdown,
    sums,
    bias,
    part,
    from_mp,
    from_y,
    from_z,
    own_sem,
    halo_sem,
    store_sem,
    stat_send,
    stat_recv,
    bias_send,
    bias_recv,
    pair_send,
    pair_recv,
    x_send,
    x_recv,
    far_send,
    far_recv,
    near_send,
    near_recv,
    y_send,
    y_recv,
    fwd_send,
    fwd_recv,
):
    mp, y, z, mp_peers, y_peer, z_places, z_peers = places()
    sibling, opposite, _ = mp_peers
    rows_here = tokens_ref.shape[0]
    rows = tokens.shape[0]
    width = query_ref.shape[1]
    blocks = rows // 32

    items = (
        [(key_ref, first, D // 2, wqkv, width, width, False) for first in (0, D // 2)]
        + [(value_ref, first, D // 2, wqkv, 2 * width, width, False) for first in (0, D // 2)]
        + [(output_ref, 0, width, wo, 0, D, False)]
        + [(up_ref, first, D // 4, wup, 0, D, False) for first in range(0, D, D // 4)]
        + [(down_ref, first, D // 4, wdown, 0, D, False) for first in (3 * D // 4,)]
        + [(query_ref, 0, D, wqkv, 0, width, True), (down_ref, 0, 3 * D // 4, wdown, 0, D, True)]
    )
    relayed = range(10)
    QUERY, DOWN = 10, 11
    HEADS, OUTPUT, HIDDEN = (0, 1, 2, 3, QUERY), 4, (5, 6, 7, 8, 9, DOWN)
    everything = range(len(items))
    near = z % 2
    far = z // 2
    near_peer = {"dp": (z + 1 - 2 * near) * 2 + y}
    far_peer = {"dp": ((z + 2) % 4) * 2 + y}

    def source(i, start, size):
        return items[i][0].at[pl.ds(items[i][1] + start, size)]

    def place(i, r, start, size):
        _, first, _, ref, column, columns, _ = items[i]
        return ref.at[r, pl.ds(first + start, size), pl.ds(column, columns)]

    def part_of(i, first, eighths):
        size = items[i][2] // 8
        return pl.multiple_of(first * size, size), eighths * size

    own_copies = [
        pltpu.make_async_copy(
            source(i, 0, items[i][2]), place(i, 0, 0, items[i][2]), own_sem.at[i]
        )
        for i in everything
    ]
    pair_copies = [
        remote(
            source(i, 0, items[i][2]),
            place(i, 1, 0, items[i][2]),
            pair_send.at[i],
            pair_recv.at[i],
            sibling,
        )
        for i in everything
    ]

    def x_copy(i):
        start, size = (
            (0, items[i][2]) if items[i][6] else part_of(i, y * 4 + near * 2 + far, 1)
        )
        return remote(
            source(i, start, size), place(i, 2, start, size), x_send.at[i], x_recv.at[i], opposite
        )

    def hop(i, first, eighths, send, recv, peer):
        start, size = part_of(i, first, eighths)
        view = place(i, 2, start, size)
        return remote(view, view, send.at[i], recv.at[i], peer)

    def far_copy(i):
        return hop(i, y * 4 + near * 2 + far, 1, far_send, far_recv, far_peer)

    def near_copy(i):
        return hop(i, y * 4 + near * 2, 2, near_send, near_recv, near_peer)

    def y_copy(i):
        return hop(i, y * 4, 4, y_send, y_recv, y_peer)

    def fwd_copy(i):
        size = items[i][2]
        return remote(
            place(i, 2, 0, size), place(i, 3, 0, size), fwd_send.at[i], fwd_recv.at[i], sibling
        )

    route = (x_copy, far_copy, near_copy, y_copy, fwd_copy)

    keep = [
        pltpu.make_async_copy(ref, ext.at[pl.ds(HALO, rows_here)], halo_sem.at[which, 2])
        for which, (ref, ext) in enumerate(
            ((tokens_ref, tokens_ext), (cotangent_ref, cotangent_ext))
        )
    ]
    start_all(keep)
    start_all(own_copies)
    bias[0, 0:1, :] = query_bias[...]
    bias[0, 1:2, :] = value_bias[...]
    for j in range(4):
        bias[0, 2 + j : 3 + j, :] = up_bias[:, j * width : (j + 1) * width]
    bias[0, 6:8, :] = jnp.zeros((2, width), F32)

    weights = [counts[groups[4 * mp + j]].astype(F32) for j in range(4)]
    weight_part = weights[0] + weights[1] + weights[2] + weights[3]
    keep[0].wait()

    def add_rows(i, carry):
        block = tokens_ext[pl.ds(pl.multiple_of(HALO + i * 16, 16), 16), :].astype(F32)
        row = mp * rows_here + i * 16 + lax.broadcasted_iota(jnp.int32, (16, 1), 0)
        kept = jnp.where(row < PAIRS * PAIR_LEN, block, 0.0)
        return carry[0] + kept, carry[1] + kept * block

    zero = jnp.zeros((16, D), F32)
    first, second = lax.fori_loop(0, rows_here // 16, add_rows, (zero, zero))
    first = jnp.sum(first, axis=0, keepdims=True)
    second = jnp.sum(second, axis=0, keepdims=True)
    for j in range(8):
        part[0, j : j + 1, :] = first[:, j * 128 : (j + 1) * 128]
        part[0, 8 + j : 9 + j, :] = second[:, j * 128 : (j + 1) * 128]
    part[0, 16:24, :] = jnp.zeros((8, 128), F32) + weight_part
    greet(mp_peers + [y_peer] + z_peers)

    sums_a = [
        remote(part.at[0], from_mp.at[m], stat_send.at[0, m], stat_recv.at[0, m], peer)
        for m, peer in enumerate(mp_peers)
    ]
    start_all(sums_a)
    after = {"mp": (mp + 1) % 4}
    halo_copies = [
        remote(
            ref.at[pl.ds(rows_here - HALO, HALO)],
            ext.at[pl.ds(0, HALO)],
            halo_sem.at[which, 0],
            halo_sem.at[which, 1],
            after,
        )
        for which, (ref, ext) in enumerate(
            ((tokens_ref, tokens_ext), (cotangent_ref, cotangent_ext))
        )
    ]
    bias_copies = [
        remote(bias.at[0], bias.at[r + 1], bias_send.at[r], bias_recv.at[r], peer)
        for r, peer in enumerate(mp_peers)
    ]
    start_all(halo_copies + bias_copies)
    start_all([x_copy(i) for i in everything])
    start_all([pair_copies[i] for i in HEADS + (OUTPUT,) + HIDDEN])
    sums_b = [
        remote(part.at[1], from_y.at[0], stat_send.at[1, 0], stat_recv.at[1, 0], y_peer)
    ]
    sums_c = [
        remote(part.at[2], from_z.at[m], stat_send.at[2, m], stat_recv.at[2, m], peer)
        for m, peer in enumerate(z_peers)
    ]

    def position_table():
        place_id = lax.broadcasted_iota(jnp.int32, (64, 1), 0)
        table_scale = choose_item(
            place_id >> 4, [scales[groups[4 * mp + j]] for j in range(4)]
        )
        quarter = D // 4
        lane = lax.broadcasted_iota(jnp.int32, (1, quarter), 1).astype(F32)
        frequency = jnp.exp(-math.log(10000.0) * lane / quarter)
        angle = ((place_id & 15).astype(F32) * table_scale) * frequency
        table = jnp.concatenate([jnp.sin(angle), jnp.cos(angle)], axis=1)
        row = lax.broadcasted_iota(jnp.int32, (rows, 64), 0)
        column = lax.broadcasted_iota(jnp.int32, (rows, 64), 1)
        item, position, in_pair, _ = item_of_rows(row, lengths, mp)
        across = (position * 9363) >> 17
        for half, code in enumerate((across, position - SIDE * across)):
            chosen = jnp.where(in_pair & (column == item * 16 + code), 1.0, 0.0)
            stream[:, half * 2 * quarter : (half + 1) * 2 * quarter] = lax.dot_general(
                chosen,
                table,
                (((1,), (0,)), ((), ())),
                precision=lax.Precision.HIGHEST,
                preferred_element_type=F32,
            )

    def place_rows():
        wait_recv_all(halo_copies)
        keep[1].wait()
        own_len = 2 * PAIR_LEN
        row = lax.broadcasted_iota(jnp.int32, (rows, HALO + rows_here), 0)
        column = lax.broadcasted_iota(jnp.int32, (rows, HALO + rows_here), 1)
        window = row >> 8
        offset = row & (WINDOW - 1)
        wanted = HALO - (rows_here - own_len) * mp + window * PAIR_LEN + offset
        tail = jnp.where(mp == 3, HALO + rows_here - PADDING, 4096) + offset
        wanted = jnp.where(window < 2, jnp.where(offset < PAIR_LEN, wanted, -1), tail)
        chosen = jnp.where(column == wanted, 1.0, 0.0).astype(BF)
        tokens[...] = dot(chosen, tokens_ext[...]).astype(BF)
        cotangent[...] = dot(chosen, cotangent_ext[...]).astype(BF)

    def norm_rows(first, count):
        slices = lax.axis_size("dp")
        count_valid = slices * PAIRS * PAIR_LEN
        column_mean = joined(sums, 0) / count_valid
        spread = joined(sums, 8) / count_valid - column_mean * column_mean
        inverse = lax.rsqrt(spread + 1e-05)
        mean_weight = sums[16:17, 0:1] / (slices * 16)

        def first_norm(i):
            here = block_rows(i, 32)
            value = (tokens[here, :].astype(F32) - column_mean) * inverse + stream[here, :]
            stream[here, :] = value
            unit, _ = stats(value)
            normed[here, :] = (unit * gain[...] + shift[...]).astype(BF)
            row = i * 32 + lax.broadcasted_iota(jnp.int32, (32, 1), 0)
            item, _, in_pair, _ = item_of_rows(row, lengths, mp)
            row_weight = jnp.where(in_pair, choose_item(item, weights), 0.0) / mean_weight
            grad_mixed[here, :] = (cotangent[here, :].astype(F32) * row_weight).astype(BF)

        def body(i):
            first_norm(first + i)

        loop(count, body)

    def group_stores(value, target, r):
        return value.at[r], target.at[r]

    def column_stores(value, target, r):
        columns = pl.ds(r * D, D)
        return value.at[:, columns], target.at[:, columns]

    plan = (
        [
            (AT_HEADS, ref, target)
            for ref, target in (
                (tokens, tokens_out),
                (cotangent, cotangent_out),
                (sums, sums_out),
                (stream, stream_out),
                (normed, normed_out),
                (grad_mixed, grad_mixed_out),
            )
        ]
        + [
            (AT_OUTPUT, ref, target)
            for ref, target in ((qkv, qkv_out), (context, context_out), (wqkv, wqkv_out))
        ]
        + [
            (AT_HIDDEN, ref, target)
            for ref, target in ((middle, middle_out), (hidden, hidden_out), (wo, wo_out))
        ]
        + [
            (when,) + group_stores(ref, target, r)
            for r, when in enumerate((AT_PAIRED, AT_PAIRED, AT_HIDDEN + 6, AT_HIDDEN + 6))
            for ref, target in ((wup, wup_out), (wdown, wdown_out))
        ]
        + [
            (AT_HIDDEN + 2 * r + 2,) + column_stores(ref, target, r)
            for r in range(4)
            for ref, target in ((active, active_out), (grad_pre, grad_pre_out))
        ]
    )
    stores = [
        pltpu.make_async_copy(ref, target, store_sem.at[i])
        for i, (_, ref, target) in enumerate(plan)
    ]
    last_tick = AT_HIDDEN + 8

    def head_product(r):
        base = r * 3 * width
        for n in range(3):
            value = dot(normed[...], wqkv[r, :, n * width : (n + 1) * width])
            if n != 1:
                value = value + bias[r, n // 2 : n // 2 + 1, :]
            qkv[:, pl.ds(pl.multiple_of(base + n * width, width), width)] = value.astype(BF)

    def head_pair(r, p):
        base = r * 3 * width
        lanes = [pl.ds(pl.multiple_of(base + n * width + p * 128, 128), 128) for n in range(3)]
        target = pl.ds(pl.multiple_of(r * width + p * 128, 128), 128)
        for first, size in blocks_of(rows):
            here = pl.ds(first, size)
            same = owner_of_rows(
                first + lax.broadcasted_iota(jnp.int32, (size, 1), 0), lengths, mp
            ) == owner_of_rows(first + lax.broadcasted_iota(jnp.int32, (1, size), 1), lengths, mp)
            q, k, v = [qkv[here, lane] for lane in lanes]
            results = []
            for h in range(2):
                cut = slice(h * HEAD_DIM, (h + 1) * HEAD_DIM)
                low = softmax_rows(q[:, cut], k[:, cut], same).astype(BF)
                results.append(dot(low, v[:, cut]).astype(BF))
            context[here, target] = jnp.concatenate(results, axis=1)

    def attention_output(n):
        columns = block_rows(n, 256)
        value = stream[:, columns] + output_bias[:, columns]
        for r in range(4):
            value = value + dot(context[:, r * width : (r + 1) * width], wo[r, :, columns])
        middle[:, columns] = value

    def second_norm(i):
        here = block_rows(i, 32)
        unit, _ = stats(middle[here, :])
        hidden[here, :] = (unit * hidden_gain[...] + hidden_shift[...]).astype(BF)

    def hidden_tile(r, n):
        columns = block_rows(n, 256)
        target = pl.ds(pl.multiple_of(r * D + n * 256, 256), 256)
        preact = dot(hidden[...], wup[r, :, columns]) + bias[r, pl.ds(2 + n, 1), :]
        value, slope = gelu_parts(preact)
        active[:, target] = value
        grad = dot_cols(grad_mixed[...], wdown[r, columns, :])
        grad_pre[:, target] = (grad * slope).astype(BF)

    actions = {}

    def at(k, action):
        actions.setdefault(k, []).append(action)

    for stage in reversed(range(4)):
        for i in relayed:

            def advance(i=i, stage=stage):
                route[stage](i).wait_recv()
                route[stage + 1](i).start()

            at(ROUTE_TICKS[stage][i], advance)

    def pass_on(i):
        x_copy(i).wait_recv()
        fwd_copy(i).start()

    def sums_stage(target, copies, slots, following):
        def action():
            value = part[target - 1]
            for m, copy in enumerate(copies):
                copy.wait_recv()
                value = value + slots[m]
            if following:
                part[target] = value
                start_all(following)
            else:
                sums[...] = value

        return action

    def received(indices, copies):
        def action():
            for i in indices:
                copies(i)

        return action

    def own(i):
        own_copies[i].wait()

    def paired(i):
        pair_copies[i].wait_recv()

    def forwarded(i):
        fwd_copy(i).wait_recv()

    at(0, sums_stage(1, sums_a, from_mp, sums_b))
    at(1, sums_stage(2, sums_b, from_y, sums_c))
    at(2, sums_stage(3, sums_c, from_z, None))
    at(AT_HEADS, lambda: wait_recv_all(bias_copies))
    at(AT_HEADS, received(HEADS, own))
    at(AT_HEADS + 3, received(HEADS, paired))
    at(AT_QUERY, lambda: pass_on(QUERY))
    at(AT_HEADS + 9, received(HEADS, forwarded))
    at(AT_OUTPUT, received((OUTPUT,), own))
    at(AT_OUTPUT, received((OUTPUT,), paired))
    at(AT_OUTPUT, received((OUTPUT,), forwarded))
    at(AT_PAIRED, received(HIDDEN, own))
    at(AT_PAIRED, received(HIDDEN, paired))
    at(AT_DOWN, lambda: pass_on(DOWN))
    at(AT_HIDDEN + 6, received(HIDDEN, forwarded))
    for copy, (when, _, _) in zip(stores, plan):
        if when < last_tick:
            at(when, copy.start)

    def tick(k, carry):
        for when, todo in sorted(actions.items()):

            @pl.when(k == when)
            def _(todo=todo):
                for action in todo:
                    action()

        @pl.when(k == 0)
        def _():
            position_table()

        @pl.when(k == 1)
        def _():
            place_rows()

        @pl.when((k >= 2) & (k < 4))
        def _():
            norm_rows((k - 2) * 10, 10 - (k - 2))

        step = k - AT_HEADS

        @pl.when((step >= 0) & (step < 12) & (step % 3 == 0))
        def _():
            head_product(step // 3)

        @pl.when((step >= 0) & (step < 12) & (step % 3 > 0))
        def _():
            head_pair(step // 3, step % 3 - 1)

        @pl.when((k >= AT_OUTPUT) & (k < AT_OUTPUT + 2))
        def _():
            def body(n):
                attention_output(2 * (k - AT_OUTPUT) + n)

            loop(2, body)

        @pl.when(k == AT_OUTPUT + 2)
        def _():
            loop(blocks, second_norm)

        @pl.when((k >= AT_HIDDEN) & (k < AT_HIDDEN + 8))
        def _():
            def body(n):
                j = 2 * (k - AT_HIDDEN) + n
                hidden_tile(j // 4, j % 4)

            loop(2, body)

        return carry

    lax.fori_loop(0, last_tick, tick, 0)
    start_all([copy for copy, (when, _, _) in zip(stores, plan) if when >= last_tick])
    for i in everything:
        pair_copies[i].wait_send()
        x_copy(i).wait_send()
        fwd_copy(i).wait_send()
        if not items[i][6]:
            for copy in (far_copy, near_copy, y_copy):
                copy(i).wait_send()
    for copy in bias_copies + halo_copies + sums_a + sums_b + sums_c:
        copy.wait_send()
    for copy in stores:
        copy.wait()


def softmax_rows(q, k, same):
    scores = jnp.where(same, dot_cols(q, k) * (1.0 / math.sqrt(HEAD_DIM)), -1e30)
    weights = jnp.exp(scores - jnp.max(scores, axis=-1, keepdims=True))
    return weights * (1.0 / jnp.sum(weights, axis=-1, keepdims=True))


def forward(smalls, vectors, tokens, cotangent, weights, rows):
    width = weights[0].shape[1]
    shape = jax.ShapeDtypeStruct
    full = shape((rows, D), F32)
    low = shape((rows, D), BF)
    wide = shape((rows, 4 * D), BF)
    outs = (
        low,
        low,
        shape((24, 128), F32),
        full,
        full,
        low,
        shape((rows, 12 * width), BF),
        low,
        low,
        low,
        wide,
        wide,
        shape((4, D, 3 * width), BF),
        shape((4, width, D), BF),
        shape((4, D, D), BF),
        shape((4, D, D), BF),
    )
    scratch = [shape((HALO + tokens.shape[0], D), BF)] * 2 + [
        low,
        low,
        full,
        full,
        low,
        outs[6],
        low,
        low,
        low,
        wide,
        wide,
    ]
    scratch += list(outs[12:]) + [
        shape((24, 128), F32),
        shape((4, 8, width), F32),
        shape((3, 24, 128), F32),
        shape((3, 24, 128), F32),
        shape((1, 24, 128), F32),
        shape((3, 24, 128), F32),
    ]
    dma = pltpu.SemaphoreType.DMA
    any_space = pl.BlockSpec(memory_space=pl.ANY)
    return pl.pallas_call(
        forward_kernel,
        out_shape=outs,
        in_specs=[pl.BlockSpec(memory_space=pltpu.SMEM)] * 4
        + [pl.BlockSpec(memory_space=pltpu.VMEM)] * 8
        + [any_space] * 8,
        out_specs=(any_space,) * len(outs),
        scratch_shapes=[pltpu.VMEM(v.shape, v.dtype) for v in scratch]
        + [
            dma((13,)),
            dma((2, 3)),
            dma((28,)),
            dma((3, 3)),
            dma((3, 3)),
            dma((3,)),
            dma((3,)),
        ]
        + [dma((13,))] * 12,
        compiler_params=pltpu.CompilerParams(
            collective_id=1, has_side_effects=True, vmem_limit_bytes=67043328
        ),
        name="forward",
    )(*smalls, *vectors, tokens, cotangent, *weights)


CHUNK = 128
CHUNKS = 24
FINISH_STEPS = 2
STAGE_DELAY = (0, 1, 3, 5, 7, 9, 11)
TICK_HIDDEN, TICK_SECOND, TICK_CONTEXT, TICK_HEADS = 1, 5, 6, 7
TICK_NORMED, TICK_FIRST, TICK_MIXED = 15, 19, 20
TICK_SUMS = (19, 21, 23, 25)
TICK_NEXT, TICK_LAYER, TICK_TOKENS = 26, 28, 29


def backward_kernel(
    lengths,
    groups,
    counts,
    gain,
    hidden_gain,
    down_bias,
    sums,
    tokens_ref,
    cotangent_ref,
    stream_ref,
    middle_ref,
    normed_ref,
    qkv_ref,
    context_ref,
    hidden_ref,
    grad_mixed_ref,
    active_ref,
    grad_pre_ref,
    wqkv_ref,
    wo_ref,
    wup_ref,
    wdown_ref,
    reduced_out,
    finals_out,
    layer_out,
    tokens_grad_out,
    made,
    pair,
    across,
    over_y,
    over_z,
    final,
    act,
    grad_pre,
    hidden,
    grad_mixed,
    context,
    normed,
    grad_attended,
    qkv,
    grad_context,
    rowbuf,
    gradient,
    trunk,
    stream,
    weight,
    packet,
    from_mp,
    from_y,
    from_z,
    layer_next,
    tokens_next,
    load_sem,
    act_sem,
    weight_sem,
    pair_send,
    pair_recv,
    across_send,
    across_recv,
    y_send,
    y_recv,
    z_send,
    z_recv,
    back_z_send,
    back_z_recv,
    back_y_send,
    back_y_recv,
    out_sem,
    stat_send,
    stat_recv,
    next_send,
    next_recv,
):
    mp, y, z, mp_peers, y_peer, z_places, z_peers = places()
    sibling, opposite, _ = mp_peers
    half = CHUNK // 2
    eighth = CHUNK // 8
    rows = normed.shape[0]
    rows_here = layer_out.shape[0]
    width = context.shape[1] // 4
    blocks = rows // 32

    loads = {
        name: pltpu.make_async_copy(source, target, load_sem.at[i])
        for i, (name, source, target) in enumerate(
            (
                ("grad_mixed", grad_mixed_ref, grad_mixed),
                ("grad_pre", grad_pre_ref, grad_pre),
                ("middle", middle_ref, trunk),
                ("cotangent", cotangent_ref, rowbuf),
                ("qkv", qkv_ref, qkv),
                ("hidden", hidden_ref, hidden),
                ("context", context_ref, context),
                ("normed", normed_ref, normed),
                ("stream", stream_ref, stream),
                ("tokens", tokens_ref, rowbuf),
                ("active", active_ref, grad_pre),
                ("middle again", middle_ref, stream),
                ("layer", normed.at[pl.ds(0, rows_here)], layer_out),
                ("tokens_grad", trunk.at[pl.ds(0, rows_here)], tokens_grad_out),
            )
        )
    }

    def act_loads(c):
        return [
            pltpu.make_async_copy(
                active_ref.at[:, pl.ds(pl.multiple_of(r * D + c * CHUNK, CHUNK), CHUNK)],
                act.at[c % 2, r],
                act_sem.at[c % 2, r],
            )
            for r in range(4)
        ]

    def weight_load(s):
        if s < 4:
            source = wup_ref.at[s]
        elif s == 4:
            source = wo_ref
        elif s < 9:
            source = wqkv_ref.at[s - 5]
        else:
            source = wdown_ref.at[s - 9]
        target = weight.at[s % 2, :, pl.ds(0, 3 * width)] if 5 <= s < 9 else weight.at[s % 2]
        return pltpu.make_async_copy(source, target, weight_sem.at[s % 2])

    for c in range(2):
        start_all(act_loads(c))
    loads["grad_mixed"].start()
    weight_load(0).start()
    loads["grad_pre"].start()
    weight_load(1).start()
    for name in ("middle", "cotangent", "qkv", "hidden", "context", "normed", "stream"):
        loads[name].start()
    greet(mp_peers + [y_peer] + z_peers)

    weights = [counts[groups[4 * mp + j]].astype(F32) for j in range(4)]
    slices = lax.axis_size("dp")
    count_valid = slices * PAIRS * PAIR_LEN
    column_mean = joined(sums, 0) / count_valid
    spread = joined(sums, 8) / count_valid - column_mean * column_mean
    inverse = lax.rsqrt(spread + 1e-05)
    mean_weight = sums[16:17, 0:1] / (slices * 16)

    def pair_copy(c):
        return remote(
            made.at[c % 2, pl.ds(0, 2)], pair.at[c], pair_send.at[c], pair_recv.at[c], sibling
        )

    def across_copy(c):
        return remote(
            pair.at[c, 1], across.at[c], across_send.at[c], across_recv.at[c], opposite
        )

    def y_copy(c):
        return remote(
            across.at[c, pl.ds(pl.multiple_of((1 - y) * half, half), half)],
            over_y.at[c],
            y_send.at[c],
            y_recv.at[c],
            y_peer,
        )

    def z_copies(c):
        return [
            remote(
                over_y.at[c, pl.ds(pl.multiple_of(place * eighth, eighth), eighth)],
                over_z.at[c, m],
                z_send.at[c, m],
                z_recv.at[c, m],
                peer,
            )
            for m, (place, peer) in enumerate(zip(z_places, z_peers))
        ]

    def back_z_copies(c):
        view = final.at[c, pl.ds(pl.multiple_of(y * half + z * eighth, eighth), eighth)]
        return [
            remote(view, view, back_z_send.at[c, m], back_z_recv.at[c, m], peer)
            for m, peer in enumerate(z_peers)
        ]

    def back_y_copy(c):
        view = final.at[c, pl.ds(pl.multiple_of(y * half, half), half)]
        return remote(view, view, back_y_send.at[c], back_y_recv.at[c], y_peer)

    def out_copy(c):
        return pltpu.make_async_copy(final.at[c], reduced_out.at[c], out_sem.at[c])

    def make(c):
        @pl.when(c < 8)
        def _():
            for copy in act_loads(c):
                copy.wait()

        def one(j):
            r = 2 * j + 1 - 5 * (j // 2)

            def store(left, right):
                made[c % 2, j] = dot_rows(left, right).astype(BF)

            @pl.when(c < 8)
            def _():
                store(act[c % 2, r], grad_mixed[...])

            @pl.when((c >= 8) & (c < 16))
            def _():
                store(
                    hidden[:, block_rows(c - 8, CHUNK)], grad_pre[:, block_rows(r, D)]
                )

            @pl.when((c >= 16) & (c < 18))
            def _():
                store(context[:, block_rows(2 * r + c - 16, CHUNK)], grad_attended[...])

            @pl.when(c >= 18)
            def _():
                store(qkv[:, block_rows(6 * r + c - 18, CHUNK)], normed[...])

        loop(4, one)

        @pl.when(c < 6)
        def _():
            start_all(act_loads(c + 2))

    def add_pair(c):
        pair_copy(c).wait()

        def body(i):
            here = block_rows(i, 32)
            for which in (1, 0):
                pair[c, which, here, :] = (
                    pair[c, which, here, :].astype(F32)
                    + made[c % 2, 2 + which, here, :].astype(F32)
                ).astype(BF)

        loop(CHUNK // 32, body)

    def add_across(c):
        across_copy(c).wait_recv()

        def body(i):
            here = block_rows(i, 32)
            across[c, here, :] = (
                across[c, here, :].astype(F32) + pair[c, 0, here, :].astype(F32)
            ).astype(BF)

        loop(CHUNK // 32, body)

    def add_y(c):
        y_copy(c).wait_recv()

        def body(i):
            here = block_rows(i, 32)
            own = pl.ds(pl.multiple_of(y * half + i * 32, 32), 32)
            over_y[c, here, :] = (
                over_y[c, here, :].astype(F32) + across[c, own, :].astype(F32)
            ).astype(BF)

        loop(half // 32, body)

    def add_z(c):
        wait_recv_all(z_copies(c))
        value = over_y[c, block_rows(z, eighth), :].astype(F32)
        for m in range(3):
            value = value + over_z[c, m].astype(F32)
        final[c, pl.ds(pl.multiple_of(y * half + z * eighth, eighth), eighth), :] = value.astype(BF)

    handle = (
        make,
        add_pair,
        add_across,
        add_y,
        add_z,
        lambda c: wait_recv_all(back_z_copies(c)),
        lambda c: back_y_copy(c).wait_recv(),
    )
    send = (
        lambda c: [pair_copy(c)],
        lambda c: [across_copy(c)],
        lambda c: [y_copy(c)],
        z_copies,
        back_z_copies,
        lambda c: [back_y_copy(c)],
        lambda c: [out_copy(c)],
    )

    def hidden_step(r):
        left = block_rows(r, D)

        def tile(n):
            columns = block_rows(n, 256)
            value = dot_cols(grad_pre[:, left], weight[r % 2, columns, :])

            @pl.when(r == 0)
            def _():
                gradient[:, columns] = value

            @pl.when(r > 0)
            def _():
                gradient[:, columns] = gradient[:, columns] + value

        loop(4, tile)

    def fold(value):
        return jnp.sum(value.reshape(4, 8, D), axis=0)

    def put(index, value):
        for j in range(8):
            packet[0, 8 * index + j : 8 * index + j + 1, :] = value[:, j * 128 : (j + 1) * 128]

    def put_all(first, values):
        for i, value in enumerate(values):
            put(first + i, jnp.sum(value, axis=0, keepdims=True))

    def ones_dot(value):
        return dot(jnp.ones((16, rows), BF), value)[0:1, :]

    def row_weight_of(i):
        row = i * 32 + lax.broadcasted_iota(jnp.int32, (32, 1), 0)
        item, _, in_pair, _ = item_of_rows(row, lengths, mp)
        return jnp.where(in_pair, choose_item(item, weights), 0.0) / mean_weight, in_pair

    zero = jnp.zeros((8, D), F32)

    def second_norm_back():
        def body(i, carry):
            here = block_rows(i, 32)
            unit, scale = stats(trunk[here, :])
            grad = gradient[here, :]
            row_weight, _ = row_weight_of(i)
            value = rowbuf[here, :].astype(F32) * row_weight + norm_back(
                grad, unit, scale, hidden_gain[...]
            )
            trunk[here, :] = value
            low = value.astype(BF)
            grad_attended[here, :] = low
            return (
                carry[0] + fold(grad * unit),
                carry[1] + fold(grad),
                carry[2] + fold(low.astype(F32)),
            )

        put_all(4, lax.fori_loop(0, blocks, body, (zero, zero, zero)))
        put(7, ones_dot(grad_mixed[...]))

    def context_step():
        def tile(n):
            columns = block_rows(n, 256)
            grad_context[:, columns] = dot_cols(grad_attended[...], weight[0, columns, :]).astype(BF)

        loop(4, tile)

    def head_pair_back(index):
        r = index // 2
        p = index % 2
        lanes = [block_rows(6 * r + 2 * n + p, 128) for n in range(3)]
        source = block_rows(2 * r + p, 128)
        factor = 1.0 / math.sqrt(HEAD_DIM)
        for first, size in blocks_of(rows):
            here = pl.ds(first, size)
            same = owner_of_rows(
                first + lax.broadcasted_iota(jnp.int32, (size, 1), 0), lengths, mp
            ) == owner_of_rows(first + lax.broadcasted_iota(jnp.int32, (1, size), 1), lengths, mp)
            q, k, v = [qkv[here, lane] for lane in lanes]
            g = grad_context[here, source]
            results = []
            for h in range(2):
                cut = slice(h * HEAD_DIM, (h + 1) * HEAD_DIM)
                soft = softmax_rows(q[:, cut], k[:, cut], same)
                grad_soft = dot_cols(g[:, cut], v[:, cut])
                center = jnp.sum(soft * grad_soft, axis=-1, keepdims=True)
                grad_scores = (soft * (grad_soft - center)).astype(BF)
                results.append(
                    (
                        (dot(grad_scores, k[:, cut]) * factor).astype(BF),
                        (dot_rows(grad_scores, q[:, cut]) * factor).astype(BF),
                        dot_rows(soft.astype(BF), g[:, cut]).astype(BF),
                    )
                )
            for n in range(3):
                qkv[here, lanes[n]] = jnp.concatenate([results[0][n], results[1][n]], axis=1)

    def normed_step(r):
        left = qkv[:, block_rows(r, 3 * width)]

        def tile(n):
            columns = block_rows(n, 256)
            value = dot_cols(left, weight[(r + 1) % 2, columns, 0 : 3 * width])

            @pl.when(r == 0)
            def _():
                gradient[:, columns] = value

            @pl.when(r > 0)
            def _():
                gradient[:, columns] = gradient[:, columns] + value

        loop(4, tile)

    def first_norm_back():
        def body(i, carry):
            here = block_rows(i, 32)
            unit, scale = stats(stream[here, :])
            grad = gradient[here, :]
            value = trunk[here, :] + norm_back(grad, unit, scale, gain[...])
            standard = (rowbuf[here, :].astype(F32) - column_mean) * inverse
            gradient[here, :] = value
            return (
                carry[0] + fold(value),
                carry[1] + fold(value * standard),
                carry[2] + fold(grad * unit),
                carry[3] + fold(grad),
            )

        put_all(0, lax.fori_loop(0, blocks, body, (zero, zero, zero, zero)))
        for r in range(4):
            if r:
                packet[r, 0:64, :] = packet[0, 0:64, :]
            parts = [
                ones_dot(qkv[:, (3 * r + n) * width : (3 * r + n + 1) * width]) for n in (0, 2)
            ] + [
                ones_dot(grad_pre[:, r * D + n * width : r * D + (n + 1) * width]) for n in range(4)
            ]
            for i, value in enumerate(parts):
                for j in range(2):
                    packet[r, 64 + 2 * i + j : 65 + 2 * i + j, :] = value[
                        :, j * 128 : (j + 1) * 128
                    ]
            packet[r, 76:80, :] = jnp.zeros((4, 128), F32)

    def mixed_step(r):
        left = grad_pre[:, block_rows(r, D)]

        def tile(n):
            columns = block_rows(n, 256)
            stream[:, columns] = stream[:, columns] + dot(left, weight[(r + 1) % 2, :, columns])

        loop(4, tile)

    def layer_step():
        def body(i):
            here = block_rows(i, 32)
            hidden[here, :] = (stream[here, :] + down_bias[...]).astype(BF)

        loop(blocks, body)

    def exchange(stage, sources, peers, slots):
        return [
            remote(
                source, slots.at[m], stat_send.at[stage, m], stat_recv.at[stage, m], peer
            )
            for m, (source, peer) in enumerate(zip(sources, peers))
        ]

    sums_a = exchange(0, [packet.at[r] for r in (1, 2, 3)], mp_peers, from_mp)
    sums_b = exchange(1, [packet.at[4]], [y_peer], from_y)
    sums_c = exchange(2, [packet.at[5]] * 3, z_peers, from_z)

    def gather_sums(first, copies, slots, target):
        value = packet[first]
        for m, copy in enumerate(copies):
            copy.wait_recv()
            value = value + slots[m]
        packet[target] = value

    def tokens_step():
        total = joined(packet[6], 0), joined(packet[6], 8)

        def body(i):
            here = block_rows(i, 32)
            standard = (rowbuf[here, :].astype(F32) - column_mean) * inverse
            _, in_pair = row_weight_of(i)
            share = jnp.where(in_pair, 1.0 / count_valid, 0.0)
            gradient[here, :] = inverse * (
                gradient[here, :] - share * (total[0] + total[1] * standard)
            )

        loop(blocks, body)

    before = {"mp": (mp + 3) % 4}
    layer_next_copy = remote(
        hidden.at[pl.ds(0, HALO)], layer_next, next_send.at[0], next_recv.at[0], before
    )
    tokens_next_copy = remote(
        gradient.at[pl.ds(0, HALO)], tokens_next, next_send.at[1], next_recv.at[1], before
    )

    def choose_rows(count, first):
        row = lax.broadcasted_iota(jnp.int32, (rows_here, count), 0)
        column = lax.broadcasted_iota(jnp.int32, (rows_here, count), 1) + first
        place = row + (rows_here - 2 * PAIR_LEN) * mp
        after = jnp.where(mp == 3, 2 * WINDOW, rows) - 2 * PAIR_LEN
        wanted = jnp.where(
            place < PAIR_LEN,
            place,
            jnp.where(place < 2 * PAIR_LEN, place + (WINDOW - PAIR_LEN), place + after),
        )
        return jnp.where(column == wanted, 1.0, 0.0).astype(BF)

    def own_rows(value, following, target):
        chosen, chosen_next = choose_rows(rows, 0), choose_rows(HALO, rows)
        pairs = ((chosen, value), (chosen_next, following))

        def tile(n):
            columns = block_rows(n, 256)
            total = jnp.zeros((rows_here, 256), F32)
            for matrix, ref in pairs:
                block = ref[:, columns]
                high = block.astype(BF)
                total = total + dot(matrix, high)
                if ref.dtype == F32:
                    middle_part = block - high.astype(F32)
                    low = middle_part.astype(BF)
                    total = total + dot(matrix, low)
                    total = total + dot(matrix, (middle_part - low.astype(F32)).astype(BF))
            target[0:rows_here, columns] = total.astype(target.dtype)

        loop(4, tile)

    def work(k):
        for s in range(4):

            @pl.when(k == TICK_HIDDEN + s)
            def _(s=s):
                if s == 0:
                    loads["grad_pre"].wait()
                weight_load(s).wait()

        @pl.when((k >= TICK_HIDDEN) & (k < TICK_HIDDEN + 4))
        def _():
            hidden_step(k - TICK_HIDDEN)

        for s in range(4):

            @pl.when(k == TICK_HIDDEN + s)
            def _(s=s):
                weight_load(s + 2).start()

        @pl.when(k == TICK_SECOND)
        def _():
            loads["middle"].wait()
            loads["cotangent"].wait()
            second_norm_back()
            loads["tokens"].start()

        @pl.when(k == TICK_CONTEXT)
        def _():
            weight_load(4).wait()
            context_step()
            weight_load(6).start()
            loads["qkv"].wait()

        @pl.when((k >= TICK_HEADS) & (k < TICK_HEADS + 8))
        def _():
            head_pair_back(k - TICK_HEADS)

        for s in range(4):

            @pl.when(k == TICK_NORMED + s)
            def _(s=s):
                weight_load(5 + s).wait()

        @pl.when((k >= TICK_NORMED) & (k < TICK_NORMED + 4))
        def _():
            normed_step(k - TICK_NORMED)

        for s in range(4):

            @pl.when(k == TICK_NORMED + s)
            def _(s=s):
                weight_load(7 + s).start()

        @pl.when(k == TICK_FIRST)
        def _():
            loads["stream"].wait()
            loads["tokens"].wait()
            first_norm_back()
            loads["active"].start()
            loads["middle again"].start()
            start_all(sums_a)

        for s in range(4):

            @pl.when(k == TICK_MIXED + s)
            def _(s=s):
                if s == 0:
                    loads["active"].wait()
                    loads["middle again"].wait()
                weight_load(9 + s).wait()

        @pl.when((k >= TICK_MIXED) & (k < TICK_MIXED + 4))
        def _():
            mixed_step(k - TICK_MIXED)

        for s in range(2):

            @pl.when(k == TICK_MIXED + s)
            def _(s=s):
                weight_load(11 + s).start()

        @pl.when(k == TICK_MIXED + 3)
        def _():
            layer_step()

        @pl.when(k == TICK_NEXT)
        def _():
            layer_next_copy.start()
            tokens_next_copy.start()

        @pl.when(k == TICK_LAYER)
        def _():
            layer_next_copy.wait_recv()
            own_rows(hidden, layer_next, normed)
            loads["layer"].start()

        @pl.when(k == TICK_TOKENS)
        def _():
            tokens_next_copy.wait_recv()
            own_rows(gradient, tokens_next, trunk)
            loads["tokens_grad"].start()

        @pl.when(k == TICK_SUMS[1])
        def _():
            gather_sums(0, sums_a, from_mp, 4)
            start_all(sums_b)

        @pl.when(k == TICK_SUMS[2])
        def _():
            gather_sums(4, sums_b, from_y, 5)
            start_all(sums_c)

        @pl.when(k == TICK_SUMS[3])
        def _():
            gather_sums(5, sums_c, from_z, 6)
            finals_out[...] = packet[6]
            tokens_step()

    waits = {0: ("grad_mixed",), 8: ("hidden",), 16: ("context",), 18: ("normed",)}

    def tick(k, carry):
        for when, names in waits.items():

            @pl.when(k == when)
            def _(names=names):
                for name in names:
                    loads[name].wait()

        def staged(stage, actions):
            c = k - STAGE_DELAY[stage]

            @pl.when((c >= 0) & (c < CHUNKS))
            def _():
                actions[stage](c)

        sends = tuple(lambda c, f=f: start_all(f(c)) for f in send)
        for stage in (6, 5, 4, 3, 2):
            staged(stage, handle)
        for stage in (2, 3, 4, 5, 6):
            staged(stage, sends)
        staged(0, handle)
        staged(1, handle)
        staged(0, sends)
        staged(1, sends)
        work(k)
        return carry

    lax.fori_loop(0, CHUNKS + STAGE_DELAY[-1], tick, 0)

    def finish(c):
        across_copy(c).wait_send()
        y_copy(c).wait_send()
        for copy in z_copies(c) + back_z_copies(c):
            copy.wait_send()
        back_y_copy(c).wait_send()
        out_copy(c).wait()

    loop(CHUNKS, finish)
    for copy in sums_a + sums_b + sums_c:
        copy.wait_send()
    layer_next_copy.wait_send()
    tokens_next_copy.wait_send()
    loads["layer"].wait()
    loads["tokens_grad"].wait()


def backward(smalls, vectors, sums, saved, rows_here):
    (
        tokens,
        cotangent,
        stream,
        middle,
        normed,
        qkv,
        context,
        hidden,
        grad_mixed,
        active,
        grad_pre,
        wqkv,
        wo,
        wup,
        wdown,
    ) = saved
    rows = normed.shape[0]
    shape = jax.ShapeDtypeStruct
    low = shape((rows, D), BF)
    full = shape((rows, D), F32)
    packed = shape((80, 128), F32)
    scratch = [
        shape((2, 4, CHUNK, D), BF),
        shape((CHUNKS, 2, CHUNK, D), BF),
        shape((CHUNKS, CHUNK, D), BF),
        shape((CHUNKS, CHUNK // 2, D), BF),
        shape((CHUNKS, 3, CHUNK // 8, D), BF),
        shape((CHUNKS, CHUNK, D), BF),
        shape((2, 4, rows, CHUNK), BF),
        shape(grad_pre.shape, BF),
        low,
        low,
        low,
        low,
        low,
        shape(qkv.shape, BF),
        low,
        low,
        full,
        full,
        full,
        shape((2, D, D), BF),
        shape((7, 80, 128), F32),
        shape((3, 80, 128), F32),
        shape((1, 80, 128), F32),
        shape((3, 80, 128), F32),
        shape((HALO, D), BF),
        shape((HALO, D), F32),
    ]
    dma = pltpu.SemaphoreType.DMA
    any_space = pl.BlockSpec(memory_space=pl.ANY)
    vmem = pl.BlockSpec(memory_space=pltpu.VMEM)
    return pl.pallas_call(
        backward_kernel,
        out_shape=(
            shape((CHUNKS, CHUNK, D), BF),
            packed,
            shape((rows_here, D), BF),
            shape((rows_here, D), F32),
        ),
        in_specs=[pl.BlockSpec(memory_space=pltpu.SMEM)] * 3 + [vmem] * 4 + [any_space] * 15,
        out_specs=(any_space, vmem, any_space, any_space),
        scratch_shapes=[pltpu.VMEM(v.shape, v.dtype) for v in scratch]
        + [
            dma((14,)),
            dma((2, 4)),
            dma((2,)),
            dma((CHUNKS,)),
            dma((CHUNKS,)),
            dma((CHUNKS,)),
            dma((CHUNKS,)),
            dma((CHUNKS,)),
            dma((CHUNKS,)),
            dma((CHUNKS, 3)),
            dma((CHUNKS, 3)),
            dma((CHUNKS, 3)),
            dma((CHUNKS, 3)),
            dma((CHUNKS,)),
            dma((CHUNKS,)),
            dma((CHUNKS,)),
            dma((3, 3)),
            dma((3, 3)),
            dma((2,)),
            dma((2,)),
        ],
        compiler_params=pltpu.CompilerParams(
            collective_id=2, has_side_effects=True, vmem_limit_bytes=67043328
        ),
        name="backward",
    )(
        *smalls,
        *vectors,
        sums,
        tokens,
        cotangent,
        stream,
        middle,
        normed,
        qkv,
        context,
        hidden,
        grad_mixed,
        active,
        grad_pre,
        wqkv,
        wo.reshape(D, D),
        wup,
        wdown,
    )


def finish_kernel(
    down_ref,
    up_ref,
    output_ref,
    query_ref,
    key_ref,
    value_ref,
    finals_ref,
    layer_ref,
    tokens_ref,
    down,
    up,
    output,
    query,
    key,
    value,
    layer,
    tokens,
    *vectors,
):
    for source, target in ((down_ref, down), (up_ref, up)):
        for i in range(source.shape[0]):
            target[i * CHUNK : (i + 1) * CHUNK, :] = source[i].astype(F32)
    output[...] = output_ref[0].astype(F32)
    for source, target in ((query_ref, query), (key_ref, key), (value_ref, value)):
        for half in range(2):
            target[:, half * CHUNK : (half + 1) * CHUNK] = source[half].astype(F32).T
    layer[...] = layer_ref[...]
    tokens[...] = tokens_ref[...]

    @pl.when(pl.program_id(0) == 0)
    def _():
        first = 0
        for target in vectors:
            size = target.shape[0]
            target[...] = finals_ref[first : first + size, :]
            first += size


def finish(reduced, finals, layer, tokens, width):
    shape = jax.ShapeDtypeStruct
    rows_here = layer.shape[0]
    steps = FINISH_STEPS
    share = rows_here // steps
    taken = 8 // steps
    sizes = (8,) * 8 + (2, 2, 8)
    own = [pl.BlockSpec((share, D), lambda c: (c, 0))] * 2
    specs = (
        [
            pl.BlockSpec((taken * CHUNK, D), lambda c: (c, 0)),
            pl.BlockSpec((taken * CHUNK, D), lambda c: (c, 0)),
            pl.BlockSpec((width // steps, D), lambda c: (c, 0)),
        ]
        + [pl.BlockSpec((taken * CHUNK, width), lambda c: (c, 0))] * 3
        + own
    )
    shapes = [
        shape((D, D), F32),
        shape((D, D), F32),
        shape((width, D), F32),
        shape((D, width), F32),
        shape((D, width), F32),
        shape((D, width), F32),
        shape((rows_here, D), BF),
        shape((rows_here, D), F32),
    ]
    return pl.pallas_call(
        finish_kernel,
        grid=(steps,),
        in_specs=[
            pl.BlockSpec((taken, CHUNK, D), lambda c: (c, 0, 0)),
            pl.BlockSpec((taken, CHUNK, D), lambda c: (steps + c, 0, 0)),
            pl.BlockSpec(
                (1, width // steps, D), lambda c: (16 + c // (steps // 2), c % (steps // 2), 0)
            ),
        ]
        + [
            pl.BlockSpec((2, CHUNK, taken * CHUNK), lambda c, first=first: (first, 0, c))
            for first in (9, 10, 11)
        ]
        + [pl.BlockSpec(finals.shape, lambda c: (0, 0))]
        + own,
        out_specs=specs + [pl.BlockSpec((size, 128), lambda c: (0, 0)) for size in sizes],
        out_shape=shapes + [shape((size, 128), F32) for size in sizes],
        name="finish",
    )(*[reduced] * 6, finals, layer, tokens)


def general_shards(
    tokens,
    cotangent,
    item_lengths,
    item_group,
    group_count,
    grid_scale,
    norm_gain,
    norm_shift,
    query_weight,
    query_bias,
    key_weight,
    value_weight,
    value_bias,
    output_weight,
    output_bias,
    hidden_gain,
    hidden_shift,
    up_weight,
    up_bias,
    down_weight,
    down_bias,
):
    shard_count = lax.axis_size("mp")
    slice_count = lax.axis_size("dp")
    mp = lax.axis_index("mp")
    rows_here = tokens.shape[0]
    item_count = item_lengths.shape[0]
    pairs_here = PAIRS // shard_count
    own_rows = pairs_here * PAIR_LEN
    shift = rows_here - own_rows
    halo = shift * (shard_count - 1)
    padding = rows_here * shard_count - PAIRS * PAIR_LEN
    tail_block = -(-padding // 32) * 32
    rows = pairs_here * WINDOW + tail_block
    is_last = mp == shard_count - 1

    width = query_weight.shape[1]
    qkv_own = jnp.concatenate([query_weight, key_weight, value_weight], axis=1)
    bias_own = jnp.concatenate([query_bias, value_bias, up_bias])[None, :]
    bias_across = swap_mp(bias_own, 2)
    bias_pair = swap_mp(jnp.concatenate([bias_own, bias_across], axis=0), 1)
    biases = [bias_own[0], bias_pair[0], bias_across[0], bias_pair[1]]

    def gather(own, direct):
        across = swap_mp(own, 2) if direct else fetch_across(own)
        return [own, swap_mp(own, 1), across, swap_mp(across, 1)]

    tokens_f = tokens.astype(F32)
    slice_row = mp * rows_here + jnp.arange(rows_here, dtype=jnp.int32)
    weighted = tokens_f * (slice_row < PAIRS * PAIR_LEN).astype(F32)[:, None]
    chosen = item_group[:, None] == jnp.arange(group_count.shape[0], dtype=jnp.int32)[None, :]
    item_scale = jnp.sum(jnp.where(chosen, grid_scale[None, :], 0.0), axis=1)
    item_weight = jnp.sum(jnp.where(chosen, group_count[None, :], 0), axis=1).astype(F32)
    sums = all_sum(
        jnp.stack(
            [
                jnp.sum(weighted, axis=0),
                jnp.sum(weighted * tokens_f, axis=0),
                jnp.broadcast_to(jnp.sum(item_weight) / shard_count, (D,)),
            ]
        )
    )

    def windows(v):
        before = lax.ppermute(
            v[rows_here - halo :], "mp", [(i, i + 1) for i in range(shard_count - 1)]
        )
        joined = jnp.concatenate([before, v], axis=0)
        start = halo - shift * mp
        parts = []
        for pair in range(pairs_here):
            parts.append(
                lax.dynamic_slice_in_dim(joined, start + pair * PAIR_LEN, PAIR_LEN, axis=0)
            )
            parts.append(jnp.zeros((WINDOW - PAIR_LEN, D), v.dtype))
        parts.append(jnp.where(is_last, v[rows_here - padding :], jnp.zeros((), v.dtype)))
        parts.append(jnp.zeros((tail_block - padding, D), v.dtype))
        return jnp.concatenate(parts, axis=0)

    def unwindows(v):
        own = jnp.concatenate(
            [v[pair * WINDOW : pair * WINDOW + PAIR_LEN] for pair in range(pairs_here)], axis=0
        )
        after = lax.ppermute(own[:halo], "mp", [(i + 1, i) for i in range(shard_count - 1)])
        after = jnp.concatenate([after, jnp.zeros((padding - halo, D), v.dtype)], axis=0)
        tail = v[pairs_here * WINDOW : pairs_here * WINDOW + padding]
        joined = jnp.concatenate([own, jnp.where(is_last, tail, after)], axis=0)
        return lax.dynamic_slice_in_dim(joined, shift * mp, rows_here, axis=0)

    tokens_w = windows(tokens).astype(F32)
    cotangent_w = windows(cotangent).astype(F32)

    row = jnp.arange(rows, dtype=jnp.int32)
    window = row // WINDOW
    offset = row % WINDOW
    in_pair = (window < pairs_here) & (offset < PAIR_LEN)
    is_padding = (window == pairs_here) & (offset < padding) & is_last
    pair = pairs_here * mp + window
    item_ids = jnp.arange(item_count, dtype=jnp.int32)
    first_len = jnp.sum(
        jnp.where(item_ids[None, :] == (2 * pair)[:, None], item_lengths[None, :], 0), axis=1
    )
    second = (offset >= first_len).astype(jnp.int32)
    owner = jnp.where(in_pair, 2 * pair + second, jnp.where(is_padding, item_count, -1))
    position = offset - second * first_len
    member = owner[:, None] == item_ids[None, :]
    row_scale = jnp.sum(jnp.where(member, item_scale[None, :], 0.0), axis=1)
    row_count = jnp.sum(jnp.where(member, item_weight[None, :], 0.0), axis=1)
    valid = in_pair.astype(F32)[:, None]
    quarter = D // 4
    frequency = jnp.exp(-math.log(10000.0) * jnp.arange(quarter, dtype=F32) / quarter)
    across_angle = ((position // SIDE).astype(F32) * row_scale)[:, None] * frequency
    side_angle = ((position % SIDE).astype(F32) * row_scale)[:, None] * frequency
    grid_table = (
        jnp.concatenate(
            [
                jnp.sin(across_angle),
                jnp.cos(across_angle),
                jnp.sin(side_angle),
                jnp.cos(side_angle),
            ],
            axis=-1,
        )
        * valid
    )
    owner_col = owner[:, None]
    owner_row = owner[None, :]

    qkv_weights = jnp.concatenate(gather(qkv_own, True), axis=1)
    output_weights = jnp.concatenate(gather(output_weight, False), axis=0)
    up_weights = jnp.concatenate(gather(up_weight, False), axis=1)
    down_weights = jnp.concatenate(gather(down_weight, False), axis=0)
    hidden_width = up_weight.shape[1]
    no_bias = jnp.zeros((width,), F32)
    qkv_bias = jnp.concatenate(
        [v for b in biases for v in (b[:width], no_bias, b[width : 2 * width])]
    )
    up_biases = jnp.concatenate([b[2 * width :] for b in biases])

    count_valid = slice_count * PAIRS * PAIR_LEN
    column_mean = sums[0] / count_valid
    spread = sums[1] / count_valid - column_mean * column_mean
    inverse = lax.rsqrt(spread + 1e-05)
    row_weight = row_count / (sums[2, 0] / (slice_count * item_count))
    standard = (tokens_w - column_mean) * inverse
    stream = standard + grid_table
    unit, unit_inverse = stats(stream)
    normed = (unit * norm_gain + norm_shift).astype(BF)

    qkv = (dot(normed, qkv_weights) + qkv_bias).astype(BF)
    context = attend(qkv, owner_col, owner_row, shard_count)
    middle = stream + (dot(context, output_weights) + output_bias)
    middle_unit, middle_inverse = stats(middle)
    hidden_in = (middle_unit * hidden_gain + hidden_shift).astype(BF)

    grad_out = cotangent_w * row_weight[:, None]
    grad_mixed = grad_out.astype(BF)
    active, slope = gelu_parts(dot(hidden_in, up_weights) + up_biases)
    mixed = dot(active, down_weights) + down_bias
    grad_pre = (dot_cols(grad_mixed, down_weights) * slope).astype(BF)
    grad_hidden = dot_cols(grad_pre, up_weights)
    layer_output = unwindows((middle + mixed).astype(BF))
    grad_middle = grad_out + norm_back(grad_hidden, middle_unit, middle_inverse, hidden_gain)
    grad_attended = grad_middle.astype(BF)

    grad_context = dot_cols(grad_attended, output_weights).astype(BF)
    grad_qkv = attend_back(qkv, grad_context, owner_col, owner_row, shard_count)
    grad_normed = dot_cols(grad_qkv, qkv_weights)

    pieces = range(shard_count)
    def columns(v, r, size):
        return v[:, r * size : (r + 1) * size]

    def reduced(left, right):
        return reduce_pieces([dot_rows(left(r), right(r)).astype(BF) for r in pieces])

    down_weight_grad = reduced(
        lambda r: columns(active, r, hidden_width), lambda r: grad_mixed
    )
    up_weight_grad = reduced(
        lambda r: hidden_in, lambda r: columns(grad_pre, r, hidden_width)
    )
    output_weight_grad = reduced(
        lambda r: columns(context, r, width), lambda r: grad_attended
    )
    qkv_weight_grad = reduced(lambda r: normed, lambda r: columns(grad_qkv, r, 3 * width))
    qkv_weight_grads = [columns(qkv_weight_grad, i, width) for i in range(3)]
    grad_stream = grad_middle + norm_back(grad_normed, unit, unit_inverse, norm_gain)

    def column_sums(v):
        return jnp.sum(v.astype(F32), axis=0)

    qkv_sums = column_sums(grad_qkv)
    up_sums = column_sums(grad_pre)
    bias_grads = [
        jnp.concatenate(
            [
                qkv_sums[3 * r * width : (3 * r + 1) * width],
                qkv_sums[(3 * r + 2) * width : 3 * (r + 1) * width],
                up_sums[r * hidden_width : (r + 1) * hidden_width],
            ]
        )[None, :]
        for r in pieces
    ]
    got = swap_mp(jnp.concatenate([bias_grads[1], bias_grads[3]], axis=0), 1)
    bias_grad = bias_grads[0] + got[:1] + swap_mp(bias_grads[2] + got[1:], 2)
    for bit in range(dp_bits()):
        bias_grad = bias_grad + swap_dp(bias_grad, 1 << bit)
    bias_grad = bias_grad[0]
    finals = all_sum(
        jnp.stack(
            [
                column_sums(grad_stream),
                column_sums(grad_stream * standard),
                column_sums(grad_normed * unit),
                column_sums(grad_normed),
                column_sums(grad_hidden * middle_unit),
                column_sums(grad_hidden),
                column_sums(grad_attended),
                column_sums(grad_mixed),
            ]
        )
    )
    tokens_grad = unwindows(
        inverse * (grad_stream - valid / count_valid * (finals[0] + finals[1] * standard))
    )
    return (
        layer_output,
        tokens_grad,
        finals[2],
        finals[3],
        qkv_weight_grads[0],
        bias_grad[:width],
        qkv_weight_grads[1],
        qkv_weight_grads[2],
        bias_grad[width : 2 * width],
        output_weight_grad,
        finals[6],
        finals[4],
        finals[5],
        up_weight_grad,
        bias_grad[2 * width :],
        down_weight_grad,
        finals[7],
    )


def fast_shards(
    tokens,
    cotangent,
    item_lengths,
    item_group,
    group_count,
    grid_scale,
    norm_gain,
    norm_shift,
    query_weight,
    query_bias,
    key_weight,
    value_weight,
    value_bias,
    output_weight,
    output_bias,
    hidden_gain,
    hidden_shift,
    up_weight,
    up_bias,
    down_weight,
    down_bias,
):
    rows = 2 * WINDOW + 96
    saved = forward(
        (item_lengths, item_group, group_count, grid_scale),
        [
            v[None, :]
            for v in (
                norm_gain,
                norm_shift,
                output_bias,
                hidden_gain,
                hidden_shift,
                query_bias,
                value_bias,
                up_bias,
            )
        ],
        tokens,
        cotangent,
        (query_weight, key_weight, value_weight, output_weight, up_weight, down_weight),
        rows,
    )
    reduced, finals, layer_output, tokens_grad = backward(
        (item_lengths, item_group, group_count),
        [v[None, :] for v in (norm_gain, hidden_gain, down_bias)],
        saved[2],
        saved[:2] + saved[3:],
        tokens.shape[0],
    )
    (
        down_weight_grad,
        up_weight_grad,
        output_weight_grad,
        query_weight_grad,
        key_weight_grad,
        value_weight_grad,
        layer_output,
        tokens_grad,
        *vectors,
    ) = finish(reduced, finals, layer_output, tokens_grad, query_weight.shape[1])
    vectors = [v.reshape(-1) for v in vectors]
    return (
        layer_output,
        tokens_grad,
        vectors[2],
        vectors[3],
        query_weight_grad,
        vectors[8],
        key_weight_grad,
        value_weight_grad,
        vectors[9],
        output_weight_grad,
        vectors[6],
        vectors[4],
        vectors[5],
        up_weight_grad,
        vectors[10],
        down_weight_grad,
        vectors[7],
    )


def shards(*args):
    if lax.axis_size("dp") == 8 and lax.axis_size("mp") == 4 and args[0].shape == (512, D):
        return fast_shards(*args)
    return general_shards(*args)


def solution(mesh):
    rows = P(("dp", "mp"), None)
    columns = P(None, "mp")
    return jax.shard_map(
        shards,
        mesh=mesh,
        in_specs=(
            rows,
            rows,
            P("dp"),
            P("dp"),
            P(),
            P(),
            P(),
            P(),
            columns,
            P("mp"),
            columns,
            columns,
            P("mp"),
            P("mp", None),
            P(),
            P(),
            P(),
            columns,
            P("mp"),
            P("mp", None),
            P(),
        ),
        out_specs=(
            rows,
            rows,
            P(),
            P(),
            columns,
            P("mp"),
            columns,
            columns,
            P("mp"),
            P("mp", None),
            P(),
            P(),
            P(),
            columns,
            P("mp"),
            P("mp", None),
            P(),
        ),
        check_vma=False,
    )
```

```python
import functools
import math

import jax
import jax.numpy as jnp
from jax import lax
from jax.experimental import pallas as pl
from jax.experimental.pallas import tpu as pltpu
from jax.sharding import PartitionSpec as P

D = 1024
HEAD_DIM = 64
SIDE = 14
PAIRS = 8
PAIR_LEN = 245
WINDOW = 256
BF = jnp.bfloat16
F32 = jnp.float32
PADDING = 88


def dot(a, b):
    return lax.dot_general(a, b, (((1,), (0,)), ((), ())), preferred_element_type=F32)


def dot_rows(a, b):
    return lax.dot_general(a, b, (((0,), (0,)), ((), ())), preferred_element_type=F32)


def dot_cols(a, b):
    return lax.dot_general(a, b, (((1,), (1,)), ((), ())), preferred_element_type=F32)


def swap_mp(v, mask):
    count = lax.axis_size("mp")
    return lax.ppermute(v, "mp", [(i, i ^ mask) for i in range(count)])


def swap_dp(v, mask):
    count = lax.axis_size("dp")
    return lax.ppermute(v, "dp", [(i, i ^ mask) for i in range(count)])


def dp_bits():
    return lax.axis_size("dp").bit_length() - 1


def all_sum(v):
    v = v + swap_mp(v, 1) + swap_mp(v, 2) + swap_mp(v, 3)
    bit = 0
    bits = dp_bits()
    while bit < bits:
        if bit + 1 < bits:
            v = v + swap_dp(v, 1 << bit) + swap_dp(v, 2 << bit) + swap_dp(v, 3 << bit)
            bit += 2
        else:
            v = v + swap_dp(v, 1 << bit)
            bit += 1
    return v


def dp_bit(bit):
    return (lax.axis_index("dp") >> bit) & 1


def join(mine, other, bit):
    return jnp.where(
        dp_bit(bit) == 0,
        jnp.concatenate([mine, other], axis=0),
        jnp.concatenate([other, mine], axis=0),
    )


def chunk_index():
    index = jnp.int32(0)
    for bit in range(dp_bits()):
        index = index * 2 + dp_bit(bit)
    return index


def fetch_across(w):
    rows = w.shape[0] // lax.axis_size("dp")
    mine = lax.dynamic_slice_in_dim(w, chunk_index() * rows, rows, axis=0)
    got = swap_mp(mine, 2)
    for bit in reversed(range(dp_bits())):
        got = join(got, swap_dp(got, 1 << bit), bit)
    return got


def reduce_pieces(pieces):
    half = pieces[1].shape[0]
    got = swap_mp(jnp.concatenate([pieces[1], pieces[3]], axis=0), 1)
    across = pieces[2].astype(F32) + got[half:].astype(F32)
    own = pieces[0].astype(F32) + got[:half].astype(F32)
    total = own + swap_mp(across.astype(BF), 2).astype(F32)
    for bit in range(dp_bits()):
        size = total.shape[0] // 2
        side = dp_bit(bit)
        send = lax.dynamic_slice_in_dim(total, (1 - side) * size, size, axis=0).astype(BF)
        keep = lax.dynamic_slice_in_dim(total, side * size, size, axis=0)
        total = keep + swap_dp(send, 1 << bit).astype(F32)
    total = total.astype(BF)
    for bit in reversed(range(dp_bits())):
        total = join(total, swap_dp(total, 1 << bit), bit)
    return total.astype(F32)


def stats(v):
    mean = jnp.mean(v, axis=-1, keepdims=True)
    center = v - mean
    spread = jnp.mean(center * center, axis=-1, keepdims=True)
    inverse = lax.rsqrt(spread + 1e-06)
    return center * inverse, inverse


def norm_back(grad, unit, inverse, gain):
    f = grad * gain
    return inverse * (
        f
        - jnp.mean(f, axis=-1, keepdims=True)
        - unit * jnp.mean(f * unit, axis=-1, keepdims=True)
    )


def blocks_of(rows):
    return [(first, min(WINDOW, rows - first)) for first in range(0, rows, WINDOW)]


def head_scores(qkv_ref, same, first, size, h, width):
    q = qkv_ref[first : first + size, h * HEAD_DIM : (h + 1) * HEAD_DIM]
    k = qkv_ref[first : first + size, width + h * HEAD_DIM : width + (h + 1) * HEAD_DIM]
    v = qkv_ref[first : first + size, 2 * width + h * HEAD_DIM : 2 * width + (h + 1) * HEAD_DIM]
    scores = jnp.where(same, dot_cols(q, k) * (1.0 / math.sqrt(HEAD_DIM)), -1e30)
    weights = jnp.exp(scores - jnp.max(scores, axis=-1, keepdims=True))
    weights = weights * (1.0 / jnp.sum(weights, axis=-1, keepdims=True))
    return q, k, v, weights


def attend_kernel(qkv_ref, col_ref, row_ref, out_ref):
    rows, width = out_ref.shape
    for first, size in blocks_of(rows):
        same = col_ref[first : first + size, :] == row_ref[:, first : first + size]
        for h in range(width // HEAD_DIM):
            q, k, v, weights = head_scores(qkv_ref, same, first, size, h, width)
            out_ref[first : first + size, h * HEAD_DIM : (h + 1) * HEAD_DIM] = dot(
                weights.astype(BF), v
            ).astype(BF)


def attend_back_kernel(qkv_ref, grad_ref, col_ref, row_ref, out_ref):
    rows, width = grad_ref.shape
    factor = 1.0 / math.sqrt(HEAD_DIM)
    for first, size in blocks_of(rows):
        same = col_ref[first : first + size, :] == row_ref[:, first : first + size]
        for h in range(width // HEAD_DIM):
            q, k, v, weights = head_scores(qkv_ref, same, first, size, h, width)
            grad = grad_ref[first : first + size, h * HEAD_DIM : (h + 1) * HEAD_DIM]
            soft = dot_cols(grad, v)
            center = jnp.sum(weights * soft, axis=-1, keepdims=True)
            grad_scores = (weights * (soft - center)).astype(BF)
            for part, value in enumerate(
                (
                    dot(grad_scores, k) * factor,
                    dot_rows(grad_scores, q) * factor,
                    dot_rows(weights.astype(BF), grad),
                )
            ):
                lane = part * width + h * HEAD_DIM
                out_ref[first : first + size, lane : lane + HEAD_DIM] = value.astype(BF)


def attend(qkv, owner_col, owner_row, groups):
    rows, width = qkv.shape[0], qkv.shape[1] // (3 * groups)
    return pl.pallas_call(
        attend_kernel,
        grid=(groups,),
        in_specs=[
            pl.BlockSpec((rows, 3 * width), lambda r: (0, r)),
            pl.BlockSpec((rows, 1), lambda r: (0, 0)),
            pl.BlockSpec((1, rows), lambda r: (0, 0)),
        ],
        out_specs=pl.BlockSpec((rows, width), lambda r: (0, r)),
        out_shape=jax.ShapeDtypeStruct((rows, groups * width), BF),
        name="attend",
    )(qkv, owner_col, owner_row)


def attend_back(qkv, grad, owner_col, owner_row, groups):
    rows, width = grad.shape[0], grad.shape[1] // groups
    return pl.pallas_call(
        attend_back_kernel,
        grid=(groups,),
        in_specs=[
            pl.BlockSpec((rows, 3 * width), lambda r: (0, r)),
            pl.BlockSpec((rows, width), lambda r: (0, r)),
            pl.BlockSpec((rows, 1), lambda r: (0, 0)),
            pl.BlockSpec((1, rows), lambda r: (0, 0)),
        ],
        out_specs=pl.BlockSpec((rows, 3 * width), lambda r: (0, r)),
        out_shape=jax.ShapeDtypeStruct((rows, 3 * groups * width), BF),
        name="attend_back",
    )(qkv, grad, owner_col, owner_row)


def gelu_parts(preact):
    phi = 0.5 * (1.0 + lax.erf(preact * (1.0 / math.sqrt(2.0))))
    slope = phi + preact * jnp.exp(-0.5 * preact * preact) * (1.0 / math.sqrt(2.0 * math.pi))
    return (preact * phi).astype(BF), slope


HALO = 80
ROUTE_TICKS = (
    (0, 0, 0, 0, 1, 1, 2, 2, 3, 4),
    (1, 1, 1, 1, 2, 3, 4, 5, 6, 7),
    (2, 2, 3, 3, 4, 5, 6, 7, 8, 9),
    (6, 6, 7, 7, 10, 12, 14, 16, 18, 20),
)
AT_HEADS, AT_PAIRED, AT_QUERY, AT_OUTPUT, AT_HIDDEN, AT_DOWN = 4, 8, 10, 16, 19, 23
MESH = pl.DeviceIdType.MESH


def places():
    mp = lax.axis_index("mp")
    dp = lax.axis_index("dp")
    y = dp % 2
    z = dp // 2
    sibling = mp + 1 - 2 * (mp % 2)
    opposite = mp + 2 - 4 * (mp // 2)
    across = opposite + 1 - 2 * (mp % 2)
    mp_peers = [{"mp": sibling}, {"mp": opposite}, {"mp": across}]
    y_peer = {"dp": dp + 1 - 2 * y}
    z_places = [(z + m) % 4 for m in (1, 2, 3)]
    z_peers = [{"dp": place * 2 + y} for place in z_places]
    return mp, y, z, mp_peers, y_peer, z_places, z_peers


def greet(peers):
    barrier = pltpu.get_barrier_semaphore()
    for peer in peers:
        pl.semaphore_signal(barrier, inc=1, device_id=peer, device_id_type=MESH)
    pl.semaphore_wait(barrier, len(peers))


def remote(source, target, send, recv, peer):
    return pltpu.make_async_remote_copy(
        src_ref=source,
        dst_ref=target,
        send_sem=send,
        recv_sem=recv,
        device_id=peer,
        device_id_type=MESH,
    )


def loop(count, body):
    def step(i, carry):
        body(i)
        return carry

    lax.fori_loop(0, count, step, 0)


def block_rows(i, size):
    return pl.ds(pl.multiple_of(i * size, size), size)


def start_all(copies):
    for copy in copies:
        copy.start()


def wait_recv_all(copies):
    for copy in copies:
        copy.wait_recv()


def item_of_rows(row, lengths, mp):
    window = row >> 8
    offset = row & (WINDOW - 1)
    length = jnp.where(window == 0, lengths[4 * mp], lengths[4 * mp + 2])
    second = jnp.where(offset >= length, 1, 0)
    in_pair = (window < 2) & (offset < PAIR_LEN)
    is_padding = (window == 2) & (offset < PADDING) & (mp == 3)
    return 2 * window + second, offset - second * length, in_pair, is_padding


def owner_of_rows(row, lengths, mp):
    item, _, in_pair, is_padding = item_of_rows(row, lengths, mp)
    return jnp.where(in_pair, item, jnp.where(is_padding, 16, -1))


def choose_item(item, values):
    result = jnp.where(item == 0, values[0], 0.0)
    for j in (1, 2, 3):
        result = jnp.where(item == j, values[j], result)
    return result


def joined(tiles, first):
    return jnp.concatenate([tiles[first + j : first + j + 1, :] for j in range(8)], axis=1)


def forward_kernel(
    lengths,
    groups,
    counts,
    scales,
    gain,
    shift,
    output_bias,
    hidden_gain,
    hidden_shift,
    query_bias,
    value_bias,
    up_bias,
    tokens_ref,
    cotangent_ref,
    query_ref,
    key_ref,
    value_ref,
    output_ref,
    up_ref,
    down_ref,
    tokens_out,
    cotangent_out,
    sums_out,
    stream_out,
    middle_out,
    normed_out,
    qkv_out,
    context_out,
    hidden_out,
    grad_mixed_out,
    active_out,
    grad_pre_out,
    wqkv_out,
    wo_out,
    wup_out,
    wdown_out,
    tokens_ext,
    cotangent_ext,
    tokens,
    cotangent,
    stream,
    middle,
    normed,
    qkv,
    context,
    hidden,
    grad_mixed,
    active,
    grad_pre,
    wqkv,
    wo,
    wup,
    wdown,
    sums,
    bias,
    part,
    from_mp,
    from_y,
    from_z,
    own_sem,
    halo_sem,
    store_sem,
    stat_send,
    stat_recv,
    bias_send,
    bias_recv,
    pair_send,
    pair_recv,
    x_send,
    x_recv,
    far_send,
    far_recv,
    near_send,
    near_recv,
    y_send,
    y_recv,
    fwd_send,
    fwd_recv,
):
    mp, y, z, mp_peers, y_peer, z_places, z_peers = places()
    sibling, opposite, _ = mp_peers
    rows_here = tokens_ref.shape[0]
    rows = tokens.shape[0]
    width = query_ref.shape[1]
    blocks = rows // 32

    items = (
        [(key_ref, first, D // 2, wqkv, width, width, False) for first in (0, D // 2)]
        + [(value_ref, first, D // 2, wqkv, 2 * width, width, False) for first in (0, D // 2)]
        + [(output_ref, 0, width, wo, 0, D, False)]
        + [(up_ref, first, D // 4, wup, 0, D, False) for first in range(0, D, D // 4)]
        + [(down_ref, first, D // 4, wdown, 0, D, False) for first in (3 * D // 4,)]
        + [(query_ref, 0, D, wqkv, 0, width, True), (down_ref, 0, 3 * D // 4, wdown, 0, D, True)]
    )
    relayed = range(10)
    QUERY, DOWN = 10, 11
    HEADS, OUTPUT, HIDDEN = (0, 1, 2, 3, QUERY), 4, (5, 6, 7, 8, 9, DOWN)
    everything = range(len(items))
    near = z % 2
    far = z // 2
    near_peer = {"dp": (z + 1 - 2 * near) * 2 + y}
    far_peer = {"dp": ((z + 2) % 4) * 2 + y}

    def source(i, start, size):
        return items[i][0].at[pl.ds(items[i][1] + start, size)]

    def place(i, r, start, size):
        _, first, _, ref, column, columns, _ = items[i]
        return ref.at[r, pl.ds(first + start, size), pl.ds(column, columns)]

    def part_of(i, first, eighths):
        size = items[i][2] // 8
        return pl.multiple_of(first * size, size), eighths * size

    own_copies = [
        pltpu.make_async_copy(
            source(i, 0, items[i][2]), place(i, 0, 0, items[i][2]), own_sem.at[i]
        )
        for i in everything
    ]
    pair_copies = [
        remote(
            source(i, 0, items[i][2]),
            place(i, 1, 0, items[i][2]),
            pair_send.at[i],
            pair_recv.at[i],
            sibling,
        )
        for i in everything
    ]

    def x_copy(i):
        start, size = (
            (0, items[i][2]) if items[i][6] else part_of(i, y * 4 + near * 2 + far, 1)
        )
        return remote(
            source(i, start, size), place(i, 2, start, size), x_send.at[i], x_recv.at[i], opposite
        )

    def hop(i, first, eighths, send, recv, peer):
        start, size = part_of(i, first, eighths)
        view = place(i, 2, start, size)
        return remote(view, view, send.at[i], recv.at[i], peer)

    def far_copy(i):
        return hop(i, y * 4 + near * 2 + far, 1, far_send, far_recv, far_peer)

    def near_copy(i):
        return hop(i, y * 4 + near * 2, 2, near_send, near_recv, near_peer)

    def y_copy(i):
        return hop(i, y * 4, 4, y_send, y_recv, y_peer)

    def fwd_copy(i):
        size = items[i][2]
        return remote(
            place(i, 2, 0, size), place(i, 3, 0, size), fwd_send.at[i], fwd_recv.at[i], sibling
        )

    route = (x_copy, far_copy, near_copy, y_copy, fwd_copy)

    keep = [
        pltpu.make_async_copy(ref, ext.at[pl.ds(HALO, rows_here)], halo_sem.at[which, 2])
        for which, (ref, ext) in enumerate(
            ((tokens_ref, tokens_ext), (cotangent_ref, cotangent_ext))
        )
    ]
    start_all(keep)
    start_all(own_copies)
    bias[0, 0:1, :] = query_bias[...]
    bias[0, 1:2, :] = value_bias[...]
    for j in range(4):
        bias[0, 2 + j : 3 + j, :] = up_bias[:, j * width : (j + 1) * width]
    bias[0, 6:8, :] = jnp.zeros((2, width), F32)

    weights = [counts[groups[4 * mp + j]].astype(F32) for j in range(4)]
    weight_part = weights[0] + weights[1] + weights[2] + weights[3]
    keep[0].wait()

    def add_rows(i, carry):
        block = tokens_ext[pl.ds(pl.multiple_of(HALO + i * 16, 16), 16), :].astype(F32)
        row = mp * rows_here + i * 16 + lax.broadcasted_iota(jnp.int32, (16, 1), 0)
        kept = jnp.where(row < PAIRS * PAIR_LEN, block, 0.0)
        return carry[0] + kept, carry[1] + kept * block

    zero = jnp.zeros((16, D), F32)
    first, second = lax.fori_loop(0, rows_here // 16, add_rows, (zero, zero))
    first = jnp.sum(first, axis=0, keepdims=True)
    second = jnp.sum(second, axis=0, keepdims=True)
    for j in range(8):
        part[0, j : j + 1, :] = first[:, j * 128 : (j + 1) * 128]
        part[0, 8 + j : 9 + j, :] = second[:, j * 128 : (j + 1) * 128]
    part[0, 16:24, :] = jnp.zeros((8, 128), F32) + weight_part
    greet(mp_peers + [y_peer] + z_peers)

    sums_a = [
        remote(part.at[0], from_mp.at[m], stat_send.at[0, m], stat_recv.at[0, m], peer)
        for m, peer in enumerate(mp_peers)
    ]
    start_all(sums_a)
    after = {"mp": (mp + 1) % 4}
    halo_copies = [
        remote(
            ref.at[pl.ds(rows_here - HALO, HALO)],
            ext.at[pl.ds(0, HALO)],
            halo_sem.at[which, 0],
            halo_sem.at[which, 1],
            after,
        )
        for which, (ref, ext) in enumerate(
            ((tokens_ref, tokens_ext), (cotangent_ref, cotangent_ext))
        )
    ]
    bias_copies = [
        remote(bias.at[0], bias.at[r + 1], bias_send.at[r], bias_recv.at[r], peer)
        for r, peer in enumerate(mp_peers)
    ]
    start_all(halo_copies + bias_copies)
    start_all([x_copy(i) for i in everything])
    start_all([pair_copies[i] for i in HEADS + (OUTPUT,) + HIDDEN])
    sums_b = [
        remote(part.at[1], from_y.at[0], stat_send.at[1, 0], stat_recv.at[1, 0], y_peer)
    ]
    sums_c = [
        remote(part.at[2], from_z.at[m], stat_send.at[2, m], stat_recv.at[2, m], peer)
        for m, peer in enumerate(z_peers)
    ]

    def position_table():
        place_id = lax.broadcasted_iota(jnp.int32, (64, 1), 0)
        table_scale = choose_item(
            place_id >> 4, [scales[groups[4 * mp + j]] for j in range(4)]
        )
        quarter = D // 4
        lane = lax.broadcasted_iota(jnp.int32, (1, quarter), 1).astype(F32)
        frequency = jnp.exp(-math.log(10000.0) * lane / quarter)
        angle = ((place_id & 15).astype(F32) * table_scale) * frequency
        table = jnp.concatenate([jnp.sin(angle), jnp.cos(angle)], axis=1)
        row = lax.broadcasted_iota(jnp.int32, (rows, 64), 0)
        column = lax.broadcasted_iota(jnp.int32, (rows, 64), 1)
        item, position, in_pair, _ = item_of_rows(row, lengths, mp)
        across = (position * 9363) >> 17
        for half, code in enumerate((across, position - SIDE * across)):
            chosen = jnp.where(in_pair & (column == item * 16 + code), 1.0, 0.0)
            stream[:, half * 2 * quarter : (half + 1) * 2 * quarter] = lax.dot_general(
                chosen,
                table,
                (((1,), (0,)), ((), ())),
                precision=lax.Precision.HIGHEST,
                preferred_element_type=F32,
            )

    def place_rows():
        wait_recv_all(halo_copies)
        keep[1].wait()
        own_len = 2 * PAIR_LEN
        row = lax.broadcasted_iota(jnp.int32, (rows, HALO + rows_here), 0)
        column = lax.broadcasted_iota(jnp.int32, (rows, HALO + rows_here), 1)
        window = row >> 8
        offset = row & (WINDOW - 1)
        wanted = HALO - (rows_here - own_len) * mp + window * PAIR_LEN + offset
        tail = jnp.where(mp == 3, HALO + rows_here - PADDING, 4096) + offset
        wanted = jnp.where(window < 2, jnp.where(offset < PAIR_LEN, wanted, -1), tail)
        chosen = jnp.where(column == wanted, 1.0, 0.0).astype(BF)
        tokens[...] = dot(chosen, tokens_ext[...]).astype(BF)
        cotangent[...] = dot(chosen, cotangent_ext[...]).astype(BF)

    def norm_rows(first, count):
        slices = lax.axis_size("dp")
        count_valid = slices * PAIRS * PAIR_LEN
        column_mean = joined(sums, 0) / count_valid
        spread = joined(sums, 8) / count_valid - column_mean * column_mean
        inverse = lax.rsqrt(spread + 1e-05)
        mean_weight = sums[16:17, 0:1] / (slices * 16)

        def first_norm(i):
            here = block_rows(i, 32)
            value = (tokens[here, :].astype(F32) - column_mean) * inverse + stream[here, :]
            stream[here, :] = value
            unit, _ = stats(value)
            normed[here, :] = (unit * gain[...] + shift[...]).astype(BF)
            row = i * 32 + lax.broadcasted_iota(jnp.int32, (32, 1), 0)
            item, _, in_pair, _ = item_of_rows(row, lengths, mp)
            row_weight = jnp.where(in_pair, choose_item(item, weights), 0.0) / mean_weight
            grad_mixed[here, :] = (cotangent[here, :].astype(F32) * row_weight).astype(BF)

        def body(i):
            first_norm(first + i)

        loop(count, body)

    def group_stores(value, target, r):
        return value.at[r], target.at[r]

    def column_stores(value, target, r):
        columns = pl.ds(r * D, D)
        return value.at[:, columns], target.at[:, columns]

    plan = (
        [
            (AT_HEADS, ref, target)
            for ref, target in (
                (tokens, tokens_out),
                (cotangent, cotangent_out),
                (sums, sums_out),
                (stream, stream_out),
                (normed, normed_out),
                (grad_mixed, grad_mixed_out),
            )
        ]
        + [
            (AT_OUTPUT, ref, target)
            for ref, target in ((qkv, qkv_out), (context, context_out), (wqkv, wqkv_out))
        ]
        + [
            (AT_HIDDEN, ref, target)
            for ref, target in ((middle, middle_out), (hidden, hidden_out), (wo, wo_out))
        ]
        + [
            (when,) + group_stores(ref, target, r)
            for r, when in enumerate((AT_PAIRED, AT_PAIRED, AT_HIDDEN + 6, AT_HIDDEN + 6))
            for ref, target in ((wup, wup_out), (wdown, wdown_out))
        ]
        + [
            (AT_HIDDEN + 2 * r + 2,) + column_stores(ref, target, r)
            for r in range(4)
            for ref, target in ((active, active_out), (grad_pre, grad_pre_out))
        ]
    )
    stores = [
        pltpu.make_async_copy(ref, target, store_sem.at[i])
        for i, (_, ref, target) in enumerate(plan)
    ]
    last_tick = AT_HIDDEN + 8

    def head_product(r):
        base = r * 3 * width
        for n in range(3):
            value = dot(normed[...], wqkv[r, :, n * width : (n + 1) * width])
            if n != 1:
                value = value + bias[r, n // 2 : n // 2 + 1, :]
            qkv[:, pl.ds(pl.multiple_of(base + n * width, width), width)] = value.astype(BF)

    def head_pair(r, p):
        base = r * 3 * width
        lanes = [pl.ds(pl.multiple_of(base + n * width + p * 128, 128), 128) for n in range(3)]
        target = pl.ds(pl.multiple_of(r * width + p * 128, 128), 128)
        for first, size in blocks_of(rows):
            here = pl.ds(first, size)
            same = owner_of_rows(
                first + lax.broadcasted_iota(jnp.int32, (size, 1), 0), lengths, mp
            ) == owner_of_rows(first + lax.broadcasted_iota(jnp.int32, (1, size), 1), lengths, mp)
            q, k, v = [qkv[here, lane] for lane in lanes]
            results = []
            for h in range(2):
                cut = slice(h * HEAD_DIM, (h + 1) * HEAD_DIM)
                low = softmax_rows(q[:, cut], k[:, cut], same).astype(BF)
                results.append(dot(low, v[:, cut]).astype(BF))
            context[here, target] = jnp.concatenate(results, axis=1)

    def attention_output(n):
        columns = block_rows(n, 256)
        value = stream[:, columns] + output_bias[:, columns]
        for r in range(4):
            value = value + dot(context[:, r * width : (r + 1) * width], wo[r, :, columns])
        middle[:, columns] = value

    def second_norm(i):
        here = block_rows(i, 32)
        unit, _ = stats(middle[here, :])
        hidden[here, :] = (unit * hidden_gain[...] + hidden_shift[...]).astype(BF)

    def hidden_tile(r, n):
        columns = block_rows(n, 256)
        target = pl.ds(pl.multiple_of(r * D + n * 256, 256), 256)
        preact = dot(hidden[...], wup[r, :, columns]) + bias[r, pl.ds(2 + n, 1), :]
        value, slope = gelu_parts(preact)
        active[:, target] = value
        grad = dot_cols(grad_mixed[...], wdown[r, columns, :])
        grad_pre[:, target] = (grad * slope).astype(BF)

    actions = {}

    def at(k, action):
        actions.setdefault(k, []).append(action)

    for stage in reversed(range(4)):
        for i in relayed:

            def advance(i=i, stage=stage):
                route[stage](i).wait_recv()
                route[stage + 1](i).start()

            at(ROUTE_TICKS[stage][i], advance)

    def pass_on(i):
        x_copy(i).wait_recv()
        fwd_copy(i).start()

    def sums_stage(target, copies, slots, following):
        def action():
            value = part[target - 1]
            for m, copy in enumerate(copies):
                copy.wait_recv()
                value = value + slots[m]
            if following:
                part[target] = value
                start_all(following)
            else:
                sums[...] = value

        return action

    def received(indices, copies):
        def action():
            for i in indices:
                copies(i)

        return action

    def own(i):
        own_copies[i].wait()

    def paired(i):
        pair_copies[i].wait_recv()

    def forwarded(i):
        fwd_copy(i).wait_recv()

    at(0, sums_stage(1, sums_a, from_mp, sums_b))
    at(1, sums_stage(2, sums_b, from_y, sums_c))
    at(2, sums_stage(3, sums_c, from_z, None))
    at(AT_HEADS, lambda: wait_recv_all(bias_copies))
    at(AT_HEADS, received(HEADS, own))
    at(AT_HEADS + 3, received(HEADS, paired))
    at(AT_QUERY, lambda: pass_on(QUERY))
    at(AT_HEADS + 9, received(HEADS, forwarded))
    at(AT_OUTPUT, received((OUTPUT,), own))
    at(AT_OUTPUT, received((OUTPUT,), paired))
    at(AT_OUTPUT, received((OUTPUT,), forwarded))
    at(AT_PAIRED, received(HIDDEN, own))
    at(AT_PAIRED, received(HIDDEN, paired))
    at(AT_DOWN, lambda: pass_on(DOWN))
    at(AT_HIDDEN + 6, received(HIDDEN, forwarded))
    for copy, (when, _, _) in zip(stores, plan):
        if when < last_tick:
            at(when, copy.start)

    def tick(k, carry):
        for when, todo in sorted(actions.items()):

            @pl.when(k == when)
            def _(todo=todo):
                for action in todo:
                    action()

        @pl.when(k == 0)
        def _():
            position_table()

        @pl.when(k == 1)
        def _():
            place_rows()

        @pl.when((k >= 2) & (k < 4))
        def _():
            norm_rows((k - 2) * 10, 10 - (k - 2))

        step = k - AT_HEADS

        @pl.when((step >= 0) & (step < 12) & (step % 3 == 0))
        def _():
            head_product(step // 3)

        @pl.when((step >= 0) & (step < 12) & (step % 3 > 0))
        def _():
            head_pair(step // 3, step % 3 - 1)

        @pl.when((k >= AT_OUTPUT) & (k < AT_OUTPUT + 2))
        def _():
            def body(n):
                attention_output(2 * (k - AT_OUTPUT) + n)

            loop(2, body)

        @pl.when(k == AT_OUTPUT + 2)
        def _():
            loop(blocks, second_norm)

        @pl.when((k >= AT_HIDDEN) & (k < AT_HIDDEN + 8))
        def _():
            def body(n):
                j = 2 * (k - AT_HIDDEN) + n
                hidden_tile(j // 4, j % 4)

            loop(2, body)

        return carry

    lax.fori_loop(0, last_tick, tick, 0)
    start_all([copy for copy, (when, _, _) in zip(stores, plan) if when >= last_tick])
    for i in everything:
        pair_copies[i].wait_send()
        x_copy(i).wait_send()
        fwd_copy(i).wait_send()
        if not items[i][6]:
            for copy in (far_copy, near_copy, y_copy):
                copy(i).wait_send()
    for copy in bias_copies + halo_copies + sums_a + sums_b + sums_c:
        copy.wait_send()
    for copy in stores:
        copy.wait()


def softmax_rows(q, k, same):
    scores = jnp.where(same, dot_cols(q, k) * (1.0 / math.sqrt(HEAD_DIM)), -1e30)
    weights = jnp.exp(scores - jnp.max(scores, axis=-1, keepdims=True))
    return weights * (1.0 / jnp.sum(weights, axis=-1, keepdims=True))


def forward(smalls, vectors, tokens, cotangent, weights, rows):
    width = weights[0].shape[1]
    shape = jax.ShapeDtypeStruct
    full = shape((rows, D), F32)
    low = shape((rows, D), BF)
    wide = shape((rows, 4 * D), BF)
    outs = (
        low,
        low,
        shape((24, 128), F32),
        full,
        full,
        low,
        shape((rows, 12 * width), BF),
        low,
        low,
        low,
        wide,
        wide,
        shape((4, D, 3 * width), BF),
        shape((4, width, D), BF),
        shape((4, D, D), BF),
        shape((4, D, D), BF),
    )
    scratch = [shape((HALO + tokens.shape[0], D), BF)] * 2 + [
        low,
        low,
        full,
        full,
        low,
        outs[6],
        low,
        low,
        low,
        wide,
        wide,
    ]
    scratch += list(outs[12:]) + [
        shape((24, 128), F32),
        shape((4, 8, width), F32),
        shape((3, 24, 128), F32),
        shape((3, 24, 128), F32),
        shape((1, 24, 128), F32),
        shape((3, 24, 128), F32),
    ]
    dma = pltpu.SemaphoreType.DMA
    any_space = pl.BlockSpec(memory_space=pl.ANY)
    return pl.pallas_call(
        forward_kernel,
        out_shape=outs,
        in_specs=[pl.BlockSpec(memory_space=pltpu.SMEM)] * 4
        + [pl.BlockSpec(memory_space=pltpu.VMEM)] * 8
        + [any_space] * 8,
        out_specs=(any_space,) * len(outs),
        scratch_shapes=[pltpu.VMEM(v.shape, v.dtype) for v in scratch]
        + [
            dma((13,)),
            dma((2, 3)),
            dma((28,)),
            dma((3, 3)),
            dma((3, 3)),
            dma((3,)),
            dma((3,)),
        ]
        + [dma((13,))] * 12,
        compiler_params=pltpu.CompilerParams(
            collective_id=1, has_side_effects=True, vmem_limit_bytes=67043328
        ),
        name="forward",
    )(*smalls, *vectors, tokens, cotangent, *weights)


CHUNK = 128
CHUNKS = 24
FINISH_STEPS = 2
STAGE_DELAY = (0, 1, 3, 5, 7, 9, 11)
TICK_HIDDEN, TICK_SECOND, TICK_CONTEXT, TICK_HEADS = 1, 5, 6, 7
TICK_NORMED, TICK_FIRST, TICK_MIXED = 15, 19, 20
TICK_SUMS = (19, 21, 23, 25)
TICK_NEXT, TICK_LAYER, TICK_TOKENS = 26, 28, 29


def backward_kernel(
    lengths,
    groups,
    counts,
    gain,
    hidden_gain,
    down_bias,
    sums,
    tokens_ref,
    cotangent_ref,
    stream_ref,
    middle_ref,
    normed_ref,
    qkv_ref,
    context_ref,
    hidden_ref,
    grad_mixed_ref,
    active_ref,
    grad_pre_ref,
    wqkv_ref,
    wo_ref,
    wup_ref,
    wdown_ref,
    reduced_out,
    finals_out,
    layer_out,
    tokens_grad_out,
    made,
    pair,
    across,
    over_y,
    over_z,
    final,
    act,
    grad_pre,
    hidden,
    grad_mixed,
    context,
    normed,
    grad_attended,
    qkv,
    grad_context,
    rowbuf,
    gradient,
    trunk,
    stream,
    weight,
    packet,
    from_mp,
    from_y,
    from_z,
    layer_next,
    tokens_next,
    load_sem,
    act_sem,
    weight_sem,
    pair_send,
    pair_recv,
    across_send,
    across_recv,
    y_send,
    y_recv,
    z_send,
    z_recv,
    back_z_send,
    back_z_recv,
    back_y_send,
    back_y_recv,
    out_sem,
    stat_send,
    stat_recv,
    next_send,
    next_recv,
):
    mp, y, z, mp_peers, y_peer, z_places, z_peers = places()
    sibling, opposite, _ = mp_peers
    half = CHUNK // 2
    eighth = CHUNK // 8
    rows = normed.shape[0]
    rows_here = layer_out.shape[0]
    width = context.shape[1] // 4
    blocks = rows // 32

    loads = {
        name: pltpu.make_async_copy(source, target, load_sem.at[i])
        for i, (name, source, target) in enumerate(
            (
                ("grad_mixed", grad_mixed_ref, grad_mixed),
                ("grad_pre", grad_pre_ref, grad_pre),
                ("middle", middle_ref, trunk),
                ("cotangent", cotangent_ref, rowbuf),
                ("qkv", qkv_ref, qkv),
                ("hidden", hidden_ref, hidden),
                ("context", context_ref, context),
                ("normed", normed_ref, normed),
                ("stream", stream_ref, stream),
                ("tokens", tokens_ref, rowbuf),
                ("active", active_ref, grad_pre),
                ("middle again", middle_ref, stream),
                ("layer", normed.at[pl.ds(0, rows_here)], layer_out),
                ("tokens_grad", trunk.at[pl.ds(0, rows_here)], tokens_grad_out),
            )
        )
    }

    def act_loads(c):
        return [
            pltpu.make_async_copy(
                active_ref.at[:, pl.ds(pl.multiple_of(r * D + c * CHUNK, CHUNK), CHUNK)],
                act.at[c % 2, r],
                act_sem.at[c % 2, r],
            )
            for r in range(4)
        ]

    def weight_load(s):
        if s < 4:
            source = wup_ref.at[s]
        elif s == 4:
            source = wo_ref
        elif s < 9:
            source = wqkv_ref.at[s - 5]
        else:
            source = wdown_ref.at[s - 9]
        target = weight.at[s % 2, :, pl.ds(0, 3 * width)] if 5 <= s < 9 else weight.at[s % 2]
        return pltpu.make_async_copy(source, target, weight_sem.at[s % 2])

    for c in range(2):
        start_all(act_loads(c))
    loads["grad_mixed"].start()
    weight_load(0).start()
    loads["grad_pre"].start()
    weight_load(1).start()
    for name in ("middle", "cotangent", "qkv", "hidden", "context", "normed", "stream"):
        loads[name].start()
    greet(mp_peers + [y_peer] + z_peers)

    weights = [counts[groups[4 * mp + j]].astype(F32) for j in range(4)]
    slices = lax.axis_size("dp")
    count_valid = slices * PAIRS * PAIR_LEN
    column_mean = joined(sums, 0) / count_valid
    spread = joined(sums, 8) / count_valid - column_mean * column_mean
    inverse = lax.rsqrt(spread + 1e-05)
    mean_weight = sums[16:17, 0:1] / (slices * 16)

    def pair_copy(c):
        return remote(
            made.at[c % 2, pl.ds(0, 2)], pair.at[c], pair_send.at[c], pair_recv.at[c], sibling
        )

    def across_copy(c):
        return remote(
            pair.at[c, 1], across.at[c], across_send.at[c], across_recv.at[c], opposite
        )

    def y_copy(c):
        return remote(
            across.at[c, pl.ds(pl.multiple_of((1 - y) * half, half), half)],
            over_y.at[c],
            y_send.at[c],
            y_recv.at[c],
            y_peer,
        )

    def z_copies(c):
        return [
            remote(
                over_y.at[c, pl.ds(pl.multiple_of(place * eighth, eighth), eighth)],
                over_z.at[c, m],
                z_send.at[c, m],
                z_recv.at[c, m],
                peer,
            )
            for m, (place, peer) in enumerate(zip(z_places, z_peers))
        ]

    def back_z_copies(c):
        view = final.at[c, pl.ds(pl.multiple_of(y * half + z * eighth, eighth), eighth)]
        return [
            remote(view, view, back_z_send.at[c, m], back_z_recv.at[c, m], peer)
            for m, peer in enumerate(z_peers)
        ]

    def back_y_copy(c):
        view = final.at[c, pl.ds(pl.multiple_of(y * half, half), half)]
        return remote(view, view, back_y_send.at[c], back_y_recv.at[c], y_peer)

    def out_copy(c):
        return pltpu.make_async_copy(final.at[c], reduced_out.at[c], out_sem.at[c])

    def make(c):
        @pl.when(c < 8)
        def _():
            for copy in act_loads(c):
                copy.wait()

        def one(j):
            r = 2 * j + 1 - 5 * (j // 2)

            def store(left, right):
                made[c % 2, j] = dot_rows(left, right).astype(BF)

            @pl.when(c < 8)
            def _():
                store(act[c % 2, r], grad_mixed[...])

            @pl.when((c >= 8) & (c < 16))
            def _():
                store(
                    hidden[:, block_rows(c - 8, CHUNK)], grad_pre[:, block_rows(r, D)]
                )

            @pl.when((c >= 16) & (c < 18))
            def _():
                store(context[:, block_rows(2 * r + c - 16, CHUNK)], grad_attended[...])

            @pl.when(c >= 18)
            def _():
                store(qkv[:, block_rows(6 * r + c - 18, CHUNK)], normed[...])

        loop(4, one)

        @pl.when(c < 6)
        def _():
            start_all(act_loads(c + 2))

    def add_pair(c):
        pair_copy(c).wait()

        def body(i):
            here = block_rows(i, 32)
            for which in (1, 0):
                pair[c, which, here, :] = (
                    pair[c, which, here, :].astype(F32)
                    + made[c % 2, 2 + which, here, :].astype(F32)
                ).astype(BF)

        loop(CHUNK // 32, body)

    def add_across(c):
        across_copy(c).wait_recv()

        def body(i):
            here = block_rows(i, 32)
            across[c, here, :] = (
                across[c, here, :].astype(F32) + pair[c, 0, here, :].astype(F32)
            ).astype(BF)

        loop(CHUNK // 32, body)

    def add_y(c):
        y_copy(c).wait_recv()

        def body(i):
            here = block_rows(i, 32)
            own = pl.ds(pl.multiple_of(y * half + i * 32, 32), 32)
            over_y[c, here, :] = (
                over_y[c, here, :].astype(F32) + across[c, own, :].astype(F32)
            ).astype(BF)

        loop(half // 32, body)

    def add_z(c):
        wait_recv_all(z_copies(c))
        value = over_y[c, block_rows(z, eighth), :].astype(F32)
        for m in range(3):
            value = value + over_z[c, m].astype(F32)
        final[c, pl.ds(pl.multiple_of(y * half + z * eighth, eighth), eighth), :] = value.astype(BF)

    handle = (
        make,
        add_pair,
        add_across,
        add_y,
        add_z,
        lambda c: wait_recv_all(back_z_copies(c)),
        lambda c: back_y_copy(c).wait_recv(),
    )
    send = (
        lambda c: [pair_copy(c)],
        lambda c: [across_copy(c)],
        lambda c: [y_copy(c)],
        z_copies,
        back_z_copies,
        lambda c: [back_y_copy(c)],
        lambda c: [out_copy(c)],
    )

    def hidden_step(r):
        left = block_rows(r, D)

        def tile(n):
            columns = block_rows(n, 256)
            value = dot_cols(grad_pre[:, left], weight[r % 2, columns, :])

            @pl.when(r == 0)
            def _():
                gradient[:, columns] = value

            @pl.when(r > 0)
            def _():
                gradient[:, columns] = gradient[:, columns] + value

        loop(4, tile)

    def fold(value):
        return jnp.sum(value.reshape(4, 8, D), axis=0)

    def put(index, value):
        for j in range(8):
            packet[0, 8 * index + j : 8 * index + j + 1, :] = value[:, j * 128 : (j + 1) * 128]

    def put_all(first, values):
        for i, value in enumerate(values):
            put(first + i, jnp.sum(value, axis=0, keepdims=True))

    def ones_dot(value):
        return dot(jnp.ones((16, rows), BF), value)[0:1, :]

    def row_weight_of(i):
        row = i * 32 + lax.broadcasted_iota(jnp.int32, (32, 1), 0)
        item, _, in_pair, _ = item_of_rows(row, lengths, mp)
        return jnp.where(in_pair, choose_item(item, weights), 0.0) / mean_weight, in_pair

    zero = jnp.zeros((8, D), F32)

    def second_norm_back():
        def body(i, carry):
            here = block_rows(i, 32)
            unit, scale = stats(trunk[here, :])
            grad = gradient[here, :]
            row_weight, _ = row_weight_of(i)
            value = rowbuf[here, :].astype(F32) * row_weight + norm_back(
                grad, unit, scale, hidden_gain[...]
            )
            trunk[here, :] = value
            low = value.astype(BF)
            grad_attended[here, :] = low
            return (
                carry[0] + fold(grad * unit),
                carry[1] + fold(grad),
                carry[2] + fold(low.astype(F32)),
            )

        put_all(4, lax.fori_loop(0, blocks, body, (zero, zero, zero)))
        put(7, ones_dot(grad_mixed[...]))

    def context_step():
        def tile(n):
            columns = block_rows(n, 256)
            grad_context[:, columns] = dot_cols(grad_attended[...], weight[0, columns, :]).astype(BF)

        loop(4, tile)

    def head_pair_back(index):
        r = index // 2
        p = index % 2
        lanes = [block_rows(6 * r + 2 * n + p, 128) for n in range(3)]
        source = block_rows(2 * r + p, 128)
        factor = 1.0 / math.sqrt(HEAD_DIM)
        for first, size in blocks_of(rows):
            here = pl.ds(first, size)
            same = owner_of_rows(
                first + lax.broadcasted_iota(jnp.int32, (size, 1), 0), lengths, mp
            ) == owner_of_rows(first + lax.broadcasted_iota(jnp.int32, (1, size), 1), lengths, mp)
            q, k, v = [qkv[here, lane] for lane in lanes]
            g = grad_context[here, source]
            results = []
            for h in range(2):
                cut = slice(h * HEAD_DIM, (h + 1) * HEAD_DIM)
                soft = softmax_rows(q[:, cut], k[:, cut], same)
                grad_soft = dot_cols(g[:, cut], v[:, cut])
                center = jnp.sum(soft * grad_soft, axis=-1, keepdims=True)
                grad_scores = (soft * (grad_soft - center)).astype(BF)
                results.append(
                    (
                        (dot(grad_scores, k[:, cut]) * factor).astype(BF),
                        (dot_rows(grad_scores, q[:, cut]) * factor).astype(BF),
                        dot_rows(soft.astype(BF), g[:, cut]).astype(BF),
                    )
                )
            for n in range(3):
                qkv[here, lanes[n]] = jnp.concatenate([results[0][n], results[1][n]], axis=1)

    def normed_step(r):
        left = qkv[:, block_rows(r, 3 * width)]

        def tile(n):
            columns = block_rows(n, 256)
            value = dot_cols(left, weight[(r + 1) % 2, columns, 0 : 3 * width])

            @pl.when(r == 0)
            def _():
                gradient[:, columns] = value

            @pl.when(r > 0)
            def _():
                gradient[:, columns] = gradient[:, columns] + value

        loop(4, tile)

    def first_norm_back():
        def body(i, carry):
            here = block_rows(i, 32)
            unit, scale = stats(stream[here, :])
            grad = gradient[here, :]
            value = trunk[here, :] + norm_back(grad, unit, scale, gain[...])
            standard = (rowbuf[here, :].astype(F32) - column_mean) * inverse
            gradient[here, :] = value
            return (
                carry[0] + fold(value),
                carry[1] + fold(value * standard),
                carry[2] + fold(grad * unit),
                carry[3] + fold(grad),
            )

        put_all(0, lax.fori_loop(0, blocks, body, (zero, zero, zero, zero)))
        for r in range(4):
            if r:
                packet[r, 0:64, :] = packet[0, 0:64, :]
            parts = [
                ones_dot(qkv[:, (3 * r + n) * width : (3 * r + n + 1) * width]) for n in (0, 2)
            ] + [
                ones_dot(grad_pre[:, r * D + n * width : r * D + (n + 1) * width]) for n in range(4)
            ]
            for i, value in enumerate(parts):
                for j in range(2):
                    packet[r, 64 + 2 * i + j : 65 + 2 * i + j, :] = value[
                        :, j * 128 : (j + 1) * 128
                    ]
            packet[r, 76:80, :] = jnp.zeros((4, 128), F32)

    def mixed_step(r):
        left = grad_pre[:, block_rows(r, D)]

        def tile(n):
            columns = block_rows(n, 256)
            stream[:, columns] = stream[:, columns] + dot(left, weight[(r + 1) % 2, :, columns])

        loop(4, tile)

    def layer_step():
        def body(i):
            here = block_rows(i, 32)
            hidden[here, :] = (stream[here, :] + down_bias[...]).astype(BF)

        loop(blocks, body)

    def exchange(stage, sources, peers, slots):
        return [
            remote(
                source, slots.at[m], stat_send.at[stage, m], stat_recv.at[stage, m], peer
            )
            for m, (source, peer) in enumerate(zip(sources, peers))
        ]

    sums_a = exchange(0, [packet.at[r] for r in (1, 2, 3)], mp_peers, from_mp)
    sums_b = exchange(1, [packet.at[4]], [y_peer], from_y)
    sums_c = exchange(2, [packet.at[5]] * 3, z_peers, from_z)

    def gather_sums(first, copies, slots, target):
        value = packet[first]
        for m, copy in enumerate(copies):
            copy.wait_recv()
            value = value + slots[m]
        packet[target] = value

    def tokens_step():
        total = joined(packet[6], 0), joined(packet[6], 8)

        def body(i):
            here = block_rows(i, 32)
            standard = (rowbuf[here, :].astype(F32) - column_mean) * inverse
            _, in_pair = row_weight_of(i)
            share = jnp.where(in_pair, 1.0 / count_valid, 0.0)
            gradient[here, :] = inverse * (
                gradient[here, :] - share * (total[0] + total[1] * standard)
            )

        loop(blocks, body)

    before = {"mp": (mp + 3) % 4}
    layer_next_copy = remote(
        hidden.at[pl.ds(0, HALO)], layer_next, next_send.at[0], next_recv.at[0], before
    )
    tokens_next_copy = remote(
        gradient.at[pl.ds(0, HALO)], tokens_next, next_send.at[1], next_recv.at[1], before
    )

    def choose_rows(count, first):
        row = lax.broadcasted_iota(jnp.int32, (rows_here, count), 0)
        column = lax.broadcasted_iota(jnp.int32, (rows_here, count), 1) + first
        place = row + (rows_here - 2 * PAIR_LEN) * mp
        after = jnp.where(mp == 3, 2 * WINDOW, rows) - 2 * PAIR_LEN
        wanted = jnp.where(
            place < PAIR_LEN,
            place,
            jnp.where(place < 2 * PAIR_LEN, place + (WINDOW - PAIR_LEN), place + after),
        )
        return jnp.where(column == wanted, 1.0, 0.0).astype(BF)

    def own_rows(value, following, target):
        chosen, chosen_next = choose_rows(rows, 0), choose_rows(HALO, rows)
        pairs = ((chosen, value), (chosen_next, following))

        def tile(n):
            columns = block_rows(n, 256)
            total = jnp.zeros((rows_here, 256), F32)
            for matrix, ref in pairs:
                block = ref[:, columns]
                high = block.astype(BF)
                total = total + dot(matrix, high)
                if ref.dtype == F32:
                    middle_part = block - high.astype(F32)
                    low = middle_part.astype(BF)
                    total = total + dot(matrix, low)
                    total = total + dot(matrix, (middle_part - low.astype(F32)).astype(BF))
            target[0:rows_here, columns] = total.astype(target.dtype)

        loop(4, tile)

    def work(k):
        for s in range(4):

            @pl.when(k == TICK_HIDDEN + s)
            def _(s=s):
                if s == 0:
                    loads["grad_pre"].wait()
                weight_load(s).wait()

        @pl.when((k >= TICK_HIDDEN) & (k < TICK_HIDDEN + 4))
        def _():
            hidden_step(k - TICK_HIDDEN)

        for s in range(4):

            @pl.when(k == TICK_HIDDEN + s)
            def _(s=s):
                weight_load(s + 2).start()

        @pl.when(k == TICK_SECOND)
        def _():
            loads["middle"].wait()
            loads["cotangent"].wait()
            second_norm_back()
            loads["tokens"].start()

        @pl.when(k == TICK_CONTEXT)
        def _():
            weight_load(4).wait()
            context_step()
            weight_load(6).start()
            loads["qkv"].wait()

        @pl.when((k >= TICK_HEADS) & (k < TICK_HEADS + 8))
        def _():
            head_pair_back(k - TICK_HEADS)

        for s in range(4):

            @pl.when(k == TICK_NORMED + s)
            def _(s=s):
                weight_load(5 + s).wait()

        @pl.when((k >= TICK_NORMED) & (k < TICK_NORMED + 4))
        def _():
            normed_step(k - TICK_NORMED)

        for s in range(4):

            @pl.when(k == TICK_NORMED + s)
            def _(s=s):
                weight_load(7 + s).start()

        @pl.when(k == TICK_FIRST)
        def _():
            loads["stream"].wait()
            loads["tokens"].wait()
            first_norm_back()
            loads["active"].start()
            loads["middle again"].start()
            start_all(sums_a)

        for s in range(4):

            @pl.when(k == TICK_MIXED + s)
            def _(s=s):
                if s == 0:
                    loads["active"].wait()
                    loads["middle again"].wait()
                weight_load(9 + s).wait()

        @pl.when((k >= TICK_MIXED) & (k < TICK_MIXED + 4))
        def _():
            mixed_step(k - TICK_MIXED)

        for s in range(2):

            @pl.when(k == TICK_MIXED + s)
            def _(s=s):
                weight_load(11 + s).start()

        @pl.when(k == TICK_MIXED + 3)
        def _():
            layer_step()

        @pl.when(k == TICK_NEXT)
        def _():
            layer_next_copy.start()
            tokens_next_copy.start()

        @pl.when(k == TICK_LAYER)
        def _():
            layer_next_copy.wait_recv()
            own_rows(hidden, layer_next, normed)
            loads["layer"].start()

        @pl.when(k == TICK_TOKENS)
        def _():
            tokens_next_copy.wait_recv()
            own_rows(gradient, tokens_next, trunk)
            loads["tokens_grad"].start()

        @pl.when(k == TICK_SUMS[1])
        def _():
            gather_sums(0, sums_a, from_mp, 4)
            start_all(sums_b)

        @pl.when(k == TICK_SUMS[2])
        def _():
            gather_sums(4, sums_b, from_y, 5)
            start_all(sums_c)

        @pl.when(k == TICK_SUMS[3])
        def _():
            gather_sums(5, sums_c, from_z, 6)
            finals_out[...] = packet[6]
            tokens_step()

    waits = {0: ("grad_mixed",), 8: ("hidden",), 16: ("context",), 18: ("normed",)}

    def tick(k, carry):
        for when, names in waits.items():

            @pl.when(k == when)
            def _(names=names):
                for name in names:
                    loads[name].wait()

        def staged(stage, actions):
            c = k - STAGE_DELAY[stage]

            @pl.when((c >= 0) & (c < CHUNKS))
            def _():
                actions[stage](c)

        sends = tuple(lambda c, f=f: start_all(f(c)) for f in send)
        for stage in (6, 5, 4, 3, 2):
            staged(stage, handle)
            staged(stage, sends)
        staged(0, handle)
        staged(1, handle)
        staged(0, sends)
        staged(1, sends)
        work(k)
        return carry

    lax.fori_loop(0, CHUNKS + STAGE_DELAY[-1], tick, 0)

    def finish(c):
        across_copy(c).wait_send()
        y_copy(c).wait_send()
        for copy in z_copies(c) + back_z_copies(c):
            copy.wait_send()
        back_y_copy(c).wait_send()
        out_copy(c).wait()

    loop(CHUNKS, finish)
    for copy in sums_a + sums_b + sums_c:
        copy.wait_send()
    layer_next_copy.wait_send()
    tokens_next_copy.wait_send()
    loads["layer"].wait()
    loads["tokens_grad"].wait()


def backward(smalls, vectors, sums, saved, rows_here):
    (
        tokens,
        cotangent,
        stream,
        middle,
        normed,
        qkv,
        context,
        hidden,
        grad_mixed,
        active,
        grad_pre,
        wqkv,
        wo,
        wup,
        wdown,
    ) = saved
    rows = normed.shape[0]
    shape = jax.ShapeDtypeStruct
    low = shape((rows, D), BF)
    full = shape((rows, D), F32)
    packed = shape((80, 128), F32)
    scratch = [
        shape((2, 4, CHUNK, D), BF),
        shape((CHUNKS, 2, CHUNK, D), BF),
        shape((CHUNKS, CHUNK, D), BF),
        shape((CHUNKS, CHUNK // 2, D), BF),
        shape((CHUNKS, 3, CHUNK // 8, D), BF),
        shape((CHUNKS, CHUNK, D), BF),
        shape((2, 4, rows, CHUNK), BF),
        shape(grad_pre.shape, BF),
        low,
        low,
        low,
        low,
        low,
        shape(qkv.shape, BF),
        low,
        low,
        full,
        full,
        full,
        shape((2, D, D), BF),
        shape((7, 80, 128), F32),
        shape((3, 80, 128), F32),
        shape((1, 80, 128), F32),
        shape((3, 80, 128), F32),
        shape((HALO, D), BF),
        shape((HALO, D), F32),
    ]
    dma = pltpu.SemaphoreType.DMA
    any_space = pl.BlockSpec(memory_space=pl.ANY)
    vmem = pl.BlockSpec(memory_space=pltpu.VMEM)
    return pl.pallas_call(
        backward_kernel,
        out_shape=(
            shape((CHUNKS, CHUNK, D), BF),
            packed,
            shape((rows_here, D), BF),
            shape((rows_here, D), F32),
        ),
        in_specs=[pl.BlockSpec(memory_space=pltpu.SMEM)] * 3 + [vmem] * 4 + [any_space] * 15,
        out_specs=(any_space, vmem, any_space, any_space),
        scratch_shapes=[pltpu.VMEM(v.shape, v.dtype) for v in scratch]
        + [
            dma((14,)),
            dma((2, 4)),
            dma((2,)),
            dma((CHUNKS,)),
            dma((CHUNKS,)),
            dma((CHUNKS,)),
            dma((CHUNKS,)),
            dma((CHUNKS,)),
            dma((CHUNKS,)),
            dma((CHUNKS, 3)),
            dma((CHUNKS, 3)),
            dma((CHUNKS, 3)),
            dma((CHUNKS, 3)),
            dma((CHUNKS,)),
            dma((CHUNKS,)),
            dma((CHUNKS,)),
            dma((3, 3)),
            dma((3, 3)),
            dma((2,)),
            dma((2,)),
        ],
        compiler_params=pltpu.CompilerParams(
            collective_id=2, has_side_effects=True, vmem_limit_bytes=67043328
        ),
        name="backward",
    )(
        *smalls,
        *vectors,
        sums,
        tokens,
        cotangent,
        stream,
        middle,
        normed,
        qkv,
        context,
        hidden,
        grad_mixed,
        active,
        grad_pre,
        wqkv,
        wo.reshape(D, D),
        wup,
        wdown,
    )


def finish_kernel(
    down_ref,
    up_ref,
    output_ref,
    query_ref,
    key_ref,
    value_ref,
    finals_ref,
    layer_ref,
    tokens_ref,
    down,
    up,
    output,
    query,
    key,
    value,
    layer,
    tokens,
    *vectors,
):
    for source, target in ((down_ref, down), (up_ref, up)):
        for i in range(source.shape[0]):
            target[i * CHUNK : (i + 1) * CHUNK, :] = source[i].astype(F32)
    output[...] = output_ref[0].astype(F32)
    for source, target in ((query_ref, query), (key_ref, key), (value_ref, value)):
        for half in range(2):
            target[:, half * CHUNK : (half + 1) * CHUNK] = source[half].astype(F32).T
    layer[...] = layer_ref[...]
    tokens[...] = tokens_ref[...]

    @pl.when(pl.program_id(0) == 0)
    def _():
        first = 0
        for target in vectors:
            size = target.shape[0]
            target[...] = finals_ref[first : first + size, :]
            first += size


def finish(reduced, finals, layer, tokens, width):
    shape = jax.ShapeDtypeStruct
    rows_here = layer.shape[0]
    steps = FINISH_STEPS
    share = rows_here // steps
    taken = 8 // steps
    sizes = (8,) * 8 + (2, 2, 8)
    own = [pl.BlockSpec((share, D), lambda c: (c, 0))] * 2
    specs = (
        [
            pl.BlockSpec((taken * CHUNK, D), lambda c: (c, 0)),
            pl.BlockSpec((taken * CHUNK, D), lambda c: (c, 0)),
            pl.BlockSpec((width // steps, D), lambda c: (c, 0)),
        ]
        + [pl.BlockSpec((taken * CHUNK, width), lambda c: (c, 0))] * 3
        + own
    )
    shapes = [
        shape((D, D), F32),
        shape((D, D), F32),
        shape((width, D), F32),
        shape((D, width), F32),
        shape((D, width), F32),
        shape((D, width), F32),
        shape((rows_here, D), BF),
        shape((rows_here, D), F32),
    ]
    return pl.pallas_call(
        finish_kernel,
        grid=(steps,),
        in_specs=[
            pl.BlockSpec((taken, CHUNK, D), lambda c: (c, 0, 0)),
            pl.BlockSpec((taken, CHUNK, D), lambda c: (steps + c, 0, 0)),
            pl.BlockSpec(
                (1, width // steps, D), lambda c: (16 + c // (steps // 2), c % (steps // 2), 0)
            ),
        ]
        + [
            pl.BlockSpec((2, CHUNK, taken * CHUNK), lambda c, first=first: (first, 0, c))
            for first in (9, 10, 11)
        ]
        + [pl.BlockSpec(finals.shape, lambda c: (0, 0))]
        + own,
        out_specs=specs + [pl.BlockSpec((size, 128), lambda c: (0, 0)) for size in sizes],
        out_shape=shapes + [shape((size, 128), F32) for size in sizes],
        name="finish",
    )(*[reduced] * 6, finals, layer, tokens)


def general_shards(
    tokens,
    cotangent,
    item_lengths,
    item_group,
    group_count,
    grid_scale,
    norm_gain,
    norm_shift,
    query_weight,
    query_bias,
    key_weight,
    value_weight,
    value_bias,
    output_weight,
    output_bias,
    hidden_gain,
    hidden_shift,
    up_weight,
    up_bias,
    down_weight,
    down_bias,
):
    shard_count = lax.axis_size("mp")
    slice_count = lax.axis_size("dp")
    mp = lax.axis_index("mp")
    rows_here = tokens.shape[0]
    item_count = item_lengths.shape[0]
    pairs_here = PAIRS // shard_count
    own_rows = pairs_here * PAIR_LEN
    shift = rows_here - own_rows
    halo = shift * (shard_count - 1)
    padding = rows_here * shard_count - PAIRS * PAIR_LEN
    tail_block = -(-padding // 32) * 32
    rows = pairs_here * WINDOW + tail_block
    is_last = mp == shard_count - 1

    width = query_weight.shape[1]
    qkv_own = jnp.concatenate([query_weight, key_weight, value_weight], axis=1)
    bias_own = jnp.concatenate([query_bias, value_bias, up_bias])[None, :]
    bias_across = swap_mp(bias_own, 2)
    bias_pair = swap_mp(jnp.concatenate([bias_own, bias_across], axis=0), 1)
    biases = [bias_own[0], bias_pair[0], bias_across[0], bias_pair[1]]

    def gather(own, direct):
        across = swap_mp(own, 2) if direct else fetch_across(own)
        return [own, swap_mp(own, 1), across, swap_mp(across, 1)]

    tokens_f = tokens.astype(F32)
    slice_row = mp * rows_here + jnp.arange(rows_here, dtype=jnp.int32)
    weighted = tokens_f * (slice_row < PAIRS * PAIR_LEN).astype(F32)[:, None]
    chosen = item_group[:, None] == jnp.arange(group_count.shape[0], dtype=jnp.int32)[None, :]
    item_scale = jnp.sum(jnp.where(chosen, grid_scale[None, :], 0.0), axis=1)
    item_weight = jnp.sum(jnp.where(chosen, group_count[None, :], 0), axis=1).astype(F32)
    sums = all_sum(
        jnp.stack(
            [
                jnp.sum(weighted, axis=0),
                jnp.sum(weighted * tokens_f, axis=0),
                jnp.broadcast_to(jnp.sum(item_weight) / shard_count, (D,)),
            ]
        )
    )

    def windows(v):
        before = lax.ppermute(
            v[rows_here - halo :], "mp", [(i, i + 1) for i in range(shard_count - 1)]
        )
        joined = jnp.concatenate([before, v], axis=0)
        start = halo - shift * mp
        parts = []
        for pair in range(pairs_here):
            parts.append(
                lax.dynamic_slice_in_dim(joined, start + pair * PAIR_LEN, PAIR_LEN, axis=0)
            )
            parts.append(jnp.zeros((WINDOW - PAIR_LEN, D), v.dtype))
        parts.append(jnp.where(is_last, v[rows_here - padding :], jnp.zeros((), v.dtype)))
        parts.append(jnp.zeros((tail_block - padding, D), v.dtype))
        return jnp.concatenate(parts, axis=0)

    def unwindows(v):
        own = jnp.concatenate(
            [v[pair * WINDOW : pair * WINDOW + PAIR_LEN] for pair in range(pairs_here)], axis=0
        )
        after = lax.ppermute(own[:halo], "mp", [(i + 1, i) for i in range(shard_count - 1)])
        after = jnp.concatenate([after, jnp.zeros((padding - halo, D), v.dtype)], axis=0)
        tail = v[pairs_here * WINDOW : pairs_here * WINDOW + padding]
        joined = jnp.concatenate([own, jnp.where(is_last, tail, after)], axis=0)
        return lax.dynamic_slice_in_dim(joined, shift * mp, rows_here, axis=0)

    tokens_w = windows(tokens).astype(F32)
    cotangent_w = windows(cotangent).astype(F32)

    row = jnp.arange(rows, dtype=jnp.int32)
    window = row // WINDOW
    offset = row % WINDOW
    in_pair = (window < pairs_here) & (offset < PAIR_LEN)
    is_padding = (window == pairs_here) & (offset < padding) & is_last
    pair = pairs_here * mp + window
    item_ids = jnp.arange(item_count, dtype=jnp.int32)
    first_len = jnp.sum(
        jnp.where(item_ids[None, :] == (2 * pair)[:, None], item_lengths[None, :], 0), axis=1
    )
    second = (offset >= first_len).astype(jnp.int32)
    owner = jnp.where(in_pair, 2 * pair + second, jnp.where(is_padding, item_count, -1))
    position = offset - second * first_len
    member = owner[:, None] == item_ids[None, :]
    row_scale = jnp.sum(jnp.where(member, item_scale[None, :], 0.0), axis=1)
    row_count = jnp.sum(jnp.where(member, item_weight[None, :], 0.0), axis=1)
    valid = in_pair.astype(F32)[:, None]
    quarter = D // 4
    frequency = jnp.exp(-math.log(10000.0) * jnp.arange(quarter, dtype=F32) / quarter)
    across_angle = ((position // SIDE).astype(F32) * row_scale)[:, None] * frequency
    side_angle = ((position % SIDE).astype(F32) * row_scale)[:, None] * frequency
    grid_table = (
        jnp.concatenate(
            [
                jnp.sin(across_angle),
                jnp.cos(across_angle),
                jnp.sin(side_angle),
                jnp.cos(side_angle),
            ],
            axis=-1,
        )
        * valid
    )
    owner_col = owner[:, None]
    owner_row = owner[None, :]

    qkv_weights = jnp.concatenate(gather(qkv_own, True), axis=1)
    output_weights = jnp.concatenate(gather(output_weight, False), axis=0)
    up_weights = jnp.concatenate(gather(up_weight, False), axis=1)
    down_weights = jnp.concatenate(gather(down_weight, False), axis=0)
    hidden_width = up_weight.shape[1]
    no_bias = jnp.zeros((width,), F32)
    qkv_bias = jnp.concatenate(
        [v for b in biases for v in (b[:width], no_bias, b[width : 2 * width])]
    )
    up_biases = jnp.concatenate([b[2 * width :] for b in biases])

    count_valid = slice_count * PAIRS * PAIR_LEN
    column_mean = sums[0] / count_valid
    spread = sums[1] / count_valid - column_mean * column_mean
    inverse = lax.rsqrt(spread + 1e-05)
    row_weight = row_count / (sums[2, 0] / (slice_count * item_count))
    standard = (tokens_w - column_mean) * inverse
    stream = standard + grid_table
    unit, unit_inverse = stats(stream)
    normed = (unit * norm_gain + norm_shift).astype(BF)

    qkv = (dot(normed, qkv_weights) + qkv_bias).astype(BF)
    context = attend(qkv, owner_col, owner_row, shard_count)
    middle = stream + (dot(context, output_weights) + output_bias)
    middle_unit, middle_inverse = stats(middle)
    hidden_in = (middle_unit * hidden_gain + hidden_shift).astype(BF)

    grad_out = cotangent_w * row_weight[:, None]
    grad_mixed = grad_out.astype(BF)
    active, slope = gelu_parts(dot(hidden_in, up_weights) + up_biases)
    mixed = dot(active, down_weights) + down_bias
    grad_pre = (dot_cols(grad_mixed, down_weights) * slope).astype(BF)
    grad_hidden = dot_cols(grad_pre, up_weights)
    layer_output = unwindows((middle + mixed).astype(BF))
    grad_middle = grad_out + norm_back(grad_hidden, middle_unit, middle_inverse, hidden_gain)
    grad_attended = grad_middle.astype(BF)

    grad_context = dot_cols(grad_attended, output_weights).astype(BF)
    grad_qkv = attend_back(qkv, grad_context, owner_col, owner_row, shard_count)
    grad_normed = dot_cols(grad_qkv, qkv_weights)

    pieces = range(shard_count)
    def columns(v, r, size):
        return v[:, r * size : (r + 1) * size]

    def reduced(left, right):
        return reduce_pieces([dot_rows(left(r), right(r)).astype(BF) for r in pieces])

    down_weight_grad = reduced(
        lambda r: columns(active, r, hidden_width), lambda r: grad_mixed
    )
    up_weight_grad = reduced(
        lambda r: hidden_in, lambda r: columns(grad_pre, r, hidden_width)
    )
    output_weight_grad = reduced(
        lambda r: columns(context, r, width), lambda r: grad_attended
    )
    qkv_weight_grad = reduced(lambda r: normed, lambda r: columns(grad_qkv, r, 3 * width))
    qkv_weight_grads = [columns(qkv_weight_grad, i, width) for i in range(3)]
    grad_stream = grad_middle + norm_back(grad_normed, unit, unit_inverse, norm_gain)

    def column_sums(v):
        return jnp.sum(v.astype(F32), axis=0)

    qkv_sums = column_sums(grad_qkv)
    up_sums = column_sums(grad_pre)
    bias_grads = [
        jnp.concatenate(
            [
                qkv_sums[3 * r * width : (3 * r + 1) * width],
                qkv_sums[(3 * r + 2) * width : 3 * (r + 1) * width],
                up_sums[r * hidden_width : (r + 1) * hidden_width],
            ]
        )[None, :]
        for r in pieces
    ]
    got = swap_mp(jnp.concatenate([bias_grads[1], bias_grads[3]], axis=0), 1)
    bias_grad = bias_grads[0] + got[:1] + swap_mp(bias_grads[2] + got[1:], 2)
    for bit in range(dp_bits()):
        bias_grad = bias_grad + swap_dp(bias_grad, 1 << bit)
    bias_grad = bias_grad[0]
    finals = all_sum(
        jnp.stack(
            [
                column_sums(grad_stream),
                column_sums(grad_stream * standard),
                column_sums(grad_normed * unit),
                column_sums(grad_normed),
                column_sums(grad_hidden * middle_unit),
                column_sums(grad_hidden),
                column_sums(grad_attended),
                column_sums(grad_mixed),
            ]
        )
    )
    tokens_grad = unwindows(
        inverse * (grad_stream - valid / count_valid * (finals[0] + finals[1] * standard))
    )
    return (
        layer_output,
        tokens_grad,
        finals[2],
        finals[3],
        qkv_weight_grads[0],
        bias_grad[:width],
        qkv_weight_grads[1],
        qkv_weight_grads[2],
        bias_grad[width : 2 * width],
        output_weight_grad,
        finals[6],
        finals[4],
        finals[5],
        up_weight_grad,
        bias_grad[2 * width :],
        down_weight_grad,
        finals[7],
    )


def fast_shards(
    tokens,
    cotangent,
    item_lengths,
    item_group,
    group_count,
    grid_scale,
    norm_gain,
    norm_shift,
    query_weight,
    query_bias,
    key_weight,
    value_weight,
    value_bias,
    output_weight,
    output_bias,
    hidden_gain,
    hidden_shift,
    up_weight,
    up_bias,
    down_weight,
    down_bias,
):
    rows = 2 * WINDOW + 96
    saved = forward(
        (item_lengths, item_group, group_count, grid_scale),
        [
            v[None, :]
            for v in (
                norm_gain,
                norm_shift,
                output_bias,
                hidden_gain,
                hidden_shift,
                query_bias,
                value_bias,
                up_bias,
            )
        ],
        tokens,
        cotangent,
        (query_weight, key_weight, value_weight, output_weight, up_weight, down_weight),
        rows,
    )
    reduced, finals, layer_output, tokens_grad = backward(
        (item_lengths, item_group, group_count),
        [v[None, :] for v in (norm_gain, hidden_gain, down_bias)],
        saved[2],
        saved[:2] + saved[3:],
        tokens.shape[0],
    )
    (
        down_weight_grad,
        up_weight_grad,
        output_weight_grad,
        query_weight_grad,
        key_weight_grad,
        value_weight_grad,
        layer_output,
        tokens_grad,
        *vectors,
    ) = finish(reduced, finals, layer_output, tokens_grad, query_weight.shape[1])
    vectors = [v.reshape(-1) for v in vectors]
    return (
        layer_output,
        tokens_grad,
        vectors[2],
        vectors[3],
        query_weight_grad,
        vectors[8],
        key_weight_grad,
        value_weight_grad,
        vectors[9],
        output_weight_grad,
        vectors[6],
        vectors[4],
        vectors[5],
        up_weight_grad,
        vectors[10],
        down_weight_grad,
        vectors[7],
    )


def shards(*args):
    if lax.axis_size("dp") == 8 and lax.axis_size("mp") == 4 and args[0].shape == (512, D):
        return fast_shards(*args)
    return general_shards(*args)


def solution(mesh):
    rows = P(("dp", "mp"), None)
    columns = P(None, "mp")
    return jax.shard_map(
        shards,
        mesh=mesh,
        in_specs=(
            rows,
            rows,
            P("dp"),
            P("dp"),
            P(),
            P(),
            P(),
            P(),
            columns,
            P("mp"),
            columns,
            columns,
            P("mp"),
            P("mp", None),
            P(),
            P(),
            P(),
            columns,
            P("mp"),
            P("mp", None),
            P(),
        ),
        out_specs=(
            rows,
            rows,
            P(),
            P(),
            columns,
            P("mp"),
            columns,
            columns,
            P("mp"),
            P("mp", None),
            P(),
            P(),
            P(),
            columns,
            P("mp"),
            P("mp", None),
            P(),
        ),
        check_vma=False,
    )
```

```python
import functools
import math

import jax
import jax.numpy as jnp
from jax import lax
from jax.experimental import pallas as pl
from jax.experimental.pallas import tpu as pltpu
from jax.sharding import PartitionSpec as P

D = 1024
HEAD_DIM = 64
SIDE = 14
PAIRS = 8
PAIR_LEN = 245
WINDOW = 256
BF = jnp.bfloat16
F32 = jnp.float32
PADDING = 88


def dot(a, b):
    return lax.dot_general(a, b, (((1,), (0,)), ((), ())), preferred_element_type=F32)


def dot_rows(a, b):
    return lax.dot_general(a, b, (((0,), (0,)), ((), ())), preferred_element_type=F32)


def dot_cols(a, b):
    return lax.dot_general(a, b, (((1,), (1,)), ((), ())), preferred_element_type=F32)


def swap_mp(v, mask):
    count = lax.axis_size("mp")
    return lax.ppermute(v, "mp", [(i, i ^ mask) for i in range(count)])


def swap_dp(v, mask):
    count = lax.axis_size("dp")
    return lax.ppermute(v, "dp", [(i, i ^ mask) for i in range(count)])


def dp_bits():
    return lax.axis_size("dp").bit_length() - 1


def all_sum(v):
    v = v + swap_mp(v, 1) + swap_mp(v, 2) + swap_mp(v, 3)
    bit = 0
    bits = dp_bits()
    while bit < bits:
        if bit + 1 < bits:
            v = v + swap_dp(v, 1 << bit) + swap_dp(v, 2 << bit) + swap_dp(v, 3 << bit)
            bit += 2
        else:
            v = v + swap_dp(v, 1 << bit)
            bit += 1
    return v


def dp_bit(bit):
    return (lax.axis_index("dp") >> bit) & 1


def join(mine, other, bit):
    return jnp.where(
        dp_bit(bit) == 0,
        jnp.concatenate([mine, other], axis=0),
        jnp.concatenate([other, mine], axis=0),
    )


def chunk_index():
    index = jnp.int32(0)
    for bit in range(dp_bits()):
        index = index * 2 + dp_bit(bit)
    return index


def fetch_across(w):
    rows = w.shape[0] // lax.axis_size("dp")
    mine = lax.dynamic_slice_in_dim(w, chunk_index() * rows, rows, axis=0)
    got = swap_mp(mine, 2)
    for bit in reversed(range(dp_bits())):
        got = join(got, swap_dp(got, 1 << bit), bit)
    return got


def reduce_pieces(pieces):
    half = pieces[1].shape[0]
    got = swap_mp(jnp.concatenate([pieces[1], pieces[3]], axis=0), 1)
    across = pieces[2].astype(F32) + got[half:].astype(F32)
    own = pieces[0].astype(F32) + got[:half].astype(F32)
    total = own + swap_mp(across.astype(BF), 2).astype(F32)
    for bit in range(dp_bits()):
        size = total.shape[0] // 2
        side = dp_bit(bit)
        send = lax.dynamic_slice_in_dim(total, (1 - side) * size, size, axis=0).astype(BF)
        keep = lax.dynamic_slice_in_dim(total, side * size, size, axis=0)
        total = keep + swap_dp(send, 1 << bit).astype(F32)
    total = total.astype(BF)
    for bit in reversed(range(dp_bits())):
        total = join(total, swap_dp(total, 1 << bit), bit)
    return total.astype(F32)


def stats(v):
    mean = jnp.mean(v, axis=-1, keepdims=True)
    center = v - mean
    spread = jnp.mean(center * center, axis=-1, keepdims=True)
    inverse = lax.rsqrt(spread + 1e-06)
    return center * inverse, inverse


def norm_back(grad, unit, inverse, gain):
    f = grad * gain
    return inverse * (
        f
        - jnp.mean(f, axis=-1, keepdims=True)
        - unit * jnp.mean(f * unit, axis=-1, keepdims=True)
    )


def blocks_of(rows):
    return [(first, min(WINDOW, rows - first)) for first in range(0, rows, WINDOW)]


def head_scores(qkv_ref, same, first, size, h, width):
    q = qkv_ref[first : first + size, h * HEAD_DIM : (h + 1) * HEAD_DIM]
    k = qkv_ref[first : first + size, width + h * HEAD_DIM : width + (h + 1) * HEAD_DIM]
    v = qkv_ref[first : first + size, 2 * width + h * HEAD_DIM : 2 * width + (h + 1) * HEAD_DIM]
    scores = jnp.where(same, dot_cols(q, k) * (1.0 / math.sqrt(HEAD_DIM)), -1e30)
    weights = jnp.exp(scores - jnp.max(scores, axis=-1, keepdims=True))
    weights = weights * (1.0 / jnp.sum(weights, axis=-1, keepdims=True))
    return q, k, v, weights


def attend_kernel(qkv_ref, col_ref, row_ref, out_ref):
    rows, width = out_ref.shape
    for first, size in blocks_of(rows):
        same = col_ref[first : first + size, :] == row_ref[:, first : first + size]
        for h in range(width // HEAD_DIM):
            q, k, v, weights = head_scores(qkv_ref, same, first, size, h, width)
            out_ref[first : first + size, h * HEAD_DIM : (h + 1) * HEAD_DIM] = dot(
                weights.astype(BF), v
            ).astype(BF)


def attend_back_kernel(qkv_ref, grad_ref, col_ref, row_ref, out_ref):
    rows, width = grad_ref.shape
    factor = 1.0 / math.sqrt(HEAD_DIM)
    for first, size in blocks_of(rows):
        same = col_ref[first : first + size, :] == row_ref[:, first : first + size]
        for h in range(width // HEAD_DIM):
            q, k, v, weights = head_scores(qkv_ref, same, first, size, h, width)
            grad = grad_ref[first : first + size, h * HEAD_DIM : (h + 1) * HEAD_DIM]
            soft = dot_cols(grad, v)
            center = jnp.sum(weights * soft, axis=-1, keepdims=True)
            grad_scores = (weights * (soft - center)).astype(BF)
            for part, value in enumerate(
                (
                    dot(grad_scores, k) * factor,
                    dot_rows(grad_scores, q) * factor,
                    dot_rows(weights.astype(BF), grad),
                )
            ):
                lane = part * width + h * HEAD_DIM
                out_ref[first : first + size, lane : lane + HEAD_DIM] = value.astype(BF)


def attend(qkv, owner_col, owner_row, groups):
    rows, width = qkv.shape[0], qkv.shape[1] // (3 * groups)
    return pl.pallas_call(
        attend_kernel,
        grid=(groups,),
        in_specs=[
            pl.BlockSpec((rows, 3 * width), lambda r: (0, r)),
            pl.BlockSpec((rows, 1), lambda r: (0, 0)),
            pl.BlockSpec((1, rows), lambda r: (0, 0)),
        ],
        out_specs=pl.BlockSpec((rows, width), lambda r: (0, r)),
        out_shape=jax.ShapeDtypeStruct((rows, groups * width), BF),
        name="attend",
    )(qkv, owner_col, owner_row)


def attend_back(qkv, grad, owner_col, owner_row, groups):
    rows, width = grad.shape[0], grad.shape[1] // groups
    return pl.pallas_call(
        attend_back_kernel,
        grid=(groups,),
        in_specs=[
            pl.BlockSpec((rows, 3 * width), lambda r: (0, r)),
            pl.BlockSpec((rows, width), lambda r: (0, r)),
            pl.BlockSpec((rows, 1), lambda r: (0, 0)),
            pl.BlockSpec((1, rows), lambda r: (0, 0)),
        ],
        out_specs=pl.BlockSpec((rows, 3 * width), lambda r: (0, r)),
        out_shape=jax.ShapeDtypeStruct((rows, 3 * groups * width), BF),
        name="attend_back",
    )(qkv, grad, owner_col, owner_row)


def gelu_parts(preact):
    phi = 0.5 * (1.0 + lax.erf(preact * (1.0 / math.sqrt(2.0))))
    slope = phi + preact * jnp.exp(-0.5 * preact * preact) * (1.0 / math.sqrt(2.0 * math.pi))
    return (preact * phi).astype(BF), slope


HALO = 80
ROUTE_TICKS = (
    (0, 0, 0, 0, 1, 1, 2, 2, 3, 4),
    (1, 1, 1, 1, 2, 3, 4, 5, 6, 7),
    (2, 2, 3, 3, 4, 5, 6, 7, 8, 9),
    (5, 5, 6, 6, 9, 11, 13, 15, 17, 19),
)
AT_HEADS, AT_PAIRED, AT_QUERY, AT_OUTPUT, AT_HIDDEN, AT_DOWN = 4, 12, 10, 16, 19, 22
MESH = pl.DeviceIdType.MESH


def places():
    mp = lax.axis_index("mp")
    dp = lax.axis_index("dp")
    y = dp % 2
    z = dp // 2
    sibling = mp + 1 - 2 * (mp % 2)
    opposite = mp + 2 - 4 * (mp // 2)
    across = opposite + 1 - 2 * (mp % 2)
    mp_peers = [{"mp": sibling}, {"mp": opposite}, {"mp": across}]
    y_peer = {"dp": dp + 1 - 2 * y}
    z_places = [(z + m) % 4 for m in (1, 2, 3)]
    z_peers = [{"dp": place * 2 + y} for place in z_places]
    return mp, y, z, mp_peers, y_peer, z_places, z_peers


def greet(peers):
    barrier = pltpu.get_barrier_semaphore()
    for peer in peers:
        pl.semaphore_signal(barrier, inc=1, device_id=peer, device_id_type=MESH)
    pl.semaphore_wait(barrier, len(peers))


def remote(source, target, send, recv, peer):
    return pltpu.make_async_remote_copy(
        src_ref=source,
        dst_ref=target,
        send_sem=send,
        recv_sem=recv,
        device_id=peer,
        device_id_type=MESH,
    )


def loop(count, body):
    def step(i, carry):
        body(i)
        return carry

    lax.fori_loop(0, count, step, 0)


def block_rows(i, size):
    return pl.ds(pl.multiple_of(i * size, size), size)


def start_all(copies):
    for copy in copies:
        copy.start()


def wait_recv_all(copies):
    for copy in copies:
        copy.wait_recv()


def item_of_rows(row, lengths, mp):
    window = row >> 8
    offset = row & (WINDOW - 1)
    length = jnp.where(window == 0, lengths[4 * mp], lengths[4 * mp + 2])
    second = jnp.where(offset >= length, 1, 0)
    in_pair = (window < 2) & (offset < PAIR_LEN)
    is_padding = (window == 2) & (offset < PADDING) & (mp == 3)
    return 2 * window + second, offset - second * length, in_pair, is_padding


def owner_of_rows(row, lengths, mp):
    item, _, in_pair, is_padding = item_of_rows(row, lengths, mp)
    return jnp.where(in_pair, item, jnp.where(is_padding, 16, -1))


def choose_item(item, values):
    result = jnp.where(item == 0, values[0], 0.0)
    for j in (1, 2, 3):
        result = jnp.where(item == j, values[j], result)
    return result


def joined(tiles, first):
    return jnp.concatenate([tiles[first + j : first + j + 1, :] for j in range(8)], axis=1)


def forward_kernel(
    lengths,
    groups,
    counts,
    scales,
    gain,
    shift,
    output_bias,
    hidden_gain,
    hidden_shift,
    query_bias,
    value_bias,
    up_bias,
    tokens_ref,
    cotangent_ref,
    query_ref,
    key_ref,
    value_ref,
    output_ref,
    up_ref,
    down_ref,
    tokens_out,
    cotangent_out,
    sums_out,
    stream_out,
    middle_out,
    normed_out,
    qkv_out,
    context_out,
    hidden_out,
    grad_mixed_out,
    active_out,
    grad_pre_out,
    wqkv_out,
    wo_out,
    wup_out,
    wdown_out,
    tokens_ext,
    cotangent_ext,
    tokens,
    cotangent,
    stream,
    middle,
    normed,
    qkv,
    context,
    hidden,
    grad_mixed,
    active,
    grad_pre,
    wqkv,
    wo,
    wup,
    wdown,
    sums,
    bias,
    part,
    from_mp,
    from_y,
    from_z,
    own_sem,
    halo_sem,
    store_sem,
    stat_send,
    stat_recv,
    bias_send,
    bias_recv,
    pair_send,
    pair_recv,
    x_send,
    x_recv,
    far_send,
    far_recv,
    near_send,
    near_recv,
    y_send,
    y_recv,
    fwd_send,
    fwd_recv,
):
    mp, y, z, mp_peers, y_peer, z_places, z_peers = places()
    sibling, opposite, _ = mp_peers
    rows_here = tokens_ref.shape[0]
    rows = tokens.shape[0]
    width = query_ref.shape[1]
    blocks = rows // 32

    items = (
        [(key_ref, first, D // 2, wqkv, width, width, False) for first in (0, D // 2)]
        + [(value_ref, first, D // 2, wqkv, 2 * width, width, False) for first in (0, D // 2)]
        + [(output_ref, 0, width, wo, 0, D, False)]
        + [(up_ref, first, D // 4, wup, 0, D, False) for first in range(0, D, D // 4)]
        + [(down_ref, first, D // 4, wdown, 0, D, False) for first in (3 * D // 4,)]
        + [(query_ref, 0, D, wqkv, 0, width, True), (down_ref, 0, 3 * D // 4, wdown, 0, D, True)]
    )
    relayed = range(10)
    QUERY, DOWN = 10, 11
    HEADS, OUTPUT, HIDDEN = (0, 1, 2, 3, QUERY), 4, (5, 6, 7, 8, 9, DOWN)
    everything = range(len(items))
    near = z % 2
    far = z // 2
    near_peer = {"dp": (z + 1 - 2 * near) * 2 + y}
    far_peer = {"dp": ((z + 2) % 4) * 2 + y}

    def source(i, start, size):
        return items[i][0].at[pl.ds(items[i][1] + start, size)]

    def place(i, r, start, size):
        _, first, _, ref, column, columns, _ = items[i]
        return ref.at[r, pl.ds(first + start, size), pl.ds(column, columns)]

    def part_of(i, first, eighths):
        size = items[i][2] // 8
        return pl.multiple_of(first * size, size), eighths * size

    own_copies = [
        pltpu.make_async_copy(
            source(i, 0, items[i][2]), place(i, 0, 0, items[i][2]), own_sem.at[i]
        )
        for i in everything
    ]
    pair_copies = [
        remote(
            source(i, 0, items[i][2]),
            place(i, 1, 0, items[i][2]),
            pair_send.at[i],
            pair_recv.at[i],
            sibling,
        )
        for i in everything
    ]

    def x_copy(i):
        start, size = (
            (0, items[i][2]) if items[i][6] else part_of(i, y * 4 + near * 2 + far, 1)
        )
        return remote(
            source(i, start, size), place(i, 2, start, size), x_send.at[i], x_recv.at[i], opposite
        )

    def hop(i, first, eighths, send, recv, peer):
        start, size = part_of(i, first, eighths)
        view = place(i, 2, start, size)
        return remote(view, view, send.at[i], recv.at[i], peer)

    def far_copy(i):
        return hop(i, y * 4 + near * 2 + far, 1, far_send, far_recv, far_peer)

    def near_copy(i):
        return hop(i, y * 4 + near * 2, 2, near_send, near_recv, near_peer)

    def y_copy(i):
        return hop(i, y * 4, 4, y_send, y_recv, y_peer)

    def fwd_copy(i):
        size = items[i][2]
        return remote(
            place(i, 2, 0, size), place(i, 3, 0, size), fwd_send.at[i], fwd_recv.at[i], sibling
        )

    route = (x_copy, far_copy, near_copy, y_copy, fwd_copy)

    keep = [
        pltpu.make_async_copy(ref, ext.at[pl.ds(HALO, rows_here)], halo_sem.at[which, 2])
        for which, (ref, ext) in enumerate(
            ((tokens_ref, tokens_ext), (cotangent_ref, cotangent_ext))
        )
    ]
    start_all(keep)
    start_all(own_copies)
    bias[0, 0:1, :] = query_bias[...]
    bias[0, 1:2, :] = value_bias[...]
    for j in range(4):
        bias[0, 2 + j : 3 + j, :] = up_bias[:, j * width : (j + 1) * width]
    bias[0, 6:8, :] = jnp.zeros((2, width), F32)

    weights = [counts[groups[4 * mp + j]].astype(F32) for j in range(4)]
    weight_part = weights[0] + weights[1] + weights[2] + weights[3]
    keep[0].wait()

    def add_rows(i, carry):
        block = tokens_ext[pl.ds(pl.multiple_of(HALO + i * 16, 16), 16), :].astype(F32)
        row = mp * rows_here + i * 16 + lax.broadcasted_iota(jnp.int32, (16, 1), 0)
        kept = jnp.where(row < PAIRS * PAIR_LEN, block, 0.0)
        return carry[0] + kept, carry[1] + kept * block

    zero = jnp.zeros((16, D), F32)
    first, second = lax.fori_loop(0, rows_here // 16, add_rows, (zero, zero))
    first = jnp.sum(first, axis=0, keepdims=True)
    second = jnp.sum(second, axis=0, keepdims=True)
    for j in range(8):
        part[0, j : j + 1, :] = first[:, j * 128 : (j + 1) * 128]
        part[0, 8 + j : 9 + j, :] = second[:, j * 128 : (j + 1) * 128]
    part[0, 16:24, :] = jnp.zeros((8, 128), F32) + weight_part
    greet(mp_peers + [y_peer] + z_peers)

    sums_a = [
        remote(part.at[0], from_mp.at[m], stat_send.at[0, m], stat_recv.at[0, m], peer)
        for m, peer in enumerate(mp_peers)
    ]
    start_all(sums_a)
    after = {"mp": (mp + 1) % 4}
    halo_copies = [
        remote(
            ref.at[pl.ds(rows_here - HALO, HALO)],
            ext.at[pl.ds(0, HALO)],
            halo_sem.at[which, 0],
            halo_sem.at[which, 1],
            after,
        )
        for which, (ref, ext) in enumerate(
            ((tokens_ref, tokens_ext), (cotangent_ref, cotangent_ext))
        )
    ]
    bias_copies = [
        remote(bias.at[0], bias.at[r + 1], bias_send.at[r], bias_recv.at[r], peer)
        for r, peer in enumerate(mp_peers)
    ]
    start_all(halo_copies + bias_copies)
    start_all([x_copy(i) for i in everything])
    start_all([pair_copies[i] for i in HEADS + (OUTPUT,) + HIDDEN])
    sums_b = [
        remote(part.at[1], from_y.at[0], stat_send.at[1, 0], stat_recv.at[1, 0], y_peer)
    ]
    sums_c = [
        remote(part.at[2], from_z.at[m], stat_send.at[2, m], stat_recv.at[2, m], peer)
        for m, peer in enumerate(z_peers)
    ]

    def position_table():
        place_id = lax.broadcasted_iota(jnp.int32, (64, 1), 0)
        table_scale = choose_item(
            place_id >> 4, [scales[groups[4 * mp + j]] for j in range(4)]
        )
        quarter = D // 4
        lane = lax.broadcasted_iota(jnp.int32, (1, quarter), 1).astype(F32)
        frequency = jnp.exp(-math.log(10000.0) * lane / quarter)
        angle = ((place_id & 15).astype(F32) * table_scale) * frequency
        table = jnp.concatenate([jnp.sin(angle), jnp.cos(angle)], axis=1)
        row = lax.broadcasted_iota(jnp.int32, (rows, 64), 0)
        column = lax.broadcasted_iota(jnp.int32, (rows, 64), 1)
        item, position, in_pair, _ = item_of_rows(row, lengths, mp)
        across = (position * 9363) >> 17
        for half, code in enumerate((across, position - SIDE * across)):
            chosen = jnp.where(in_pair & (column == item * 16 + code), 1.0, 0.0)
            stream[:, half * 2 * quarter : (half + 1) * 2 * quarter] = lax.dot_general(
                chosen,
                table,
                (((1,), (0,)), ((), ())),
                precision=lax.Precision.HIGHEST,
                preferred_element_type=F32,
            )

    def place_rows():
        wait_recv_all(halo_copies)
        keep[1].wait()
        own_len = 2 * PAIR_LEN
        row = lax.broadcasted_iota(jnp.int32, (rows, HALO + rows_here), 0)
        column = lax.broadcasted_iota(jnp.int32, (rows, HALO + rows_here), 1)
        window = row >> 8
        offset = row & (WINDOW - 1)
        wanted = HALO - (rows_here - own_len) * mp + window * PAIR_LEN + offset
        tail = jnp.where(mp == 3, HALO + rows_here - PADDING, 4096) + offset
        wanted = jnp.where(window < 2, jnp.where(offset < PAIR_LEN, wanted, -1), tail)
        chosen = jnp.where(column == wanted, 1.0, 0.0).astype(BF)
        tokens[...] = dot(chosen, tokens_ext[...]).astype(BF)
        cotangent[...] = dot(chosen, cotangent_ext[...]).astype(BF)

    def norm_rows(first, count):
        slices = lax.axis_size("dp")
        count_valid = slices * PAIRS * PAIR_LEN
        column_mean = joined(sums, 0) / count_valid
        spread = joined(sums, 8) / count_valid - column_mean * column_mean
        inverse = lax.rsqrt(spread + 1e-05)
        mean_weight = sums[16:17, 0:1] / (slices * 16)

        def first_norm(i):
            here = block_rows(i, 32)
            value = (tokens[here, :].astype(F32) - column_mean) * inverse + stream[here, :]
            stream[here, :] = value
            unit, _ = stats(value)
            normed[here, :] = (unit * gain[...] + shift[...]).astype(BF)
            row = i * 32 + lax.broadcasted_iota(jnp.int32, (32, 1), 0)
            item, _, in_pair, _ = item_of_rows(row, lengths, mp)
            row_weight = jnp.where(in_pair, choose_item(item, weights), 0.0) / mean_weight
            grad_mixed[here, :] = (cotangent[here, :].astype(F32) * row_weight).astype(BF)

        def body(i):
            first_norm(first + i)

        loop(count, body)

    def group_stores(value, target, r):
        return value.at[r], target.at[r]

    def column_stores(value, target, r):
        columns = pl.ds(r * D, D)
        return value.at[:, columns], target.at[:, columns]

    plan = (
        [
            (AT_HEADS, ref, target)
            for ref, target in (
                (tokens, tokens_out),
                (cotangent, cotangent_out),
                (sums, sums_out),
                (stream, stream_out),
                (normed, normed_out),
                (grad_mixed, grad_mixed_out),
            )
        ]
        + [
            (AT_OUTPUT, ref, target)
            for ref, target in ((qkv, qkv_out), (context, context_out), (wqkv, wqkv_out))
        ]
        + [
            (AT_HIDDEN, ref, target)
            for ref, target in ((middle, middle_out), (hidden, hidden_out), (wo, wo_out))
        ]
        + [
            (when,) + group_stores(ref, target, r)
            for r, when in enumerate((AT_PAIRED, AT_PAIRED, AT_HIDDEN + 6, AT_HIDDEN + 6))
            for ref, target in ((wup, wup_out), (wdown, wdown_out))
        ]
        + [
            (AT_HIDDEN + 2 * r + 2,) + column_stores(ref, target, r)
            for r in range(4)
            for ref, target in ((active, active_out), (grad_pre, grad_pre_out))
        ]
    )
    stores = [
        pltpu.make_async_copy(ref, target, store_sem.at[i])
        for i, (_, ref, target) in enumerate(plan)
    ]
    last_tick = AT_HIDDEN + 8

    def head_product(r):
        base = r * 3 * width
        for n in range(3):
            value = dot(normed[...], wqkv[r, :, n * width : (n + 1) * width])
            if n != 1:
                value = value + bias[r, n // 2 : n // 2 + 1, :]
            qkv[:, pl.ds(pl.multiple_of(base + n * width, width), width)] = value.astype(BF)

    def head_pair(r, p):
        base = r * 3 * width
        lanes = [pl.ds(pl.multiple_of(base + n * width + p * 128, 128), 128) for n in range(3)]
        target = pl.ds(pl.multiple_of(r * width + p * 128, 128), 128)
        for first, size in blocks_of(rows):
            here = pl.ds(first, size)
            same = owner_of_rows(
                first + lax.broadcasted_iota(jnp.int32, (size, 1), 0), lengths, mp
            ) == owner_of_rows(first + lax.broadcasted_iota(jnp.int32, (1, size), 1), lengths, mp)
            q, k, v = [qkv[here, lane] for lane in lanes]
            results = []
            for h in range(2):
                cut = slice(h * HEAD_DIM, (h + 1) * HEAD_DIM)
                low = softmax_rows(q[:, cut], k[:, cut], same).astype(BF)
                results.append(dot(low, v[:, cut]).astype(BF))
            context[here, target] = jnp.concatenate(results, axis=1)

    def attention_output(n):
        columns = block_rows(n, 256)
        value = stream[:, columns] + output_bias[:, columns]
        for r in range(4):
            value = value + dot(context[:, r * width : (r + 1) * width], wo[r, :, columns])
        middle[:, columns] = value

    def second_norm(i):
        here = block_rows(i, 32)
        unit, _ = stats(middle[here, :])
        hidden[here, :] = (unit * hidden_gain[...] + hidden_shift[...]).astype(BF)

    def hidden_tile(r, n):
        columns = block_rows(n, 256)
        target = pl.ds(pl.multiple_of(r * D + n * 256, 256), 256)
        preact = dot(hidden[...], wup[r, :, columns]) + bias[r, pl.ds(2 + n, 1), :]
        value, slope = gelu_parts(preact)
        active[:, target] = value
        grad = dot_cols(grad_mixed[...], wdown[r, columns, :])
        grad_pre[:, target] = (grad * slope).astype(BF)

    actions = {}

    def at(k, action):
        actions.setdefault(k, []).append(action)

    for stage in reversed(range(4)):
        for i in relayed:

            def advance(i=i, stage=stage):
                route[stage](i).wait_recv()
                route[stage + 1](i).start()

            at(ROUTE_TICKS[stage][i], advance)

    def pass_on(i):
        x_copy(i).wait_recv()
        fwd_copy(i).start()

    def sums_stage(target, copies, slots, following):
        def action():
            value = part[target - 1]
            for m, copy in enumerate(copies):
                copy.wait_recv()
                value = value + slots[m]
            if following:
                part[target] = value
                start_all(following)
            else:
                sums[...] = value

        return action

    def received(indices, copies):
        def action():
            for i in indices:
                copies(i)

        return action

    def own(i):
        own_copies[i].wait()

    def paired(i):
        pair_copies[i].wait_recv()

    def forwarded(i):
        fwd_copy(i).wait_recv()

    at(0, sums_stage(1, sums_a, from_mp, sums_b))
    at(1, sums_stage(2, sums_b, from_y, sums_c))
    at(2, sums_stage(3, sums_c, from_z, None))
    at(AT_HEADS, lambda: wait_recv_all(bias_copies))
    at(AT_HEADS, received(HEADS, own))
    at(AT_HEADS + 3, received(HEADS, paired))
    at(AT_QUERY, lambda: pass_on(QUERY))
    at(AT_HEADS + 9, received(HEADS, forwarded))
    at(AT_OUTPUT, received((OUTPUT,), own))
    at(AT_OUTPUT, received((OUTPUT,), paired))
    at(AT_OUTPUT, received((OUTPUT,), forwarded))
    at(AT_PAIRED, received(HIDDEN, own))
    at(AT_PAIRED, received(HIDDEN, paired))
    at(AT_DOWN, lambda: pass_on(DOWN))
    at(AT_HIDDEN + 6, received(HIDDEN, forwarded))
    for copy, (when, _, _) in zip(stores, plan):
        if when < last_tick:
            at(when, copy.start)

    def tick(k, carry):
        for when, todo in sorted(actions.items()):

            @pl.when(k == when)
            def _(todo=todo):
                for action in todo:
                    action()

        @pl.when(k == 0)
        def _():
            position_table()

        @pl.when(k == 1)
        def _():
            place_rows()

        @pl.when((k >= 2) & (k < 4))
        def _():
            norm_rows((k - 2) * 10, 10 - (k - 2))

        step = k - AT_HEADS

        @pl.when((step >= 0) & (step < 12) & (step % 3 == 0))
        def _():
            head_product(step // 3)

        @pl.when((step >= 0) & (step < 12) & (step % 3 > 0))
        def _():
            head_pair(step // 3, step % 3 - 1)

        @pl.when((k >= AT_OUTPUT) & (k < AT_OUTPUT + 2))
        def _():
            def body(n):
                attention_output(2 * (k - AT_OUTPUT) + n)

            loop(2, body)

        @pl.when(k == AT_OUTPUT + 2)
        def _():
            loop(blocks, second_norm)

        @pl.when((k >= AT_HIDDEN) & (k < AT_HIDDEN + 8))
        def _():
            def body(n):
                j = 2 * (k - AT_HIDDEN) + n
                hidden_tile(j // 4, j % 4)

            loop(2, body)

        return carry

    lax.fori_loop(0, last_tick, tick, 0)
    start_all([copy for copy, (when, _, _) in zip(stores, plan) if when >= last_tick])
    for i in everything:
        pair_copies[i].wait_send()
        x_copy(i).wait_send()
        fwd_copy(i).wait_send()
        if not items[i][6]:
            for copy in (far_copy, near_copy, y_copy):
                copy(i).wait_send()
    for copy in bias_copies + halo_copies + sums_a + sums_b + sums_c:
        copy.wait_send()
    for copy in stores:
        copy.wait()


def softmax_rows(q, k, same):
    scores = jnp.where(same, dot_cols(q, k) * (1.0 / math.sqrt(HEAD_DIM)), -1e30)
    weights = jnp.exp(scores - jnp.max(scores, axis=-1, keepdims=True))
    return weights * (1.0 / jnp.sum(weights, axis=-1, keepdims=True))


def forward(smalls, vectors, tokens, cotangent, weights, rows):
    width = weights[0].shape[1]
    shape = jax.ShapeDtypeStruct
    full = shape((rows, D), F32)
    low = shape((rows, D), BF)
    wide = shape((rows, 4 * D), BF)
    outs = (
        low,
        low,
        shape((24, 128), F32),
        full,
        full,
        low,
        shape((rows, 12 * width), BF),
        low,
        low,
        low,
        wide,
        wide,
        shape((4, D, 3 * width), BF),
        shape((4, width, D), BF),
        shape((4, D, D), BF),
        shape((4, D, D), BF),
    )
    scratch = [shape((HALO + tokens.shape[0], D), BF)] * 2 + [
        low,
        low,
        full,
        full,
        low,
        outs[6],
        low,
        low,
        low,
        wide,
        wide,
    ]
    scratch += list(outs[12:]) + [
        shape((24, 128), F32),
        shape((4, 8, width), F32),
        shape((3, 24, 128), F32),
        shape((3, 24, 128), F32),
        shape((1, 24, 128), F32),
        shape((3, 24, 128), F32),
    ]
    dma = pltpu.SemaphoreType.DMA
    any_space = pl.BlockSpec(memory_space=pl.ANY)
    return pl.pallas_call(
        forward_kernel,
        out_shape=outs,
        in_specs=[pl.BlockSpec(memory_space=pltpu.SMEM)] * 4
        + [pl.BlockSpec(memory_space=pltpu.VMEM)] * 8
        + [any_space] * 8,
        out_specs=(any_space,) * len(outs),
        scratch_shapes=[pltpu.VMEM(v.shape, v.dtype) for v in scratch]
        + [
            dma((13,)),
            dma((2, 3)),
            dma((28,)),
            dma((3, 3)),
            dma((3, 3)),
            dma((3,)),
            dma((3,)),
        ]
        + [dma((13,))] * 12,
        compiler_params=pltpu.CompilerParams(
            collective_id=1, has_side_effects=True, vmem_limit_bytes=67043328
        ),
        name="forward",
    )(*smalls, *vectors, tokens, cotangent, *weights)


CHUNK = 128
CHUNKS = 24
FINISH_STEPS = 2
STAGE_DELAY = (0, 1, 3, 5, 7, 9, 11)
TICK_HIDDEN, TICK_SECOND, TICK_CONTEXT, TICK_HEADS = 1, 5, 6, 7
TICK_NORMED, TICK_FIRST, TICK_MIXED = 15, 19, 20
TICK_SUMS = (19, 21, 23, 25)
TICK_NEXT, TICK_LAYER, TICK_TOKENS = 26, 28, 29


def backward_kernel(
    lengths,
    groups,
    counts,
    gain,
    hidden_gain,
    down_bias,
    sums,
    tokens_ref,
    cotangent_ref,
    stream_ref,
    middle_ref,
    normed_ref,
    qkv_ref,
    context_ref,
    hidden_ref,
    grad_mixed_ref,
    active_ref,
    grad_pre_ref,
    wqkv_ref,
    wo_ref,
    wup_ref,
    wdown_ref,
    reduced_out,
    finals_out,
    layer_out,
    tokens_grad_out,
    made,
    pair,
    across,
    over_y,
    over_z,
    final,
    act,
    grad_pre,
    hidden,
    grad_mixed,
    context,
    normed,
    grad_attended,
    qkv,
    grad_context,
    rowbuf,
    gradient,
    trunk,
    stream,
    weight,
    packet,
    from_mp,
    from_y,
    from_z,
    layer_next,
    tokens_next,
    load_sem,
    act_sem,
    weight_sem,
    pair_send,
    pair_recv,
    across_send,
    across_recv,
    y_send,
    y_recv,
    z_send,
    z_recv,
    back_z_send,
    back_z_recv,
    back_y_send,
    back_y_recv,
    out_sem,
    stat_send,
    stat_recv,
    next_send,
    next_recv,
):
    mp, y, z, mp_peers, y_peer, z_places, z_peers = places()
    sibling, opposite, _ = mp_peers
    half = CHUNK // 2
    eighth = CHUNK // 8
    rows = normed.shape[0]
    rows_here = layer_out.shape[0]
    width = context.shape[1] // 4
    blocks = rows // 32

    loads = {
        name: pltpu.make_async_copy(source, target, load_sem.at[i])
        for i, (name, source, target) in enumerate(
            (
                ("grad_mixed", grad_mixed_ref, grad_mixed),
                ("grad_pre", grad_pre_ref, grad_pre),
                ("middle", middle_ref, trunk),
                ("cotangent", cotangent_ref, rowbuf),
                ("qkv", qkv_ref, qkv),
                ("hidden", hidden_ref, hidden),
                ("context", context_ref, context),
                ("normed", normed_ref, normed),
                ("stream", stream_ref, stream),
                ("tokens", tokens_ref, rowbuf),
                ("active", active_ref, grad_pre),
                ("middle again", middle_ref, stream),
                ("layer", normed.at[pl.ds(0, rows_here)], layer_out),
                ("tokens_grad", trunk.at[pl.ds(0, rows_here)], tokens_grad_out),
            )
        )
    }

    def act_loads(c):
        return [
            pltpu.make_async_copy(
                active_ref.at[:, pl.ds(pl.multiple_of(r * D + c * CHUNK, CHUNK), CHUNK)],
                act.at[c % 2, r],
                act_sem.at[c % 2, r],
            )
            for r in range(4)
        ]

    def weight_load(s):
        if s < 4:
            source = wup_ref.at[s]
        elif s == 4:
            source = wo_ref
        elif s < 9:
            source = wqkv_ref.at[s - 5]
        else:
            source = wdown_ref.at[s - 9]
        target = weight.at[s % 2, :, pl.ds(0, 3 * width)] if 5 <= s < 9 else weight.at[s % 2]
        return pltpu.make_async_copy(source, target, weight_sem.at[s % 2])

    for c in range(2):
        start_all(act_loads(c))
    loads["grad_mixed"].start()
    weight_load(0).start()
    loads["grad_pre"].start()
    weight_load(1).start()
    for name in ("middle", "cotangent", "qkv", "hidden", "context", "normed", "stream"):
        loads[name].start()
    greet(mp_peers + [y_peer] + z_peers)

    weights = [counts[groups[4 * mp + j]].astype(F32) for j in range(4)]
    slices = lax.axis_size("dp")
    count_valid = slices * PAIRS * PAIR_LEN
    column_mean = joined(sums, 0) / count_valid
    spread = joined(sums, 8) / count_valid - column_mean * column_mean
    inverse = lax.rsqrt(spread + 1e-05)
    mean_weight = sums[16:17, 0:1] / (slices * 16)

    def pair_copy(c):
        return remote(
            made.at[c % 2, pl.ds(0, 2)], pair.at[c], pair_send.at[c], pair_recv.at[c], sibling
        )

    def across_copy(c):
        return remote(
            pair.at[c, 1], across.at[c], across_send.at[c], across_recv.at[c], opposite
        )

    def y_copy(c):
        return remote(
            across.at[c, pl.ds(pl.multiple_of((1 - y) * half, half), half)],
            over_y.at[c],
            y_send.at[c],
            y_recv.at[c],
            y_peer,
        )

    def z_copies(c):
        return [
            remote(
                over_y.at[c, pl.ds(pl.multiple_of(place * eighth, eighth), eighth)],
                over_z.at[c, m],
                z_send.at[c, m],
                z_recv.at[c, m],
                peer,
            )
            for m, (place, peer) in enumerate(zip(z_places, z_peers))
        ]

    def back_z_copies(c):
        view = final.at[c, pl.ds(pl.multiple_of(y * half + z * eighth, eighth), eighth)]
        return [
            remote(view, view, back_z_send.at[c, m], back_z_recv.at[c, m], peer)
            for m, peer in enumerate(z_peers)
        ]

    def back_y_copy(c):
        view = final.at[c, pl.ds(pl.multiple_of(y * half, half), half)]
        return remote(view, view, back_y_send.at[c], back_y_recv.at[c], y_peer)

    def out_copy(c):
        return pltpu.make_async_copy(final.at[c], reduced_out.at[c], out_sem.at[c])

    def make(c):
        @pl.when(c < 8)
        def _():
            for copy in act_loads(c):
                copy.wait()

        def one(j):
            r = 2 * j + 1 - 5 * (j // 2)

            def store(left, right):
                made[c % 2, j] = dot_rows(left, right).astype(BF)

            @pl.when(c < 8)
            def _():
                store(act[c % 2, r], grad_mixed[...])

            @pl.when((c >= 8) & (c < 16))
            def _():
                store(
                    hidden[:, block_rows(c - 8, CHUNK)], grad_pre[:, block_rows(r, D)]
                )

            @pl.when((c >= 16) & (c < 18))
            def _():
                store(context[:, block_rows(2 * r + c - 16, CHUNK)], grad_attended[...])

            @pl.when(c >= 18)
            def _():
                store(qkv[:, block_rows(6 * r + c - 18, CHUNK)], normed[...])

        loop(4, one)

        @pl.when(c < 6)
        def _():
            start_all(act_loads(c + 2))

    def add_pair(c):
        pair_copy(c).wait()

        def body(i):
            here = block_rows(i, 32)
            for which in (1, 0):
                pair[c, which, here, :] = (
                    pair[c, which, here, :].astype(F32)
                    + made[c % 2, 2 + which, here, :].astype(F32)
                ).astype(BF)

        loop(CHUNK // 32, body)

    def add_across(c):
        across_copy(c).wait_recv()

        def body(i):
            here = block_rows(i, 32)
            across[c, here, :] = (
                across[c, here, :].astype(F32) + pair[c, 0, here, :].astype(F32)
            ).astype(BF)

        loop(CHUNK // 32, body)

    def add_y(c):
        y_copy(c).wait_recv()

        def body(i):
            here = block_rows(i, 32)
            own = pl.ds(pl.multiple_of(y * half + i * 32, 32), 32)
            over_y[c, here, :] = (
                over_y[c, here, :].astype(F32) + across[c, own, :].astype(F32)
            ).astype(BF)

        loop(half // 32, body)

    def add_z(c):
        wait_recv_all(z_copies(c))
        value = over_y[c, block_rows(z, eighth), :].astype(F32)
        for m in range(3):
            value = value + over_z[c, m].astype(F32)
        final[c, pl.ds(pl.multiple_of(y * half + z * eighth, eighth), eighth), :] = value.astype(BF)

    handle = (
        make,
        add_pair,
        add_across,
        add_y,
        add_z,
        lambda c: wait_recv_all(back_z_copies(c)),
        lambda c: back_y_copy(c).wait_recv(),
    )
    send = (
        lambda c: [pair_copy(c)],
        lambda c: [across_copy(c)],
        lambda c: [y_copy(c)],
        z_copies,
        back_z_copies,
        lambda c: [back_y_copy(c)],
        lambda c: [out_copy(c)],
    )

    def hidden_step(r):
        left = block_rows(r, D)

        def tile(n):
            columns = block_rows(n, 256)
            value = dot_cols(grad_pre[:, left], weight[r % 2, columns, :])

            @pl.when(r == 0)
            def _():
                gradient[:, columns] = value

            @pl.when(r > 0)
            def _():
                gradient[:, columns] = gradient[:, columns] + value

        loop(4, tile)

    def fold(value):
        return jnp.sum(value.reshape(4, 8, D), axis=0)

    def put(index, value):
        for j in range(8):
            packet[0, 8 * index + j : 8 * index + j + 1, :] = value[:, j * 128 : (j + 1) * 128]

    def put_all(first, values):
        for i, value in enumerate(values):
            put(first + i, jnp.sum(value, axis=0, keepdims=True))

    def ones_dot(value):
        return dot(jnp.ones((16, rows), BF), value)[0:1, :]

    def row_weight_of(i):
        row = i * 32 + lax.broadcasted_iota(jnp.int32, (32, 1), 0)
        item, _, in_pair, _ = item_of_rows(row, lengths, mp)
        return jnp.where(in_pair, choose_item(item, weights), 0.0) / mean_weight, in_pair

    zero = jnp.zeros((8, D), F32)

    def second_norm_back():
        def body(i, carry):
            here = block_rows(i, 32)
            unit, scale = stats(trunk[here, :])
            grad = gradient[here, :]
            row_weight, _ = row_weight_of(i)
            value = rowbuf[here, :].astype(F32) * row_weight + norm_back(
                grad, unit, scale, hidden_gain[...]
            )
            trunk[here, :] = value
            low = value.astype(BF)
            grad_attended[here, :] = low
            return (
                carry[0] + fold(grad * unit),
                carry[1] + fold(grad),
                carry[2] + fold(low.astype(F32)),
            )

        put_all(4, lax.fori_loop(0, blocks, body, (zero, zero, zero)))
        put(7, ones_dot(grad_mixed[...]))

    def context_step():
        def tile(n):
            columns = block_rows(n, 256)
            grad_context[:, columns] = dot_cols(grad_attended[...], weight[0, columns, :]).astype(BF)

        loop(4, tile)

    def head_pair_back(index):
        r = index // 2
        p = index % 2
        lanes = [block_rows(6 * r + 2 * n + p, 128) for n in range(3)]
        source = block_rows(2 * r + p, 128)
        factor = 1.0 / math.sqrt(HEAD_DIM)
        for first, size in blocks_of(rows):
            here = pl.ds(first, size)
            same = owner_of_rows(
                first + lax.broadcasted_iota(jnp.int32, (size, 1), 0), lengths, mp
            ) == owner_of_rows(first + lax.broadcasted_iota(jnp.int32, (1, size), 1), lengths, mp)
            q, k, v = [qkv[here, lane] for lane in lanes]
            g = grad_context[here, source]
            results = []
            for h in range(2):
                cut = slice(h * HEAD_DIM, (h + 1) * HEAD_DIM)
                soft = softmax_rows(q[:, cut], k[:, cut], same)
                grad_soft = dot_cols(g[:, cut], v[:, cut])
                center = jnp.sum(soft * grad_soft, axis=-1, keepdims=True)
                grad_scores = (soft * (grad_soft - center)).astype(BF)
                results.append(
                    (
                        (dot(grad_scores, k[:, cut]) * factor).astype(BF),
                        (dot_rows(grad_scores, q[:, cut]) * factor).astype(BF),
                        dot_rows(soft.astype(BF), g[:, cut]).astype(BF),
                    )
                )
            for n in range(3):
                qkv[here, lanes[n]] = jnp.concatenate([results[0][n], results[1][n]], axis=1)

    def normed_step(r):
        left = qkv[:, block_rows(r, 3 * width)]

        def tile(n):
            columns = block_rows(n, 256)
            value = dot_cols(left, weight[(r + 1) % 2, columns, 0 : 3 * width])

            @pl.when(r == 0)
            def _():
                gradient[:, columns] = value

            @pl.when(r > 0)
            def _():
                gradient[:, columns] = gradient[:, columns] + value

        loop(4, tile)

    def first_norm_back():
        def body(i, carry):
            here = block_rows(i, 32)
            unit, scale = stats(stream[here, :])
            grad = gradient[here, :]
            value = trunk[here, :] + norm_back(grad, unit, scale, gain[...])
            standard = (rowbuf[here, :].astype(F32) - column_mean) * inverse
            gradient[here, :] = value
            return (
                carry[0] + fold(value),
                carry[1] + fold(value * standard),
                carry[2] + fold(grad * unit),
                carry[3] + fold(grad),
            )

        put_all(0, lax.fori_loop(0, blocks, body, (zero, zero, zero, zero)))
        for r in range(4):
            if r:
                packet[r, 0:64, :] = packet[0, 0:64, :]
            parts = [
                ones_dot(qkv[:, (3 * r + n) * width : (3 * r + n + 1) * width]) for n in (0, 2)
            ] + [
                ones_dot(grad_pre[:, r * D + n * width : r * D + (n + 1) * width]) for n in range(4)
            ]
            for i, value in enumerate(parts):
                for j in range(2):
                    packet[r, 64 + 2 * i + j : 65 + 2 * i + j, :] = value[
                        :, j * 128 : (j + 1) * 128
                    ]
            packet[r, 76:80, :] = jnp.zeros((4, 128), F32)

    def mixed_step(r):
        left = grad_pre[:, block_rows(r, D)]

        def tile(n):
            columns = block_rows(n, 256)
            stream[:, columns] = stream[:, columns] + dot(left, weight[(r + 1) % 2, :, columns])

        loop(4, tile)

    def layer_step():
        def body(i):
            here = block_rows(i, 32)
            hidden[here, :] = (stream[here, :] + down_bias[...]).astype(BF)

        loop(blocks, body)

    def exchange(stage, sources, peers, slots):
        return [
            remote(
                source, slots.at[m], stat_send.at[stage, m], stat_recv.at[stage, m], peer
            )
            for m, (source, peer) in enumerate(zip(sources, peers))
        ]

    sums_a = exchange(0, [packet.at[r] for r in (1, 2, 3)], mp_peers, from_mp)
    sums_b = exchange(1, [packet.at[4]], [y_peer], from_y)
    sums_c = exchange(2, [packet.at[5]] * 3, z_peers, from_z)

    def gather_sums(first, copies, slots, target):
        value = packet[first]
        for m, copy in enumerate(copies):
            copy.wait_recv()
            value = value + slots[m]
        packet[target] = value

    def tokens_step():
        total = joined(packet[6], 0), joined(packet[6], 8)

        def body(i):
            here = block_rows(i, 32)
            standard = (rowbuf[here, :].astype(F32) - column_mean) * inverse
            _, in_pair = row_weight_of(i)
            share = jnp.where(in_pair, 1.0 / count_valid, 0.0)
            gradient[here, :] = inverse * (
                gradient[here, :] - share * (total[0] + total[1] * standard)
            )

        loop(blocks, body)

    before = {"mp": (mp + 3) % 4}
    layer_next_copy = remote(
        hidden.at[pl.ds(0, HALO)], layer_next, next_send.at[0], next_recv.at[0], before
    )
    tokens_next_copy = remote(
        gradient.at[pl.ds(0, HALO)], tokens_next, next_send.at[1], next_recv.at[1], before
    )

    def choose_rows(count, first):
        row = lax.broadcasted_iota(jnp.int32, (rows_here, count), 0)
        column = lax.broadcasted_iota(jnp.int32, (rows_here, count), 1) + first
        place = row + (rows_here - 2 * PAIR_LEN) * mp
        after = jnp.where(mp == 3, 2 * WINDOW, rows) - 2 * PAIR_LEN
        wanted = jnp.where(
            place < PAIR_LEN,
            place,
            jnp.where(place < 2 * PAIR_LEN, place + (WINDOW - PAIR_LEN), place + after),
        )
        return jnp.where(column == wanted, 1.0, 0.0).astype(BF)

    def own_rows(value, following, target):
        chosen, chosen_next = choose_rows(rows, 0), choose_rows(HALO, rows)
        pairs = ((chosen, value), (chosen_next, following))

        def tile(n):
            columns = block_rows(n, 256)
            total = jnp.zeros((rows_here, 256), F32)
            for matrix, ref in pairs:
                block = ref[:, columns]
                high = block.astype(BF)
                total = total + dot(matrix, high)
                if ref.dtype == F32:
                    middle_part = block - high.astype(F32)
                    low = middle_part.astype(BF)
                    total = total + dot(matrix, low)
                    total = total + dot(matrix, (middle_part - low.astype(F32)).astype(BF))
            target[0:rows_here, columns] = total.astype(target.dtype)

        loop(4, tile)

    def work(k):
        for s in range(4):

            @pl.when(k == TICK_HIDDEN + s)
            def _(s=s):
                if s == 0:
                    loads["grad_pre"].wait()
                weight_load(s).wait()

        @pl.when((k >= TICK_HIDDEN) & (k < TICK_HIDDEN + 4))
        def _():
            hidden_step(k - TICK_HIDDEN)

        for s in range(4):

            @pl.when(k == TICK_HIDDEN + s)
            def _(s=s):
                weight_load(s + 2).start()

        @pl.when(k == TICK_SECOND)
        def _():
            loads["middle"].wait()
            loads["cotangent"].wait()
            second_norm_back()
            loads["tokens"].start()

        @pl.when(k == TICK_CONTEXT)
        def _():
            weight_load(4).wait()
            context_step()
            weight_load(6).start()
            loads["qkv"].wait()

        @pl.when((k >= TICK_HEADS) & (k < TICK_HEADS + 8))
        def _():
            head_pair_back(k - TICK_HEADS)

        for s in range(4):

            @pl.when(k == TICK_NORMED + s)
            def _(s=s):
                weight_load(5 + s).wait()

        @pl.when((k >= TICK_NORMED) & (k < TICK_NORMED + 4))
        def _():
            normed_step(k - TICK_NORMED)

        for s in range(4):

            @pl.when(k == TICK_NORMED + s)
            def _(s=s):
                weight_load(7 + s).start()

        @pl.when(k == TICK_FIRST)
        def _():
            loads["stream"].wait()
            loads["tokens"].wait()
            first_norm_back()
            loads["active"].start()
            loads["middle again"].start()
            start_all(sums_a)

        for s in range(4):

            @pl.when(k == TICK_MIXED + s)
            def _(s=s):
                if s == 0:
                    loads["active"].wait()
                    loads["middle again"].wait()
                weight_load(9 + s).wait()

        @pl.when((k >= TICK_MIXED) & (k < TICK_MIXED + 4))
        def _():
            mixed_step(k - TICK_MIXED)

        for s in range(2):

            @pl.when(k == TICK_MIXED + s)
            def _(s=s):
                weight_load(11 + s).start()

        @pl.when(k == TICK_MIXED + 3)
        def _():
            layer_step()

        @pl.when(k == TICK_NEXT)
        def _():
            layer_next_copy.start()
            tokens_next_copy.start()

        @pl.when(k == TICK_LAYER)
        def _():
            layer_next_copy.wait_recv()
            own_rows(hidden, layer_next, normed)
            loads["layer"].start()

        @pl.when(k == TICK_TOKENS)
        def _():
            tokens_next_copy.wait_recv()
            own_rows(gradient, tokens_next, trunk)
            loads["tokens_grad"].start()

        @pl.when(k == TICK_SUMS[1])
        def _():
            gather_sums(0, sums_a, from_mp, 4)
            start_all(sums_b)

        @pl.when(k == TICK_SUMS[2])
        def _():
            gather_sums(4, sums_b, from_y, 5)
            start_all(sums_c)

        @pl.when(k == TICK_SUMS[3])
        def _():
            gather_sums(5, sums_c, from_z, 6)
            finals_out[...] = packet[6]
            tokens_step()

    waits = {0: ("grad_mixed",), 8: ("hidden",), 16: ("context",), 18: ("normed",)}

    def tick(k, carry):
        for when, names in waits.items():

            @pl.when(k == when)
            def _(names=names):
                for name in names:
                    loads[name].wait()

        def staged(stage, actions):
            c = k - STAGE_DELAY[stage]

            @pl.when((c >= 0) & (c < CHUNKS))
            def _():
                actions[stage](c)

        sends = tuple(lambda c, f=f: start_all(f(c)) for f in send)
        for stage in (6, 5, 4, 3, 2):
            staged(stage, handle)
        for stage in (2, 3, 4, 5, 6):
            staged(stage, sends)
        staged(0, handle)
        staged(1, handle)
        staged(0, sends)
        staged(1, sends)
        work(k)
        return carry

    lax.fori_loop(0, CHUNKS + STAGE_DELAY[-1], tick, 0)

    def finish(c):
        across_copy(c).wait_send()
        y_copy(c).wait_send()
        for copy in z_copies(c) + back_z_copies(c):
            copy.wait_send()
        back_y_copy(c).wait_send()
        out_copy(c).wait()

    loop(CHUNKS, finish)
    for copy in sums_a + sums_b + sums_c:
        copy.wait_send()
    layer_next_copy.wait_send()
    tokens_next_copy.wait_send()
    loads["layer"].wait()
    loads["tokens_grad"].wait()


def backward(smalls, vectors, sums, saved, rows_here):
    (
        tokens,
        cotangent,
        stream,
        middle,
        normed,
        qkv,
        context,
        hidden,
        grad_mixed,
        active,
        grad_pre,
        wqkv,
        wo,
        wup,
        wdown,
    ) = saved
    rows = normed.shape[0]
    shape = jax.ShapeDtypeStruct
    low = shape((rows, D), BF)
    full = shape((rows, D), F32)
    packed = shape((80, 128), F32)
    scratch = [
        shape((2, 4, CHUNK, D), BF),
        shape((CHUNKS, 2, CHUNK, D), BF),
        shape((CHUNKS, CHUNK, D), BF),
        shape((CHUNKS, CHUNK // 2, D), BF),
        shape((CHUNKS, 3, CHUNK // 8, D), BF),
        shape((CHUNKS, CHUNK, D), BF),
        shape((2, 4, rows, CHUNK), BF),
        shape(grad_pre.shape, BF),
        low,
        low,
        low,
        low,
        low,
        shape(qkv.shape, BF),
        low,
        low,
        full,
        full,
        full,
        shape((2, D, D), BF),
        shape((7, 80, 128), F32),
        shape((3, 80, 128), F32),
        shape((1, 80, 128), F32),
        shape((3, 80, 128), F32),
        shape((HALO, D), BF),
        shape((HALO, D), F32),
    ]
    dma = pltpu.SemaphoreType.DMA
    any_space = pl.BlockSpec(memory_space=pl.ANY)
    vmem = pl.BlockSpec(memory_space=pltpu.VMEM)
    return pl.pallas_call(
        backward_kernel,
        out_shape=(
            shape((CHUNKS, CHUNK, D), BF),
            packed,
            shape((rows_here, D), BF),
            shape((rows_here, D), F32),
        ),
        in_specs=[pl.BlockSpec(memory_space=pltpu.SMEM)] * 3 + [vmem] * 4 + [any_space] * 15,
        out_specs=(any_space, vmem, any_space, any_space),
        scratch_shapes=[pltpu.VMEM(v.shape, v.dtype) for v in scratch]
        + [
            dma((14,)),
            dma((2, 4)),
            dma((2,)),
            dma((CHUNKS,)),
            dma((CHUNKS,)),
            dma((CHUNKS,)),
            dma((CHUNKS,)),
            dma((CHUNKS,)),
            dma((CHUNKS,)),
            dma((CHUNKS, 3)),
            dma((CHUNKS, 3)),
            dma((CHUNKS, 3)),
            dma((CHUNKS, 3)),
            dma((CHUNKS,)),
            dma((CHUNKS,)),
            dma((CHUNKS,)),
            dma((3, 3)),
            dma((3, 3)),
            dma((2,)),
            dma((2,)),
        ],
        compiler_params=pltpu.CompilerParams(
            collective_id=2, has_side_effects=True, vmem_limit_bytes=67043328
        ),
        name="backward",
    )(
        *smalls,
        *vectors,
        sums,
        tokens,
        cotangent,
        stream,
        middle,
        normed,
        qkv,
        context,
        hidden,
        grad_mixed,
        active,
        grad_pre,
        wqkv,
        wo.reshape(D, D),
        wup,
        wdown,
    )


def finish_kernel(
    down_ref,
    up_ref,
    output_ref,
    query_ref,
    key_ref,
    value_ref,
    finals_ref,
    layer_ref,
    tokens_ref,
    down,
    up,
    output,
    query,
    key,
    value,
    layer,
    tokens,
    *vectors,
):
    for source, target in ((down_ref, down), (up_ref, up)):
        for i in range(source.shape[0]):
            target[i * CHUNK : (i + 1) * CHUNK, :] = source[i].astype(F32)
    output[...] = output_ref[0].astype(F32)
    for source, target in ((query_ref, query), (key_ref, key), (value_ref, value)):
        for half in range(2):
            target[:, half * CHUNK : (half + 1) * CHUNK] = source[half].astype(F32).T
    layer[...] = layer_ref[...]
    tokens[...] = tokens_ref[...]

    @pl.when(pl.program_id(0) == 0)
    def _():
        first = 0
        for target in vectors:
            size = target.shape[0]
            target[...] = finals_ref[first : first + size, :]
            first += size


def finish(reduced, finals, layer, tokens, width):
    shape = jax.ShapeDtypeStruct
    rows_here = layer.shape[0]
    steps = FINISH_STEPS
    share = rows_here // steps
    taken = 8 // steps
    sizes = (8,) * 8 + (2, 2, 8)
    own = [pl.BlockSpec((share, D), lambda c: (c, 0))] * 2
    specs = (
        [
            pl.BlockSpec((taken * CHUNK, D), lambda c: (c, 0)),
            pl.BlockSpec((taken * CHUNK, D), lambda c: (c, 0)),
            pl.BlockSpec((width // steps, D), lambda c: (c, 0)),
        ]
        + [pl.BlockSpec((taken * CHUNK, width), lambda c: (c, 0))] * 3
        + own
    )
    shapes = [
        shape((D, D), F32),
        shape((D, D), F32),
        shape((width, D), F32),
        shape((D, width), F32),
        shape((D, width), F32),
        shape((D, width), F32),
        shape((rows_here, D), BF),
        shape((rows_here, D), F32),
    ]
    return pl.pallas_call(
        finish_kernel,
        grid=(steps,),
        in_specs=[
            pl.BlockSpec((taken, CHUNK, D), lambda c: (c, 0, 0)),
            pl.BlockSpec((taken, CHUNK, D), lambda c: (steps + c, 0, 0)),
            pl.BlockSpec(
                (1, width // steps, D), lambda c: (16 + c // (steps // 2), c % (steps // 2), 0)
            ),
        ]
        + [
            pl.BlockSpec((2, CHUNK, taken * CHUNK), lambda c, first=first: (first, 0, c))
            for first in (9, 10, 11)
        ]
        + [pl.BlockSpec(finals.shape, lambda c: (0, 0))]
        + own,
        out_specs=specs + [pl.BlockSpec((size, 128), lambda c: (0, 0)) for size in sizes],
        out_shape=shapes + [shape((size, 128), F32) for size in sizes],
        name="finish",
    )(*[reduced] * 6, finals, layer, tokens)


def general_shards(
    tokens,
    cotangent,
    item_lengths,
    item_group,
    group_count,
    grid_scale,
    norm_gain,
    norm_shift,
    query_weight,
    query_bias,
    key_weight,
    value_weight,
    value_bias,
    output_weight,
    output_bias,
    hidden_gain,
    hidden_shift,
    up_weight,
    up_bias,
    down_weight,
    down_bias,
):
    shard_count = lax.axis_size("mp")
    slice_count = lax.axis_size("dp")
    mp = lax.axis_index("mp")
    rows_here = tokens.shape[0]
    item_count = item_lengths.shape[0]
    pairs_here = PAIRS // shard_count
    own_rows = pairs_here * PAIR_LEN
    shift = rows_here - own_rows
    halo = shift * (shard_count - 1)
    padding = rows_here * shard_count - PAIRS * PAIR_LEN
    tail_block = -(-padding // 32) * 32
    rows = pairs_here * WINDOW + tail_block
    is_last = mp == shard_count - 1

    width = query_weight.shape[1]
    qkv_own = jnp.concatenate([query_weight, key_weight, value_weight], axis=1)
    bias_own = jnp.concatenate([query_bias, value_bias, up_bias])[None, :]
    bias_across = swap_mp(bias_own, 2)
    bias_pair = swap_mp(jnp.concatenate([bias_own, bias_across], axis=0), 1)
    biases = [bias_own[0], bias_pair[0], bias_across[0], bias_pair[1]]

    def gather(own, direct):
        across = swap_mp(own, 2) if direct else fetch_across(own)
        return [own, swap_mp(own, 1), across, swap_mp(across, 1)]

    tokens_f = tokens.astype(F32)
    slice_row = mp * rows_here + jnp.arange(rows_here, dtype=jnp.int32)
    weighted = tokens_f * (slice_row < PAIRS * PAIR_LEN).astype(F32)[:, None]
    chosen = item_group[:, None] == jnp.arange(group_count.shape[0], dtype=jnp.int32)[None, :]
    item_scale = jnp.sum(jnp.where(chosen, grid_scale[None, :], 0.0), axis=1)
    item_weight = jnp.sum(jnp.where(chosen, group_count[None, :], 0), axis=1).astype(F32)
    sums = all_sum(
        jnp.stack(
            [
                jnp.sum(weighted, axis=0),
                jnp.sum(weighted * tokens_f, axis=0),
                jnp.broadcast_to(jnp.sum(item_weight) / shard_count, (D,)),
            ]
        )
    )

    def windows(v):
        before = lax.ppermute(
            v[rows_here - halo :], "mp", [(i, i + 1) for i in range(shard_count - 1)]
        )
        joined = jnp.concatenate([before, v], axis=0)
        start = halo - shift * mp
        parts = []
        for pair in range(pairs_here):
            parts.append(
                lax.dynamic_slice_in_dim(joined, start + pair * PAIR_LEN, PAIR_LEN, axis=0)
            )
            parts.append(jnp.zeros((WINDOW - PAIR_LEN, D), v.dtype))
        parts.append(jnp.where(is_last, v[rows_here - padding :], jnp.zeros((), v.dtype)))
        parts.append(jnp.zeros((tail_block - padding, D), v.dtype))
        return jnp.concatenate(parts, axis=0)

    def unwindows(v):
        own = jnp.concatenate(
            [v[pair * WINDOW : pair * WINDOW + PAIR_LEN] for pair in range(pairs_here)], axis=0
        )
        after = lax.ppermute(own[:halo], "mp", [(i + 1, i) for i in range(shard_count - 1)])
        after = jnp.concatenate([after, jnp.zeros((padding - halo, D), v.dtype)], axis=0)
        tail = v[pairs_here * WINDOW : pairs_here * WINDOW + padding]
        joined = jnp.concatenate([own, jnp.where(is_last, tail, after)], axis=0)
        return lax.dynamic_slice_in_dim(joined, shift * mp, rows_here, axis=0)

    tokens_w = windows(tokens).astype(F32)
    cotangent_w = windows(cotangent).astype(F32)

    row = jnp.arange(rows, dtype=jnp.int32)
    window = row // WINDOW
    offset = row % WINDOW
    in_pair = (window < pairs_here) & (offset < PAIR_LEN)
    is_padding = (window == pairs_here) & (offset < padding) & is_last
    pair = pairs_here * mp + window
    item_ids = jnp.arange(item_count, dtype=jnp.int32)
    first_len = jnp.sum(
        jnp.where(item_ids[None, :] == (2 * pair)[:, None], item_lengths[None, :], 0), axis=1
    )
    second = (offset >= first_len).astype(jnp.int32)
    owner = jnp.where(in_pair, 2 * pair + second, jnp.where(is_padding, item_count, -1))
    position = offset - second * first_len
    member = owner[:, None] == item_ids[None, :]
    row_scale = jnp.sum(jnp.where(member, item_scale[None, :], 0.0), axis=1)
    row_count = jnp.sum(jnp.where(member, item_weight[None, :], 0.0), axis=1)
    valid = in_pair.astype(F32)[:, None]
    quarter = D // 4
    frequency = jnp.exp(-math.log(10000.0) * jnp.arange(quarter, dtype=F32) / quarter)
    across_angle = ((position // SIDE).astype(F32) * row_scale)[:, None] * frequency
    side_angle = ((position % SIDE).astype(F32) * row_scale)[:, None] * frequency
    grid_table = (
        jnp.concatenate(
            [
                jnp.sin(across_angle),
                jnp.cos(across_angle),
                jnp.sin(side_angle),
                jnp.cos(side_angle),
            ],
            axis=-1,
        )
        * valid
    )
    owner_col = owner[:, None]
    owner_row = owner[None, :]

    qkv_weights = jnp.concatenate(gather(qkv_own, True), axis=1)
    output_weights = jnp.concatenate(gather(output_weight, False), axis=0)
    up_weights = jnp.concatenate(gather(up_weight, False), axis=1)
    down_weights = jnp.concatenate(gather(down_weight, False), axis=0)
    hidden_width = up_weight.shape[1]
    no_bias = jnp.zeros((width,), F32)
    qkv_bias = jnp.concatenate(
        [v for b in biases for v in (b[:width], no_bias, b[width : 2 * width])]
    )
    up_biases = jnp.concatenate([b[2 * width :] for b in biases])

    count_valid = slice_count * PAIRS * PAIR_LEN
    column_mean = sums[0] / count_valid
    spread = sums[1] / count_valid - column_mean * column_mean
    inverse = lax.rsqrt(spread + 1e-05)
    row_weight = row_count / (sums[2, 0] / (slice_count * item_count))
    standard = (tokens_w - column_mean) * inverse
    stream = standard + grid_table
    unit, unit_inverse = stats(stream)
    normed = (unit * norm_gain + norm_shift).astype(BF)

    qkv = (dot(normed, qkv_weights) + qkv_bias).astype(BF)
    context = attend(qkv, owner_col, owner_row, shard_count)
    middle = stream + (dot(context, output_weights) + output_bias)
    middle_unit, middle_inverse = stats(middle)
    hidden_in = (middle_unit * hidden_gain + hidden_shift).astype(BF)

    grad_out = cotangent_w * row_weight[:, None]
    grad_mixed = grad_out.astype(BF)
    active, slope = gelu_parts(dot(hidden_in, up_weights) + up_biases)
    mixed = dot(active, down_weights) + down_bias
    grad_pre = (dot_cols(grad_mixed, down_weights) * slope).astype(BF)
    grad_hidden = dot_cols(grad_pre, up_weights)
    layer_output = unwindows((middle + mixed).astype(BF))
    grad_middle = grad_out + norm_back(grad_hidden, middle_unit, middle_inverse, hidden_gain)
    grad_attended = grad_middle.astype(BF)

    grad_context = dot_cols(grad_attended, output_weights).astype(BF)
    grad_qkv = attend_back(qkv, grad_context, owner_col, owner_row, shard_count)
    grad_normed = dot_cols(grad_qkv, qkv_weights)

    pieces = range(shard_count)
    def columns(v, r, size):
        return v[:, r * size : (r + 1) * size]

    def reduced(left, right):
        return reduce_pieces([dot_rows(left(r), right(r)).astype(BF) for r in pieces])

    down_weight_grad = reduced(
        lambda r: columns(active, r, hidden_width), lambda r: grad_mixed
    )
    up_weight_grad = reduced(
        lambda r: hidden_in, lambda r: columns(grad_pre, r, hidden_width)
    )
    output_weight_grad = reduced(
        lambda r: columns(context, r, width), lambda r: grad_attended
    )
    qkv_weight_grad = reduced(lambda r: normed, lambda r: columns(grad_qkv, r, 3 * width))
    qkv_weight_grads = [columns(qkv_weight_grad, i, width) for i in range(3)]
    grad_stream = grad_middle + norm_back(grad_normed, unit, unit_inverse, norm_gain)

    def column_sums(v):
        return jnp.sum(v.astype(F32), axis=0)

    qkv_sums = column_sums(grad_qkv)
    up_sums = column_sums(grad_pre)
    bias_grads = [
        jnp.concatenate(
            [
                qkv_sums[3 * r * width : (3 * r + 1) * width],
                qkv_sums[(3 * r + 2) * width : 3 * (r + 1) * width],
                up_sums[r * hidden_width : (r + 1) * hidden_width],
            ]
        )[None, :]
        for r in pieces
    ]
    got = swap_mp(jnp.concatenate([bias_grads[1], bias_grads[3]], axis=0), 1)
    bias_grad = bias_grads[0] + got[:1] + swap_mp(bias_grads[2] + got[1:], 2)
    for bit in range(dp_bits()):
        bias_grad = bias_grad + swap_dp(bias_grad, 1 << bit)
    bias_grad = bias_grad[0]
    finals = all_sum(
        jnp.stack(
            [
                column_sums(grad_stream),
                column_sums(grad_stream * standard),
                column_sums(grad_normed * unit),
                column_sums(grad_normed),
                column_sums(grad_hidden * middle_unit),
                column_sums(grad_hidden),
                column_sums(grad_attended),
                column_sums(grad_mixed),
            ]
        )
    )
    tokens_grad = unwindows(
        inverse * (grad_stream - valid / count_valid * (finals[0] + finals[1] * standard))
    )
    return (
        layer_output,
        tokens_grad,
        finals[2],
        finals[3],
        qkv_weight_grads[0],
        bias_grad[:width],
        qkv_weight_grads[1],
        qkv_weight_grads[2],
        bias_grad[width : 2 * width],
        output_weight_grad,
        finals[6],
        finals[4],
        finals[5],
        up_weight_grad,
        bias_grad[2 * width :],
        down_weight_grad,
        finals[7],
    )


def fast_shards(
    tokens,
    cotangent,
    item_lengths,
    item_group,
    group_count,
    grid_scale,
    norm_gain,
    norm_shift,
    query_weight,
    query_bias,
    key_weight,
    value_weight,
    value_bias,
    output_weight,
    output_bias,
    hidden_gain,
    hidden_shift,
    up_weight,
    up_bias,
    down_weight,
    down_bias,
):
    rows = 2 * WINDOW + 96
    saved = forward(
        (item_lengths, item_group, group_count, grid_scale),
        [
            v[None, :]
            for v in (
                norm_gain,
                norm_shift,
                output_bias,
                hidden_gain,
                hidden_shift,
                query_bias,
                value_bias,
                up_bias,
            )
        ],
        tokens,
        cotangent,
        (query_weight, key_weight, value_weight, output_weight, up_weight, down_weight),
        rows,
    )
    reduced, finals, layer_output, tokens_grad = backward(
        (item_lengths, item_group, group_count),
        [v[None, :] for v in (norm_gain, hidden_gain, down_bias)],
        saved[2],
        saved[:2] + saved[3:],
        tokens.shape[0],
    )
    (
        down_weight_grad,
        up_weight_grad,
        output_weight_grad,
        query_weight_grad,
        key_weight_grad,
        value_weight_grad,
        layer_output,
        tokens_grad,
        *vectors,
    ) = finish(reduced, finals, layer_output, tokens_grad, query_weight.shape[1])
    vectors = [v.reshape(-1) for v in vectors]
    return (
        layer_output,
        tokens_grad,
        vectors[2],
        vectors[3],
        query_weight_grad,
        vectors[8],
        key_weight_grad,
        value_weight_grad,
        vectors[9],
        output_weight_grad,
        vectors[6],
        vectors[4],
        vectors[5],
        up_weight_grad,
        vectors[10],
        down_weight_grad,
        vectors[7],
    )


def shards(*args):
    if lax.axis_size("dp") == 8 and lax.axis_size("mp") == 4 and args[0].shape == (512, D):
        return fast_shards(*args)
    return general_shards(*args)


def solution(mesh):
    rows = P(("dp", "mp"), None)
    columns = P(None, "mp")
    return jax.shard_map(
        shards,
        mesh=mesh,
        in_specs=(
            rows,
            rows,
            P("dp"),
            P("dp"),
            P(),
            P(),
            P(),
            P(),
            columns,
            P("mp"),
            columns,
            columns,
            P("mp"),
            P("mp", None),
            P(),
            P(),
            P(),
            columns,
            P("mp"),
            P("mp", None),
            P(),
        ),
        out_specs=(
            rows,
            rows,
            P(),
            P(),
            columns,
            P("mp"),
            columns,
            columns,
            P("mp"),
            P("mp", None),
            P(),
            P(),
            P(),
            columns,
            P("mp"),
            P("mp", None),
            P(),
        ),
        check_vma=False,
    )
```
